32 devices in a mesh: row: 8 (over y, x, core), col: 4 (over z).
Axes of the slice: x: 2, y: 2, z: 4, core: 2. Of those that a mesh axis runs over, the one named last changes fastest.
Arguments:
- tokens_in: bfloat16 [32768, 1024], P('row', 'col'), may hold values from -36 to 36
- pad_offsets: int32 [8, 2], P('row'), may hold values from 0 to 6
- norm1_gain: float32 [1024], P('col'), may hold values from 0.5 to 1.5
- norm1_bias: float32 [1024], P('col'), may hold values from -1.25 to 1.25
- qkv_weight: bfloat16 [1024, 3, 1024], P('row', None, 'col'), may hold values from -0.1875 to 0.1875
- qv_bias: bfloat16 [2, 1024], P(None, 'col'), may hold values from -1.75 to 1.75
- table_height: float32 [27, 64], replicated, may hold values from -0.875 to 0.875
- table_width: float32 [27, 64], replicated, may hold values from -0.875 to 0.875
- proj_weight: bfloat16 [1024, 1024], P('col', 'row'), may hold values from -0.5 to 0.5
- proj_bias: bfloat16 [1024], P('col'), may hold values from -1.75 to 1.75
- norm2_gain: float32 [1024], P('col'), may hold values from 0.5 to 1.5
- norm2_bias: float32 [1024], P('col'), may hold values from -1.25 to 1.25
- fc1_weight: bfloat16 [1024, 4096], P('row', 'col'), may hold values from -0.1875 to 0.1875
- fc1_bias: bfloat16 [4096], P('col'), may hold values from -1.75 to 1.75
- fc2_weight: bfloat16 [4096, 1024], P('col', 'row'), may hold values from -0.09375 to 0.09375
- fc2_bias: bfloat16 [1024], P('col'), may hold values from -1.75 to 1.75
- out_grad: bfloat16 [32768, 1024], P('row', 'col'), may hold values from -8 to 8
Outputs:
- block_out: bfloat16 [32768, 1024], P('row', 'col')
- input_grad: float32 [32768, 1024], P('row', 'col')
- norm1_gain_grad: float32 [1024], P('col')
- norm1_bias_grad: float32 [1024], P('col')
- qkv_weight_grad: float32 [1024, 3, 1024], P('row', None, 'col')
- qv_bias_grad: float32 [2, 1024], P(None, 'col')
- table_height_grad: float32 [27, 64], replicated
- table_width_grad: float32 [27, 64], replicated
- proj_weight_grad: float32 [1024, 1024], P('col', 'row')
- proj_bias_grad: float32 [1024], P('col')
- norm2_gain_grad: float32 [1024], P('col')
- norm2_bias_grad: float32 [1024], P('col')
- fc1_weight_grad: float32 [1024, 4096], P('row', 'col')
- fc1_bias_grad: float32 [4096], P('col')
- fc2_weight_grad: float32 [4096, 1024], P('col', 'row')
- fc2_bias_grad: float32 [1024], P('col')
The draws below stay inside these ranges and needn't reach their ends.
All inputs are finite; a program needn't handle non-finite values.
Results may differ from the reference program's by a relative error of at most 0.012.
The reference program's roundings to bfloat16 on the way count: a program that leaves them out, or rounds other values in their place, can miss the bound.
Values may be sent and summed in bfloat16 or wider, within the bound.
No kernel may reach another device: no remote copies, remote signals or barrier semaphores. Data moves between devices by JAX's collectives and lax.ppermute only.
A program may use at most 256 MiB of HBM per device.

```python
import math
import jax
import jax.numpy as jnp
from jax import lax

D = 1024
H = 16
HD = 64
FF = 4096
WIN = 14
SIDE = 64
GRID = 5
CANVAS = 70
SLOTS = 4900
PIX = 4096
RELN = 27
IMAGES = 8
TOKENS = 32768


def draw_tokens_in(key, part):
    key_base, key_rows, key_cols = jax.random.split(key, 3)
    base = jnp.clip(jax.random.normal(key_base, (TOKENS, D), jnp.float32), -4.0, 4.0)
    row_scale = jnp.exp(jax.random.uniform(key_rows, (TOKENS, 1), jnp.float32, math.log(0.3), math.log(3.0)))
    ramp = jnp.exp(jnp.arange(D, dtype=jnp.float32) * (math.log(3.0) / D))[None, :]
    col_scale = jnp.exp(jax.random.uniform(key_cols, (1, D), jnp.float32, math.log(0.3), math.log(1.0))) * ramp
    return (base * row_scale * col_scale).astype(jnp.bfloat16)


def with_ends(drawn, key, low, largest):
    spot = [jax.random.randint(jax.random.fold_in(key, axis), (), 0, length) for axis, length in enumerate(drawn.shape)]
    widest = drawn.shape.index(max(drawn.shape))
    next_to = spot[:widest] + [(spot[widest] + 1) % drawn.shape[widest]] + spot[widest + 1:]
    return drawn.at[tuple(spot)].set(low).at[tuple(next_to)].set(largest)


def with_spikes(array, own_key, source, target, parts, factor):
    def block_of(axis_at):
        return (jnp.arange(array.shape[axis_at]) // (array.shape[axis_at] // parts)).reshape((-1,) + (1,) * (array.ndim - 1 - axis_at))

    first = jax.random.permutation(own_key, parts)[block_of(target)]
    other_side = (block_of(target) + parts // 2) % parts
    return jnp.where((block_of(source) == first) | (block_of(source) == other_side), factor * array, array)


def levels(stream_key, shape, cuts, least, top_value):
    factor_of = 1.0
    for dim, shards_of in cuts:
        steps = jax.random.uniform(jax.random.fold_in(jax.random.fold_in(stream_key, 6), dim), (shards_of,), jnp.float32, least / len(cuts), top_value / len(cuts))
        factor_of = factor_of * jnp.repeat(jnp.exp(steps), shape[dim] // shards_of).reshape((-1,) + (1,) * (len(shape) - 1 - dim))
    return factor_of


def noise(key, extent, deviation, most, cuts=(), kind=jnp.bfloat16):
    factor_of = levels(key, extent, cuts, -0.22, 0.18) if cuts else 1.0
    entries = jax.random.normal(key, extent, jnp.float32) * deviation * factor_of
    return jnp.minimum(jnp.maximum(entries, -most), most).astype(kind)


def noise_with(stream_key, shape, width, limit, cuts, heavy, kind=jnp.bfloat16):
    values = width * jax.random.normal(stream_key, shape, jnp.float32)
    if cuts:
        values = values * levels(stream_key, shape, cuts, -0.22, 0.18)
    return jnp.clip(with_spikes(values, jax.random.fold_in(stream_key, 3), *heavy), -limit, limit).astype(kind)


def setup_inputs(seed: int = 0) -> dict:
    keys = jax.random.split(jax.random.key(seed), 18)
    return {
        "tokens_in": draw_tokens_in(jax.random.fold_in(keys[17], 71), 0),
        "pad_offsets": with_ends(jax.random.randint(keys[1], (IMAGES, 2), 0, CANVAS - SIDE + 1), jax.random.fold_in(keys[1], 1), 0, CANVAS - SIDE).astype(jnp.int32),
        "norm1_gain": jnp.clip(1.0 + 0.1 * jax.random.normal(keys[2], (D,), jnp.float32), 0.5, 1.5),
        "norm1_bias": noise(keys[3], (D,), 0.2, 1.25, ((0, 4),), jnp.float32),
        "qkv_weight": noise(keys[4], (D, 3, D), D ** -0.5, 0.1875, ((0, 8), (2, 4))),
        "qv_bias": noise(keys[5], (2, D), 0.3, 1.75, ((1, 4),)),
        "table_height": noise(keys[6], (RELN, HD), 0.15, 0.875, (), jnp.float32),
        "table_width": noise(keys[7], (RELN, HD), 0.15, 0.875, (), jnp.float32),
        "proj_weight": noise(keys[8], (D, D), (D // 8) ** -0.5, 0.5, ((0, 4), (1, 8))),
        "proj_bias": noise(keys[9], (D,), 0.3, 1.75, ((0, 4),)),
        "norm2_gain": jnp.clip(1.0 + 0.1 * jax.random.normal(keys[10], (D,), jnp.float32), 0.5, 1.5),
        "norm2_bias": noise(keys[11], (D,), 0.2, 1.25, ((0, 4),), jnp.float32),
        "fc1_weight": noise(keys[12], (D, FF), D ** -0.5, 0.1875, ((0, 8), (1, 4))),
        "fc1_bias": noise(keys[13], (FF,), 0.3, 1.75, ((0, 4),)),
        "fc2_weight": noise(keys[14], (FF, D), FF ** -0.5, 0.09375, ((0, 4), (1, 8))),
        "fc2_bias": noise(keys[15], (D,), 0.3, 1.75, ((0, 4),)),
        "out_grad": noise_with(keys[16], (TOKENS, D), 1.0, 8.0, ((0, 8), (1, 4)), (0, 1, 8, 2.0)),
    }


EPSILON = 1e-06
HIGHEST = lax.Precision.HIGHEST

@jax.custom_vjp
def low(v):
    return lax.optimization_barrier(v.astype(jnp.bfloat16)).astype(jnp.float32)

@jax.custom_vjp
def low_back(v):
    return v

def low_keep(v):
    return (low(v), None)

def low_pass(kept, grad):
    return (grad,)

def back_keep(v):
    return (v, None)

def back_low(kept, grad):
    return (low(grad),)
low.defvjp(low_keep, low_pass)
low_back.defvjp(back_keep, back_low)

def slot_layout(offsets):
    top_row = offsets[0]
    left_col = offsets[1]
    slot_ids = jnp.arange(SLOTS, dtype=jnp.int32)
    window = slot_ids // (WIN * WIN)
    inside = slot_ids % (WIN * WIN)
    canvas_row = window // GRID * WIN + inside // WIN - top_row
    canvas_col = window % GRID * WIN + inside % WIN - left_col
    present = (canvas_row >= 0) & (canvas_row < SIDE) & (canvas_col >= 0) & (canvas_col < SIDE)
    source = jnp.clip(canvas_row, 0, SIDE - 1) * SIDE + jnp.clip(canvas_col, 0, SIDE - 1)
    pixels = jnp.arange(PIX, dtype=jnp.int32)
    pixel_row = pixels // SIDE + top_row
    pixel_col = pixels % SIDE + left_col
    target = ((pixel_row // WIN * GRID + pixel_col // WIN) * WIN + pixel_row % WIN) * WIN + pixel_col % WIN
    return (source.astype(jnp.int32), present, target.astype(jnp.int32))

def pick_tables():
    places = jnp.arange(WIN * WIN, dtype=jnp.int32)
    others = jnp.arange(WIN, dtype=jnp.int32)
    rel_index = jnp.arange(2 * WIN - 1, dtype=jnp.int32)
    pick_h = ((places // WIN)[:, None, None] - others[None, :, None] + WIN - 1 == rel_index[None, None, :]).astype(jnp.float32)
    pick_w = ((places % WIN)[:, None, None] - others[None, :, None] + WIN - 1 == rel_index[None, None, :]).astype(jnp.float32)
    return (pick_h, pick_w)

def layer_norm(values, gain_vec, bias_vec):
    row_mean = lax.optimization_barrier(jnp.mean(values, axis=-1, keepdims=True))
    centred = values - row_mean
    spread = lax.optimization_barrier(jnp.mean(centred * centred, axis=-1, keepdims=True))
    return centred * lax.rsqrt(spread + EPSILON) * gain_vec + bias_vec

def window_group(queries, keys_in, values_in, table_h, table_w):
    pick_h, pick_w = pick_tables()
    groups = queries.shape[0]
    head_count = queries.shape[2]
    direct = jnp.einsum('wqhc,wkhc->whqk', queries, keys_in, precision=HIGHEST) * HD ** (-0.5)
    along_h = jnp.einsum('wqhc,jc->wqhj', queries, table_h, precision=HIGHEST)
    along_w = jnp.einsum('wqhc,jc->wqhj', queries, table_w, precision=HIGHEST)
    rel_h = jnp.einsum('wqhj,qkj->whqk', along_h, pick_h, precision=HIGHEST)
    rel_w = jnp.einsum('wqhj,qkj->whqk', along_w, pick_w, precision=HIGHEST)
    scores = direct.reshape(groups, head_count, WIN * WIN, WIN, WIN) + rel_h[..., :, None] + rel_w[..., None, :]
    scores = low_back(scores.reshape(groups, head_count, WIN * WIN, WIN * WIN))
    probs_low = low(jax.nn.softmax(scores, axis=-1))
    attended = jnp.einsum('whqk,wkhc->wqhc', probs_low, values_in, precision=HIGHEST)
    return low(low_back(attended))

def forward(tokens, offsets, norm1_gain, norm1_bias, qkv_weight, qv_bias, table_height, table_width, proj_weight, proj_bias, norm2_gain, norm2_bias, fc1_weight, fc1_bias, fc2_weight, fc2_bias):
    source, present, target = slot_layout(offsets)
    norm_one = low(layer_norm(tokens, norm1_gain, norm1_bias))
    bias_row = jnp.concatenate([qv_bias[0], jnp.zeros_like(qv_bias[0]), qv_bias[1]])
    qkv_tok = jnp.dot(norm_one, qkv_weight.reshape(D, 3 * D), precision=HIGHEST) + bias_row
    slot_vals = jnp.where(present[:, None], qkv_tok[source], bias_row[None, :])
    slot_vals = low(low_back(slot_vals))
    grouped = slot_vals.reshape(GRID, GRID, WIN * WIN, 3, H, HD)
    table_h = low(table_height)
    table_w = low(table_width)

    def group_fn(window_set):
        return window_group(window_set[:, :, 0], window_set[:, :, 1], window_set[:, :, 2], table_h, table_w)
    attended = lax.map(jax.checkpoint(group_fn), grouped)
    attended_tok = attended.reshape(SLOTS, D)[target]
    proj_out = low_back(jnp.dot(attended_tok, proj_weight, precision=HIGHEST) + proj_bias)
    residual = tokens + proj_out
    norm_two = low(layer_norm(residual, norm2_gain, norm2_bias))
    pre_act = low_back(jnp.dot(norm_two, fc1_weight, precision=HIGHEST) + fc1_bias)
    act_low = low(jax.nn.gelu(pre_act, approximate=False))
    mlp_out = low_back(jnp.dot(act_low, fc2_weight, precision=HIGHEST) + fc2_bias)
    return residual + mlp_out

def reference(tokens_in, pad_offsets, norm1_gain, norm1_bias, qkv_weight, qv_bias, table_height, table_width, proj_weight, proj_bias, norm2_gain, norm2_bias, fc1_weight, fc1_bias, fc2_weight, fc2_bias, out_grad):
    params = tuple((p.astype(jnp.float32) for p in (norm1_gain, norm1_bias, qkv_weight, qv_bias, table_height, table_width, proj_weight, proj_bias, norm2_gain, norm2_bias, fc1_weight, fc1_bias, fc2_weight, fc2_bias)))
    image_x = tokens_in.astype(jnp.float32).reshape(IMAGES, PIX, D)
    image_cot = out_grad.astype(jnp.float32).reshape(IMAGES, PIX, D)

    def image_step(totals, image_item):
        tok_rows, offsets, cot_rows = image_item

        def local_fn(tok_in, *params_in):
            return forward(tok_in, offsets, *params_in)
        image_out, pullback = jax.vjp(local_fn, tok_rows, *params)
        all_grads = pullback(cot_rows)
        totals = tuple((t + g for t, g in zip(totals, all_grads[1:])))
        return (totals, (image_out.astype(jnp.bfloat16), all_grads[0]))
    zero_grads = tuple((jnp.zeros_like(p) for p in params))
    totals, (out_rows, grad_rows) = lax.scan(image_step, zero_grads, (image_x, pad_offsets, image_cot))
    return (out_rows.reshape(TOKENS, D), grad_rows.reshape(TOKENS, D), totals[0], totals[1], totals[2], totals[3], totals[4], totals[5], totals[6], totals[7], totals[8], totals[9], totals[10], totals[11], totals[12], totals[13])
```

```python
from functools import partial
import math

import jax
import jax.numpy as jnp
import numpy as np
from jax import lax
from jax.experimental import pallas as pl
from jax.experimental.pallas import tpu as pltpu
from jax.sharding import PartitionSpec as P

D = 1024
HD = 64
WIN = 14
SIDE = 64
GRID = 5
WINDOWS = 25
REAL = 196
SLOT = 200
KEYS = 256
PIX = 4096
EPSILON = 1e-06
MARGIN = 6
PADROWS = 84
BF = jnp.bfloat16
F32 = jnp.float32
VMEM_LIMIT = 60 * 1024 * 1024


def iota(shape, dim):
    return lax.broadcasted_iota(jnp.int32, shape, dim)


def params(n=1):
    return pltpu.CompilerParams(
        dimension_semantics=("arbitrary",) * n, vmem_limit_bytes=VMEM_LIMIT
    )


def nt_dot(a, b):
    return lax.dot_general(a, b, (((1,), (1,)), ((), ())), preferred_element_type=F32)


def tn_dot(a, b):
    return lax.dot_general(a, b, (((0,), (0,)), ((), ())), preferred_element_type=F32)


def nn_dot(a, b):
    return lax.dot_general(a, b, (((1,), (0,)), ((), ())), preferred_element_type=F32)


def spread_kernel(cols, per, info, x_ref, *refs):
    outs, padded = refs[:cols], refs[cols]
    step = pl.program_id(0)
    me = info[0]
    top = info[1]
    left = info[2]
    width = x_ref.shape[1]

    @pl.when(step == 0)
    def _():
        padded[: MARGIN * SIDE, :] = jnp.zeros((MARGIN * SIDE, width), BF)
        padded[(MARGIN + SIDE) * SIDE :, :] = jnp.zeros(
            ((PADROWS - MARGIN - SIDE) * SIDE, width), BF
        )
        padded[MARGIN * SIDE : (MARGIN + SIDE) * SIDE, :] = x_ref[...]

    slot = iota((56, 256), 0)
    token = iota((56, 256), 1)
    same_row = slot // WIN == token // SIDE
    for k in range(cols):
        window = (me ^ k) * per + step
        win_row = jnp.minimum(window // GRID, GRID - 1)
        win_col = window % GRID
        pick = same_row & (slot % WIN + (WIN * win_col - left) == token % SIDE)
        pick = pick & (window < WINDOWS)
        tail = pick & (slot < 28)
        pick = pick.astype(F32).astype(BF)
        tail = tail.astype(F32).astype(BF)
        parts = []
        for g in range(4):
            base = pl.multiple_of((WIN * win_row + 4 * g - top + MARGIN) * SIDE, SIDE)
            rows = padded[pl.ds(base, 256), :]
            parts.append(nn_dot(pick if g < 3 else tail[:32], rows))
        outs[k][0] = jnp.concatenate(parts, axis=0).astype(BF)


def spread(x, info, cols, per):
    width = x.shape[1]
    piece = jax.ShapeDtypeStruct((per, SLOT, width), BF)
    return pl.pallas_call(
        partial(spread_kernel, cols, per),
        out_shape=[piece] * cols,
        grid_spec=pltpu.PrefetchScalarGridSpec(
            num_scalar_prefetch=1,
            grid=(per,),
            in_specs=[pl.BlockSpec((PIX, width), lambda i, s: (0, 0))],
            out_specs=[pl.BlockSpec((1, SLOT, width), lambda i, s: (i, 0, 0))] * cols,
            scratch_shapes=[pltpu.VMEM((PADROWS * SIDE, width), BF)],
        ),
        compiler_params=params(),
        name="spread",
    )(info, x)


def collect_kernel(cols, per, info, *refs):
    pieces, out, held, picks, padded = refs[:cols], refs[cols], refs[cols + 1], refs[cols + 2], refs[cols + 3]
    step = pl.program_id(0)
    me = info[0]
    top = info[1]
    left = info[2]

    @pl.when(step == 0)
    def _():
        for k in range(cols):
            first = (me ^ k) * per
            for i in range(per):
                held[first + i] = pieces[k][i]
        token = iota((WIN * SIDE, SLOT), 0)
        slot = iota((WIN * SIDE, SLOT), 1)
        same_row = (slot // WIN == token // SIDE) & (slot < REAL)
        shift = token % SIDE - slot % WIN + left
        for j in range(GRID):
            picks[j] = (same_row & (shift == WIN * j)).astype(F32).astype(BF)

    total = nn_dot(picks[0], held[step * GRID])
    for j in range(1, GRID):
        total = total + nn_dot(picks[j], held[step * GRID + j])
    base = pl.multiple_of((WIN * step - top + MARGIN) * SIDE, SIDE)
    padded[pl.ds(base, WIN * SIDE), :] = total.astype(padded.dtype)

    @pl.when(step == GRID - 1)
    def _():
        out[...] = padded[MARGIN * SIDE : (MARGIN + SIDE) * SIDE, :].astype(out.dtype)


def collect(pieces, info, cols, per, dtype):
    width = pieces[0].shape[-1]
    return pl.pallas_call(
        partial(collect_kernel, cols, per),
        out_shape=jax.ShapeDtypeStruct((PIX, width), dtype),
        grid_spec=pltpu.PrefetchScalarGridSpec(
            num_scalar_prefetch=1,
            grid=(GRID,),
            in_specs=[pl.BlockSpec((per, SLOT, width), lambda i, s: (0, 0, 0))] * cols,
            out_specs=pl.BlockSpec((PIX, width), lambda i, s: (0, 0)),
            scratch_shapes=[
                pltpu.VMEM((cols * per, SLOT, width), BF),
                pltpu.VMEM((GRID, WIN * SIDE, SLOT), BF),
                pltpu.VMEM((PADROWS * SIDE, width), BF),
            ],
        ),
        compiler_params=params(),
        name="collect",
    )(info, *pieces)


def present_mask(window, top, left, shape):
    slot = iota(shape, 0)
    row = WIN * (window // GRID) - top + slot // WIN
    col = WIN * (window % GRID) - left + slot % WIN
    inside = (row >= 0) & (row < SIDE) & (col >= 0) & (col < SIDE)
    return inside & (slot < REAL) & (window < WINDOWS)


def gather_features(pieces, me, whole):
    width = pieces[0].shape[-1]
    for k, piece in enumerate(pieces):
        first = pl.multiple_of((me ^ k) * width, 128)
        whole[:, pl.ds(first, width)] = piece[0].astype(F32)
    return whole[...]


def norm1_kernel(cols, per, info, *refs):
    pieces = refs[:cols]
    gain, bias, x_out, n_out, whole = refs[cols:]
    me = info[0]
    values = gather_features(pieces, me, whole)
    x_out[...] = values.astype(BF)
    mean = jnp.mean(values, axis=1, keepdims=True)
    centred = values - mean
    spread_sq = jnp.mean(centred * centred, axis=1, keepdims=True)
    normed = centred * lax.rsqrt(spread_sq + EPSILON) * gain[...] + bias[...]
    keep = present_mask(me * per + pl.program_id(0), info[1], info[2], (SLOT, D))
    n_out[...] = jnp.where(keep, normed, 0.0).astype(BF)


def norm1(pieces, info, gain, bias, cols, per):
    width = pieces[0].shape[-1]
    rows = per * SLOT
    vec = pl.BlockSpec((1, D), lambda i, s: (0, 0))
    out = jax.ShapeDtypeStruct((rows, D), BF)
    return pl.pallas_call(
        partial(norm1_kernel, cols, per),
        out_shape=[out, out],
        grid_spec=pltpu.PrefetchScalarGridSpec(
            num_scalar_prefetch=1,
            grid=(per,),
            in_specs=[pl.BlockSpec((1, SLOT, width), lambda i, s: (i, 0, 0))] * cols + [vec, vec],
            out_specs=[pl.BlockSpec((SLOT, D), lambda i, s: (i, 0))] * 2,
            scratch_shapes=[pltpu.VMEM((SLOT, D), F32)],
        ),
        compiler_params=params(),
        name="norm1",
    )(info, *pieces, gain, bias)


def join_kernel(cols, info, *refs):
    pieces, out, whole = refs[:cols], refs[cols], refs[cols + 1]
    out[...] = gather_features(pieces, info[0], whole).astype(BF)


def join(pieces, info, cols, per):
    width = pieces[0].shape[-1]
    return pl.pallas_call(
        partial(join_kernel, cols),
        out_shape=jax.ShapeDtypeStruct((per * SLOT, D), BF),
        grid_spec=pltpu.PrefetchScalarGridSpec(
            num_scalar_prefetch=1,
            grid=(per,),
            in_specs=[pl.BlockSpec((1, SLOT, width), lambda i, s: (i, 0, 0))] * cols,
            out_specs=pl.BlockSpec((SLOT, D), lambda i, s: (i, 0)),
            scratch_shapes=[pltpu.VMEM((SLOT, D), F32)],
        ),
        compiler_params=params(),
        name="join",
    )(info, *pieces)


def rel_constants():
    place = np.arange(SLOT)
    lanes = np.arange(128)
    group = lanes // 32
    row_shift = np.clip(WIN - 1 - place // WIN, 0, WIN - 1)
    col_shift = WIN - 1 - place % WIN
    shifts = np.where(group[None, :] % 2 == 0, row_shift[:, None], col_shift[:, None])
    onehot = np.zeros((2, KEYS, 128), np.float32)
    for head in range(2):
        for key in range(KEYS):
            if key >= REAL:
                onehot[head, key, 64 * head + 28] = -1e9
                continue
            for extra in (0, WIN):
                onehot[head, key, 64 * head + key // WIN + extra] = 1.0
                onehot[head, key, 64 * head + 32 + key % WIN + extra] = 1.0
    return shifts.astype(np.int32), onehot


def table_matrix(table_h, table_w):
    flipped = jnp.stack([table_h, table_w])[:, ::-1, :].astype(BF)
    block = jnp.pad(jnp.transpose(flipped, (2, 0, 1)), ((0, 0), (0, 0), (0, 5)))
    block = block.reshape(HD, HD)
    zero = jnp.zeros_like(block)
    return jnp.concatenate(
        [jnp.concatenate([block, zero], axis=1), jnp.concatenate([zero, block], axis=1)], axis=0
    )


def shift_left(values, shifts):
    for bit in (1, 2, 4, 8):
        values = jnp.where((shifts & bit) != 0, pltpu.roll(values, 128 - bit, 1), values)
    return values


def shift_right(values, shifts):
    for bit in (1, 2, 4, 8):
        values = jnp.where((shifts & bit) != 0, pltpu.roll(values, bit, 1), values)
    return values


def attend_kernel(width, qkv, tables, shifts, onehot, att, exps, inv, keys, vals):
    first = (pl.program_id(0) == 0) & (pl.program_id(1) == 0)

    @pl.when(first)
    def _():
        for head in range(2):
            keys[head, :, :128] = jnp.zeros((KEYS, 128), BF)
            keys[head, :, 128:] = onehot[head]
        vals[:, :128] = jnp.zeros((KEYS, 128), BF)
        vals[:, 128:] = jnp.ones((KEYS, 128), BF)

    lane = iota((SLOT, 128), 1)
    low = lane < HD
    inner = lane % 32
    for pair in range(width // 128):
        at = pair * 128
        q2 = qkv[:, at : at + 128]
        k2 = qkv[:, width + at : width + at + 128]
        v2 = qkv[:, 2 * width + at : 2 * width + at + 128]
        rel = shift_left(nn_dot(q2, tables[...]), shifts[...])
        rel_hi = rel.astype(BF).astype(F32)
        rel_lo = pltpu.roll(rel - rel_hi, WIN, 1)
        rel = jnp.where(inner < WIN, rel_hi, jnp.where(inner < 2 * WIN, rel_lo, 1.0))
        queries = jnp.concatenate([q2 * BF(0.125), rel.astype(BF)], axis=1)
        vals[:SLOT, :128] = v2
        zero = jnp.zeros_like(k2)
        keys[0, :SLOT, :128] = jnp.where(low, k2, zero)
        keys[1, :SLOT, :128] = jnp.where(low, zero, k2)
        outs = []
        for head in range(2):
            scores = nt_dot(queries, keys[head])
            peak = jnp.max(scores, axis=1, keepdims=True)
            weights = jnp.exp(scores - peak).astype(BF)
            exps[pair * 2 + head] = weights
            outs.append(nn_dot(weights, vals[...]))
        total = jnp.where(low, outs[0][:, 128:], outs[1][:, 128:])
        scale = 1.0 / total
        inv[:, at : at + 128] = scale
        att[:, at : at + 128] = (
            jnp.where(low, outs[0][:, :128], outs[1][:, :128]) * scale
        ).astype(BF)


def attend(qkv, tables, shifts, onehot, cols, per):
    rows = per * SLOT
    width = D // cols
    pairs = width // 128
    return pl.pallas_call(
        partial(attend_kernel, width),
        out_shape=[
            jax.ShapeDtypeStruct((rows, D), BF),
            jax.ShapeDtypeStruct((D // HD, rows, KEYS), BF),
            jax.ShapeDtypeStruct((rows, D), F32),
        ],
        grid=(cols, per),
        in_specs=[
            pl.BlockSpec((SLOT, 3 * width), lambda c, w: (w, c)),
            pl.BlockSpec((128, 128), lambda c, w: (0, 0)),
            pl.BlockSpec((SLOT, 128), lambda c, w: (0, 0)),
            pl.BlockSpec((2, KEYS, 128), lambda c, w: (0, 0, 0)),
        ],
        out_specs=[
            pl.BlockSpec((SLOT, width), lambda c, w: (w, c)),
            pl.BlockSpec((2 * pairs, SLOT, KEYS), lambda c, w: (c, w, 0)),
            pl.BlockSpec((SLOT, width), lambda c, w: (w, c)),
        ],
        scratch_shapes=[pltpu.VMEM((2, KEYS, 256), BF), pltpu.VMEM((KEYS, 256), BF)],
        compiler_params=params(2),
        name="attend",
    )(qkv, tables, shifts, onehot)


def attend_back_kernel(
    width, qkv, exps, inv, att, att_grad, tables2, shifts, onehot, out, table_sum, bias_sum, keys, vals
):
    first = (pl.program_id(0) == 0) & (pl.program_id(1) == 0)

    @pl.when(first)
    def _():
        for head in range(2):
            keys[head, :, :128] = jnp.zeros((KEYS, 128), BF)
            keys[head, :, 128:] = onehot[head]
        vals[...] = jnp.zeros_like(vals)
        table_sum[...] = jnp.zeros_like(table_sum)

    @pl.when(pl.program_id(1) == 0)
    def _():
        bias_sum[...] = jnp.zeros_like(bias_sum)

    lane = iota((SLOT, 128), 1)
    low = lane < HD
    inner = lane % 32

    def eight(values):
        total = values[:8]
        for r in range(8, SLOT, 8):
            total = total + values[r : r + 8]
        return total

    for pair in range(width // 128):
        at = pair * 128
        q2 = qkv[:, at : at + 128]
        k2 = qkv[:, width + at : width + at + 128]
        v2 = qkv[:, 2 * width + at : 2 * width + at + 128]
        zero = jnp.zeros_like(k2)
        keys[0, :SLOT, :128] = jnp.where(low, k2, zero)
        keys[1, :SLOT, :128] = jnp.where(low, zero, k2)
        vals[0, :SLOT, :] = jnp.where(low, v2, zero)
        vals[1, :SLOT, :] = jnp.where(low, zero, v2)
        grad = (att_grad[:, at : at + 128].astype(F32) * inv[:, at : at + 128]).astype(BF)
        cross = grad.astype(F32) * att[:, at : at + 128].astype(F32)
        dots = (
            jnp.sum(jnp.where(low, cross, 0.0), axis=1, keepdims=True),
            jnp.sum(jnp.where(low, 0.0, cross), axis=1, keepdims=True),
        )
        q_scaled = q2 * BF(0.125)
        grad_heads = (jnp.where(low, grad, zero), jnp.where(low, zero, grad))
        q_heads = (jnp.where(low, q_scaled, zero), jnp.where(low, zero, q_scaled))
        q_sum = jnp.zeros((SLOT, 256), F32)
        k_sum = jnp.zeros((KEYS, 128), F32)
        v_sum = jnp.zeros((KEYS, 128), F32)
        for head in range(2):
            weights = exps[pair * 2 + head]
            probs_grad = nt_dot(grad, vals[head])
            scores_grad = (weights.astype(F32) * (probs_grad - dots[head])).astype(BF)
            q_sum = q_sum + nn_dot(scores_grad, keys[head])
            k_sum = k_sum + tn_dot(scores_grad, q_heads[head])
            v_sum = v_sum + tn_dot(weights, grad_heads[head])
        rel = shift_right(jnp.where(inner < WIN, q_sum[:, 128:], 0.0), shifts[...])
        rel_hi = rel.astype(BF)
        rel_lo = (rel - rel_hi.astype(F32)).astype(BF)
        rel2 = jnp.concatenate([rel_hi, rel_lo], axis=1)
        q_grad = q_sum[:, :128] * 0.125 + nt_dot(rel2, tables2[...])
        table_sum[...] += tn_dot(q2, rel2)
        k_grad = k_sum[:SLOT]
        v_grad = v_sum[:SLOT]
        out[:, at : at + 128] = q_grad.astype(BF)
        out[:, width + at : width + at + 128] = k_grad.astype(BF)
        out[:, 2 * width + at : 2 * width + at + 128] = v_grad.astype(BF)
        bias_sum[:, at : at + 128] += eight(q_grad)
        bias_sum[:, 2 * width + at : 2 * width + at + 128] += eight(v_grad)


def attend_back(qkv, exps, inv, att, att_grad, tables, shifts, onehot, cols, per):
    rows = per * SLOT
    width = D // cols
    pairs = width // 128
    tables2 = jnp.concatenate([tables, tables], axis=1)
    return pl.pallas_call(
        partial(attend_back_kernel, width),
        out_shape=[
            jax.ShapeDtypeStruct((rows, 3 * D), BF),
            jax.ShapeDtypeStruct((128, 256), F32),
            jax.ShapeDtypeStruct((8, 3 * D), F32),
        ],
        grid=(cols, per),
        in_specs=[
            pl.BlockSpec((SLOT, 3 * width), lambda c, w: (w, c)),
            pl.BlockSpec((2 * pairs, SLOT, KEYS), lambda c, w: (c, w, 0)),
            pl.BlockSpec((SLOT, width), lambda c, w: (w, c)),
            pl.BlockSpec((SLOT, width), lambda c, w: (w, c)),
            pl.BlockSpec((SLOT, width), lambda c, w: (w, c)),
            pl.BlockSpec((128, 256), lambda c, w: (0, 0)),
            pl.BlockSpec((SLOT, 128), lambda c, w: (0, 0)),
            pl.BlockSpec((2, KEYS, 128), lambda c, w: (0, 0, 0)),
        ],
        out_specs=[
            pl.BlockSpec((SLOT, 3 * width), lambda c, w: (w, c)),
            pl.BlockSpec((128, 256), lambda c, w: (0, 0)),
            pl.BlockSpec((8, 3 * width), lambda c, w: (0, c)),
        ],
        scratch_shapes=[pltpu.VMEM((2, KEYS, 256), BF), pltpu.VMEM((2, KEYS, 128), BF)],
        compiler_params=params(2),
        name="attend_back",
    )(qkv, exps, inv, att, att_grad, tables2, shifts, onehot)


def split_table(total):
    total = (total[:, :128] + total[:, 128:]).reshape(2, HD, 2, 2, 32)
    both = total[0, :, 0] + total[1, :, 1]
    both = jnp.transpose(both, (1, 2, 0))[:, :27][:, ::-1]
    return both[0], both[1]


def exchange(pieces, cols):
    return [pieces[0]] + [
        lax.ppermute(pieces[k], "col", [(i, i ^ k) for i in range(cols)]) for k in range(1, cols)
    ]


def pieces_of(full, me, cols, per):
    width = D // cols
    parts = full.reshape(per, SLOT, cols, width)
    return [
        lax.dynamic_index_in_dim(parts, me ^ k, 2, keepdims=False) for k in range(cols)
    ]


def norm_stats(values):
    mean = jnp.mean(values, axis=1, keepdims=True)
    centred = values - mean
    var = jnp.mean(centred * centred, axis=1, keepdims=True)
    inv = lax.rsqrt(var + EPSILON)
    return centred * inv, inv


def norm_back(grad, hat, inv, gain):
    scaled = grad * gain
    first = jnp.mean(scaled, axis=1, keepdims=True)
    second = jnp.mean(scaled * hat, axis=1, keepdims=True)
    return (scaled - first - hat * second) * inv


def body(
    cols,
    rows_n,
    tokens_in,
    pad_offsets,
    norm1_gain,
    norm1_bias,
    qkv_weight,
    qv_bias,
    table_height,
    table_width,
    proj_weight,
    proj_bias,
    norm2_gain,
    norm2_bias,
    fc1_weight,
    fc1_bias,
    fc2_weight,
    fc2_bias,
    out_grad,
):
    width = D // cols
    per = -(-WINDOWS // cols)
    rows = per * SLOT
    me = lax.axis_index("col")
    info = jnp.concatenate([me.astype(jnp.int32)[None], pad_offsets[0]])
    both = ("row", "col")

    x_pieces = exchange(spread(tokens_in, info, cols, per), cols)
    g_pieces = exchange(spread(out_grad, info, cols, per), cols)

    vec = jnp.concatenate(
        [
            norm1_gain,
            norm1_bias,
            norm2_gain,
            norm2_bias,
            proj_bias.astype(F32),
            fc2_bias.astype(F32),
            qv_bias[0].astype(F32),
            qv_bias[1].astype(F32),
            fc1_bias.astype(F32),
        ]
    )
    vecs = lax.all_gather(vec, "col", axis=0)
    picked = [vecs[:, i * width : (i + 1) * width].reshape(1, D) for i in range(8)]
    gain1, bias1, gain2, bias2, bias_p, bias_2, bias_q, bias_v = picked
    bias_h = vecs[:, 8 * width :].reshape(1, -1)
    bias_qkv = jnp.stack(
        [bias_q.reshape(cols, width), jnp.zeros((cols, width), F32), bias_v.reshape(cols, width)],
        axis=1,
    ).reshape(1, 3 * D)

    w_qkv = lax.all_gather(qkv_weight.reshape(-1, 3 * width), both, axis=0)
    w_qkv = w_qkv.reshape(rows_n, cols, -1, 3 * width).transpose(0, 2, 1, 3).reshape(D, 3 * D)
    w_proj = lax.all_gather(proj_weight, both, axis=0)
    w_proj = w_proj.reshape(rows_n, cols, width, -1).transpose(1, 2, 0, 3).reshape(D, D)
    fc_local = jnp.stack([fc1_weight, fc2_weight.T])
    fc_full = lax.all_gather(fc_local, both, axis=0)
    fc_full = fc_full.reshape(rows_n, cols, 2, fc_local.shape[1], fc_local.shape[2])
    fc_full = fc_full.transpose(2, 0, 3, 1, 4).reshape(2, D, -1)
    w_fc1, w_fc2 = fc_full[0], fc_full[1]

    x_full, n1 = norm1(x_pieces, info, gain1, bias1, cols, per)
    qkv = (nn_dot(n1, w_qkv) + bias_qkv).astype(BF)
    shifts_np, onehot_np = rel_constants()
    shifts = jnp.asarray(shifts_np)
    onehot = jnp.asarray(onehot_np, BF)
    tables = table_matrix(table_height, table_width)
    att, exps, inv = attend(qkv, tables, shifts, onehot, cols, per)

    resid = x_full.astype(F32) + nn_dot(att, w_proj) + bias_p
    hat2, inv2 = norm_stats(resid)
    n2 = (hat2 * gain2 + bias2).astype(BF)
    g_full = join(g_pieces, info, cols, per)

    pre = nn_dot(n2, w_fc1) + bias_h
    act_f, pull = jax.vjp(partial(jax.nn.gelu, approximate=False), pre)
    act = act_f.astype(BF)
    mlp = nt_dot(act, w_fc2) + bias_2
    block = (resid + mlp).astype(BF)
    block_pieces = exchange(pieces_of(block, me, cols, per), cols)
    block_out = collect(block_pieces, info, cols, per, BF)

    act_grad = nn_dot(g_full, w_fc2)
    pre_grad = pull(act_grad)[0].astype(BF)
    fc2_grad = tn_dot(g_full, act).astype(BF)
    fc1_grad = tn_dot(n2, pre_grad).astype(BF)
    n2_grad = nt_dot(pre_grad, w_fc1)

    def scatter(grad, r_dim):
        return lax.psum_scatter(grad, both, scatter_dimension=0, tiled=True)

    fc_grads = jnp.stack([fc1_grad, fc2_grad]).reshape(2, rows_n, D // rows_n, cols, -1)
    fc_grads = fc_grads.transpose(1, 3, 0, 2, 4).reshape(rows_n * cols, 2, D // rows_n, -1)
    fc_mine = scatter(fc_grads, 0)[0]

    g_f = g_full.astype(F32)
    resid_grad = g_f + norm_back(n2_grad, hat2, inv2, gain2)
    proj_grad = resid_grad.astype(BF)
    proj_w_grad = tn_dot(att, proj_grad).astype(BF)
    att_grad = nt_dot(proj_grad, w_proj).astype(BF)
    dqkv, table_sum, bias_sum = attend_back(
        qkv, exps, inv, att, att_grad, tables, shifts, onehot, cols, per
    )
    qkv_w_grad = tn_dot(n1, dqkv).astype(BF)
    n1_grad = nt_dot(dqkv, w_qkv)
    qkv_mine = scatter(
        qkv_w_grad.reshape(rows_n, D // rows_n, cols, 3 * width)
        .transpose(0, 2, 1, 3)
        .reshape(rows_n * cols, D // rows_n, 3 * width),
        0,
    )[0]
    proj_mine = scatter(
        proj_w_grad.reshape(cols, width, rows_n, D // rows_n)
        .transpose(2, 0, 1, 3)
        .reshape(rows_n * cols, width, D // rows_n),
        0,
    )[0]

    hat1, inv1 = norm_stats(x_full.astype(F32))
    input_part = (resid_grad + norm_back(n1_grad, hat1, inv1, gain1)).astype(BF)
    in_pieces = exchange(pieces_of(input_part, me, cols, per), cols)
    input_grad = collect(in_pieces, info, cols, per, F32)

    slot_windows = jnp.arange(per, dtype=jnp.int32)[:, None] + me * per
    place = jnp.arange(SLOT, dtype=jnp.int32)[None, :]
    row = WIN * (slot_windows // GRID) - info[1] + place // WIN
    col = WIN * (slot_windows % GRID) - info[2] + place % WIN
    keep = (row >= 0) & (row < SIDE) & (col >= 0) & (col < SIDE)
    keep = (keep & (place < REAL) & (slot_windows < WINDOWS)).reshape(rows, 1)
    n1_kept = jnp.where(keep, n1_grad, 0.0)
    bias_cols = jnp.sum(bias_sum, axis=0).reshape(cols, 3, width)

    def by_col(v):
        return v.reshape(cols, width)

    small = jnp.concatenate(
        [
            by_col(jnp.sum(n1_kept * hat1, axis=0)),
            by_col(jnp.sum(n1_kept, axis=0)),
            bias_cols[:, 0],
            bias_cols[:, 2],
            by_col(jnp.sum(proj_grad.astype(F32), axis=0)),
            by_col(jnp.sum(n2_grad * hat2, axis=0)),
            by_col(jnp.sum(n2_grad, axis=0)),
            by_col(jnp.sum(g_f, axis=0)),
            jnp.sum(pre_grad.astype(F32), axis=0).reshape(cols, -1),
        ],
        axis=1,
    )
    table_h_grad, table_w_grad = split_table(table_sum)
    small, table_h_grad, table_w_grad = lax.psum((small, table_h_grad, table_w_grad), both)
    mine = lax.dynamic_index_in_dim(small, me, 0, keepdims=False)

    def part(i):
        return mine[i * width : (i + 1) * width]

    return (
        block_out,
        input_grad,
        part(0),
        part(1),
        qkv_mine.astype(F32).reshape(-1, 3, width),
        jnp.stack([part(2), part(3)]),
        table_h_grad,
        table_w_grad,
        proj_mine.astype(F32),
        part(4),
        part(5),
        part(6),
        fc_mine[0].astype(F32),
        mine[8 * width :],
        fc_mine[1].astype(F32).T,
        part(7),
    )


def solution(mesh):
    placed = (
        P("row", "col"),
        P("row", None),
        P("col"),
        P("col"),
        P("row", None, "col"),
        P(None, "col"),
        P(),
        P(),
        P("col", "row"),
        P("col"),
        P("col"),
        P("col"),
        P("row", "col"),
        P("col"),
        P("col", "row"),
        P("col"),
        P("row", "col"),
    )
    return jax.shard_map(
        partial(body, mesh.shape["col"], mesh.shape["row"]),
        mesh=mesh,
        in_specs=placed,
        out_specs=(
            P("row", "col"),
            P("row", "col"),
            P("col"),
            P("col"),
            P("row", None, "col"),
            P(None, "col"),
            P(),
            P(),
            P("col", "row"),
            P("col"),
            P("col"),
            P("col"),
            P("row", "col"),
            P("col"),
            P("col", "row"),
            P("col"),
        ),
        check_vma=False,
    )
```

```python
from functools import partial

import jax
import jax.numpy as jnp
import numpy as np
from jax import lax
from jax.experimental import pallas as pl
from jax.experimental.pallas import tpu as pltpu
from jax.sharding import PartitionSpec as P

D = 1024
HD = 64
WIN = 14
SIDE = 64
GRID = 5
WINDOWS = 25
REAL = 196
SLOT = 200
KEYS = 256
PIX = 4096
EPSILON = 1e-06
MARGIN = 6
PADROWS = 84
BF = jnp.bfloat16
F32 = jnp.float32
VMEM_LIMIT = 60 * 1024 * 1024
SPLITS = 4
BLOCKS = 4
SLAB = 224
FIELDS = 7
HEAD = 5
TAIL = 16


def iota(shape, dim):
    return lax.broadcasted_iota(jnp.int32, shape, dim)


def params(n=1):
    return pltpu.CompilerParams(
        dimension_semantics=("arbitrary",) * n, vmem_limit_bytes=VMEM_LIMIT
    )


def cost(micros):
    return pl.CostEstimate(
        flops=int(micros * 1.1e9), bytes_accessed=int(micros * 1e6), transcendentals=0
    )


def nt_dot(a, b):
    return lax.dot_general(a, b, (((1,), (1,)), ((), ())), preferred_element_type=F32)


def tn_dot(a, b):
    return lax.dot_general(a, b, (((0,), (0,)), ((), ())), preferred_element_type=F32)


def nn_dot(a, b):
    return lax.dot_general(a, b, (((1,), (0,)), ((), ())), preferred_element_type=F32)


def window_sets(cols, per):
    units = [[0, 4, 20, 24]]
    units += [[j, 20 + j] for j in (1, 2, 3)] + [[5 * i, 5 * i + 4] for i in (1, 2, 3)]
    units += [[5 * i + j] for i in (1, 2, 3) for j in (1, 2, 3)]
    sizes = [484] + [308] * 6 + [196] * 9
    sets = [[] for _ in range(cols)]
    loads = [0] * cols
    for unit, size in zip(units, sizes):
        open_sets = [d for d in range(cols) if len(sets[d]) + len(unit) <= per]
        best = min(open_sets, key=lambda d: loads[d])
        sets[best] += unit
        loads[best] += size
    capacity = -(-(max(loads) + TAIL) // 64) * 64
    return [own + [WINDOWS] * (per - len(own)) for own in sets], capacity


def layout_info(sets, offsets, me, my_row):
    ids = np.array(sets, np.int32)
    win_row, win_col = ids // GRID, ids % GRID

    def extent(place, shift):
        low = jnp.maximum(0, shift - WIN * place)
        high = jnp.minimum(WIN, SIDE + shift - WIN * place)
        return low, jnp.maximum(high - low, 0)

    row_low, height = extent(win_row, offsets[0])
    col_low, width = extent(win_col, offsets[1])
    size = height * width
    earlier = np.tril(np.ones((ids.shape[1],) * 2, np.int32), -1)
    base = jnp.sum(size[:, None, :] * earlier[None], axis=2)
    kept_row = jnp.asarray(np.minimum(win_row, GRID - 1))
    fields = [base, row_low, height, col_low, width, kept_row, jnp.asarray(win_col)]
    own = jnp.arange(ids.shape[0], dtype=jnp.int32) == me
    count = jnp.sum(jnp.where(own[:, None], size, 0))
    head = jnp.concatenate([me[None], offsets, my_row[None], count[None]])
    return jnp.concatenate([head, jnp.stack(fields, axis=-1).reshape(-1)])


def window_at(info, index):
    at = HEAD + index * FIELDS
    return [info[at + f] for f in range(FIELDS)]


def target_of(field, left, row, token_col):
    base, row_low, height, col_low, width, _, win_col = field
    col = token_col + (left - WIN * win_col)
    inside = (row >= row_low) & (row < row_low + height) & (col >= col_low) & (col < col_low + width)
    return jnp.where(inside, base + (row - row_low) * width + (col - col_low), -(1 << 20))


def as_pick(mask):
    return mask.astype(F32).astype(BF)


def spread_kernel(per, info, x_ref, out, padded, total):
    top, left = info[1], info[2]
    cols, rows, width = out.shape
    padded[: MARGIN * SIDE, :] = jnp.zeros((MARGIN * SIDE, width), BF)
    padded[(MARGIN + SIDE) * SIDE :, :] = jnp.zeros(((PADROWS - MARGIN - SIDE) * SIDE, width), BF)
    padded[MARGIN * SIDE : (MARGIN + SIDE) * SIDE, :] = x_ref[...]
    token = iota((1, 256), 1)
    row, col = token // SIDE, token % SIDE
    line = iota((64, 256), 0)
    for d in range(cols):
        total[...] = jnp.zeros_like(total)

        def step(i, carry):
            field = window_at(info, d * per + i)
            base, row_low, height, _, across, win_row, _ = field
            for g in range(4):
                start = base + jnp.clip(4 * g - row_low, 0, height) * across
                start = pl.multiple_of(start // 8 * 8, 8)
                pick = as_pick(line == target_of(field, left, row + 4 * g, col) - start)
                first = pl.multiple_of((WIN * win_row + 4 * g - top + MARGIN) * SIDE, SIDE)
                total[pl.ds(start, 64), :] += nn_dot(pick, padded[pl.ds(first, 256), :])
            return carry

        lax.fori_loop(0, per, step, 0)
        out[d] = total[:rows].astype(BF)


def spread(x, info, cols, per, rows):
    width = x.shape[1]
    return pl.pallas_call(
        partial(spread_kernel, per),
        out_shape=jax.ShapeDtypeStruct((cols, rows, width), BF),
        grid_spec=pltpu.PrefetchScalarGridSpec(
            num_scalar_prefetch=1,
            grid=(1,),
            in_specs=[pl.BlockSpec((PIX, width), lambda i, s: (0, 0))],
            out_specs=pl.BlockSpec((cols, rows, width), lambda i, s: (0, 0, 0)),
            scratch_shapes=[
                pltpu.VMEM((PADROWS * SIDE, width), BF),
                pltpu.VMEM((rows + 64, width), F32),
            ],
        ),
        compiler_params=params(),
        cost_estimate=cost(7),
        name="spread",
    )(info, x)


def collect_kernel(per, info, pieces, out, padded):
    top, left = info[1], info[2]
    cols, rows, _ = pieces.shape
    padded[...] = jnp.zeros_like(padded)
    token = iota((1, 256), 1)
    row, col = token // SIDE, token % SIDE
    line = iota((80, 256), 0)
    for d in range(cols):

        def step(i, carry):
            field = window_at(info, d * per + i)
            base, row_low, height, _, across, win_row, _ = field
            for g in range(4):
                start = base + jnp.clip(4 * g - row_low, 0, height) * across
                start = pl.multiple_of(jnp.minimum(start // 16 * 16, rows - 80), 16)
                pick = as_pick(line == target_of(field, left, row + 4 * g, col) - start)
                first = pl.multiple_of((WIN * win_row + 4 * g - top + MARGIN) * SIDE, SIDE)
                padded[pl.ds(first, 256), :] += tn_dot(pick, pieces[d, pl.ds(start, 80), :])
            return carry

        lax.fori_loop(0, per, step, 0)
    out[...] = padded[MARGIN * SIDE : (MARGIN + SIDE) * SIDE, :].astype(out.dtype)


def collect(pieces, info, per, dtype):
    cols, rows, width = pieces.shape
    return pl.pallas_call(
        partial(collect_kernel, per),
        out_shape=jax.ShapeDtypeStruct((PIX, width), dtype),
        grid_spec=pltpu.PrefetchScalarGridSpec(
            num_scalar_prefetch=1,
            grid=(1,),
            in_specs=[pl.BlockSpec((cols, rows, width), lambda i, s: (0, 0, 0))],
            out_specs=pl.BlockSpec((PIX, width), lambda i, s: (0, 0)),
            scratch_shapes=[pltpu.VMEM((PADROWS * SIDE, width), F32)],
        ),
        compiler_params=params(),
        cost_estimate=cost(9),
        name="collect",
    )(info, pieces)


def chunk_place(col, part, width, info, parts):
    return (col * (width // 128) + part) ^ (info[3] // parts)


def swap_halves(values, info, parts):
    if parts == 1:
        return values
    return jnp.where(info[3] % 2 == 1, pltpu.roll(values.astype(F32), 64, 1), values.astype(F32))


def place_features(pieces, info, parts, whole):
    cols, _, width = pieces.shape
    for d in range(cols):
        for c in range(width // 128):
            at = pl.multiple_of(chunk_place(d, c, width, info, parts) * 128, 128)
            values = swap_halves(pieces[d, :, c * 128 : (c + 1) * 128], info, parts)
            whole[:, pl.ds(at, 128)] = values.astype(whole.dtype)


def take_features(whole, pieces, info, parts):
    cols, _, width = pieces.shape
    for d in range(cols):
        for c in range(width // 128):
            at = pl.multiple_of(chunk_place(d, c, width, info, parts) * 128, 128)
            values = swap_halves(whole[:, pl.ds(at, 128)], info, parts)
            pieces[d, :, c * 128 : (c + 1) * 128] = values.astype(BF)


def eight(values):
    total = values[:8]
    for r in range(8, values.shape[0], 8):
        total = total + values[r : r + 8]
    return total


def row_places(nr, flip):
    order = outer_bits(nr)
    order = order[::-1] if flip else order
    held = [0]
    for bit in order[:-1]:
        held = held + [place | bit for place in held]
    groups = [held, [place | order[-1] for place in held]]
    groups = groups + [[place | 1 for place in group] for group in groups]
    where = {place: (g, i) for g, group in enumerate(groups) for i, place in enumerate(group)}
    return [where[place] for place in range(nr)]


def outer_bits(nr):
    return [1 << b for b in range(1, nr.bit_length() - 1)]


def load_rows(bufs, flip, scratch, nr, first=0):
    stride = D // nr
    for p, (g, i) in enumerate(row_places(nr, flip)):
        cols, size, n = bufs[g].shape[1:]
        for k in range(cols):
            at = p * stride + first
            scratch[at : at + size, k * n : (k + 1) * n] = bufs[g][i, k]


def const_spec(shape):
    zeros = (0,) * len(shape)
    return pl.BlockSpec(shape, lambda *a: zeros, pipeline_mode=pl.Buffered(1))


def norm_qkv_kernel(cols, nr, info, *refs):
    pieces = refs[0]
    bufs_a, bufs_b = refs[1:5], refs[5:9]
    gain, bias, bias_qkv, x_out, n_out, qkv_out, whole, weight = refs[9:]
    parts = max(1, 128 * nr // D)
    bw = D // nr

    @pl.when(pl.program_id(0) == 0)
    def _():
        load_rows(bufs_a, False, weight, nr)
        load_rows(bufs_b, True, weight, nr, bw // 2)

    place_features(pieces, info, parts, whole)
    values = whole[...]
    x_out[...] = values.astype(BF)
    mean = jnp.mean(values, axis=1, keepdims=True)
    centred = values - mean
    spread_sq = jnp.mean(centred * centred, axis=1, keepdims=True)
    normed = centred * lax.rsqrt(spread_sq + EPSILON) * gain[...] + bias[...]
    size = values.shape[0]
    real = iota((size, 1), 0) < info[4] - pl.program_id(0) * size
    normed = jnp.where(real, normed, 0.0).astype(BF)
    n_out[...] = normed
    qkv_out[...] = (nn_dot(normed, weight[...]) + bias_qkv[...]).astype(BF)


def norm_qkv(pieces, bufs_a, bufs_b, info, gain, bias, bias_qkv, cols, rows, nr):
    width = D // cols
    return pl.pallas_call(
        partial(norm_qkv_kernel, cols, nr),
        out_shape=[
            jax.ShapeDtypeStruct((rows, D), BF),
            jax.ShapeDtypeStruct((rows, D), BF),
            jax.ShapeDtypeStruct((rows, 3 * D), BF),
        ],
        grid_spec=pltpu.PrefetchScalarGridSpec(
            num_scalar_prefetch=1,
            grid=(BLOCKS,),
            in_specs=[pl.BlockSpec((cols, rows // BLOCKS, width), lambda i, s: (0, i, 0))]
            + [const_spec(bufs_a[0].shape)] * 8
            + [const_spec((1, D)), const_spec((1, D)), const_spec((1, 3 * D))],
            out_specs=[
                pl.BlockSpec((rows // BLOCKS, D), lambda i, s: (i, 0)),
                pl.BlockSpec((rows // BLOCKS, D), lambda i, s: (i, 0)),
                pl.BlockSpec((rows // BLOCKS, 3 * D), lambda i, s: (i, 0)),
            ],
            scratch_shapes=[pltpu.VMEM((rows // BLOCKS, D), F32), pltpu.VMEM((D, 3 * D), BF)],
        ),
        compiler_params=params(),
        cost_estimate=cost(19),
        name="norm_qkv",
    )(info, pieces, *bufs_a, *bufs_b, gain, bias, bias_qkv)


def join_kernel(cols, nr, info, *refs):
    place_features(refs[0], info, max(1, 128 * nr // D), refs[1])


def join(pieces, info, cols, rows, nr):
    width = pieces.shape[-1]
    return pl.pallas_call(
        partial(join_kernel, cols, nr),
        out_shape=jax.ShapeDtypeStruct((rows, D), BF),
        grid_spec=pltpu.PrefetchScalarGridSpec(
            num_scalar_prefetch=1,
            grid=(BLOCKS,),
            in_specs=[pl.BlockSpec((cols, rows // BLOCKS, width), lambda i, s: (0, i, 0))],
            out_specs=pl.BlockSpec((rows // BLOCKS, D), lambda i, s: (i, 0)),
        ),
        compiler_params=params(),
        cost_estimate=cost(7),
        name="join",
    )(info, pieces)


def proj_norm_kernel(nr, *refs):
    att, x, bias_p, gain, bias, resid_out, n_out, weight = refs[4:]

    @pl.when(pl.program_id(0) == 0)
    def _():
        load_rows(refs[:4], False, weight, nr)

    values = x[...].astype(F32) + nt_dot(att[...], weight[...]) + bias_p[...]
    resid_out[...] = values
    mean = jnp.mean(values, axis=1, keepdims=True)
    centred = values - mean
    spread_sq = jnp.mean(centred * centred, axis=1, keepdims=True)
    n_out[...] = (centred * lax.rsqrt(spread_sq + EPSILON) * gain[...] + bias[...]).astype(BF)


def proj_spec(buf, cols, whole):
    n = D // cols
    shape = (buf.shape[0], cols if whole else 1, buf.shape[2], n)
    last = buf.shape[3] // n - 1
    if whole:
        return pl.BlockSpec(shape, lambda *a: (0, 0, 0, last), pipeline_mode=pl.Buffered(1))
    return pl.BlockSpec(shape, lambda k: (0, k, 0, last))


def proj_norm(bufs, att, x, bias_p, gain, bias, cols, rows, nr):
    row_spec = pl.BlockSpec((rows // BLOCKS, D), lambda i: (i, 0))
    return pl.pallas_call(
        partial(proj_norm_kernel, nr),
        out_shape=[jax.ShapeDtypeStruct((rows, D), F32), jax.ShapeDtypeStruct((rows, D), BF)],
        grid=(BLOCKS,),
        in_specs=[proj_spec(bufs[0], cols, True)] * 4
        + [row_spec, row_spec, const_spec((1, D)), const_spec((1, D)), const_spec((1, D))],
        out_specs=[row_spec, row_spec],
        scratch_shapes=[pltpu.VMEM((D, D), BF)],
        compiler_params=params(),
        cost_estimate=cost(11),
        name="proj_norm",
    )(*bufs, att, x, bias_p, gain, bias)


def gelu_and_slope(v):
    t = 1.0 / (1.0 + 0.23164189 * jnp.abs(v))
    poly = t * (
        0.127414796
        + t * (-0.142248368 + t * (0.7107068705 + t * (-0.7265760135 + t * 0.5307027145)))
    )
    bell = jnp.exp(-0.5 * v * v)
    half = poly * bell
    below = jnp.where(v >= 0, 1.0 - half, half)
    return v * below, below + v * bell * 0.3989422804014327


def store_halves(grad, keep, send, nr, lanes=slice(None)):
    bw = D // nr
    for q in range(nr // 2):
        at = 2 * q * bw
        keep[q, 0, :, lanes] = grad[at : at + bw].astype(BF)
        send[q, 0, :, lanes] = grad[at + bw : at + 2 * bw].astype(BF)


def mlp_grads_kernel(nr, *refs):
    n2, g, bias, act, pre_grad, keep, send, bias_sum, w1, w2 = refs[8:]
    n = w1.shape[1]
    load_rows(refs[:4], False, w1, nr)
    load_rows(refs[4:8], True, w2, nr)
    total = None
    size = n2.shape[0] // BLOCKS
    for r in range(0, n2.shape[0], size):
        pre = nn_dot(n2[r : r + size], w1[...]) + bias[0]
        act_grad = nn_dot(g[r : r + size], w2[...])
        value, slope = gelu_and_slope(pre)
        act[r : r + size] = value.astype(BF)
        grad = act_grad * slope
        pre_grad[r : r + size] = grad.astype(BF)
        part = eight(grad)
        total = part if total is None else total + part
    bias_sum[0] = total
    store_halves(tn_dot(n2[...], pre_grad[...]), keep, send, nr, slice(0, n))
    store_halves(tn_dot(g[...], act[...]), keep, send, nr, slice(n, 2 * n))


def mlp_grads(bufs1, bufs2, n2, g, bias, cols, rows, nr):
    bw = D // nr
    n = bufs2[0].shape[-1]
    w_spec = pl.BlockSpec((nr // 4, 1, bw, n), lambda k: (0, k, 0, 0))
    row_spec = pl.BlockSpec((rows, n), lambda k: (0, k))
    half_spec = pl.BlockSpec((nr // 2, 1, bw, 2 * n), lambda k: (0, k, 0, 0))
    half = jax.ShapeDtypeStruct((nr // 2, cols, bw, 2 * n), BF)
    act = jax.ShapeDtypeStruct((rows, cols * n), BF)
    return pl.pallas_call(
        partial(mlp_grads_kernel, nr),
        out_shape=[act, act, half, half, jax.ShapeDtypeStruct((cols, 8, n), F32)],
        grid=(cols,),
        in_specs=[w_spec] * 8
        + [const_spec((rows, D)), const_spec((rows, D)), pl.BlockSpec((1, 1, n), lambda k: (k, 0, 0))],
        out_specs=[row_spec, row_spec, half_spec, half_spec]
        + [pl.BlockSpec((1, 8, n), lambda k: (k, 0, 0))],
        scratch_shapes=[pltpu.VMEM((D, n), BF)] * 2,
        compiler_params=params(),
        cost_estimate=cost(38),
        name="mlp_grads",
    )(*bufs1, *bufs2, n2, g, bias)


def norm_back(grad, values, gain):
    mean = jnp.mean(values, axis=1, keepdims=True)
    centred = values - mean
    spread_sq = jnp.mean(centred * centred, axis=1, keepdims=True)
    inv = lax.rsqrt(spread_sq + EPSILON)
    hat = centred * inv
    scaled = grad * gain
    first = jnp.mean(scaled, axis=1, keepdims=True)
    second = jnp.mean(scaled * hat, axis=1, keepdims=True)
    return (scaled - first - hat * second) * inv, hat


def block_out_kernel(cols, nr, info, *refs):
    act0, act1, resid, bias_2 = refs[8:12]
    pieces, weight, whole = refs[12:]

    @pl.when(pl.program_id(0) == 0)
    def _():
        load_rows(refs[:4], True, weight.at[0], nr)
        load_rows(refs[4:8], True, weight.at[1], nr)

    out = nt_dot(act0[...], weight[0]) + nt_dot(act1[...], weight[1])
    whole[...] = resid[...] + out + bias_2[...]
    take_features(whole, pieces, info, max(1, 128 * nr // D))


def block_rows(groups, acts, resid, bias_2, info, cols, rows, nr):
    width = D // cols
    wide = acts[0].shape[1]
    row_spec = pl.BlockSpec((rows // BLOCKS, D), lambda i, s: (i, 0))
    wide_spec = pl.BlockSpec((rows // BLOCKS, wide), lambda i, s: (i, 0))
    flat = [b for group in groups for b in group]
    return pl.pallas_call(
        partial(block_out_kernel, cols, nr),
        out_shape=[jax.ShapeDtypeStruct((cols, rows, width), BF)],
        grid_spec=pltpu.PrefetchScalarGridSpec(
            num_scalar_prefetch=1,
            grid=(BLOCKS,),
            in_specs=[const_spec(flat[-1].shape)] * 8
            + [wide_spec] * 2
            + [row_spec, const_spec((1, D))],
            out_specs=[pl.BlockSpec((cols, rows // BLOCKS, width), lambda i, s: (0, i, 0))],
            scratch_shapes=[pltpu.VMEM((2, D, wide), BF), pltpu.VMEM((rows // BLOCKS, D), F32)],
        ),
        compiler_params=params(),
        cost_estimate=cost(26),
        name="block_rows",
    )(info, *flat, *acts, resid, bias_2)[0]


def mlp_back_kernel(nr, *refs):
    grad0, grad1, resid, g, gain, resid_grad, proj_grad, sums, weight = refs[8:]

    @pl.when(pl.program_id(0) == 0)
    def _():
        load_rows(refs[:4], False, weight.at[0], nr)
        load_rows(refs[4:8], False, weight.at[1], nr)
        sums[...] = jnp.zeros_like(sums)

    grad = nt_dot(grad0[...], weight[0]) + nt_dot(grad1[...], weight[1])
    g_f = g[...].astype(F32)
    back, hat = norm_back(grad, resid[...], gain[...])
    total = g_f + back
    resid_grad[...] = total
    low = total.astype(BF)
    proj_grad[...] = low
    sums[0] += eight(low.astype(F32))
    sums[1] += eight(grad * hat)
    sums[2] += eight(grad)
    sums[3] += eight(g_f)


def mlp_back(groups, grads, resid, g, gain, cols, rows, nr):
    wide = grads[0].shape[1]
    row_spec = pl.BlockSpec((rows // BLOCKS, D), lambda i: (i, 0))
    wide_spec = pl.BlockSpec((rows // BLOCKS, wide), lambda i: (i, 0))
    flat = [b for group in groups for b in group]
    shape = flat[-1].shape
    return pl.pallas_call(
        partial(mlp_back_kernel, nr),
        out_shape=[
            jax.ShapeDtypeStruct((rows, D), F32),
            jax.ShapeDtypeStruct((rows, D), BF),
            jax.ShapeDtypeStruct((4, 8, D), F32),
        ],
        grid=(BLOCKS,),
        in_specs=[const_spec(shape)] * 8
        + [wide_spec] * 2
        + [row_spec, row_spec, const_spec((1, D))],
        out_specs=[row_spec, row_spec, pl.BlockSpec((4, 8, D), lambda i: (0, 0, 0))],
        scratch_shapes=[pltpu.VMEM((2, D, wide), BF)],
        compiler_params=params(),
        cost_estimate=cost(28),
        name="mlp_back",
    )(*flat, *grads, resid, g, gain)


def proj_back_kernel(nr, *refs):
    proj_grad, att, att_grad, keep, send, weight = refs[4:]
    load_rows(refs[:4], False, weight, nr)
    store_halves(tn_dot(proj_grad[...], att[...]), keep, send, nr)
    att_grad[...] = nn_dot(proj_grad[...], weight[...]).astype(BF)


def proj_back(bufs, proj_grad, att, cols, rows, nr):
    bw = D // nr
    n = D // cols
    half = jax.ShapeDtypeStruct((nr // 2, cols, bw, n), BF)
    half_spec = pl.BlockSpec((nr // 2, 1, bw, n), lambda k: (0, k, 0, 0))
    col_spec = pl.BlockSpec((rows, n), lambda k: (0, k))
    return pl.pallas_call(
        partial(proj_back_kernel, nr),
        out_shape=[jax.ShapeDtypeStruct((rows, D), BF), half, half],
        grid=(cols,),
        in_specs=[proj_spec(bufs[0], cols, False)] * 4 + [const_spec((rows, D)), col_spec],
        out_specs=[col_spec, half_spec, half_spec],
        scratch_shapes=[pltpu.VMEM((D, n), BF)],
        compiler_params=params(),
        cost_estimate=cost(11),
        name="proj_back",
    )(*bufs, proj_grad, att)


def qkv_grad_kernel(nr, n1, dqkv, keep, send):
    store_halves(tn_dot(n1[...], dqkv[...]), keep, send, nr)


def qkv_grad(n1, dqkv, cols, rows, nr):
    n = 3 * D // cols
    bw = D // nr
    half = jax.ShapeDtypeStruct((nr // 2, cols, bw, n), BF)
    return pl.pallas_call(
        partial(qkv_grad_kernel, nr),
        out_shape=[half] * 2,
        grid=(cols,),
        in_specs=[const_spec((rows, D)), pl.BlockSpec((rows, n), lambda k: (0, k))],
        out_specs=[pl.BlockSpec((nr // 2, 1, bw, n), lambda k: (0, k, 0, 0))] * 2,
        compiler_params=params(),
        cost_estimate=cost(14),
        name="qkv_grad",
    )(n1, dqkv)


def input_back_kernel(cols, nr, info, *refs):
    bufs_a, bufs_b = refs[:4], refs[4:8]
    rest = refs[8:]
    dqkv, x, resid_grad, gain = rest[:4]
    pieces, sums, whole, weight = rest[4:]
    bw = D // nr

    @pl.when(pl.program_id(0) == 0)
    def _():
        load_rows(bufs_a, False, weight, nr)
        load_rows(bufs_b, True, weight, nr, bw // 2)
        sums[...] = jnp.zeros_like(sums)

    grad = nt_dot(dqkv[...], weight[...])
    back, hat = norm_back(grad, x[...].astype(F32), gain[...])
    whole[...] = resid_grad[...] + back
    take_features(whole, pieces, info, max(1, 128 * nr // D))
    sums[0] += eight(grad * hat)
    sums[1] += eight(grad)


def input_back(bufs_a, bufs_b, dqkv, x, resid_grad, gain, info, cols, rows, nr):
    width = D // cols
    row_spec = pl.BlockSpec((rows // BLOCKS, D), lambda i, s: (i, 0))
    piece = jax.ShapeDtypeStruct((cols, rows, width), BF)
    return pl.pallas_call(
        partial(input_back_kernel, cols, nr),
        out_shape=[piece, jax.ShapeDtypeStruct((2, 8, D), F32)],
        grid_spec=pltpu.PrefetchScalarGridSpec(
            num_scalar_prefetch=1,
            grid=(BLOCKS,),
            in_specs=[const_spec(bufs_a[0].shape)] * 8
            + [pl.BlockSpec((rows // BLOCKS, 3 * D), lambda i, s: (i, 0)), row_spec, row_spec]
            + [const_spec((1, D))],
            out_specs=[pl.BlockSpec((cols, rows // BLOCKS, width), lambda i, s: (0, i, 0))]
            + [pl.BlockSpec((2, 8, D), lambda i, s: (0, 0, 0))],
            scratch_shapes=[pltpu.VMEM((rows // BLOCKS, D), F32), pltpu.VMEM((D, 3 * D), BF)],
        ),
        compiler_params=params(),
        cost_estimate=cost(25),
        name="input_back",
    )(info, *bufs_a, *bufs_b, dqkv, x, resid_grad, gain)


def rel_constants():
    place = np.arange(SLOT)
    lanes = np.arange(128)
    group = lanes // 32
    row_shift = np.clip(WIN - 1 - place // WIN, 0, WIN - 1)
    col_shift = WIN - 1 - place % WIN
    shifts = np.where(group[None, :] % 2 == 0, row_shift[:, None], col_shift[:, None])
    onehot = np.zeros((2, KEYS, 128), np.float32)
    for head in range(2):
        for key in range(KEYS):
            if key >= REAL:
                onehot[head, key, 64 * head + 28] = -1e9
                continue
            for extra in (0, WIN):
                onehot[head, key, 64 * head + key // WIN + extra] = 1.0
                onehot[head, key, 64 * head + 32 + key % WIN + extra] = 1.0
    return shifts.astype(np.int32), onehot


def table_matrix(table_h, table_w):
    flipped = jnp.stack([table_h, table_w])[:, ::-1, :].astype(BF)
    block = jnp.pad(jnp.transpose(flipped, (2, 0, 1)), ((0, 0), (0, 0), (0, 5)))
    block = block.reshape(HD, HD)
    zero = jnp.zeros_like(block)
    return jnp.concatenate(
        [jnp.concatenate([block, zero], axis=1), jnp.concatenate([zero, block], axis=1)], axis=0
    )


def shift_left(values, shifts):
    for bit in (1, 2, 4, 8):
        values = jnp.where((shifts & bit) != 0, pltpu.roll(values, 128 - bit, 1), values)
    return values


def shift_right(values, shifts):
    for bit in (1, 2, 4, 8):
        values = jnp.where((shifts & bit) != 0, pltpu.roll(values, bit, 1), values)
    return values


def slot_target(field, start, rows, shape):
    base, row_low, height, col_low, width, _, _ = field
    slot = iota(shape, 0 if shape[0] > 1 else 1)
    row, col = slot // WIN, slot % WIN
    inside = (row >= row_low) & (row < row_low + height) & (col >= col_low) & (col < col_low + width)
    return jnp.where(inside, base - start + (row - row_low) * width + (col - col_low), rows)


def slots_from(field, start, source):
    rows = source.shape[0]
    line = iota((SLOT, SLAB + TAIL), 1)
    pick = as_pick(line == slot_target(field, start, SLAB + TAIL - 1, (SLOT, 1)))
    slab = jnp.concatenate([source[pl.ds(start, SLAB), :], source[rows - TAIL :, :]], axis=0)
    return pick, nn_dot(pick, slab)


def pack_of(field, start):
    line = iota((SLAB, SLOT), 0)
    return as_pick(line == slot_target(field, start, -1, (1, SLOT)))


def slab_start(field, rows):
    return pl.multiple_of(jnp.minimum(field[0] // 16 * 16, rows - SLAB), 16)


def attend_kernel(width, held, info, qkv, tables, shifts, onehot, *refs):
    att, exps, inv, keys, vals, slots, total = refs[held:]
    window = pl.program_id(1)
    first = (pl.program_id(0) == 0) & (window == 0)

    @pl.when(first)
    def _():
        for head in range(2):
            keys[head, :, :128] = jnp.zeros((KEYS, 128), BF)
            keys[head, :, 128:] = onehot[head]
        vals[:, :128] = jnp.zeros((KEYS, 128), BF)
        vals[:, 128:] = jnp.ones((KEYS, 128), BF)

    @pl.when(window == 0)
    def _():
        total[...] = jnp.zeros_like(total)

    field = window_at(info, info[0] * pl.num_programs(1) + window)
    start = slab_start(field, qkv.shape[0])
    slots[...] = slots_from(field, start, qkv)[1].astype(BF)

    lane = iota((SLOT, 128), 1)
    low = lane < HD
    inner = lane % 32
    parts = []
    for pair in range(width // 128):
        at = pair * 128
        q2 = slots[:, at : at + 128]
        k2 = slots[:, width + at : width + at + 128]
        v2 = slots[:, 2 * width + at : 2 * width + at + 128]
        rel = shift_left(nn_dot(q2, tables[...]), shifts[...])
        rel_hi = rel.astype(BF).astype(F32)
        rel_lo = pltpu.roll(rel - rel_hi, WIN, 1)
        rel = jnp.where(inner < WIN, rel_hi, jnp.where(inner < 2 * WIN, rel_lo, 1.0))
        queries = jnp.concatenate([q2 * BF(0.125), rel.astype(BF)], axis=1)
        vals[:SLOT, :128] = v2
        zero = jnp.zeros_like(k2)
        keys[0, :SLOT, :128] = jnp.where(low, k2, zero)
        keys[1, :SLOT, :128] = jnp.where(low, zero, k2)
        outs = []
        for head in range(2):
            scores = nt_dot(queries, keys[head])
            peak = jnp.max(scores, axis=1, keepdims=True)
            weights = jnp.exp(scores - peak).astype(BF)
            exps[pair * 2 + head] = weights
            outs.append(nn_dot(weights, vals[...]))
        scale = 1.0 / jnp.where(low, outs[0][:, 128:], outs[1][:, 128:])
        inv[:, at : at + 128] = scale
        parts.append((jnp.where(low, outs[0][:, :128], outs[1][:, :128]) * scale).astype(BF))
    pack = pack_of(field, start)
    total[pl.ds(start, SLAB), :] += nn_dot(pack, jnp.concatenate(parts, axis=1))

    @pl.when(window == pl.num_programs(1) - 1)
    def _():
        att[...] = total[...].astype(BF)


def attend(qkv, info, tables, shifts, onehot, base, count, held, cols, per):
    rows = qkv.shape[0]
    width = D // cols
    pairs = width // 128
    held = list(held)
    return pl.pallas_call(
        partial(attend_kernel, width, len(held)),
        out_shape=[
            jax.ShapeDtypeStruct((rows, D), BF),
            jax.ShapeDtypeStruct((D // HD, per * SLOT, KEYS), BF),
            jax.ShapeDtypeStruct((per * SLOT, D), F32),
        ],
        grid_spec=pltpu.PrefetchScalarGridSpec(
            num_scalar_prefetch=1,
            grid=(count, per),
            in_specs=[
                pl.BlockSpec((rows, 3 * width), lambda c, w, s: (0, c + base)),
                pl.BlockSpec((128, 128), lambda c, w, s: (0, 0)),
                pl.BlockSpec((SLOT, 128), lambda c, w, s: (0, 0)),
                pl.BlockSpec((2, KEYS, 128), lambda c, w, s: (0, 0, 0)),
            ]
            + [pl.BlockSpec(memory_space=pl.ANY)] * len(held),
            out_specs=[
                pl.BlockSpec((rows, width), lambda c, w, s: (0, c + base)),
                pl.BlockSpec((2 * pairs, SLOT, KEYS), lambda c, w, s: (c + base, w, 0)),
                pl.BlockSpec((SLOT, width), lambda c, w, s: (w, c + base)),
            ],
            scratch_shapes=[
                pltpu.VMEM((2, KEYS, 256), BF),
                pltpu.VMEM((KEYS, 256), BF),
                pltpu.VMEM((SLOT, 3 * width), BF),
                pltpu.VMEM((rows, width), F32),
            ],
        ),
        input_output_aliases={5 + i: i for i in range(len(held))},
        compiler_params=params(2),
        cost_estimate=cost(58 * count // cols),
        name="attend",
    )(info, qkv, tables, shifts, onehot, *held)


def attend_back_kernel(
    width, held, info, qkv, exps, inv, att, att_grad, tables2, shifts, onehot, *refs
):
    out, table_sum, bias_sum, keys, vals, slots, att_slots, grad_slots, fresh, total = refs[held:]
    window = pl.program_id(1)
    first = (pl.program_id(0) == 0) & (window == 0)

    @pl.when(first)
    def _():
        for head in range(2):
            keys[head, :, :128] = jnp.zeros((KEYS, 128), BF)
            keys[head, :, 128:] = onehot[head]
        vals[...] = jnp.zeros_like(vals)
        table_sum[...] = jnp.zeros_like(table_sum)

    @pl.when(window == 0)
    def _():
        bias_sum[...] = jnp.zeros_like(bias_sum)
        total[...] = jnp.zeros_like(total)

    field = window_at(info, info[0] * pl.num_programs(1) + window)
    start = slab_start(field, qkv.shape[0])
    pick, pulled = slots_from(field, start, qkv)
    slots[...] = pulled.astype(BF)
    att_slots[...] = nn_dot(pick[:, :SLAB], att[pl.ds(start, SLAB), :])
    grad_slots[...] = nn_dot(pick[:, :SLAB], att_grad[pl.ds(start, SLAB), :])

    lane = iota((SLOT, 128), 1)
    low = lane < HD
    inner = lane % 32
    for pair in range(width // 128):
        at = pair * 128
        q2 = slots[:, at : at + 128]
        k2 = slots[:, width + at : width + at + 128]
        v2 = slots[:, 2 * width + at : 2 * width + at + 128]
        zero = jnp.zeros_like(k2)
        keys[0, :SLOT, :128] = jnp.where(low, k2, zero)
        keys[1, :SLOT, :128] = jnp.where(low, zero, k2)
        vals[0, :SLOT, :] = jnp.where(low, v2, zero)
        vals[1, :SLOT, :] = jnp.where(low, zero, v2)
        grad = (grad_slots[:, at : at + 128] * inv[:, at : at + 128]).astype(BF)
        cross = grad.astype(F32) * att_slots[:, at : at + 128]
        dots = (
            jnp.sum(jnp.where(low, cross, 0.0), axis=1, keepdims=True),
            jnp.sum(jnp.where(low, 0.0, cross), axis=1, keepdims=True),
        )
        q_scaled = q2 * BF(0.125)
        grad_heads = (jnp.where(low, grad, zero), jnp.where(low, zero, grad))
        q_heads = (jnp.where(low, q_scaled, zero), jnp.where(low, zero, q_scaled))
        q_sum = jnp.zeros((SLOT, 256), F32)
        k_sum = jnp.zeros((KEYS, 128), F32)
        v_sum = jnp.zeros((KEYS, 128), F32)
        for head in range(2):
            weights = exps[pair * 2 + head]
            probs_grad = nt_dot(grad, vals[head])
            scores_grad = (weights.astype(F32) * (probs_grad - dots[head])).astype(BF)
            q_sum = q_sum + nn_dot(scores_grad, keys[head])
            k_sum = k_sum + tn_dot(scores_grad, q_heads[head])
            v_sum = v_sum + tn_dot(weights, grad_heads[head])
        rel = shift_right(jnp.where(inner < WIN, q_sum[:, 128:], 0.0), shifts[...])
        rel_hi = rel.astype(BF)
        rel_lo = (rel - rel_hi.astype(F32)).astype(BF)
        rel2 = jnp.concatenate([rel_hi, rel_lo], axis=1)
        q_grad = q_sum[:, :128] * 0.125 + nt_dot(rel2, tables2[...])
        table_sum[...] += tn_dot(q2, rel2)
        v_grad = v_sum[:SLOT]
        fresh[:, at : at + 128] = q_grad.astype(BF)
        fresh[:, width + at : width + at + 128] = k_sum[:SLOT].astype(BF)
        fresh[:, 2 * width + at : 2 * width + at + 128] = v_grad.astype(BF)
        bias_sum[:, at : at + 128] += eight(q_grad)
        bias_sum[:, 2 * width + at : 2 * width + at + 128] += eight(v_grad)
    pack = pack_of(field, start)
    total[pl.ds(start, SLAB), :] += nn_dot(pack, fresh[...])

    @pl.when(window == pl.num_programs(1) - 1)
    def _():
        out[...] = total[...].astype(BF)


def attend_back(
    qkv, info, exps, inv, att, att_grad, tables, shifts, onehot, base, count, held, cols, per
):
    rows = qkv.shape[0]
    width = D // cols
    pairs = width // 128
    tables2 = jnp.concatenate([tables, tables], axis=1)
    row_spec = pl.BlockSpec((rows, width), lambda c, w, s: (0, c + base))
    qkv_spec = pl.BlockSpec((rows, 3 * width), lambda c, w, s: (0, c + base))
    held = list(held)
    return pl.pallas_call(
        partial(attend_back_kernel, width, len(held)),
        out_shape=[
            jax.ShapeDtypeStruct((rows, 3 * D), BF),
            jax.ShapeDtypeStruct((128, 256), F32),
            jax.ShapeDtypeStruct((8, count * 3 * width), F32),
        ],
        grid_spec=pltpu.PrefetchScalarGridSpec(
            num_scalar_prefetch=1,
            grid=(count, per),
            in_specs=[
                qkv_spec,
                pl.BlockSpec((2 * pairs, SLOT, KEYS), lambda c, w, s: (c + base, w, 0)),
                pl.BlockSpec((SLOT, width), lambda c, w, s: (w, c + base)),
                row_spec,
                row_spec,
                pl.BlockSpec((128, 256), lambda c, w, s: (0, 0)),
                pl.BlockSpec((SLOT, 128), lambda c, w, s: (0, 0)),
                pl.BlockSpec((2, KEYS, 128), lambda c, w, s: (0, 0, 0)),
            ]
            + [pl.BlockSpec(memory_space=pl.ANY)] * len(held),
            out_specs=[
                qkv_spec,
                pl.BlockSpec((128, 256), lambda c, w, s: (0, 0)),
                pl.BlockSpec((8, 3 * width), lambda c, w, s: (0, c)),
            ],
            scratch_shapes=[
                pltpu.VMEM((2, KEYS, 256), BF),
                pltpu.VMEM((2, KEYS, 128), BF),
                pltpu.VMEM((SLOT, 3 * width), BF),
                pltpu.VMEM((SLOT, width), F32),
                pltpu.VMEM((SLOT, width), F32),
                pltpu.VMEM((SLOT, 3 * width), BF),
                pltpu.VMEM((rows, 3 * width), F32),
            ],
        ),
        input_output_aliases={9 + i: i for i in range(len(held))},
        compiler_params=params(2),
        cost_estimate=cost(54 * count // cols),
        name="attend_back",
    )(info, qkv, exps, inv, att, att_grad, tables2, shifts, onehot, *held)


def split_table(total):
    total = (total[:, :128] + total[:, 128:]).reshape(2, HD, 2, 2, 32)
    both = total[0, :, 0] + total[1, :, 1]
    both = jnp.transpose(both, (1, 2, 0))[:, :27][:, ::-1]
    return both[0], both[1]


def col_exchange(values):
    return lax.all_to_all(values, "col", 0, 0, tiled=True)


def row_swap(values, bit, nr):
    return lax.ppermute(values, "row", [(i, i ^ bit) for i in range(nr)])


def after(values, *others):
    return lax.optimization_barrier((values, *others))[0]


def gather_cols(shard, cols):
    return col_exchange(jnp.broadcast_to(shard[None], (cols,) + shard.shape))


def gather_rows(stack, nr, flip):
    order = outer_bits(nr)
    order = order[::-1] if flip else order
    held = stack[None]
    for bit in order[:-1]:
        held = jnp.concatenate([held, row_swap(held, bit, nr)], axis=0)
        yield [held]
    bufs = [held, row_swap(held, order[-1], nr)]
    yield bufs
    bufs = bufs + [row_swap(buf, 1, nr) for buf in bufs]
    yield bufs


def place_of(step, free, fixed, weights):
    total = sum(weights[b] for b in fixed)
    for i, bit in enumerate(free):
        total = total + ((step >> i) & 1) * weights[bit]
    return total


def add_kernel(counts, *refs):
    at = 0
    outs = refs[sum(counts) :]
    for count, out in zip(counts, outs):
        total = refs[at][...].astype(F32)
        for ref in refs[at + 1 : at + count]:
            total = total + ref[...].astype(F32)
        out[...] = total.astype(BF)
        at += count


def split_kernel(counts, axis, *refs):
    out = refs[sum(counts)]
    for k in range(out.shape[0]):
        at = 0
        for h, count in enumerate(counts):
            total = refs[at][0, k].astype(F32)
            for ref in refs[at + 1 : at + count]:
                total = total + ref[0, k].astype(F32)
            at += count
            size = total.shape[axis]
            where = slice(h * size, (h + 1) * size)
            if axis == -1:
                out[k, :, where] = total.astype(out.dtype)
            else:
                out[k, where, :] = total.astype(out.dtype)


def reduce_weight(keep, send, axis, cols, nr):
    arrived = row_swap(send, 1, nr)
    yield [arrived]
    bits = outer_bits(nr)
    _, _, bw, n = keep.shape
    shape = [bw, n]
    halves = 1
    if axis is not None:
        halves = 2
        shape[axis] //= 2
    block = (1, cols, shape[0], shape[1])
    terms = [[(keep, bits, True), (arrived, bits, True)] for _ in range(halves)]
    left = [list(bits) for _ in range(halves)]

    def spec(term, h, free, fixed):
        _, own, whole = term
        weights = {b: 1 << i for i, b in enumerate(own)}

        def place(step):
            spot = [place_of(step, free, fixed, weights), 0, 0, 0]
            if whole and axis is not None:
                spot[axis] = h
            return tuple(spot)

        return pl.BlockSpec(block, place)

    for step in range(len(bits)):
        sizes, specs, arrays, taken = [], [], [], []
        for h in range(halves):
            bit = bits[step] if h else bits[-1 - step]
            left[h].remove(bit)
            taken.append(bit)
            sizes.append(len(terms[h]))
            for term in terms[h]:
                specs.append(spec(term, h, left[h], [bit]))
                arrays.append(term[0])
        count = 1 << len(left[0])
        out_spec = pl.BlockSpec(block, lambda i: (i, 0, 0, 0))
        outs = pl.pallas_call(
            partial(add_kernel, sizes),
            out_shape=[jax.ShapeDtypeStruct((count,) + block[1:], BF)] * halves,
            grid=(count,),
            in_specs=specs,
            out_specs=[out_spec] * halves,
            compiler_params=params(),
            cost_estimate=cost(3),
            name="add_rows",
        )(*arrays)
        fresh = [row_swap(out, bit, nr) for out, bit in zip(outs, taken)]
        for h in range(halves):
            terms[h].append((fresh[h], list(left[h]), False))
        yield fresh

    sizes = [len(t) for t in terms]
    specs = [spec(term, h, [], []) for h in range(halves) for term in terms[h]]
    arrays = [term[0] for h in range(halves) for term in terms[h]]
    outs = pl.pallas_call(
        partial(split_kernel, sizes, -1 if axis is None else axis),
        out_shape=jax.ShapeDtypeStruct((cols, bw, n), BF),
        grid=(1,),
        in_specs=specs,
        out_specs=pl.BlockSpec((cols, bw, n), lambda i: (0, 0, 0)),
        compiler_params=params(),
        cost_estimate=cost(3),
        name="add_cols",
    )(*arrays)
    yield [outs]
    arrived = col_exchange(outs)
    yield [arrived]
    yield jnp.sum(arrived.astype(F32), axis=0)


def reduce_small(by_place, whole, cols, nr):
    size = by_place.shape[1]
    if whole is not None:
        whole = jnp.broadcast_to(whole, (cols,) + whole.shape)
        by_place = jnp.concatenate([by_place, whole], axis=1)
    arrived = col_exchange(by_place)
    yield arrived
    total = jnp.sum(arrived, axis=0)
    bit = 1
    while bit < nr:
        total = total + row_swap(total, bit, nr)
        bit *= 2
    yield total[:size], total[size:]


def pick_rows(values, order):
    rows = jnp.arange(values.shape[0], dtype=jnp.int32)
    chosen = (order[:, None] == rows[None, :]).reshape(order.shape + rows.shape + (1,) * (values.ndim - 1))
    return jnp.sum(jnp.where(chosen, values[None], 0.0), axis=1)


def body(
    cols,
    nr,
    tokens_in,
    pad_offsets,
    norm1_gain,
    norm1_bias,
    qkv_weight,
    qv_bias,
    table_height,
    table_width,
    proj_weight,
    proj_bias,
    norm2_gain,
    norm2_bias,
    fc1_weight,
    fc1_bias,
    fc2_weight,
    fc2_bias,
    out_grad,
):
    width = D // cols
    bw = D // nr
    per = -(-WINDOWS // cols)
    me = lax.axis_index("col").astype(jnp.int32)
    my_row = lax.axis_index("row").astype(jnp.int32)
    sets, rows = window_sets(cols, per)
    info = layout_info(sets, pad_offsets[0], me, my_row)
    row_order = my_row ^ jnp.arange(nr, dtype=jnp.int32)

    vec = jnp.concatenate(
        [
            norm1_gain,
            norm1_bias,
            norm2_gain,
            norm2_bias,
            proj_bias.astype(F32),
            fc2_bias.astype(F32),
            qv_bias[0].astype(F32),
            qv_bias[1].astype(F32),
            fc1_bias.astype(F32),
        ]
    )
    hidden = fc1_weight.shape[1]
    half = hidden // 2
    fc2_t = fc2_weight.T
    size = vec.shape[0]
    high = lax.reduce_precision(vec, 8, 7)
    mid = lax.reduce_precision(vec - high, 8, 7)
    low = vec - high - mid
    vec_rows = jnp.stack([high, mid, low]).astype(BF).reshape(-1, 3 * width)
    qkv_shard = jnp.concatenate([qkv_weight.reshape(bw, 3 * width), vec_rows], axis=0)
    x_sent = spread(tokens_in, info, cols, per, rows)
    qkv_stack = gather_cols(qkv_shard, cols)
    x_pieces = col_exchange(x_sent)
    vecs = jnp.sum(qkv_stack[:, bw:].astype(F32).reshape(cols, 3, size), axis=1)
    qkv_a = list(gather_rows(qkv_stack[:, : bw // 2], nr, False))[-1]
    qkv_b = list(gather_rows(qkv_stack[:, bw // 2 : bw], nr, True))[-1]
    wide0 = jnp.concatenate([fc1_weight[:, :half], proj_weight.T, fc2_t[:, :half]], axis=1)
    wide1 = jnp.concatenate([fc1_weight[:, half:], fc2_t[:, half:]], axis=1)
    stack0 = gather_cols(after(wide0, x_pieces, *qkv_a, *qkv_b), cols)
    first = half + width
    hops0 = [gather_rows(stack0[:, :, :first], nr, False), gather_rows(stack0[:, :, first:], nr, True)]

    features = vecs[:, : 6 * width].reshape(cols, 6, width // bw, bw)
    features = features.transpose(0, 2, 1, 3).reshape(nr, 6, bw)
    features = pick_rows(features, row_order).transpose(1, 0, 2).reshape(6, 1, D)
    gain1, bias1, gain2, bias2, bias_p, bias_2 = [features[i] for i in range(6)]
    q_bias = vecs[:, 6 * width : 7 * width]
    v_bias = vecs[:, 7 * width : 8 * width]
    bias_qkv = jnp.stack([q_bias, jnp.zeros_like(q_bias), v_bias], axis=1).reshape(1, 3 * D)
    bias_h = vecs[:, 8 * width :]

    x_full, n1, qkv = norm_qkv(
        x_pieces, qkv_a, qkv_b, info, gain1, bias1, bias_qkv, cols, rows, nr
    )
    shifts_np, onehot_np = rel_constants()
    shifts = jnp.asarray(shifts_np)
    onehot = jnp.asarray(onehot_np, BF)
    tables = table_matrix(table_height, table_width)
    g_pieces = col_exchange(spread(after(out_grad, n1), info, cols, per, rows))
    held = ()
    arrived = []
    for part, base in enumerate(range(0, cols, cols // SPLITS)):
        held = attend(
            after(qkv, *arrived),
            info,
            tables,
            shifts,
            onehot,
            base,
            cols // SPLITS,
            held,
            cols,
            per,
        )
        if part == 0:
            arrived = [stack0]
            stack1 = gather_cols(after(wide1, held[0]), cols)
            hops1 = [
                gather_rows(stack1[:, :, :half], nr, False),
                gather_rows(stack1[:, :, half:], nr, True),
            ]
        if part == 1:
            bufs0 = [next(hop) for hop in hops0]
            arrived = bufs0[0] + bufs0[1]
        if part == 2:
            bufs0 = [next(hop) for hop in hops0]
            arrived = bufs0[0] + bufs0[1] + [stack1]
    att, exps, inv = held
    bufs0 = [list(hop)[-1] for hop in hops0]
    bufs1 = [next(hop) for hop in hops1]
    resid, n2 = proj_norm(
        bufs0[0], after(att, *bufs1[0], *bufs1[1]), x_full, bias_p, gain2, bias2, cols, rows, nr
    )
    g_full = join(g_pieces, info, cols, rows, nr)
    bufs1 = [next(hop) for hop in hops1]
    n2 = after(n2, *bufs1[0], *bufs1[1])
    bufs1 = [list(hop)[-1] for hop in hops1]
    fc1_bufs = [bufs0[0], bufs1[0]]
    fc2_bufs = [bufs0[1], bufs1[1]]

    acts, grads, sends, hidden_sums = [], [], [], []
    for c in range(2):
        act, grad, keep, send, bias_sum = mlp_grads(
            fc1_bufs[c],
            fc2_bufs[c],
            n2,
            g_full,
            bias_h[:, None, c * half : (c + 1) * half],
            cols,
            rows,
            nr,
        )
        acts.append(act)
        grads.append(grad)
        hidden_sums.append(jnp.sum(bias_sum, axis=1))
        sends.append(reduce_weight(keep, send, -1, cols, nr))
    block_sent = block_rows(
        fc2_bufs, acts, after(resid, *next(sends[0])), bias_2, info, cols, rows, nr
    )
    block_pieces = col_exchange(block_sent)
    resid_grad, proj_grad, sums2 = mlp_back(
        fc1_bufs,
        grads,
        after(resid, block_sent, *next(sends[0]), *next(sends[1])),
        g_full,
        gain2,
        cols,
        rows,
        nr,
    )
    proj_grad = after(proj_grad, *next(sends[0]), *next(sends[1]))
    att_grad, keep, send = proj_back(fc1_bufs[0], proj_grad, att, cols, rows, nr)
    sends.append(reduce_weight(keep, send, None, cols, nr))
    held, table_sums, bias_sums = (), [], []
    for part, base in enumerate(range(0, cols, cols // SPLITS)):
        arrived = []
        if part == 1:
            arrived = [block_pieces, *next(sends[1]), *next(sends[2])]
        if part == 2:
            arrived = [*next(sends[0]), *next(sends[2])]
        if part == 3:
            arrived = [*next(sends[0]), *next(sends[1]), *next(sends[2])]
        dqkv, table_sum, bias_sum = attend_back(
            after(qkv, *arrived),
            info,
            exps,
            inv,
            att,
            att_grad,
            tables,
            shifts,
            onehot,
            base,
            cols // SPLITS,
            held,
            cols,
            per,
        )
        held = (dqkv,)
        table_sums.append(table_sum)
        bias_sums.append(bias_sum)
    table_sum = sum(table_sums[1:], table_sums[0])
    bias_sum = jnp.concatenate(bias_sums, axis=1)
    n1_back = after(n1, *next(sends[1]), *next(sends[2]), *next(sends[2]))
    keep, send = qkv_grad(n1_back, dqkv, cols, rows, nr)
    sends.append(reduce_weight(keep, send, -2, cols, nr))
    fc_grads = [list(sends[c])[-1] for c in range(2)]
    proj_w_grad = list(sends[2])[-1]
    qkv_w_grad = list(sends[3])[-1]
    ratio = width // bw
    places = jnp.arange(cols * ratio, dtype=jnp.int32) ^ my_row

    def by_col(sums):
        count = sums.shape[0]
        blocks = jnp.sum(sums, axis=1).reshape(count, nr, bw).transpose(1, 0, 2)
        picked = pick_rows(blocks, places).reshape(cols, ratio, count, bw)
        return picked.transpose(0, 2, 1, 3).reshape(cols, count * width)

    bias_cols = jnp.sum(bias_sum, axis=0).reshape(cols, 3, width)
    small = jnp.concatenate([by_col(sums2), bias_cols[:, 0], bias_cols[:, 2]] + hidden_sums, axis=1)
    table_h_grad, table_w_grad = split_table(table_sum)
    table_flat = jnp.concatenate([table_h_grad.reshape(-1), table_w_grad.reshape(-1)])
    early = reduce_small(small, table_flat, cols, nr)
    early_arrived = next(early)

    in_sent, in_sums = input_back(
        qkv_a,
        qkv_b,
        after(dqkv, keep, early_arrived),
        x_full,
        resid_grad,
        gain1,
        info,
        cols,
        rows,
        nr,
    )
    late = reduce_small(by_col(in_sums), None, cols, nr)
    late_arrived = next(late)
    in_pieces = col_exchange(after(in_sent, late_arrived))
    block_out = collect(after(block_pieces, in_sent), info, per, BF)
    input_grad = collect(in_pieces, info, per, F32)
    small, table_flat = list(early)[-1]
    late, _ = list(late)[-1]
    table_flat = table_flat.reshape(2, 27, HD)

    def part(i):
        return small[i * width : (i + 1) * width]

    return (
        block_out,
        input_grad,
        late[:width],
        late[width:],
        qkv_w_grad.reshape(bw, 3, width),
        jnp.stack([part(4), part(5)]),
        table_flat[0],
        table_flat[1],
        proj_w_grad.T,
        part(0),
        part(1),
        part(2),
        jnp.concatenate([grad[:, :half] for grad in fc_grads], axis=1),
        small[6 * width :],
        jnp.concatenate([grad[:, half:] for grad in fc_grads], axis=1).T,
        part(3),
    )


def solution(mesh):
    placed = (
        P("row", "col"),
        P("row", None),
        P("col"),
        P("col"),
        P("row", None, "col"),
        P(None, "col"),
        P(),
        P(),
        P("col", "row"),
        P("col"),
        P("col"),
        P("col"),
        P("row", "col"),
        P("col"),
        P("col", "row"),
        P("col"),
        P("row", "col"),
    )
    return jax.shard_map(
        partial(body, mesh.shape["col"], mesh.shape["row"]),
        mesh=mesh,
        in_specs=placed,
        out_specs=(
            P("row", "col"),
            P("row", "col"),
            P("col"),
            P("col"),
            P("row", None, "col"),
            P(None, "col"),
            P(),
            P(),
            P("col", "row"),
            P("col"),
            P("col"),
            P("col"),
            P("row", "col"),
            P("col"),
            P("col", "row"),
            P("col"),
        ),
        check_vma=False,
    )
```

```python
from functools import partial

import jax
import jax.numpy as jnp
import numpy as np
from jax import lax
from jax.experimental import pallas as pl
from jax.experimental.pallas import tpu as pltpu
from jax.sharding import PartitionSpec as P

D = 1024
HD = 64
WIN = 14
SIDE = 64
GRID = 5
WINDOWS = 25
REAL = 196
SLOT = 200
KEYS = 256
PIX = 4096
EPSILON = 1e-06
MARGIN = 6
PADROWS = 84
BF = jnp.bfloat16
F32 = jnp.float32
VMEM_LIMIT = 60 * 1024 * 1024
SPLITS = 4
BLOCKS = 4
SLAB = 224
FIELDS = 7
HEAD = 5
TAIL = 16


def iota(shape, dim):
    return lax.broadcasted_iota(jnp.int32, shape, dim)


def params(n=1):
    return pltpu.CompilerParams(
        dimension_semantics=("arbitrary",) * n, vmem_limit_bytes=VMEM_LIMIT
    )


def cost(micros):
    return pl.CostEstimate(
        flops=int(micros * 1.1e9), bytes_accessed=int(micros * 1e6), transcendentals=0
    )


def nt_dot(a, b):
    return lax.dot_general(a, b, (((1,), (1,)), ((), ())), preferred_element_type=F32)


def tn_dot(a, b):
    return lax.dot_general(a, b, (((0,), (0,)), ((), ())), preferred_element_type=F32)


def nn_dot(a, b):
    return lax.dot_general(a, b, (((1,), (0,)), ((), ())), preferred_element_type=F32)


def window_sets(cols, per):
    units = [[0, 4, 20, 24]]
    units += [[j, 20 + j] for j in (1, 2, 3)] + [[5 * i, 5 * i + 4] for i in (1, 2, 3)]
    units += [[5 * i + j] for i in (1, 2, 3) for j in (1, 2, 3)]
    sizes = [484] + [308] * 6 + [196] * 9
    sets = [[] for _ in range(cols)]
    loads = [0] * cols
    for unit, size in zip(units, sizes):
        open_sets = [d for d in range(cols) if len(sets[d]) + len(unit) <= per]
        best = min(open_sets, key=lambda d: loads[d])
        sets[best] += unit
        loads[best] += size
    capacity = -(-(max(loads) + TAIL) // 64) * 64
    return [own + [WINDOWS] * (per - len(own)) for own in sets], capacity


def plan_kernel(cols, per, ids, offsets, info):
    top, left = offsets[0, 0], offsets[0, 1]
    me = lax.axis_index("col").astype(jnp.int32)
    info[0] = me
    info[1] = top
    info[2] = left
    info[3] = lax.axis_index("row").astype(jnp.int32)

    def each_set(d, carry):
        def each_window(i, base):
            at = d * per + i
            win_row, win_col = ids[at] // GRID, ids[at] % GRID
            row_low = jnp.maximum(0, top - WIN * win_row)
            height = jnp.maximum(jnp.minimum(WIN, SIDE + top - WIN * win_row) - row_low, 0)
            col_low = jnp.maximum(0, left - WIN * win_col)
            width = jnp.maximum(jnp.minimum(WIN, SIDE + left - WIN * win_col) - col_low, 0)
            first = HEAD + at * FIELDS
            info[first] = base
            info[first + 1] = row_low
            info[first + 2] = height
            info[first + 3] = col_low
            info[first + 4] = width
            info[first + 5] = jnp.minimum(win_row, GRID - 1)
            info[first + 6] = win_col
            return base + height * width

        count = lax.fori_loop(0, per, each_window, jnp.int32(0))

        @pl.when(d == me)
        def _():
            info[4] = count

        return carry

    lax.fori_loop(0, cols, each_set, jnp.int32(0))


def plan(sets, offsets):
    cols, per = len(sets), len(sets[0])
    smem = pl.BlockSpec(memory_space=pltpu.SMEM)
    return pl.pallas_call(
        partial(plan_kernel, cols, per),
        out_shape=jax.ShapeDtypeStruct((HEAD + cols * per * FIELDS,), jnp.int32),
        in_specs=[smem, smem],
        out_specs=smem,
        cost_estimate=cost(2),
        name="plan",
    )(jnp.asarray(np.array(sets, np.int32).reshape(-1)), offsets)


def pack_kernel(width, weight, *refs):
    vectors, out = refs[:-1], refs[-1]
    cols, _, n = out.shape
    bw = weight.shape[0]
    rows = []
    held = jnp.concatenate([v[...].astype(F32) for v in vectors], axis=1)
    count = held.shape[1] // n
    lines = [held[:, r * n : (r + 1) * n] for r in range(count)]
    for part in range(3):
        for r in range(count):
            low = lines[r].astype(BF)
            rows.append(low.astype(F32))
            lines[r] = lines[r] - low.astype(F32)
    pad = -(3 * count) % 16
    rows = rows + [jnp.zeros((pad, n), F32)] * (pad > 0)
    extra = jnp.concatenate(rows, axis=0).astype(BF)
    for d in range(cols):
        out[d, :bw] = weight[...]
        out[d, bw:] = extra


def pack_first(weight, vectors, cols):
    bw, n = weight.shape
    total = sum(v.shape[0] for v in vectors)
    lines = -(-(3 * total // n) // 16) * 16
    return pl.pallas_call(
        partial(pack_kernel, n),
        out_shape=jax.ShapeDtypeStruct((cols, bw + lines, n), BF),
        compiler_params=pltpu.CompilerParams(vmem_limit_bytes=VMEM_LIMIT),
        cost_estimate=cost(2),
        name="pack",
    )(weight, *[v.reshape(1, -1) for v in vectors])


def window_at(info, index):
    at = HEAD + index * FIELDS
    return [info[at + f] for f in range(FIELDS)]


def target_of(field, left, row, token_col):
    base, row_low, height, col_low, width, _, win_col = field
    col = token_col + (left - WIN * win_col)
    inside = (row >= row_low) & (row < row_low + height) & (col >= col_low) & (col < col_low + width)
    return jnp.where(inside, base + (row - row_low) * width + (col - col_low), -(1 << 20))


def as_pick(mask):
    return mask.astype(F32).astype(BF)


def spread_kernel(per, info, x_ref, out, padded, total):
    top, left = info[1], info[2]
    cols, rows, width = out.shape
    padded[: MARGIN * SIDE, :] = jnp.zeros((MARGIN * SIDE, width), BF)
    padded[(MARGIN + SIDE) * SIDE :, :] = jnp.zeros(((PADROWS - MARGIN - SIDE) * SIDE, width), BF)
    padded[MARGIN * SIDE : (MARGIN + SIDE) * SIDE, :] = x_ref[...]
    token = iota((1, 256), 1)
    row, col = token // SIDE, token % SIDE
    line = iota((64, 256), 0)
    for d in range(cols):
        total[...] = jnp.zeros_like(total)

        def step(i, carry):
            field = window_at(info, d * per + i)
            base, row_low, height, _, across, win_row, _ = field
            for g in range(4):
                start = base + jnp.clip(4 * g - row_low, 0, height) * across
                start = pl.multiple_of(start // 8 * 8, 8)
                pick = as_pick(line == target_of(field, left, row + 4 * g, col) - start)
                first = pl.multiple_of((WIN * win_row + 4 * g - top + MARGIN) * SIDE, SIDE)
                total[pl.ds(start, 64), :] += nn_dot(pick, padded[pl.ds(first, 256), :])
            return carry

        lax.fori_loop(0, per, step, 0)
        out[d] = total[:rows].astype(BF)


def spread(x, info, cols, per, rows):
    width = x.shape[1]
    return pl.pallas_call(
        partial(spread_kernel, per),
        out_shape=jax.ShapeDtypeStruct((cols, rows, width), BF),
        grid_spec=pltpu.PrefetchScalarGridSpec(
            num_scalar_prefetch=1,
            grid=(1,),
            in_specs=[pl.BlockSpec((PIX, width), lambda i, s: (0, 0))],
            out_specs=pl.BlockSpec((cols, rows, width), lambda i, s: (0, 0, 0)),
            scratch_shapes=[
                pltpu.VMEM((PADROWS * SIDE, width), BF),
                pltpu.VMEM((rows + 64, width), F32),
            ],
        ),
        compiler_params=params(),
        cost_estimate=cost(7),
        name="spread",
    )(info, x)


def collect_kernel(places, per, info, pieces, out, padded):
    top, left = info[1], info[2]
    _, rows, _ = pieces.shape
    token = iota((1, 256), 1)
    row, col = token // SIDE, token % SIDE
    line = iota((80, 256), 0)
    for win_row in range(GRID):

        def step(g, carry):
            picks, slabs = [], []
            for win_col in range(GRID):
                d, i = places[win_row * GRID + win_col]
                field = window_at(info, d * per + i)
                base, row_low, height, _, across, _, _ = field
                start = base + jnp.clip(4 * g - row_low, 0, height) * across
                start = pl.multiple_of(jnp.minimum(start // 16 * 16, rows - 80), 16)
                picks.append(as_pick(line == target_of(field, left, row + 4 * g, col) - start))
                slabs.append(pieces[d, pl.ds(start, 80), :])
            found = tn_dot(jnp.concatenate(picks, axis=0), jnp.concatenate(slabs, axis=0))
            first = pl.multiple_of((WIN * win_row + 4 * g - top + MARGIN) * SIDE, SIDE)
            padded[pl.ds(first, 256), :] = found.astype(BF)
            return carry

        lax.fori_loop(0, 4, step, 0)
    out[...] = padded[MARGIN * SIDE : (MARGIN + SIDE) * SIDE, :].astype(out.dtype)


def collect(pieces, sets, info, dtype):
    cols, rows, width = pieces.shape
    per = len(sets[0])
    places = {w: (d, i) for d, own in enumerate(sets) for i, w in enumerate(own)}
    return pl.pallas_call(
        partial(collect_kernel, places, per),
        out_shape=jax.ShapeDtypeStruct((PIX, width), dtype),
        grid_spec=pltpu.PrefetchScalarGridSpec(
            num_scalar_prefetch=1,
            grid=(1,),
            in_specs=[pl.BlockSpec((cols, rows, width), lambda i, s: (0, 0, 0))],
            out_specs=pl.BlockSpec((PIX, width), lambda i, s: (0, 0)),
            scratch_shapes=[pltpu.VMEM((PADROWS * SIDE, width), BF)],
        ),
        compiler_params=params(),
        cost_estimate=cost(8),
        name="collect",
    )(info, pieces)


def chunk_place(col, part, width, info, parts):
    return (col * (width // 128) + part) ^ (info[3] // parts)


def swap_halves(values, info, parts):
    if parts == 1:
        return values
    return jnp.where(info[3] % 2 == 1, pltpu.roll(values.astype(F32), 64, 1), values.astype(F32))


def place_features(pieces, info, parts, whole):
    cols, _, width = pieces.shape
    for d in range(cols):
        for c in range(width // 128):
            at = pl.multiple_of(chunk_place(d, c, width, info, parts) * 128, 128)
            values = swap_halves(pieces[d, :, c * 128 : (c + 1) * 128], info, parts)
            whole[:, pl.ds(at, 128)] = values.astype(whole.dtype)


def take_features(whole, pieces, info, parts):
    cols, _, width = pieces.shape
    for d in range(cols):
        for c in range(width // 128):
            at = pl.multiple_of(chunk_place(d, c, width, info, parts) * 128, 128)
            values = swap_halves(whole[:, pl.ds(at, 128)], info, parts)
            pieces[d, :, c * 128 : (c + 1) * 128] = values.astype(BF)


def eight(values):
    total = values[:8]
    for r in range(8, values.shape[0], 8):
        total = total + values[r : r + 8]
    return total


def row_places(nr, flip):
    order = outer_bits(nr)
    order = order[::-1] if flip else order
    held = [0]
    for bit in order[:-1]:
        held = held + [place | bit for place in held]
    groups = [held, [place | order[-1] for place in held]]
    groups = groups + [[place | 1 for place in group] for group in groups]
    where = {place: (g, i) for g, group in enumerate(groups) for i, place in enumerate(group)}
    return [where[place] for place in range(nr)]


def outer_bits(nr):
    return [1 << b for b in range(1, nr.bit_length() - 1)]


def load_rows(bufs, flip, scratch, nr, first=0):
    stride = D // nr
    for p, (g, i) in enumerate(row_places(nr, flip)):
        cols, size, n = bufs[g].shape[1:]
        for k in range(cols):
            at = p * stride + first
            scratch[at : at + size, k * n : (k + 1) * n] = bufs[g][i, k]


def const_spec(shape):
    zeros = (0,) * len(shape)
    return pl.BlockSpec(shape, lambda *a: zeros, pipeline_mode=pl.Buffered(1))


def norm_qkv_kernel(cols, nr, info, *refs):
    pieces = refs[0]
    bufs_a, bufs_b = refs[1:5], refs[5:9]
    gain, bias, bias_qkv, x_out, n_out, qkv_out, whole, weight = refs[9:]
    parts = max(1, 128 * nr // D)
    bw = D // nr

    @pl.when(pl.program_id(0) == 0)
    def _():
        load_rows(bufs_a, False, weight, nr)
        load_rows(bufs_b, True, weight, nr, bw // 2)

    place_features(pieces, info, parts, whole)
    values = whole[...]
    x_out[...] = values.astype(BF)
    mean = jnp.mean(values, axis=1, keepdims=True)
    centred = values - mean
    spread_sq = jnp.mean(centred * centred, axis=1, keepdims=True)
    normed = centred * lax.rsqrt(spread_sq + EPSILON) * gain[...] + bias[...]
    size = values.shape[0]
    real = iota((size, 1), 0) < info[4] - pl.program_id(0) * size
    normed = jnp.where(real, normed, 0.0).astype(BF)
    n_out[...] = normed
    qkv_out[...] = (nn_dot(normed, weight[...]) + bias_qkv[...]).astype(BF)


def norm_qkv(pieces, bufs_a, bufs_b, info, gain, bias, bias_qkv, cols, rows, nr):
    width = D // cols
    return pl.pallas_call(
        partial(norm_qkv_kernel, cols, nr),
        out_shape=[
            jax.ShapeDtypeStruct((rows, D), BF),
            jax.ShapeDtypeStruct((rows, D), BF),
            jax.ShapeDtypeStruct((rows, 3 * D), BF),
        ],
        grid_spec=pltpu.PrefetchScalarGridSpec(
            num_scalar_prefetch=1,
            grid=(BLOCKS,),
            in_specs=[pl.BlockSpec((cols, rows // BLOCKS, width), lambda i, s: (0, i, 0))]
            + [const_spec(bufs_a[0].shape)] * 8
            + [const_spec((1, D)), const_spec((1, D)), const_spec((1, 3 * D))],
            out_specs=[
                pl.BlockSpec((rows // BLOCKS, D), lambda i, s: (i, 0)),
                pl.BlockSpec((rows // BLOCKS, D), lambda i, s: (i, 0)),
                pl.BlockSpec((rows // BLOCKS, 3 * D), lambda i, s: (i, 0)),
            ],
            scratch_shapes=[pltpu.VMEM((rows // BLOCKS, D), F32), pltpu.VMEM((D, 3 * D), BF)],
        ),
        compiler_params=params(),
        cost_estimate=cost(19),
        name="norm_qkv",
    )(info, pieces, *bufs_a, *bufs_b, gain, bias, bias_qkv)


def join_kernel(cols, nr, info, *refs):
    place_features(refs[0], info, max(1, 128 * nr // D), refs[1])


def join(pieces, info, cols, rows, nr):
    width = pieces.shape[-1]
    return pl.pallas_call(
        partial(join_kernel, cols, nr),
        out_shape=jax.ShapeDtypeStruct((rows, D), BF),
        grid_spec=pltpu.PrefetchScalarGridSpec(
            num_scalar_prefetch=1,
            grid=(BLOCKS,),
            in_specs=[pl.BlockSpec((cols, rows // BLOCKS, width), lambda i, s: (0, i, 0))],
            out_specs=pl.BlockSpec((rows // BLOCKS, D), lambda i, s: (i, 0)),
        ),
        compiler_params=params(),
        cost_estimate=cost(7),
        name="join",
    )(info, pieces)


def proj_norm_kernel(nr, *refs):
    att, x, bias_p, gain, bias, resid_out, n_out, weight = refs[4:]

    @pl.when(pl.program_id(0) == 0)
    def _():
        load_rows(refs[:4], False, weight, nr)

    values = x[...].astype(F32) + nt_dot(att[...], weight[...]) + bias_p[...]
    resid_out[...] = values
    mean = jnp.mean(values, axis=1, keepdims=True)
    centred = values - mean
    spread_sq = jnp.mean(centred * centred, axis=1, keepdims=True)
    n_out[...] = (centred * lax.rsqrt(spread_sq + EPSILON) * gain[...] + bias[...]).astype(BF)


def proj_spec(buf, cols, whole):
    n = D // cols
    shape = (buf.shape[0], cols if whole else 1, buf.shape[2], n)
    last = buf.shape[3] // n - 1
    if whole:
        return pl.BlockSpec(shape, lambda *a: (0, 0, 0, last), pipeline_mode=pl.Buffered(1))
    return pl.BlockSpec(shape, lambda k: (0, k, 0, last))


def proj_norm(bufs, att, x, bias_p, gain, bias, cols, rows, nr):
    row_spec = pl.BlockSpec((rows // BLOCKS, D), lambda i: (i, 0))
    return pl.pallas_call(
        partial(proj_norm_kernel, nr),
        out_shape=[jax.ShapeDtypeStruct((rows, D), F32), jax.ShapeDtypeStruct((rows, D), BF)],
        grid=(BLOCKS,),
        in_specs=[proj_spec(bufs[0], cols, True)] * 4
        + [row_spec, row_spec, const_spec((1, D)), const_spec((1, D)), const_spec((1, D))],
        out_specs=[row_spec, row_spec],
        scratch_shapes=[pltpu.VMEM((D, D), BF)],
        compiler_params=params(),
        cost_estimate=cost(11),
        name="proj_norm",
    )(*bufs, att, x, bias_p, gain, bias)


def gelu_and_slope(v):
    below = 0.5 + 0.5 * lax.erf(v * 0.7071067811865476)
    bell = jnp.exp(v * v * -0.5)
    return v * below, below + v * bell * 0.3989422804014327


def store_halves(grad, keep, send, nr, lanes=slice(None)):
    bw = D // nr
    for q in range(nr // 2):
        at = 2 * q * bw
        keep[q, 0, :, lanes] = grad[at : at + bw].astype(BF)
        send[q, 0, :, lanes] = grad[at + bw : at + 2 * bw].astype(BF)


def mlp_grads_kernel(nr, *refs):
    n2, g, bias, act, pre_grad, keep, send, bias_sum, w1, w2 = refs[8:]
    n = w1.shape[1]
    load_rows(refs[:4], False, w1, nr)
    load_rows(refs[4:8], True, w2, nr)
    total = None
    size = n2.shape[0] // BLOCKS
    for r in range(0, n2.shape[0], size):
        pre = nn_dot(n2[r : r + size], w1[...]) + bias[0]
        act_grad = nn_dot(g[r : r + size], w2[...])
        value, slope = gelu_and_slope(pre)
        act[r : r + size] = value.astype(BF)
        grad = act_grad * slope
        pre_grad[r : r + size] = grad.astype(BF)
        part = eight(grad)
        total = part if total is None else total + part
    bias_sum[0] = total
    store_halves(tn_dot(n2[...], pre_grad[...]), keep, send, nr, slice(0, n))
    store_halves(tn_dot(g[...], act[...]), keep, send, nr, slice(n, 2 * n))


def mlp_grads(bufs1, bufs2, n2, g, bias, cols, rows, nr):
    bw = D // nr
    n = bufs2[0].shape[-1]
    w_spec = pl.BlockSpec((nr // 4, 1, bw, n), lambda k: (0, k, 0, 0))
    row_spec = pl.BlockSpec((rows, n), lambda k: (0, k))
    half_spec = pl.BlockSpec((nr // 2, 1, bw, 2 * n), lambda k: (0, k, 0, 0))
    half = jax.ShapeDtypeStruct((nr // 2, cols, bw, 2 * n), BF)
    act = jax.ShapeDtypeStruct((rows, cols * n), BF)
    return pl.pallas_call(
        partial(mlp_grads_kernel, nr),
        out_shape=[act, act, half, half, jax.ShapeDtypeStruct((cols, 8, n), F32)],
        grid=(cols,),
        in_specs=[w_spec] * 8
        + [const_spec((rows, D)), const_spec((rows, D)), pl.BlockSpec((1, 1, n), lambda k: (k, 0, 0))],
        out_specs=[row_spec, row_spec, half_spec, half_spec]
        + [pl.BlockSpec((1, 8, n), lambda k: (k, 0, 0))],
        scratch_shapes=[pltpu.VMEM((D, n), BF)] * 2,
        compiler_params=params(),
        cost_estimate=cost(38),
        name="mlp_grads",
    )(*bufs1, *bufs2, n2, g, bias)


def norm_back(grad, values, gain):
    mean = jnp.mean(values, axis=1, keepdims=True)
    centred = values - mean
    spread_sq = jnp.mean(centred * centred, axis=1, keepdims=True)
    inv = lax.rsqrt(spread_sq + EPSILON)
    hat = centred * inv
    scaled = grad * gain
    first = jnp.mean(scaled, axis=1, keepdims=True)
    second = jnp.mean(scaled * hat, axis=1, keepdims=True)
    return (scaled - first - hat * second) * inv, hat


def block_out_kernel(cols, nr, info, *refs):
    act0, act1, resid, bias_2 = refs[8:12]
    pieces, weight, whole = refs[12:]

    @pl.when(pl.program_id(0) == 0)
    def _():
        load_rows(refs[:4], True, weight.at[0], nr)
        load_rows(refs[4:8], True, weight.at[1], nr)

    out = nt_dot(act0[...], weight[0]) + nt_dot(act1[...], weight[1])
    whole[...] = resid[...] + out + bias_2[...]
    take_features(whole, pieces, info, max(1, 128 * nr // D))


def block_rows(groups, acts, resid, bias_2, info, cols, rows, nr):
    width = D // cols
    wide = acts[0].shape[1]
    row_spec = pl.BlockSpec((rows // BLOCKS, D), lambda i, s: (i, 0))
    wide_spec = pl.BlockSpec((rows // BLOCKS, wide), lambda i, s: (i, 0))
    flat = [b for group in groups for b in group]
    return pl.pallas_call(
        partial(block_out_kernel, cols, nr),
        out_shape=[jax.ShapeDtypeStruct((cols, rows, width), BF)],
        grid_spec=pltpu.PrefetchScalarGridSpec(
            num_scalar_prefetch=1,
            grid=(BLOCKS,),
            in_specs=[const_spec(flat[-1].shape)] * 8
            + [wide_spec] * 2
            + [row_spec, const_spec((1, D))],
            out_specs=[pl.BlockSpec((cols, rows // BLOCKS, width), lambda i, s: (0, i, 0))],
            scratch_shapes=[pltpu.VMEM((2, D, wide), BF), pltpu.VMEM((rows // BLOCKS, D), F32)],
        ),
        compiler_params=params(),
        cost_estimate=cost(26),
        name="block_rows",
    )(info, *flat, *acts, resid, bias_2)[0]


def mlp_back_kernel(nr, *refs):
    grad0, grad1, resid, g, gain, resid_grad, proj_grad, sums, weight = refs[8:]

    @pl.when(pl.program_id(0) == 0)
    def _():
        load_rows(refs[:4], False, weight.at[0], nr)
        load_rows(refs[4:8], False, weight.at[1], nr)
        sums[...] = jnp.zeros_like(sums)

    grad = nt_dot(grad0[...], weight[0]) + nt_dot(grad1[...], weight[1])
    g_f = g[...].astype(F32)
    back, hat = norm_back(grad, resid[...], gain[...])
    total = g_f + back
    resid_grad[...] = total
    low = total.astype(BF)
    proj_grad[...] = low
    sums[0] += eight(low.astype(F32))
    sums[1] += eight(grad * hat)
    sums[2] += eight(grad)
    sums[3] += eight(g_f)


def mlp_back(groups, grads, resid, g, gain, cols, rows, nr):
    wide = grads[0].shape[1]
    row_spec = pl.BlockSpec((rows // BLOCKS, D), lambda i: (i, 0))
    wide_spec = pl.BlockSpec((rows // BLOCKS, wide), lambda i: (i, 0))
    flat = [b for group in groups for b in group]
    shape = flat[-1].shape
    return pl.pallas_call(
        partial(mlp_back_kernel, nr),
        out_shape=[
            jax.ShapeDtypeStruct((rows, D), F32),
            jax.ShapeDtypeStruct((rows, D), BF),
            jax.ShapeDtypeStruct((4, 8, D), F32),
        ],
        grid=(BLOCKS,),
        in_specs=[const_spec(shape)] * 8
        + [wide_spec] * 2
        + [row_spec, row_spec, const_spec((1, D))],
        out_specs=[row_spec, row_spec, pl.BlockSpec((4, 8, D), lambda i: (0, 0, 0))],
        scratch_shapes=[pltpu.VMEM((2, D, wide), BF)],
        compiler_params=params(),
        cost_estimate=cost(28),
        name="mlp_back",
    )(*flat, *grads, resid, g, gain)


def proj_back_kernel(nr, *refs):
    proj_grad, att, att_grad, keep, send, weight = refs[4:]
    load_rows(refs[:4], False, weight, nr)
    store_halves(tn_dot(proj_grad[...], att[...]), keep, send, nr)
    att_grad[...] = nn_dot(proj_grad[...], weight[...]).astype(BF)


def proj_back(bufs, proj_grad, att, cols, rows, nr):
    bw = D // nr
    n = D // cols
    half = jax.ShapeDtypeStruct((nr // 2, cols, bw, n), BF)
    half_spec = pl.BlockSpec((nr // 2, 1, bw, n), lambda k: (0, k, 0, 0))
    col_spec = pl.BlockSpec((rows, n), lambda k: (0, k))
    return pl.pallas_call(
        partial(proj_back_kernel, nr),
        out_shape=[jax.ShapeDtypeStruct((rows, D), BF), half, half],
        grid=(cols,),
        in_specs=[proj_spec(bufs[0], cols, False)] * 4 + [const_spec((rows, D)), col_spec],
        out_specs=[col_spec, half_spec, half_spec],
        scratch_shapes=[pltpu.VMEM((D, n), BF)],
        compiler_params=params(),
        cost_estimate=cost(11),
        name="proj_back",
    )(*bufs, proj_grad, att)


def qkv_grad_kernel(nr, n1, dqkv, keep, send):
    store_halves(tn_dot(n1[...], dqkv[...]), keep, send, nr)


def qkv_grad(n1, dqkv, cols, rows, nr):
    n = 3 * D // cols
    bw = D // nr
    half = jax.ShapeDtypeStruct((nr // 2, cols, bw, n), BF)
    return pl.pallas_call(
        partial(qkv_grad_kernel, nr),
        out_shape=[half] * 2,
        grid=(cols,),
        in_specs=[const_spec((rows, D)), pl.BlockSpec((rows, n), lambda k: (0, k))],
        out_specs=[pl.BlockSpec((nr // 2, 1, bw, n), lambda k: (0, k, 0, 0))] * 2,
        compiler_params=params(),
        cost_estimate=cost(14),
        name="qkv_grad",
    )(n1, dqkv)


def input_back_kernel(cols, nr, info, *refs):
    bufs_a, bufs_b = refs[:4], refs[4:8]
    rest = refs[8:]
    dqkv, x, resid_grad, gain = rest[:4]
    pieces, sums, whole, weight = rest[4:]
    bw = D // nr

    @pl.when(pl.program_id(0) == 0)
    def _():
        load_rows(bufs_a, False, weight, nr)
        load_rows(bufs_b, True, weight, nr, bw // 2)
        sums[...] = jnp.zeros_like(sums)

    grad = nt_dot(dqkv[...], weight[...])
    back, hat = norm_back(grad, x[...].astype(F32), gain[...])
    whole[...] = resid_grad[...] + back
    take_features(whole, pieces, info, max(1, 128 * nr // D))
    sums[0] += eight(grad * hat)
    sums[1] += eight(grad)


def input_back(bufs_a, bufs_b, dqkv, x, resid_grad, gain, info, cols, rows, nr):
    width = D // cols
    row_spec = pl.BlockSpec((rows // BLOCKS, D), lambda i, s: (i, 0))
    piece = jax.ShapeDtypeStruct((cols, rows, width), BF)
    return pl.pallas_call(
        partial(input_back_kernel, cols, nr),
        out_shape=[piece, jax.ShapeDtypeStruct((2, 8, D), F32)],
        grid_spec=pltpu.PrefetchScalarGridSpec(
            num_scalar_prefetch=1,
            grid=(BLOCKS,),
            in_specs=[const_spec(bufs_a[0].shape)] * 8
            + [pl.BlockSpec((rows // BLOCKS, 3 * D), lambda i, s: (i, 0)), row_spec, row_spec]
            + [const_spec((1, D))],
            out_specs=[pl.BlockSpec((cols, rows // BLOCKS, width), lambda i, s: (0, i, 0))]
            + [pl.BlockSpec((2, 8, D), lambda i, s: (0, 0, 0))],
            scratch_shapes=[pltpu.VMEM((rows // BLOCKS, D), F32), pltpu.VMEM((D, 3 * D), BF)],
        ),
        compiler_params=params(),
        cost_estimate=cost(25),
        name="input_back",
    )(info, *bufs_a, *bufs_b, dqkv, x, resid_grad, gain)


def rel_constants():
    place = np.arange(SLOT)
    lanes = np.arange(128)
    group = lanes // 32
    row_shift = np.clip(WIN - 1 - place // WIN, 0, WIN - 1)
    col_shift = WIN - 1 - place % WIN
    shifts = np.where(group[None, :] % 2 == 0, row_shift[:, None], col_shift[:, None])
    onehot = np.zeros((2, KEYS, 128), np.float32)
    for head in range(2):
        for key in range(KEYS):
            if key >= REAL:
                onehot[head, key, 64 * head + 28] = -1e9
                continue
            for extra in (0, WIN):
                onehot[head, key, 64 * head + key // WIN + extra] = 1.0
                onehot[head, key, 64 * head + 32 + key % WIN + extra] = 1.0
    return shifts.astype(np.int32), onehot


def table_matrix(table_h, table_w):
    flipped = jnp.stack([table_h, table_w])[:, ::-1, :].astype(BF)
    block = jnp.pad(jnp.transpose(flipped, (2, 0, 1)), ((0, 0), (0, 0), (0, 5)))
    block = block.reshape(HD, HD)
    zero = jnp.zeros_like(block)
    return jnp.concatenate(
        [jnp.concatenate([block, zero], axis=1), jnp.concatenate([zero, block], axis=1)], axis=0
    )


def shift_left(values, shifts):
    for bit in (1, 2, 4, 8):
        values = jnp.where((shifts & bit) != 0, pltpu.roll(values, 128 - bit, 1), values)
    return values


def shift_right(values, shifts):
    for bit in (1, 2, 4, 8):
        values = jnp.where((shifts & bit) != 0, pltpu.roll(values, bit, 1), values)
    return values


def slot_target(field, start, rows, shape):
    base, row_low, height, col_low, width, _, _ = field
    slot = iota(shape, 0 if shape[0] > 1 else 1)
    row, col = slot // WIN, slot % WIN
    inside = (row >= row_low) & (row < row_low + height) & (col >= col_low) & (col < col_low + width)
    return jnp.where(inside, base - start + (row - row_low) * width + (col - col_low), rows)


def slots_from(field, start, source):
    rows = source.shape[0]
    line = iota((SLOT, SLAB + TAIL), 1)
    pick = as_pick(line == slot_target(field, start, SLAB + TAIL - 1, (SLOT, 1)))
    slab = jnp.concatenate([source[pl.ds(start, SLAB), :], source[rows - TAIL :, :]], axis=0)
    return pick, nn_dot(pick, slab)


def pack_of(field, start):
    line = iota((SLAB, SLOT), 0)
    return as_pick(line == slot_target(field, start, -1, (1, SLOT)))


def slab_start(field, rows):
    return pl.multiple_of(jnp.minimum(field[0] // 16 * 16, rows - SLAB), 16)


def attend_kernel(width, held, info, qkv, tables, shifts, onehot, *refs):
    att, exps, inv, keys, vals, slots, total = refs[held:]
    window = pl.program_id(1)
    first = (pl.program_id(0) == 0) & (window == 0)

    @pl.when(first)
    def _():
        for head in range(2 * (width // 128)):
            keys[head, :, :128] = jnp.zeros((KEYS, 128), BF)
            keys[head, :, 128:] = onehot[head % 2]
        for pair in range(width // 128):
            vals[pair, :, :128] = jnp.zeros((KEYS, 128), BF)
            vals[pair, :, 128:] = jnp.ones((KEYS, 128), BF)

    @pl.when(window == 0)
    def _():
        total[...] = jnp.zeros_like(total)

    field = window_at(info, info[0] * pl.num_programs(1) + window)
    start = slab_start(field, qkv.shape[0])
    slots[...] = slots_from(field, start, qkv)[1].astype(BF)

    lane = iota((SLOT, 128), 1)
    low = lane < HD
    inner = lane % 32
    pairs = width // 128
    queries = []
    for pair in range(pairs):
        at = pair * 128
        q2 = slots[:, at : at + 128]
        k2 = slots[:, width + at : width + at + 128]
        vals[pair, :SLOT, :128] = slots[:, 2 * width + at : 2 * width + at + 128]
        zero = jnp.zeros_like(k2)
        keys[2 * pair, :SLOT, :128] = jnp.where(low, k2, zero)
        keys[2 * pair + 1, :SLOT, :128] = jnp.where(low, zero, k2)
        rel = shift_left(nn_dot(q2, tables[...]), shifts[...])
        rel_hi = rel.astype(BF).astype(F32)
        rel_lo = pltpu.roll(rel - rel_hi, WIN, 1)
        rel = jnp.where(inner < WIN, rel_hi, jnp.where(inner < 2 * WIN, rel_lo, 1.0))
        queries.append(jnp.concatenate([q2 * BF(0.125), rel.astype(BF)], axis=1))
    scores = [nt_dot(queries[head // 2], keys[head]) for head in range(2 * pairs)]
    weights = []
    for head in range(2 * pairs):
        peak = jnp.max(scores[head], axis=1, keepdims=True)
        weights.append(jnp.exp(scores[head] - peak).astype(BF))
        exps[head] = weights[head]
    outs = [nn_dot(weights[head], vals[head // 2]) for head in range(2 * pairs)]
    parts = []
    for pair in range(pairs):
        at = pair * 128
        first, second = outs[2 * pair], outs[2 * pair + 1]
        scale = 1.0 / jnp.where(low, first[:, 128:], second[:, 128:])
        inv[:, at : at + 128] = scale
        parts.append((jnp.where(low, first[:, :128], second[:, :128]) * scale).astype(BF))
    pack = pack_of(field, start)
    total[pl.ds(start, SLAB), :] += nn_dot(pack, jnp.concatenate(parts, axis=1))

    @pl.when(window == pl.num_programs(1) - 1)
    def _():
        att[...] = total[...].astype(BF)


def attend(qkv, info, tables, shifts, onehot, base, count, held, cols, per):
    rows = qkv.shape[0]
    width = D // cols
    pairs = width // 128
    held = list(held)
    return pl.pallas_call(
        partial(attend_kernel, width, len(held)),
        out_shape=[
            jax.ShapeDtypeStruct((rows, D), BF),
            jax.ShapeDtypeStruct((D // HD, per * SLOT, KEYS), BF),
            jax.ShapeDtypeStruct((per * SLOT, D), F32),
        ],
        grid_spec=pltpu.PrefetchScalarGridSpec(
            num_scalar_prefetch=1,
            grid=(count, per),
            in_specs=[
                pl.BlockSpec((rows, 3 * width), lambda c, w, s: (0, c + base)),
                pl.BlockSpec((128, 128), lambda c, w, s: (0, 0)),
                pl.BlockSpec((SLOT, 128), lambda c, w, s: (0, 0)),
                pl.BlockSpec((2, KEYS, 128), lambda c, w, s: (0, 0, 0)),
            ]
            + [pl.BlockSpec(memory_space=pl.ANY)] * len(held),
            out_specs=[
                pl.BlockSpec((rows, width), lambda c, w, s: (0, c + base)),
                pl.BlockSpec((2 * pairs, SLOT, KEYS), lambda c, w, s: (c + base, w, 0)),
                pl.BlockSpec((SLOT, width), lambda c, w, s: (w, c + base)),
            ],
            scratch_shapes=[
                pltpu.VMEM((2 * pairs, KEYS, 256), BF),
                pltpu.VMEM((pairs, KEYS, 256), BF),
                pltpu.VMEM((SLOT, 3 * width), BF),
                pltpu.VMEM((rows, width), F32),
            ],
        ),
        input_output_aliases={5 + i: i for i in range(len(held))},
        compiler_params=params(2),
        cost_estimate=cost(58 * count // cols),
        name="attend",
    )(info, qkv, tables, shifts, onehot, *held)


def attend_back_kernel(
    width, held, info, qkv, exps, inv, att, att_grad, tables2, shifts, onehot, *refs
):
    out, table_sum, bias_sum, keys, vals, slots, att_slots, grad_slots, fresh, total = refs[held:]
    window = pl.program_id(1)
    first = (pl.program_id(0) == 0) & (window == 0)

    @pl.when(first)
    def _():
        for head in range(2 * (width // 128)):
            keys[head, :, :128] = jnp.zeros((KEYS, 128), BF)
            keys[head, :, 128:] = onehot[head % 2]
        vals[...] = jnp.zeros_like(vals)
        table_sum[...] = jnp.zeros_like(table_sum)

    @pl.when(window == 0)
    def _():
        bias_sum[...] = jnp.zeros_like(bias_sum)
        total[...] = jnp.zeros_like(total)

    field = window_at(info, info[0] * pl.num_programs(1) + window)
    start = slab_start(field, qkv.shape[0])
    pick, pulled = slots_from(field, start, qkv)
    slots[...] = pulled.astype(BF)
    att_slots[...] = nn_dot(pick[:, :SLAB], att[pl.ds(start, SLAB), :])
    grad_slots[...] = nn_dot(pick[:, :SLAB], att_grad[pl.ds(start, SLAB), :])

    lane = iota((SLOT, 128), 1)
    low = lane < HD
    inner = lane % 32
    pairs = width // 128
    q_all, grads, dots = [], [], []
    for pair in range(pairs):
        at = pair * 128
        q2 = slots[:, at : at + 128]
        k2 = slots[:, width + at : width + at + 128]
        v2 = slots[:, 2 * width + at : 2 * width + at + 128]
        zero = jnp.zeros_like(k2)
        keys[2 * pair, :SLOT, :128] = jnp.where(low, k2, zero)
        keys[2 * pair + 1, :SLOT, :128] = jnp.where(low, zero, k2)
        vals[2 * pair, :SLOT, :] = jnp.where(low, v2, zero)
        vals[2 * pair + 1, :SLOT, :] = jnp.where(low, zero, v2)
        grad = (grad_slots[:, at : at + 128] * inv[:, at : at + 128]).astype(BF)
        cross = grad.astype(F32) * att_slots[:, at : at + 128]
        dots.append(jnp.sum(jnp.where(low, cross, 0.0), axis=1, keepdims=True))
        dots.append(jnp.sum(jnp.where(low, 0.0, cross), axis=1, keepdims=True))
        q_all.append(q2)
        grads.append(grad)
    probs_grads = [nt_dot(grads[head // 2], vals[head]) for head in range(2 * pairs)]
    scores_grads = []
    for head in range(2 * pairs):
        weights = exps[head].astype(F32)
        scores_grads.append((weights * (probs_grads[head] - dots[head])).astype(BF))
    for pair in range(pairs):
        at = pair * 128
        q2, grad = q_all[pair], grads[pair]
        zero = jnp.zeros_like(grad)
        q_scaled = q2 * BF(0.125)
        grad_heads = (jnp.where(low, grad, zero), jnp.where(low, zero, grad))
        q_heads = (jnp.where(low, q_scaled, zero), jnp.where(low, zero, q_scaled))
        q_sum, k_sum, v_sum = None, None, None
        for head in range(2):
            which = 2 * pair + head
            q_part = nn_dot(scores_grads[which], keys[which])
            k_part = tn_dot(scores_grads[which], q_heads[head])
            v_part = tn_dot(exps[which], grad_heads[head])
            q_sum = q_part if q_sum is None else q_sum + q_part
            k_sum = k_part if k_sum is None else k_sum + k_part
            v_sum = v_part if v_sum is None else v_sum + v_part
        rel = shift_right(jnp.where(inner < WIN, q_sum[:, 128:], 0.0), shifts[...])
        rel_hi = rel.astype(BF)
        rel_lo = (rel - rel_hi.astype(F32)).astype(BF)
        rel2 = jnp.concatenate([rel_hi, rel_lo], axis=1)
        q_grad = q_sum[:, :128] * 0.125 + nt_dot(rel2, tables2[...])
        table_sum[...] += tn_dot(q2, rel2)
        v_grad = v_sum[:SLOT]
        fresh[:, at : at + 128] = q_grad.astype(BF)
        fresh[:, width + at : width + at + 128] = k_sum[:SLOT].astype(BF)
        fresh[:, 2 * width + at : 2 * width + at + 128] = v_grad.astype(BF)
        bias_sum[:, at : at + 128] += eight(q_grad)
        bias_sum[:, 2 * width + at : 2 * width + at + 128] += eight(v_grad)
    pack = pack_of(field, start)
    total[pl.ds(start, SLAB), :] += nn_dot(pack, fresh[...])

    @pl.when(window == pl.num_programs(1) - 1)
    def _():
        out[...] = total[...].astype(BF)


def attend_back(
    qkv, info, exps, inv, att, att_grad, tables, shifts, onehot, base, count, held, cols, per
):
    rows = qkv.shape[0]
    width = D // cols
    pairs = width // 128
    tables2 = jnp.concatenate([tables, tables], axis=1)
    row_spec = pl.BlockSpec((rows, width), lambda c, w, s: (0, c + base))
    qkv_spec = pl.BlockSpec((rows, 3 * width), lambda c, w, s: (0, c + base))
    held = list(held)
    return pl.pallas_call(
        partial(attend_back_kernel, width, len(held)),
        out_shape=[
            jax.ShapeDtypeStruct((rows, 3 * D), BF),
            jax.ShapeDtypeStruct((128, 256), F32),
            jax.ShapeDtypeStruct((8, count * 3 * width), F32),
        ],
        grid_spec=pltpu.PrefetchScalarGridSpec(
            num_scalar_prefetch=1,
            grid=(count, per),
            in_specs=[
                qkv_spec,
                pl.BlockSpec((2 * pairs, SLOT, KEYS), lambda c, w, s: (c + base, w, 0)),
                pl.BlockSpec((SLOT, width), lambda c, w, s: (w, c + base)),
                row_spec,
                row_spec,
                pl.BlockSpec((128, 256), lambda c, w, s: (0, 0)),
                pl.BlockSpec((SLOT, 128), lambda c, w, s: (0, 0)),
                pl.BlockSpec((2, KEYS, 128), lambda c, w, s: (0, 0, 0)),
            ]
            + [pl.BlockSpec(memory_space=pl.ANY)] * len(held),
            out_specs=[
                qkv_spec,
                pl.BlockSpec((128, 256), lambda c, w, s: (0, 0)),
                pl.BlockSpec((8, 3 * width), lambda c, w, s: (0, c)),
            ],
            scratch_shapes=[
                pltpu.VMEM((2 * pairs, KEYS, 256), BF),
                pltpu.VMEM((2 * pairs, KEYS, 128), BF),
                pltpu.VMEM((SLOT, 3 * width), BF),
                pltpu.VMEM((SLOT, width), F32),
                pltpu.VMEM((SLOT, width), F32),
                pltpu.VMEM((SLOT, 3 * width), BF),
                pltpu.VMEM((rows, 3 * width), F32),
            ],
        ),
        input_output_aliases={9 + i: i for i in range(len(held))},
        compiler_params=params(2),
        cost_estimate=cost(54 * count // cols),
        name="attend_back",
    )(info, qkv, exps, inv, att, att_grad, tables2, shifts, onehot, *held)


def split_table(total):
    total = (total[:, :128] + total[:, 128:]).reshape(2, HD, 2, 2, 32)
    both = total[0, :, 0] + total[1, :, 1]
    both = jnp.transpose(both, (1, 2, 0))[:, :27][:, ::-1]
    return both[0], both[1]


def col_exchange(values):
    return lax.all_to_all(values, "col", 0, 0, tiled=True)


def row_swap(values, bit, nr):
    return lax.ppermute(values, "row", [(i, i ^ bit) for i in range(nr)])


def after(values, *others):
    return lax.optimization_barrier((values, *others))[0]


def gather_cols(shard, cols):
    return col_exchange(jnp.broadcast_to(shard[None], (cols,) + shard.shape))


def gather_rows(stack, nr, flip):
    order = outer_bits(nr)
    order = order[::-1] if flip else order
    held = stack[None]
    for bit in order[:-1]:
        fresh = row_swap(held, bit, nr)
        gate = yield [fresh]
        held = jnp.concatenate([held, after(fresh, *(gate or ()))], axis=0)
    fresh = row_swap(held, order[-1], nr)
    gate = yield [held, fresh]
    bufs = [held, after(fresh, *(gate or ()))]
    bufs = bufs + [row_swap(buf, 1, nr) for buf in bufs]
    yield bufs


class Hops(list):
    def __init__(self, arrived, sent):
        super().__init__(arrived)
        self.sent = sent


def last_terms(stages):
    found = stages.send(None)
    while isinstance(found, Hops):
        found = stages.send(None)
    return found


def place_of(step, free, fixed, weights):
    total = sum(weights[b] for b in fixed)
    for i, bit in enumerate(free):
        total = total + ((step >> i) & 1) * weights[bit]
    return total


def add_kernel(counts, *refs):
    at = 0
    outs = refs[sum(counts) :]
    for count, out in zip(counts, outs):
        total = refs[at][...].astype(F32)
        for ref in refs[at + 1 : at + count]:
            total = total + ref[...].astype(F32)
        out[...] = total.astype(BF)
        at += count


def split_kernel(counts, axis, lane, *refs):
    out = refs[sum(counts)]
    for k in range(out.shape[0]):
        at = 0
        for h, count in enumerate(counts):
            total = refs[at][0, k].astype(F32)
            for ref in refs[at + 1 : at + count]:
                total = total + ref[0, k].astype(F32)
            at += count
            high, wide = total.shape
            row = h * high if axis == -2 else 0
            col = lane + (h * wide if axis == -1 else 0)
            out[k, row : row + high, col : col + wide] = total.astype(out.dtype)


def reduce_weight(keep, send, axis, cols, nr):
    arrived = row_swap(send, 1, nr)
    gate = yield [arrived]
    bits = outer_bits(nr)
    _, _, bw, n = keep.shape
    shape = [bw, n]
    halves = 1
    if axis is not None:
        halves = 2
        shape[axis] //= 2
    block = (1, cols, shape[0], shape[1])
    terms = [[(keep, bits, True), (arrived, bits, True)] for _ in range(halves)]
    left = [list(bits) for _ in range(halves)]

    def spec(term, h, free, fixed):
        _, own, whole = term
        weights = {b: 1 << i for i, b in enumerate(own)}

        def place(step):
            spot = [place_of(step, free, fixed, weights), 0, 0, 0]
            if whole and axis is not None:
                spot[axis] = h
            return tuple(spot)

        return pl.BlockSpec(block, place)

    for step in range(len(bits)):
        sizes, specs, arrays, taken = [], [], [], []
        for h in range(halves):
            bit = bits[step] if h else bits[-1 - step]
            left[h].remove(bit)
            taken.append(bit)
            sizes.append(len(terms[h]))
            for term in terms[h]:
                specs.append(spec(term, h, left[h], [bit]))
                arrays.append(term[0])
        count = 1 << len(left[0])
        arrays[0] = after(arrays[0], *(gate or ()))
        out_spec = pl.BlockSpec(block, lambda i: (i, 0, 0, 0))
        outs = pl.pallas_call(
            partial(add_kernel, sizes),
            out_shape=[jax.ShapeDtypeStruct((count,) + block[1:], BF)] * halves,
            grid=(count,),
            in_specs=specs,
            out_specs=[out_spec] * halves,
            compiler_params=params(),
            cost_estimate=cost(3),
            name="add_rows",
        )(*arrays)
        fresh = [row_swap(out, bit, nr) for out, bit in zip(outs, taken)]
        for h in range(halves):
            terms[h].append((fresh[h], list(left[h]), False))
        gate = yield Hops(fresh, outs)

    sizes = [len(t) for t in terms]
    specs = [spec(term, h, [], []) for h in range(halves) for term in terms[h]]
    arrays = [term[0] for h in range(halves) for term in terms[h]]
    yield sizes, axis, specs, arrays, (cols, bw, n)


def add_cols_kernel(groups, *refs):
    outs = refs[-1]
    at, lane = 0, 0
    for sizes, axis, n in groups:
        count = sum(sizes)
        split_kernel(sizes, axis, lane, *refs[at : at + count], outs)
        at += count
        lane += n


def finish_weights(parts, *gate):
    cols, bw, _ = parts[0][4]
    groups = [(sizes, axis, shape[2]) for sizes, axis, _, _, shape in parts]
    wide = sum(n for _, _, n in groups)
    arrays = [array for part in parts for array in part[3]]
    arrays[0] = after(arrays[0], *gate)
    outs = pl.pallas_call(
        partial(add_cols_kernel, groups),
        out_shape=jax.ShapeDtypeStruct((cols, bw, wide), BF),
        grid=(1,),
        in_specs=[sp for part in parts for sp in part[2]],
        out_specs=pl.BlockSpec((cols, bw, wide), lambda i: (0, 0, 0)),
        compiler_params=params(),
        cost_estimate=cost(3),
        name="add_cols",
    )(*arrays)
    return outs, col_exchange(outs)


def last_sum(arrived, sizes, *gate):
    total = jnp.sum(after(arrived, *gate).astype(F32), axis=0)
    found, lane = [], 0
    for n in sizes:
        found.append(total[:, lane : lane + n])
        lane += n
    return found


def sum_cols(by_place, whole, me, cols):
    size = by_place.shape[1]
    if whole is not None:
        whole = jnp.broadcast_to(whole, (cols,) + whole.shape)
        by_place = jnp.concatenate([by_place, whole], axis=1)
    arrived = [lax.dynamic_index_in_dim(by_place, me, 0, keepdims=False)]
    for k in range(1, cols):
        sent = lax.dynamic_index_in_dim(by_place, me ^ k, 0, keepdims=False)
        arrived.append(lax.ppermute(sent, "col", [(i, i ^ k) for i in range(cols)]))
    gate = yield arrived[1:]
    arrived = list(lax.optimization_barrier((*arrived, *(gate or ())))[:cols])
    if whole is None:
        yield sum(arrived[1:], arrived[0])
    order = me ^ jnp.arange(cols, dtype=jnp.int32)
    total = jnp.sum(pick_rows(jnp.stack(arrived), order), axis=0)
    yield total[:size], total[size:]


def sum_rows(total, nr):
    bit = 1
    while bit < nr:
        total = total + row_swap(total, bit, nr)
        bit *= 2
    return total


def pick_rows(values, order):
    rows = jnp.arange(values.shape[0], dtype=jnp.int32)
    chosen = (order[:, None] == rows[None, :]).reshape(order.shape + rows.shape + (1,) * (values.ndim - 1))
    return jnp.sum(jnp.where(chosen, values[None], 0.0), axis=1)


def body(
    cols,
    nr,
    tokens_in,
    pad_offsets,
    norm1_gain,
    norm1_bias,
    qkv_weight,
    qv_bias,
    table_height,
    table_width,
    proj_weight,
    proj_bias,
    norm2_gain,
    norm2_bias,
    fc1_weight,
    fc1_bias,
    fc2_weight,
    fc2_bias,
    out_grad,
):
    width = D // cols
    bw = D // nr
    per = -(-WINDOWS // cols)
    me = lax.axis_index("col").astype(jnp.int32)
    my_row = lax.axis_index("row").astype(jnp.int32)
    sets, rows = window_sets(cols, per)
    info = plan(sets, pad_offsets)
    row_order = my_row ^ jnp.arange(nr, dtype=jnp.int32)

    vectors = [
        norm1_gain,
        norm1_bias,
        norm2_gain,
        norm2_bias,
        proj_bias,
        fc2_bias,
        qv_bias[0],
        qv_bias[1],
        fc1_bias,
    ]
    hidden = fc1_weight.shape[1]
    half = hidden // 2
    fc2_t = fc2_weight.T
    size = 8 * width + hidden
    qkv_stack = col_exchange(pack_first(qkv_weight.reshape(bw, 3 * width), vectors, cols))
    x_sent = spread(tokens_in, info, cols, per, rows)
    x_pieces = col_exchange(x_sent)
    lines = 3 * size // (3 * width)
    vecs = qkv_stack[:, bw : bw + lines].astype(F32)
    vecs = jnp.sum(vecs.reshape(cols, 3, size), axis=1)
    qkv_a = list(gather_rows(qkv_stack[:, : bw // 2], nr, False))[-1]
    qkv_b = list(gather_rows(qkv_stack[:, bw // 2 : bw], nr, True))[-1]
    wide0 = jnp.concatenate([fc1_weight[:, :half], proj_weight.T, fc2_t[:, :half]], axis=1)
    wide1 = jnp.concatenate([fc1_weight[:, half:], fc2_t[:, half:]], axis=1)
    stack0 = gather_cols(after(wide0, x_pieces, *qkv_a, *qkv_b), cols)
    first = half + width
    g_sent = spread(after(out_grad, x_sent), info, cols, per, rows)

    features = vecs[:, : 6 * width].reshape(cols, 6, width // bw, bw)
    features = features.transpose(0, 2, 1, 3).reshape(nr, 6, bw)
    features = pick_rows(features, row_order).transpose(1, 0, 2).reshape(6, 1, D)
    gain1, bias1, gain2, bias2, bias_p, bias_2 = [features[i] for i in range(6)]
    q_bias = vecs[:, 6 * width : 7 * width]
    v_bias = vecs[:, 7 * width : 8 * width]
    bias_qkv = jnp.stack([q_bias, jnp.zeros_like(q_bias), v_bias], axis=1).reshape(1, 3 * D)
    bias_h = vecs[:, 8 * width :]

    x_full, n1, qkv = norm_qkv(
        after(x_pieces, g_sent), qkv_a, qkv_b, info, gain1, bias1, bias_qkv, cols, rows, nr
    )
    shifts_np, onehot_np = rel_constants()
    shifts = jnp.asarray(shifts_np)
    onehot = jnp.asarray(onehot_np, BF)
    tables = table_matrix(table_height, table_width)
    stack0 = after(stack0, n1)
    hops0 = [gather_rows(stack0[:, :, :first], nr, False), gather_rows(stack0[:, :, first:], nr, True)]
    stack1 = gather_cols(after(wide1, stack0), cols)
    bufs0 = [next(hop) for hop in hops0]
    held = ()
    arrived = [stack0]
    bits = outer_bits(nr)
    for part, base in enumerate(range(0, cols, cols // SPLITS)):
        held = attend(
            after(qkv, *arrived),
            info,
            tables,
            shifts,
            onehot,
            base,
            cols // SPLITS,
            held,
            cols,
            per,
        )
        att = held[0]
        arrived = []
        if part == 0:
            stack1 = after(stack1, att)
            g_pieces = col_exchange(after(g_sent, stack1))
            bufs0 = [hop.send((att, *bufs0[0], *bufs0[1])) for hop in hops0]
            arrived = [stack1]
        if part == 2:
            for _ in range(len(bits) - 2):
                bufs0 = [hop.send(None) for hop in hops0]
            bufs0 = [hop.send((att, *bufs0[0], *bufs0[1])) for hop in hops0]
            stack1 = after(stack1, att)
            hops1 = [
                gather_rows(stack1[:, :, :half], nr, False),
                gather_rows(stack1[:, :, half:], nr, True),
            ]
            bufs1 = [next(hop) for hop in hops1]
        if part == 3:
            bufs1 = [hop.send((att, *bufs1[0], *bufs1[1])) for hop in hops1]
    att, exps, inv = held
    resid, n2 = proj_norm(bufs0[0], att, x_full, bias_p, gain2, bias2, cols, rows, nr)
    g_full = join(g_pieces, info, cols, rows, nr)
    fc1_bufs, fc2_bufs = [bufs0[0]], [bufs0[1]]

    acts, grads, sends, hidden_sums = [], [], [], []
    for c in range(2):
        if c == 1:
            for _ in range(len(bits) - 2):
                bufs1 = [hop.send(None) for hop in hops1]
            bufs1 = [hop.send((acts[0], *bufs1[0], *bufs1[1])) for hop in hops1]
            fc1_bufs.append(bufs1[0])
            fc2_bufs.append(bufs1[1])
        act, grad, keep, send, bias_sum = mlp_grads(
            fc1_bufs[c],
            fc2_bufs[c],
            n2,
            g_full,
            bias_h[:, None, c * half : (c + 1) * half],
            cols,
            rows,
            nr,
        )
        acts.append(act)
        grads.append(grad)
        hidden_sums.append(jnp.sum(bias_sum, axis=1))
        sends.append(reduce_weight(keep, send, -1, cols, nr))
    core0, core1 = [next(send) for send in sends]
    rows0 = sends[0].send((*core0, acts[1]))
    block_sent = block_rows(
        fc2_bufs, acts, after(resid, *core1), bias_2, info, cols, rows, nr
    )
    block_pieces = col_exchange(block_sent)
    rows0 = sends[0].send((*rows0, block_sent))
    rows1 = sends[1].send((block_sent,))
    resid_grad, proj_grad, sums2 = mlp_back(
        fc1_bufs,
        grads,
        after(resid, block_sent),
        g_full,
        gain2,
        cols,
        rows,
        nr,
    )
    rows1 = sends[1].send((*rows1, proj_grad))
    att_grad, keep, send = proj_back(
        fc1_bufs[0], after(proj_grad, *rows0), att, cols, rows, nr
    )
    sends.append(reduce_weight(keep, send, None, cols, nr))
    core2 = next(sends[2])
    ratio = width // bw
    places = jnp.arange(cols * ratio, dtype=jnp.int32) ^ my_row

    def by_col(sums):
        count = sums.shape[0]
        blocks = jnp.sum(sums, axis=1).reshape(count, nr, bw).transpose(1, 0, 2)
        picked = pick_rows(blocks, places).reshape(cols, ratio, count, bw)
        return picked.transpose(0, 2, 1, 3).reshape(cols, count * width)

    held, table_sums, bias_sums = (), [], []
    for part, base in enumerate(range(0, cols, cols // SPLITS)):
        arrived = []
        if part == 1:
            done0, arrived0 = finish_weights([last_terms(sends[0])], dqkv, block_pieces)
            rows2 = sends[2].send((*core2, dqkv))
            arrived = [block_pieces, *rows1, done0]
        if part == 2:
            rows2 = sends[2].send((*rows2, dqkv))
        if part == 3:
            arrived = [arrived0]
            done1, arrived1 = finish_weights(
                [last_terms(sends[1]), last_terms(sends[2])], dqkv, arrived0, *rows2
            )
            arrived = [arrived0, done1]
        dqkv, table_sum, bias_sum = attend_back(
            after(qkv, *arrived),
            info,
            exps,
            inv,
            att,
            att_grad,
            tables,
            shifts,
            onehot,
            base,
            cols // SPLITS,
            held,
            cols,
            per,
        )
        held = (dqkv,)
        table_sums.append(table_sum)
        bias_sums.append(bias_sum)
    table_sum = sum(table_sums[1:], table_sums[0])
    bias_sum = jnp.concatenate(bias_sums, axis=1)
    bias_cols = jnp.sum(bias_sum, axis=0).reshape(cols, 3, width)
    table_h_grad, table_w_grad = split_table(table_sum)
    table_flat = jnp.concatenate([table_h_grad.reshape(-1), table_w_grad.reshape(-1)])
    small = jnp.concatenate(
        [by_col(sums2), bias_cols[:, 0], bias_cols[:, 2]] + hidden_sums, axis=1
    )
    early = sum_cols(small, table_flat, me, cols)
    next(early)
    keep, send = qkv_grad(after(n1, dqkv), dqkv, cols, rows, nr)
    sends.append(reduce_weight(keep, send, -2, cols, nr))
    core3 = next(sends[3])
    block_out = collect(after(block_pieces, keep), sets, info, BF)
    rows3 = sends[3].send((*core3, block_out))
    small, table_flat = early.send((block_out,))
    in_sent, in_sums = input_back(
        qkv_a,
        qkv_b,
        after(dqkv, block_out, arrived1, small, *rows3.sent),
        x_full,
        resid_grad,
        gain1,
        info,
        cols,
        rows,
        nr,
    )
    late = sum_cols(by_col(in_sums), None, me, cols)
    late_arrived = next(late)
    in_pieces = col_exchange(after(in_sent, *late_arrived))
    rows3 = sends[3].send((in_sent,))
    for _ in range(len(outer_bits(nr)) - 2):
        rows3 = sends[3].send(None)
    sizes = [2 * width, small.shape[0], table_flat.shape[0]]
    total = sum_rows(
        jnp.concatenate([late.send(None), small, after(table_flat, *rows3.sent)]), nr
    )
    done3, arrived3 = finish_weights([sends[3].send(None)], in_pieces, total)
    late, small = total[: sizes[0]], total[sizes[0] : sizes[0] + sizes[1]]
    table_flat = total[sizes[0] + sizes[1] :].reshape(2, 27, HD)
    input_grad = collect(after(in_pieces, done3), sets, info, F32)
    (qkv_w_grad,) = last_sum(arrived3, [3 * width])
    fc_grads = last_sum(arrived0, [2 * half], done3)
    fc_grad, proj_w_grad = last_sum(arrived1, [2 * half, width], done3)
    fc_grads.append(fc_grad)

    def part(i):
        return small[i * width : (i + 1) * width]

    return (
        block_out,
        input_grad,
        late[:width],
        late[width:],
        qkv_w_grad.reshape(bw, 3, width),
        jnp.stack([part(4), part(5)]),
        table_flat[0],
        table_flat[1],
        proj_w_grad.T,
        part(0),
        part(1),
        part(2),
        jnp.concatenate([grad[:, :half] for grad in fc_grads], axis=1),
        small[6 * width :],
        jnp.concatenate([grad[:, half:] for grad in fc_grads], axis=1).T,
        part(3),
    )


def solution(mesh):
    placed = (
        P("row", "col"),
        P("row", None),
        P("col"),
        P("col"),
        P("row", None, "col"),
        P(None, "col"),
        P(),
        P(),
        P("col", "row"),
        P("col"),
        P("col"),
        P("col"),
        P("row", "col"),
        P("col"),
        P("col", "row"),
        P("col"),
        P("row", "col"),
    )
    return jax.shard_map(
        partial(body, mesh.shape["col"], mesh.shape["row"]),
        mesh=mesh,
        in_specs=placed,
        out_specs=(
            P("row", "col"),
            P("row", "col"),
            P("col"),
            P("col"),
            P("row", None, "col"),
            P(None, "col"),
            P(),
            P(),
            P("col", "row"),
            P("col"),
            P("col"),
            P("col"),
            P("row", "col"),
            P("col"),
            P("col", "row"),
            P("col"),
        ),
        check_vma=False,
    )
```

```python
from functools import partial

import jax
import jax.numpy as jnp
import numpy as np
from jax import lax
from jax.experimental import pallas as pl
from jax.experimental.pallas import tpu as pltpu
from jax.sharding import PartitionSpec as P

D = 1024
HD = 64
WIN = 14
SIDE = 64
GRID = 5
WINDOWS = 25
REAL = 196
SLOT = 200
KEYS = 256
PIX = 4096
EPSILON = 1e-06
MARGIN = 6
PADROWS = 84
BF = jnp.bfloat16
F32 = jnp.float32
SPLITS = 4
BLOCKS = 4
SLAB = 224
FIELDS = 7
HEAD = 5
TAIL = 16


def iota(shape, dim):
    return lax.broadcasted_iota(jnp.int32, shape, dim)


def params(n=1, mib=60):
    return pltpu.CompilerParams(
        dimension_semantics=("arbitrary",) * n, vmem_limit_bytes=mib * 1024 * 1024
    )


def cost(micros):
    return pl.CostEstimate(
        flops=int(micros * 1.1e9), bytes_accessed=int(micros * 1e6), transcendentals=0
    )


def nt_dot(a, b):
    return lax.dot_general(a, b, (((1,), (1,)), ((), ())), preferred_element_type=F32)


def tn_dot(a, b):
    return lax.dot_general(a, b, (((0,), (0,)), ((), ())), preferred_element_type=F32)


def nn_dot(a, b):
    return lax.dot_general(a, b, (((1,), (0,)), ((), ())), preferred_element_type=F32)


def window_sets(cols, per):
    units = [[0, 4, 20, 24]]
    units += [[j, 20 + j] for j in (1, 2, 3)] + [[5 * i, 5 * i + 4] for i in (1, 2, 3)]
    units += [[5 * i + j] for i in (1, 2, 3) for j in (1, 2, 3)]
    sizes = [484] + [308] * 6 + [196] * 9
    sets = [[] for _ in range(cols)]
    loads = [0] * cols
    for unit, size in zip(units, sizes):
        open_sets = [d for d in range(cols) if len(sets[d]) + len(unit) <= per]
        best = min(open_sets, key=lambda d: loads[d])
        sets[best] += unit
        loads[best] += size
    capacity = -(-(max(loads) + TAIL) // 64) * 64
    return [own + [WINDOWS] * (per - len(own)) for own in sets], capacity


def plan_kernel(cols, per, ids, offsets, info):
    top, left = offsets[0, 0], offsets[0, 1]
    me = lax.axis_index("col").astype(jnp.int32)
    info[0] = me
    info[1] = top
    info[2] = left
    info[3] = lax.axis_index("row").astype(jnp.int32)

    def each_set(d, carry):
        def each_window(i, base):
            at = d * per + i
            win_row, win_col = ids[at] // GRID, ids[at] % GRID
            row_low = jnp.maximum(0, top - WIN * win_row)
            height = jnp.maximum(jnp.minimum(WIN, SIDE + top - WIN * win_row) - row_low, 0)
            col_low = jnp.maximum(0, left - WIN * win_col)
            width = jnp.maximum(jnp.minimum(WIN, SIDE + left - WIN * win_col) - col_low, 0)
            first = HEAD + at * FIELDS
            info[first] = base
            info[first + 1] = row_low
            info[first + 2] = height
            info[first + 3] = col_low
            info[first + 4] = width
            info[first + 5] = jnp.minimum(win_row, GRID - 1)
            info[first + 6] = win_col
            return base + height * width

        count = lax.fori_loop(0, per, each_window, jnp.int32(0))

        @pl.when(d == me)
        def _():
            info[4] = count

        return carry

    lax.fori_loop(0, cols, each_set, jnp.int32(0))


def plan(sets, offsets):
    cols, per = len(sets), len(sets[0])
    smem = pl.BlockSpec(memory_space=pltpu.SMEM)
    return pl.pallas_call(
        partial(plan_kernel, cols, per),
        out_shape=jax.ShapeDtypeStruct((HEAD + cols * per * FIELDS,), jnp.int32),
        in_specs=[smem, smem],
        out_specs=smem,
        cost_estimate=cost(2),
        name="plan",
    )(jnp.asarray(np.array(sets, np.int32).reshape(-1)), offsets)


def window_at(info, index):
    at = HEAD + index * FIELDS
    return [info[at + f] for f in range(FIELDS)]


def target_of(field, left, row, token_col):
    base, row_low, height, col_low, width, _, win_col = field
    col = token_col + (left - WIN * win_col)
    inside = (row >= row_low) & (row < row_low + height) & (col >= col_low) & (col < col_low + width)
    return jnp.where(inside, base + (row - row_low) * width + (col - col_low), -(1 << 20))


def as_pick(mask):
    return mask.astype(F32).astype(BF)


def spread_kernel(per, info, x_ref, out, padded, total):
    top, left = info[1], info[2]
    cols, rows, width = out.shape
    padded[: MARGIN * SIDE, :] = jnp.zeros((MARGIN * SIDE, width), BF)
    padded[(MARGIN + SIDE) * SIDE :, :] = jnp.zeros(((PADROWS - MARGIN - SIDE) * SIDE, width), BF)
    padded[MARGIN * SIDE : (MARGIN + SIDE) * SIDE, :] = x_ref[...]
    token = iota((1, 256), 1)
    row, col = token // SIDE, token % SIDE
    line = iota((64, 256), 0)
    for d in range(cols):
        total[...] = jnp.zeros_like(total)

        def step(i, carry):
            field = window_at(info, d * per + i)
            base, row_low, height, _, across, win_row, _ = field
            for g in range(4):
                start = base + jnp.clip(4 * g - row_low, 0, height) * across
                start = pl.multiple_of(start // 8 * 8, 8)
                pick = as_pick(line == target_of(field, left, row + 4 * g, col) - start)
                first = pl.multiple_of((WIN * win_row + 4 * g - top + MARGIN) * SIDE, SIDE)
                found = nn_dot(pick, padded[pl.ds(first, 256), :])
                total[pl.ds(start, 8), :] += found[:8]
                total[pl.ds(pl.multiple_of(start + 8, 8), 56), :] = found[8:]
            return carry

        lax.fori_loop(0, per, step, 0)
        out[d] = total[:rows].astype(BF)


def spread(x, info, cols, per, rows):
    width = x.shape[1]
    return pl.pallas_call(
        partial(spread_kernel, per),
        out_shape=jax.ShapeDtypeStruct((cols, rows, width), BF),
        grid_spec=pltpu.PrefetchScalarGridSpec(
            num_scalar_prefetch=1,
            grid=(1,),
            in_specs=[pl.BlockSpec((PIX, width), lambda i, s: (0, 0))],
            out_specs=pl.BlockSpec((cols, rows, width), lambda i, s: (0, 0, 0)),
            scratch_shapes=[
                pltpu.VMEM((PADROWS * SIDE, width), BF),
                pltpu.VMEM((rows + 64, width), F32),
            ],
        ),
        compiler_params=params(),
        cost_estimate=cost(7),
        name="spread",
    )(info, x)


def collect_kernel(places, per, info, pieces, out, padded):
    top, left = info[1], info[2]
    _, rows, _ = pieces.shape
    token = iota((1, 256), 1)
    row, col = token // SIDE, token % SIDE
    line = iota((80, 256), 0)
    for win_row in range(GRID):

        def step(g, carry):
            picks, slabs = [], []
            for win_col in range(GRID):
                d, i = places[win_row * GRID + win_col]
                field = window_at(info, d * per + i)
                base, row_low, height, _, across, _, _ = field
                start = base + jnp.clip(4 * g - row_low, 0, height) * across
                start = pl.multiple_of(jnp.minimum(start // 16 * 16, rows - 80), 16)
                picks.append(as_pick(line == target_of(field, left, row + 4 * g, col) - start))
                slabs.append(pieces[d, pl.ds(start, 80), :])
            found = tn_dot(jnp.concatenate(picks, axis=0), jnp.concatenate(slabs, axis=0))
            first = pl.multiple_of((WIN * win_row + 4 * g - top + MARGIN) * SIDE, SIDE)
            padded[pl.ds(first, 256), :] = found.astype(BF)
            return carry

        lax.fori_loop(0, 4, step, 0)
    out[...] = padded[MARGIN * SIDE : (MARGIN + SIDE) * SIDE, :].astype(out.dtype)


def collect(pieces, sets, info, dtype):
    cols, rows, width = pieces.shape
    per = len(sets[0])
    places = {w: (d, i) for d, own in enumerate(sets) for i, w in enumerate(own)}
    return pl.pallas_call(
        partial(collect_kernel, places, per),
        out_shape=jax.ShapeDtypeStruct((PIX, width), dtype),
        grid_spec=pltpu.PrefetchScalarGridSpec(
            num_scalar_prefetch=1,
            grid=(1,),
            in_specs=[pl.BlockSpec((cols, rows, width), lambda i, s: (0, 0, 0))],
            out_specs=pl.BlockSpec((PIX, width), lambda i, s: (0, 0)),
            scratch_shapes=[pltpu.VMEM((PADROWS * SIDE, width), BF)],
        ),
        compiler_params=params(),
        cost_estimate=cost(8),
        name="collect",
    )(info, pieces)


def chunk_place(col, part, width, info, parts):
    return (col * (width // 128) + part) ^ (info[3] // parts)


def swap_halves(values, info, parts):
    if parts == 1:
        return values
    return jnp.where(info[3] % 2 == 1, pltpu.roll(values.astype(F32), 64, 1), values.astype(F32))


def place_features(pieces, info, parts, whole):
    cols, _, width = pieces.shape
    for d in range(cols):
        for c in range(width // 128):
            at = pl.multiple_of(chunk_place(d, c, width, info, parts) * 128, 128)
            values = swap_halves(pieces[d, :, c * 128 : (c + 1) * 128], info, parts)
            whole[:, pl.ds(at, 128)] = values.astype(whole.dtype)


def take_features(whole, pieces, info, parts):
    cols, _, width = pieces.shape
    for d in range(cols):
        for c in range(width // 128):
            at = pl.multiple_of(chunk_place(d, c, width, info, parts) * 128, 128)
            values = swap_halves(whole[:, pl.ds(at, 128)], info, parts)
            pieces[d, :, c * 128 : (c + 1) * 128] = values.astype(BF)


def eight(values):
    total = values[:8]
    for r in range(8, values.shape[0], 8):
        total = total + values[r : r + 8]
    return total


def row_places(nr, flip):
    order = outer_bits(nr)
    order = order[::-1] if flip else order
    held = [0]
    for bit in order[:-1]:
        held = held + [place | bit for place in held]
    groups = [held, [place | order[-1] for place in held]]
    groups = groups + [[place | 1 for place in group] for group in groups]
    where = {place: (g, i) for g, group in enumerate(groups) for i, place in enumerate(group)}
    return [where[place] for place in range(nr)]


def outer_bits(nr):
    return [1 << b for b in range(1, nr.bit_length() - 1)]


def load_rows(bufs, flip, scratch, nr, first=0):
    stride = D // nr
    for p, (g, i) in enumerate(row_places(nr, flip)):
        cols, size, n = bufs[g].shape[1], bufs[g].shape[-2], bufs[g].shape[-1]
        at = p * stride + first
        for k in range(cols):
            if len(bufs[g].shape) == 4:
                scratch[at : at + size, k * n : (k + 1) * n] = bufs[g][i, k]
                continue
            for part in range(3):
                lane = (3 * k + part) * n
                scratch[at : at + size, lane : lane + n] = bufs[g][i, k, part]


def const_spec(shape):
    zeros = (0,) * len(shape)
    return pl.BlockSpec(shape, lambda *a: zeros, pipeline_mode=pl.Buffered(1))


def norm_qkv_kernel(cols, nr, info, *refs):
    pieces = refs[0]
    bufs_a, bufs_b = refs[1:5], refs[5:9]
    gain, bias, bias_qkv, x_out, n_out, qkv_out, whole, weight = refs[9:]
    parts = max(1, 128 * nr // D)
    bw = D // nr

    @pl.when(pl.program_id(0) == 0)
    def _():
        load_rows(bufs_a, False, weight, nr)
        load_rows(bufs_b, True, weight, nr, bw // 2)

    place_features(pieces, info, parts, whole)
    values = whole[...]
    x_out[...] = values.astype(BF)
    mean = jnp.mean(values, axis=1, keepdims=True)
    centred = values - mean
    spread_sq = jnp.mean(centred * centred, axis=1, keepdims=True)
    normed = centred * lax.rsqrt(spread_sq + EPSILON) * gain[...] + bias[...]
    size = values.shape[0]
    real = iota((size, 1), 0) < info[4] - pl.program_id(0) * size
    normed = jnp.where(real, normed, 0.0).astype(BF)
    n_out[...] = normed
    qkv_out[...] = (nn_dot(normed, weight[...]) + bias_qkv[...]).astype(BF)


def norm_qkv(pieces, bufs_a, bufs_b, info, gain, bias, bias_qkv, cols, rows, nr):
    width = D // cols
    return pl.pallas_call(
        partial(norm_qkv_kernel, cols, nr),
        out_shape=[
            jax.ShapeDtypeStruct((rows, D), BF),
            jax.ShapeDtypeStruct((rows, D), BF),
            jax.ShapeDtypeStruct((rows, 3 * D), BF),
        ],
        grid_spec=pltpu.PrefetchScalarGridSpec(
            num_scalar_prefetch=1,
            grid=(BLOCKS,),
            in_specs=[pl.BlockSpec((cols, rows // BLOCKS, width), lambda i, s: (0, i, 0))]
            + [const_spec(bufs_a[0].shape)] * 8
            + [const_spec((1, D)), const_spec((1, D)), const_spec((1, 3 * D))],
            out_specs=[
                pl.BlockSpec((rows // BLOCKS, D), lambda i, s: (i, 0)),
                pl.BlockSpec((rows // BLOCKS, D), lambda i, s: (i, 0)),
                pl.BlockSpec((rows // BLOCKS, 3 * D), lambda i, s: (i, 0)),
            ],
            scratch_shapes=[pltpu.VMEM((rows // BLOCKS, D), F32), pltpu.VMEM((D, 3 * D), BF)],
        ),
        compiler_params=params(),
        cost_estimate=cost(19),
        name="norm_qkv",
    )(info, pieces, *bufs_a, *bufs_b, gain, bias, bias_qkv)


def join_kernel(cols, nr, info, *refs):
    place_features(refs[0], info, max(1, 128 * nr // D), refs[1])


def join(pieces, info, cols, rows, nr):
    width = pieces.shape[-1]
    return pl.pallas_call(
        partial(join_kernel, cols, nr),
        out_shape=jax.ShapeDtypeStruct((rows, D), BF),
        grid_spec=pltpu.PrefetchScalarGridSpec(
            num_scalar_prefetch=1,
            grid=(BLOCKS,),
            in_specs=[pl.BlockSpec((cols, rows // BLOCKS, width), lambda i, s: (0, i, 0))],
            out_specs=pl.BlockSpec((rows // BLOCKS, D), lambda i, s: (i, 0)),
        ),
        compiler_params=params(),
        cost_estimate=cost(7),
        name="join",
    )(info, pieces)


def proj_norm_kernel(nr, *refs):
    att, x, bias_p, gain, bias, resid_out, n_out, weight = refs[4:]

    @pl.when(pl.program_id(0) == 0)
    def _():
        load_rows(refs[:4], False, weight, nr)

    values = x[...].astype(F32) + nt_dot(att[...], weight[...]) + bias_p[...]
    resid_out[...] = values
    mean = jnp.mean(values, axis=1, keepdims=True)
    centred = values - mean
    spread_sq = jnp.mean(centred * centred, axis=1, keepdims=True)
    n_out[...] = (centred * lax.rsqrt(spread_sq + EPSILON) * gain[...] + bias[...]).astype(BF)


def proj_spec(buf, cols, whole):
    n = D // cols
    shape = (buf.shape[0], cols if whole else 1, buf.shape[2], n)
    last = buf.shape[3] // n - 1
    if whole:
        return pl.BlockSpec(shape, lambda *a: (0, 0, 0, last), pipeline_mode=pl.Buffered(1))
    return pl.BlockSpec(shape, lambda k: (0, k, 0, last))


def proj_norm(bufs, att, x, bias_p, gain, bias, cols, rows, nr):
    row_spec = pl.BlockSpec((rows // BLOCKS, D), lambda i: (i, 0))
    return pl.pallas_call(
        partial(proj_norm_kernel, nr),
        out_shape=[jax.ShapeDtypeStruct((rows, D), F32), jax.ShapeDtypeStruct((rows, D), BF)],
        grid=(BLOCKS,),
        in_specs=[proj_spec(bufs[0], cols, True)] * 4
        + [row_spec, row_spec, const_spec((1, D)), const_spec((1, D)), const_spec((1, D))],
        out_specs=[row_spec, row_spec],
        scratch_shapes=[pltpu.VMEM((D, D), BF)],
        compiler_params=params(),
        cost_estimate=cost(11),
        name="proj_norm",
    )(*bufs, att, x, bias_p, gain, bias)


def gelu_and_slope(v):
    below = 0.5 + 0.5 * lax.erf(v * 0.7071067811865476)
    bell = jnp.exp(v * v * -0.5)
    return v * below, below + v * bell * 0.3989422804014327


def store_halves(grad, keep, send, nr, lanes=slice(None)):
    bw = D // nr
    for q in range(nr // 2):
        at = 2 * q * bw
        keep[q, 0, :, lanes] = grad[at : at + bw].astype(BF)
        send[q, 0, :, lanes] = grad[at + bw : at + 2 * bw].astype(BF)


def mlp_grads_kernel(nr, *refs):
    n2, g, bias, act, pre_grad, keep, send, bias_sum, w1, w2 = refs[8:]
    n = w1.shape[1]
    load_rows(refs[:4], False, w1, nr)
    load_rows(refs[4:8], True, w2, nr)
    total = None
    size = n2.shape[0] // BLOCKS
    for r in range(0, n2.shape[0], size):
        pre = nn_dot(n2[r : r + size], w1[...]) + bias[0]
        act_grad = nn_dot(g[r : r + size], w2[...])
        value, slope = gelu_and_slope(pre)
        act[r : r + size] = value.astype(BF)
        grad = act_grad * slope
        pre_grad[r : r + size] = grad.astype(BF)
        part = eight(grad)
        total = part if total is None else total + part
    bias_sum[0] = total
    store_halves(tn_dot(n2[...], pre_grad[...]), keep, send, nr, slice(0, n))
    store_halves(tn_dot(g[...], act[...]), keep, send, nr, slice(n, 2 * n))


def mlp_grads(bufs1, bufs2, n2, g, bias, cols, rows, nr):
    bw = D // nr
    n = bufs2[0].shape[-1]
    w_spec = pl.BlockSpec((nr // 4, 1, bw, n), lambda k: (0, k, 0, 0))
    row_spec = pl.BlockSpec((rows, n), lambda k: (0, k))
    half_spec = pl.BlockSpec((nr // 2, 1, bw, 2 * n), lambda k: (0, k, 0, 0))
    half = jax.ShapeDtypeStruct((nr // 2, cols, bw, 2 * n), BF)
    act = jax.ShapeDtypeStruct((rows, cols * n), BF)
    return pl.pallas_call(
        partial(mlp_grads_kernel, nr),
        out_shape=[act, act, half, half, jax.ShapeDtypeStruct((cols, 8, n), F32)],
        grid=(cols,),
        in_specs=[w_spec] * 8
        + [const_spec((rows, D)), const_spec((rows, D)), pl.BlockSpec((1, 1, n), lambda k: (k, 0, 0))],
        out_specs=[row_spec, row_spec, half_spec, half_spec]
        + [pl.BlockSpec((1, 8, n), lambda k: (k, 0, 0))],
        scratch_shapes=[pltpu.VMEM((D, n), BF)] * 2,
        compiler_params=params(),
        cost_estimate=cost(38),
        name="mlp_grads",
    )(*bufs1, *bufs2, n2, g, bias)


def norm_back(grad, values, gain):
    mean = jnp.mean(values, axis=1, keepdims=True)
    centred = values - mean
    spread_sq = jnp.mean(centred * centred, axis=1, keepdims=True)
    inv = lax.rsqrt(spread_sq + EPSILON)
    hat = centred * inv
    scaled = grad * gain
    first = jnp.mean(scaled, axis=1, keepdims=True)
    second = jnp.mean(scaled * hat, axis=1, keepdims=True)
    return (scaled - first - hat * second) * inv, hat


def block_out_kernel(cols, nr, info, *refs):
    act0, act1, resid, bias_2 = refs[8:12]
    pieces, weight, whole = refs[12:]

    @pl.when(pl.program_id(0) == 0)
    def _():
        load_rows(refs[:4], True, weight.at[0], nr)
        load_rows(refs[4:8], True, weight.at[1], nr)

    out = nt_dot(act0[...], weight[0]) + nt_dot(act1[...], weight[1])
    whole[...] = resid[...] + out + bias_2[...]
    take_features(whole, pieces, info, max(1, 128 * nr // D))


def block_rows(groups, acts, resid, bias_2, info, cols, rows, nr):
    width = D // cols
    wide = acts[0].shape[1]
    row_spec = pl.BlockSpec((rows // BLOCKS, D), lambda i, s: (i, 0))
    wide_spec = pl.BlockSpec((rows // BLOCKS, wide), lambda i, s: (i, 0))
    flat = [b for group in groups for b in group]
    return pl.pallas_call(
        partial(block_out_kernel, cols, nr),
        out_shape=[jax.ShapeDtypeStruct((cols, rows, width), BF)],
        grid_spec=pltpu.PrefetchScalarGridSpec(
            num_scalar_prefetch=1,
            grid=(BLOCKS,),
            in_specs=[const_spec(flat[-1].shape)] * 8
            + [wide_spec] * 2
            + [row_spec, const_spec((1, D))],
            out_specs=[pl.BlockSpec((cols, rows // BLOCKS, width), lambda i, s: (0, i, 0))],
            scratch_shapes=[pltpu.VMEM((2, D, wide), BF), pltpu.VMEM((rows // BLOCKS, D), F32)],
        ),
        compiler_params=params(),
        cost_estimate=cost(26),
        name="block_rows",
    )(info, *flat, *acts, resid, bias_2)[0]


def mlp_back_kernel(nr, *refs):
    grad0, grad1, resid, g, gain, resid_grad, proj_grad, sums, weight = refs[8:]

    @pl.when(pl.program_id(0) == 0)
    def _():
        load_rows(refs[:4], False, weight.at[0], nr)
        load_rows(refs[4:8], False, weight.at[1], nr)
        sums[...] = jnp.zeros_like(sums)

    grad = nt_dot(grad0[...], weight[0]) + nt_dot(grad1[...], weight[1])
    g_f = g[...].astype(F32)
    back, hat = norm_back(grad, resid[...], gain[...])
    total = g_f + back
    resid_grad[...] = total
    low = total.astype(BF)
    proj_grad[...] = low
    sums[0] += eight(low.astype(F32))
    sums[1] += eight(grad * hat)
    sums[2] += eight(grad)
    sums[3] += eight(g_f)


def mlp_back(groups, grads, resid, g, gain, cols, rows, nr):
    wide = grads[0].shape[1]
    row_spec = pl.BlockSpec((rows // BLOCKS, D), lambda i: (i, 0))
    wide_spec = pl.BlockSpec((rows // BLOCKS, wide), lambda i: (i, 0))
    flat = [b for group in groups for b in group]
    shape = flat[-1].shape
    return pl.pallas_call(
        partial(mlp_back_kernel, nr),
        out_shape=[
            jax.ShapeDtypeStruct((rows, D), F32),
            jax.ShapeDtypeStruct((rows, D), BF),
            jax.ShapeDtypeStruct((4, 8, D), F32),
        ],
        grid=(BLOCKS,),
        in_specs=[const_spec(shape)] * 8
        + [wide_spec] * 2
        + [row_spec, row_spec, const_spec((1, D))],
        out_specs=[row_spec, row_spec, pl.BlockSpec((4, 8, D), lambda i: (0, 0, 0))],
        scratch_shapes=[pltpu.VMEM((2, D, wide), BF)],
        compiler_params=params(),
        cost_estimate=cost(28),
        name="mlp_back",
    )(*flat, *grads, resid, g, gain)


def proj_back_kernel(nr, *refs):
    proj_grad, att, att_grad, keep, send, weight = refs[4:]
    load_rows(refs[:4], False, weight, nr)
    store_halves(tn_dot(proj_grad[...], att[...]), keep, send, nr)
    att_grad[...] = nn_dot(proj_grad[...], weight[...]).astype(BF)


def proj_back(bufs, proj_grad, att, cols, rows, nr):
    bw = D // nr
    n = D // cols
    half = jax.ShapeDtypeStruct((nr // 2, cols, bw, n), BF)
    half_spec = pl.BlockSpec((nr // 2, 1, bw, n), lambda k: (0, k, 0, 0))
    col_spec = pl.BlockSpec((rows, n), lambda k: (0, k))
    return pl.pallas_call(
        partial(proj_back_kernel, nr),
        out_shape=[jax.ShapeDtypeStruct((rows, D), BF), half, half],
        grid=(cols,),
        in_specs=[proj_spec(bufs[0], cols, False)] * 4 + [const_spec((rows, D)), col_spec],
        out_specs=[col_spec, half_spec, half_spec],
        scratch_shapes=[pltpu.VMEM((D, n), BF)],
        compiler_params=params(),
        cost_estimate=cost(11),
        name="proj_back",
    )(*bufs, proj_grad, att)


def qkv_grad_kernel(nr, n1, dqkv, keep, send):
    store_halves(tn_dot(n1[...], dqkv[...]), keep, send, nr)


def qkv_grad(n1, dqkv, cols, rows, nr):
    n = 3 * D // cols
    bw = D // nr
    half = jax.ShapeDtypeStruct((nr // 2, cols, bw, n), BF)
    return pl.pallas_call(
        partial(qkv_grad_kernel, nr),
        out_shape=[half] * 2,
        grid=(cols,),
        in_specs=[const_spec((rows, D)), pl.BlockSpec((rows, n), lambda k: (0, k))],
        out_specs=[pl.BlockSpec((nr // 2, 1, bw, n), lambda k: (0, k, 0, 0))] * 2,
        compiler_params=params(),
        cost_estimate=cost(14),
        name="qkv_grad",
    )(n1, dqkv)


def input_back_kernel(cols, nr, info, *refs):
    bufs_a, bufs_b = refs[:4], refs[4:8]
    rest = refs[8:]
    dqkv, x, resid_grad, gain = rest[:4]
    pieces, sums, whole, weight = rest[4:]
    bw = D // nr

    @pl.when(pl.program_id(0) == 0)
    def _():
        load_rows(bufs_a, False, weight, nr)
        load_rows(bufs_b, True, weight, nr, bw // 2)
        sums[...] = jnp.zeros_like(sums)

    grad = nt_dot(dqkv[...], weight[...])
    back, hat = norm_back(grad, x[...].astype(F32), gain[...])
    whole[...] = resid_grad[...] + back
    take_features(whole, pieces, info, max(1, 128 * nr // D))
    sums[0] += eight(grad * hat)
    sums[1] += eight(grad)


def input_back(bufs_a, bufs_b, dqkv, x, resid_grad, gain, info, cols, rows, nr):
    width = D // cols
    row_spec = pl.BlockSpec((rows // BLOCKS, D), lambda i, s: (i, 0))
    piece = jax.ShapeDtypeStruct((cols, rows, width), BF)
    return pl.pallas_call(
        partial(input_back_kernel, cols, nr),
        out_shape=[piece, jax.ShapeDtypeStruct((2, 8, D), F32)],
        grid_spec=pltpu.PrefetchScalarGridSpec(
            num_scalar_prefetch=1,
            grid=(BLOCKS,),
            in_specs=[const_spec(bufs_a[0].shape)] * 8
            + [pl.BlockSpec((rows // BLOCKS, 3 * D), lambda i, s: (i, 0)), row_spec, row_spec]
            + [const_spec((1, D))],
            out_specs=[pl.BlockSpec((cols, rows // BLOCKS, width), lambda i, s: (0, i, 0))]
            + [pl.BlockSpec((2, 8, D), lambda i, s: (0, 0, 0))],
            scratch_shapes=[pltpu.VMEM((rows // BLOCKS, D), F32), pltpu.VMEM((D, 3 * D), BF)],
        ),
        compiler_params=params(),
        cost_estimate=cost(25),
        name="input_back",
    )(info, *bufs_a, *bufs_b, dqkv, x, resid_grad, gain)


def rel_constants():
    place = np.arange(SLOT)
    lanes = np.arange(128)
    group = lanes // 32
    row_shift = np.clip(WIN - 1 - place // WIN, 0, WIN - 1)
    col_shift = WIN - 1 - place % WIN
    shifts = np.where(group[None, :] % 2 == 0, row_shift[:, None], col_shift[:, None])
    onehot = np.zeros((2, KEYS, 128), np.float32)
    for head in range(2):
        for key in range(KEYS):
            if key >= REAL:
                onehot[head, key, 64 * head + 28] = -1e9
                continue
            for extra in (0, WIN):
                onehot[head, key, 64 * head + key // WIN + extra] = 1.0
                onehot[head, key, 64 * head + 32 + key % WIN + extra] = 1.0
    return shifts.astype(np.int32), onehot


def table_matrix(table_h, table_w):
    flipped = jnp.stack([table_h, table_w])[:, ::-1, :].astype(BF)
    block = jnp.pad(jnp.transpose(flipped, (2, 0, 1)), ((0, 0), (0, 0), (0, 5)))
    block = block.reshape(HD, HD)
    zero = jnp.zeros_like(block)
    return jnp.concatenate(
        [jnp.concatenate([block, zero], axis=1), jnp.concatenate([zero, block], axis=1)], axis=0
    )


def shift_left(values, shifts):
    for bit in (1, 2, 4, 8):
        values = jnp.where((shifts & bit) != 0, pltpu.roll(values, 128 - bit, 1), values)
    return values


def shift_right(values, shifts):
    for bit in (1, 2, 4, 8):
        values = jnp.where((shifts & bit) != 0, pltpu.roll(values, bit, 1), values)
    return values


def slot_target(field, start, rows, shape):
    base, row_low, height, col_low, width, _, _ = field
    slot = iota(shape, 0 if shape[0] > 1 else 1)
    row, col = slot // WIN, slot % WIN
    inside = (row >= row_low) & (row < row_low + height) & (col >= col_low) & (col < col_low + width)
    return jnp.where(inside, base - start + (row - row_low) * width + (col - col_low), rows)


def slots_from(field, start, source):
    rows = source.shape[0]
    line = iota((SLOT, SLAB + TAIL), 1)
    pick = as_pick(line == slot_target(field, start, SLAB + TAIL - 1, (SLOT, 1)))
    slab = jnp.concatenate([source[pl.ds(start, SLAB), :], source[rows - TAIL :, :]], axis=0)
    return pick, nn_dot(pick, slab)


def pack_of(field, start):
    line = iota((SLAB, SLOT), 0)
    return as_pick(line == slot_target(field, start, -1, (1, SLOT)))


def slab_start(field, rows):
    return pl.multiple_of(jnp.minimum(field[0] // 16 * 16, rows - SLAB), 16)


def attend_kernel(width, held, info, qkv, tables, shifts, onehot, *refs):
    att, exps, inv, keys, vals, slots, total = refs[held:]
    window = pl.program_id(1)
    first = (pl.program_id(0) == 0) & (window == 0)

    @pl.when(first)
    def _():
        for head in range(2 * (width // 128)):
            keys[head, :, :128] = jnp.zeros((KEYS, 128), BF)
            keys[head, :, 128:] = onehot[head % 2]
        for pair in range(width // 128):
            vals[pair, :, :128] = jnp.zeros((KEYS, 128), BF)
            vals[pair, :, 128:] = jnp.ones((KEYS, 128), BF)

    @pl.when(window == 0)
    def _():
        total[...] = jnp.zeros_like(total)

    field = window_at(info, info[0] * pl.num_programs(1) + window)
    start = slab_start(field, qkv.shape[0])
    slots[...] = slots_from(field, start, qkv)[1].astype(BF)

    lane = iota((SLOT, 128), 1)
    low = lane < HD
    inner = lane % 32
    pairs = width // 128
    queries = []
    for pair in range(pairs):
        at = pair * 128
        q2 = slots[:, at : at + 128]
        k2 = slots[:, width + at : width + at + 128]
        vals[pair, :SLOT, :128] = slots[:, 2 * width + at : 2 * width + at + 128]
        zero = jnp.zeros_like(k2)
        keys[2 * pair, :SLOT, :128] = jnp.where(low, k2, zero)
        keys[2 * pair + 1, :SLOT, :128] = jnp.where(low, zero, k2)
        rel = shift_left(nn_dot(q2, tables[...]), shifts[...])
        rel_hi = rel.astype(BF).astype(F32)
        rel_lo = pltpu.roll(rel - rel_hi, WIN, 1)
        rel = jnp.where(inner < WIN, rel_hi, jnp.where(inner < 2 * WIN, rel_lo, 1.0))
        queries.append(jnp.concatenate([q2 * BF(0.125), rel.astype(BF)], axis=1))
    scores = [nt_dot(queries[head // 2], keys[head]) for head in range(2 * pairs)]
    weights = []
    for head in range(2 * pairs):
        peak = jnp.max(scores[head], axis=1, keepdims=True)
        weights.append(jnp.exp(scores[head] - peak).astype(BF))
        exps[head] = weights[head]
    outs = [nn_dot(weights[head], vals[head // 2]) for head in range(2 * pairs)]
    parts = []
    for pair in range(pairs):
        at = pair * 128
        first, second = outs[2 * pair], outs[2 * pair + 1]
        scale = 1.0 / jnp.where(low, first[:, 128:], second[:, 128:])
        inv[:, at : at + 128] = scale
        parts.append((jnp.where(low, first[:, :128], second[:, :128]) * scale).astype(BF))
    pack = pack_of(field, start)
    total[pl.ds(start, SLAB), :] += nn_dot(pack, jnp.concatenate(parts, axis=1))

    @pl.when(window == pl.num_programs(1) - 1)
    def _():
        att[...] = total[...].astype(BF)


def attend(qkv, info, tables, shifts, onehot, base, count, held, cols, per):
    rows = qkv.shape[0]
    width = D // cols
    pairs = width // 128
    held = list(held)
    return pl.pallas_call(
        partial(attend_kernel, width, len(held)),
        out_shape=[
            jax.ShapeDtypeStruct((rows, D), BF),
            jax.ShapeDtypeStruct((D // HD, per * SLOT, KEYS), BF),
            jax.ShapeDtypeStruct((per * SLOT, D), F32),
        ],
        grid_spec=pltpu.PrefetchScalarGridSpec(
            num_scalar_prefetch=1,
            grid=(count, per),
            in_specs=[
                pl.BlockSpec((rows, 3 * width), lambda c, w, s: (0, c + base)),
                pl.BlockSpec((128, 128), lambda c, w, s: (0, 0)),
                pl.BlockSpec((SLOT, 128), lambda c, w, s: (0, 0)),
                pl.BlockSpec((2, KEYS, 128), lambda c, w, s: (0, 0, 0)),
            ]
            + [pl.BlockSpec(memory_space=pl.ANY)] * len(held),
            out_specs=[
                pl.BlockSpec((rows, width), lambda c, w, s: (0, c + base)),
                pl.BlockSpec((2 * pairs, SLOT, KEYS), lambda c, w, s: (c + base, w, 0)),
                pl.BlockSpec((SLOT, width), lambda c, w, s: (w, c + base)),
            ],
            scratch_shapes=[
                pltpu.VMEM((2 * pairs, KEYS, 256), BF),
                pltpu.VMEM((pairs, KEYS, 256), BF),
                pltpu.VMEM((SLOT, 3 * width), BF),
                pltpu.VMEM((rows, width), F32),
            ],
        ),
        input_output_aliases={5 + i: i for i in range(len(held))},
        compiler_params=params(2),
        cost_estimate=cost(58 * count // cols),
        name="attend",
    )(info, qkv, tables, shifts, onehot, *held)


def attend_back_kernel(
    width, held, info, qkv, exps, inv, att, att_grad, tables2, shifts, onehot, *refs
):
    out, table_sum, bias_sum, keys, vals, slots, att_slots, grad_slots, fresh, total = refs[held:]
    window = pl.program_id(1)
    first = (pl.program_id(0) == 0) & (window == 0)

    @pl.when(first)
    def _():
        for head in range(2 * (width // 128)):
            keys[head, :, :128] = jnp.zeros((KEYS, 128), BF)
            keys[head, :, 128:] = onehot[head % 2]
        vals[...] = jnp.zeros_like(vals)
        table_sum[...] = jnp.zeros_like(table_sum)

    @pl.when(window == 0)
    def _():
        bias_sum[...] = jnp.zeros_like(bias_sum)
        total[...] = jnp.zeros_like(total)

    field = window_at(info, info[0] * pl.num_programs(1) + window)
    start = slab_start(field, qkv.shape[0])
    pick, pulled = slots_from(field, start, qkv)
    slots[...] = pulled.astype(BF)
    att_slots[...] = nn_dot(pick[:, :SLAB], att[pl.ds(start, SLAB), :])
    grad_slots[...] = nn_dot(pick[:, :SLAB], att_grad[pl.ds(start, SLAB), :])

    lane = iota((SLOT, 128), 1)
    low = lane < HD
    inner = lane % 32
    pairs = width // 128
    q_all, grads, dots = [], [], []
    for pair in range(pairs):
        at = pair * 128
        q2 = slots[:, at : at + 128]
        k2 = slots[:, width + at : width + at + 128]
        v2 = slots[:, 2 * width + at : 2 * width + at + 128]
        zero = jnp.zeros_like(k2)
        keys[2 * pair, :SLOT, :128] = jnp.where(low, k2, zero)
        keys[2 * pair + 1, :SLOT, :128] = jnp.where(low, zero, k2)
        vals[2 * pair, :SLOT, :] = jnp.where(low, v2, zero)
        vals[2 * pair + 1, :SLOT, :] = jnp.where(low, zero, v2)
        grad = (grad_slots[:, at : at + 128] * inv[:, at : at + 128]).astype(BF)
        cross = grad.astype(F32) * att_slots[:, at : at + 128]
        dots.append(jnp.sum(jnp.where(low, cross, 0.0), axis=1, keepdims=True))
        dots.append(jnp.sum(jnp.where(low, 0.0, cross), axis=1, keepdims=True))
        q_all.append(q2)
        grads.append(grad)
    probs_grads = [nt_dot(grads[head // 2], vals[head]) for head in range(2 * pairs)]
    scores_grads = []
    for head in range(2 * pairs):
        weights = exps[head].astype(F32)
        scores_grads.append((weights * (probs_grads[head] - dots[head])).astype(BF))
    for pair in range(pairs):
        at = pair * 128
        q2, grad = q_all[pair], grads[pair]
        zero = jnp.zeros_like(grad)
        q_scaled = q2 * BF(0.125)
        grad_heads = (jnp.where(low, grad, zero), jnp.where(low, zero, grad))
        q_heads = (jnp.where(low, q_scaled, zero), jnp.where(low, zero, q_scaled))
        q_sum, k_sum, v_sum = None, None, None
        for head in range(2):
            which = 2 * pair + head
            q_part = nn_dot(scores_grads[which], keys[which])
            k_part = tn_dot(scores_grads[which], q_heads[head])
            v_part = tn_dot(exps[which], grad_heads[head])
            q_sum = q_part if q_sum is None else q_sum + q_part
            k_sum = k_part if k_sum is None else k_sum + k_part
            v_sum = v_part if v_sum is None else v_sum + v_part
        rel = shift_right(jnp.where(inner < WIN, q_sum[:, 128:], 0.0), shifts[...])
        rel_hi = rel.astype(BF)
        rel_lo = (rel - rel_hi.astype(F32)).astype(BF)
        rel2 = jnp.concatenate([rel_hi, rel_lo], axis=1)
        q_grad = q_sum[:, :128] * 0.125 + nt_dot(rel2, tables2[...])
        table_sum[...] += tn_dot(q2, rel2)
        v_grad = v_sum[:SLOT]
        fresh[:, at : at + 128] = q_grad.astype(BF)
        fresh[:, width + at : width + at + 128] = k_sum[:SLOT].astype(BF)
        fresh[:, 2 * width + at : 2 * width + at + 128] = v_grad.astype(BF)
        bias_sum[:, at : at + 128] += eight(q_grad)
        bias_sum[:, 2 * width + at : 2 * width + at + 128] += eight(v_grad)
    pack = pack_of(field, start)
    total[pl.ds(start, SLAB), :] += nn_dot(pack, fresh[...])

    @pl.when(window == pl.num_programs(1) - 1)
    def _():
        out[...] = total[...].astype(BF)


def attend_back(
    qkv, info, exps, inv, att, att_grad, tables, shifts, onehot, base, count, held, cols, per
):
    rows = qkv.shape[0]
    width = D // cols
    pairs = width // 128
    tables2 = jnp.concatenate([tables, tables], axis=1)
    row_spec = pl.BlockSpec((rows, width), lambda c, w, s: (0, c + base))
    qkv_spec = pl.BlockSpec((rows, 3 * width), lambda c, w, s: (0, c + base))
    held = list(held)
    return pl.pallas_call(
        partial(attend_back_kernel, width, len(held)),
        out_shape=[
            jax.ShapeDtypeStruct((rows, 3 * D), BF),
            jax.ShapeDtypeStruct((128, 256), F32),
            jax.ShapeDtypeStruct((8, count * 3 * width), F32),
        ],
        grid_spec=pltpu.PrefetchScalarGridSpec(
            num_scalar_prefetch=1,
            grid=(count, per),
            in_specs=[
                qkv_spec,
                pl.BlockSpec((2 * pairs, SLOT, KEYS), lambda c, w, s: (c + base, w, 0)),
                pl.BlockSpec((SLOT, width), lambda c, w, s: (w, c + base)),
                row_spec,
                row_spec,
                pl.BlockSpec((128, 256), lambda c, w, s: (0, 0)),
                pl.BlockSpec((SLOT, 128), lambda c, w, s: (0, 0)),
                pl.BlockSpec((2, KEYS, 128), lambda c, w, s: (0, 0, 0)),
            ]
            + [pl.BlockSpec(memory_space=pl.ANY)] * len(held),
            out_specs=[
                qkv_spec,
                pl.BlockSpec((128, 256), lambda c, w, s: (0, 0)),
                pl.BlockSpec((8, 3 * width), lambda c, w, s: (0, c)),
            ],
            scratch_shapes=[
                pltpu.VMEM((2 * pairs, KEYS, 256), BF),
                pltpu.VMEM((2 * pairs, KEYS, 128), BF),
                pltpu.VMEM((SLOT, 3 * width), BF),
                pltpu.VMEM((SLOT, width), F32),
                pltpu.VMEM((SLOT, width), F32),
                pltpu.VMEM((SLOT, 3 * width), BF),
                pltpu.VMEM((rows, 3 * width), F32),
            ],
        ),
        input_output_aliases={9 + i: i for i in range(len(held))},
        compiler_params=params(2),
        cost_estimate=cost(54 * count // cols),
        name="attend_back",
    )(info, qkv, exps, inv, att, att_grad, tables2, shifts, onehot, *held)


def split_table(total):
    total = (total[:, :128] + total[:, 128:]).reshape(2, HD, 2, 2, 32)
    both = total[0, :, 0] + total[1, :, 1]
    both = jnp.transpose(both, (1, 2, 0))[:, :27][:, ::-1]
    return both[0], both[1]


def col_exchange(values):
    return lax.all_to_all(values, "col", 0, 0, tiled=True)


def row_swap(values, bit, nr):
    return lax.ppermute(values, "row", [(i, i ^ bit) for i in range(nr)])


def after(values, *others):
    return lax.optimization_barrier((values, *others))[0]


def gather_cols(shard, cols):
    return col_exchange(jnp.broadcast_to(shard[None], (cols,) + shard.shape))


def gather_rows(stack, nr, flip):
    order = outer_bits(nr)
    order = order[::-1] if flip else order
    held = stack[None]
    for bit in order[:-1]:
        fresh = row_swap(held, bit, nr)
        gate = yield [fresh]
        held = jnp.concatenate([held, after(fresh, *(gate or ()))], axis=0)
    fresh = row_swap(held, order[-1], nr)
    gate = yield [held, fresh]
    bufs = [held, after(fresh, *(gate or ()))]
    bufs = bufs + [row_swap(buf, 1, nr) for buf in bufs]
    yield bufs


class Hops(list):
    def __init__(self, arrived, sent):
        super().__init__(arrived)
        self.sent = sent


def last_terms(stages):
    found = stages.send(None)
    while isinstance(found, Hops):
        found = stages.send(None)
    return found


def place_of(step, free, fixed, weights):
    total = sum(weights[b] for b in fixed)
    for i, bit in enumerate(free):
        total = total + ((step >> i) & 1) * weights[bit]
    return total


def add_kernel(counts, *refs):
    at = 0
    outs = refs[sum(counts) :]
    for count, out in zip(counts, outs):
        total = refs[at][...].astype(F32)
        for ref in refs[at + 1 : at + count]:
            total = total + ref[...].astype(F32)
        out[...] = total.astype(BF)
        at += count


def split_kernel(counts, axis, lane, *refs):
    out = refs[sum(counts)]
    for k in range(out.shape[0]):
        at = 0
        for h, count in enumerate(counts):
            total = refs[at][0, k].astype(F32)
            for ref in refs[at + 1 : at + count]:
                total = total + ref[0, k].astype(F32)
            at += count
            high, wide = total.shape
            row = h * high if axis == -2 else 0
            col = lane + (h * wide if axis == -1 else 0)
            out[k, row : row + high, col : col + wide] = total.astype(out.dtype)


def reduce_weight(keep, send, axis, cols, nr):
    arrived = row_swap(send, 1, nr)
    gate = yield [arrived]
    bits = outer_bits(nr)
    _, _, bw, n = keep.shape
    shape = [bw, n]
    halves = 1
    if axis is not None:
        halves = 2
        shape[axis] //= 2
    block = (1, cols, shape[0], shape[1])
    terms = [[(keep, bits, True), (arrived, bits, True)] for _ in range(halves)]
    left = [list(bits) for _ in range(halves)]

    def spec(term, h, free, fixed):
        _, own, whole = term
        weights = {b: 1 << i for i, b in enumerate(own)}

        def place(step):
            spot = [place_of(step, free, fixed, weights), 0, 0, 0]
            if whole and axis is not None:
                spot[axis] = h
            return tuple(spot)

        return pl.BlockSpec(block, place)

    for step in range(len(bits)):
        sizes, specs, arrays, taken = [], [], [], []
        for h in range(halves):
            bit = bits[step] if h else bits[-1 - step]
            left[h].remove(bit)
            taken.append(bit)
            sizes.append(len(terms[h]))
            for term in terms[h]:
                specs.append(spec(term, h, left[h], [bit]))
                arrays.append(term[0])
        count = 1 << len(left[0])
        arrays[0] = after(arrays[0], *(gate or ()))
        out_spec = pl.BlockSpec(block, lambda i: (i, 0, 0, 0))
        outs = pl.pallas_call(
            partial(add_kernel, sizes),
            out_shape=[jax.ShapeDtypeStruct((count,) + block[1:], BF)] * halves,
            grid=(count,),
            in_specs=specs,
            out_specs=[out_spec] * halves,
            compiler_params=params(),
            cost_estimate=cost(3),
            name="add_rows",
        )(*arrays)
        fresh = [row_swap(out, bit, nr) for out, bit in zip(outs, taken)]
        for h in range(halves):
            terms[h].append((fresh[h], list(left[h]), False))
        gate = yield Hops(fresh, outs)

    sizes = [len(t) for t in terms]
    specs = [spec(term, h, [], []) for h in range(halves) for term in terms[h]]
    arrays = [term[0] for h in range(halves) for term in terms[h]]
    yield sizes, axis, specs, arrays, (cols, bw, n)


def add_cols_kernel(groups, *refs):
    outs = refs[-1]
    at, lane = 0, 0
    for sizes, axis, n in groups:
        count = sum(sizes)
        split_kernel(sizes, axis, lane, *refs[at : at + count], outs)
        at += count
        lane += n


def finish_weights(parts, *gate):
    cols, bw, _ = parts[0][4]
    groups = [(sizes, axis, shape[2]) for sizes, axis, _, _, shape in parts]
    wide = sum(n for _, _, n in groups)
    arrays = [array for part in parts for array in part[3]]
    arrays[0] = after(arrays[0], *gate)
    outs = pl.pallas_call(
        partial(add_cols_kernel, groups),
        out_shape=jax.ShapeDtypeStruct((cols, bw, wide), BF),
        grid=(1,),
        in_specs=[sp for part in parts for sp in part[2]],
        out_specs=pl.BlockSpec((cols, bw, wide), lambda i: (0, 0, 0)),
        compiler_params=params(),
        cost_estimate=cost(3),
        name="add_cols",
    )(*arrays)
    return outs, col_exchange(outs)


def last_sum(arrived, sizes, *gate):
    total = jnp.sum(after(arrived, *gate).astype(F32), axis=0)
    found, lane = [], 0
    for n in sizes:
        found.append(total[:, lane : lane + n])
        lane += n
    return found


def sum_cols(by_place, whole, me, cols):
    size = by_place.shape[1]
    if whole is not None:
        whole = jnp.broadcast_to(whole, (cols,) + whole.shape)
        by_place = jnp.concatenate([by_place, whole], axis=1)
    arrived = [lax.dynamic_index_in_dim(by_place, me, 0, keepdims=False)]
    for k in range(1, cols):
        sent = lax.dynamic_index_in_dim(by_place, me ^ k, 0, keepdims=False)
        arrived.append(lax.ppermute(sent, "col", [(i, i ^ k) for i in range(cols)]))
    gate = yield arrived[1:]
    arrived = list(lax.optimization_barrier((*arrived, *(gate or ())))[:cols])
    if whole is None:
        yield sum(arrived[1:], arrived[0])
    order = me ^ jnp.arange(cols, dtype=jnp.int32)
    total = jnp.sum(pick_rows(jnp.stack(arrived), order), axis=0)
    yield total[:size], total[size:]


def sum_rows(total, nr):
    bit = 1
    while bit < nr:
        total = total + row_swap(total, bit, nr)
        bit *= 2
    return total


def pick_rows(values, order):
    rows = jnp.arange(values.shape[0], dtype=jnp.int32)
    chosen = (order[:, None] == rows[None, :]).reshape(order.shape + rows.shape + (1,) * (values.ndim - 1))
    return jnp.sum(jnp.where(chosen, values[None], 0.0), axis=1)


def body(
    cols,
    nr,
    tokens_in,
    pad_offsets,
    norm1_gain,
    norm1_bias,
    qkv_weight,
    qv_bias,
    table_height,
    table_width,
    proj_weight,
    proj_bias,
    norm2_gain,
    norm2_bias,
    fc1_weight,
    fc1_bias,
    fc2_weight,
    fc2_bias,
    out_grad,
):
    width = D // cols
    bw = D // nr
    per = -(-WINDOWS // cols)
    me = lax.axis_index("col").astype(jnp.int32)
    my_row = lax.axis_index("row").astype(jnp.int32)
    sets, rows = window_sets(cols, per)
    info = plan(sets, pad_offsets)
    row_order = my_row ^ jnp.arange(nr, dtype=jnp.int32)

    hidden = fc1_weight.shape[1]
    half = hidden // 2
    fc2_t = fc2_weight.T
    qkv_stack = gather_cols(jnp.transpose(qkv_weight, (1, 0, 2)), cols)
    x_sent = spread(tokens_in, info, cols, per, rows)
    x_pieces = col_exchange(x_sent)
    qkv_stack = after(qkv_stack, x_sent)
    hop_a = gather_rows(qkv_stack[:, :, : bw // 2], nr, False)
    hop_b = gather_rows(qkv_stack[:, :, bw // 2 :], nr, True)
    first_a, first_b = next(hop_a), next(hop_b)
    g_sent = spread(after(out_grad, *first_a, *first_b), info, cols, per, rows)
    for _ in outer_bits(nr)[1:]:
        first_a, first_b = hop_a.send(None), hop_b.send(None)
    qkv_a, qkv_b = hop_a.send((g_sent,)), hop_b.send((g_sent,))
    small_args = (norm1_gain, proj_bias, fc2_bias, qv_bias, fc1_bias)
    norm1_gain, proj_bias, fc2_bias, qv_bias, fc1_bias = lax.optimization_barrier(
        (*small_args, *qkv_a, *qkv_b)
    )[:5]
    vec = jnp.concatenate(
        [
            norm1_gain,
            norm1_bias,
            norm2_gain,
            norm2_bias,
            proj_bias.astype(F32),
            fc2_bias.astype(F32),
            qv_bias[0].astype(F32),
            qv_bias[1].astype(F32),
            fc1_bias.astype(F32),
        ]
    )
    vecs = [vec] + [lax.ppermute(vec, "col", [(i, i ^ k) for i in range(cols)]) for k in range(1, cols)]
    vecs = pick_rows(jnp.stack(vecs), me ^ jnp.arange(cols, dtype=jnp.int32))
    wide0 = jnp.concatenate([fc1_weight[:, :half], proj_weight.T, fc2_t[:, :half]], axis=1)
    wide1 = jnp.concatenate([fc1_weight[:, half:], fc2_t[:, half:]], axis=1)
    stack0 = gather_cols(after(wide0, x_pieces, *qkv_a, *qkv_b), cols)
    first = half + width
    features = vecs[:, : 6 * width].reshape(cols, 6, width // bw, bw)
    features = features.transpose(0, 2, 1, 3).reshape(nr, 6, bw)
    features = pick_rows(features, row_order).transpose(1, 0, 2).reshape(6, 1, D)
    gain1, bias1, gain2, bias2, bias_p, bias_2 = [features[i] for i in range(6)]
    q_bias = vecs[:, 6 * width : 7 * width]
    v_bias = vecs[:, 7 * width : 8 * width]
    bias_qkv = jnp.stack([q_bias, jnp.zeros_like(q_bias), v_bias], axis=1).reshape(1, 3 * D)
    bias_h = vecs[:, 8 * width :]

    x_full, n1, qkv = norm_qkv(
        after(x_pieces, g_sent), qkv_a, qkv_b, info, gain1, bias1, bias_qkv, cols, rows, nr
    )
    shifts_np, onehot_np = rel_constants()
    shifts = jnp.asarray(shifts_np)
    onehot = jnp.asarray(onehot_np, BF)
    tables = table_matrix(table_height, table_width)
    stack1 = gather_cols(after(wide1, stack0), cols)
    held = ()
    arrived = []
    bits = outer_bits(nr)
    for part, base in enumerate(range(0, cols, cols // SPLITS)):
        held = attend(
            after(qkv, *arrived),
            info,
            tables,
            shifts,
            onehot,
            base,
            cols // SPLITS,
            held,
            cols,
            per,
        )
        att = held[0]
        arrived = []
        if part == 0:
            stack0 = after(stack0, att)
            hops0 = [
                gather_rows(stack0[:, :, :first], nr, False),
                gather_rows(stack0[:, :, first:], nr, True),
            ]
            bufs0 = [next(hop) for hop in hops0]
        if part == 1:
            stack1 = after(stack1, att)
            g_pieces = col_exchange(after(g_sent, stack1))
            bufs0 = [hop.send((att, *bufs0[0], *bufs0[1])) for hop in hops0]
            arrived = [stack1]
        if part == 3:
            for _ in range(len(bits) - 2):
                bufs0 = [hop.send(None) for hop in hops0]
            bufs0 = [hop.send((att, *bufs0[0], *bufs0[1])) for hop in hops0]
            stack1 = after(stack1, att)
            hops1 = [
                gather_rows(stack1[:, :, :half], nr, False),
                gather_rows(stack1[:, :, half:], nr, True),
            ]
            bufs1 = [next(hop) for hop in hops1]
    att, exps, inv = held
    resid, n2 = proj_norm(bufs0[0], att, x_full, bias_p, gain2, bias2, cols, rows, nr)
    bufs1 = [hop.send((n2, *bufs1[0], *bufs1[1])) for hop in hops1]
    g_full = join(g_pieces, info, cols, rows, nr)
    fc1_bufs, fc2_bufs = [bufs0[0]], [bufs0[1]]

    acts, grads, sends, hidden_sums = [], [], [], []
    for c in range(2):
        if c == 1:
            for _ in range(len(bits) - 2):
                bufs1 = [hop.send(None) for hop in hops1]
            bufs1 = [hop.send((acts[0], *bufs1[0], *bufs1[1])) for hop in hops1]
            fc1_bufs.append(bufs1[0])
            fc2_bufs.append(bufs1[1])
        act, grad, keep, send, bias_sum = mlp_grads(
            fc1_bufs[c],
            fc2_bufs[c],
            n2,
            g_full,
            bias_h[:, None, c * half : (c + 1) * half],
            cols,
            rows,
            nr,
        )
        acts.append(act)
        grads.append(grad)
        hidden_sums.append(jnp.sum(bias_sum, axis=1))
        sends.append(reduce_weight(keep, send, -1, cols, nr))
    core0, core1 = [next(send) for send in sends]
    rows0 = sends[0].send((*core0, acts[1]))
    block_sent = block_rows(
        fc2_bufs, acts, after(resid, *core1), bias_2, info, cols, rows, nr
    )
    block_pieces = col_exchange(block_sent)
    rows0 = sends[0].send((*rows0, block_sent))
    rows1 = sends[1].send((block_sent,))
    resid_grad, proj_grad, sums2 = mlp_back(
        fc1_bufs,
        grads,
        after(resid, block_sent),
        g_full,
        gain2,
        cols,
        rows,
        nr,
    )
    rows1 = sends[1].send((*rows1, proj_grad))
    att_grad, keep, send = proj_back(
        fc1_bufs[0], after(proj_grad, *rows0), att, cols, rows, nr
    )
    sends.append(reduce_weight(keep, send, None, cols, nr))
    core2 = next(sends[2])
    ratio = width // bw
    places = jnp.arange(cols * ratio, dtype=jnp.int32) ^ my_row

    def by_col(sums):
        count = sums.shape[0]
        blocks = jnp.sum(sums, axis=1).reshape(count, nr, bw).transpose(1, 0, 2)
        picked = pick_rows(blocks, places).reshape(cols, ratio, count, bw)
        return picked.transpose(0, 2, 1, 3).reshape(cols, count * width)

    held, table_sums, bias_sums = (), [], []
    for part, base in enumerate(range(0, cols, cols // SPLITS)):
        arrived = []
        if part == 1:
            done0, arrived0 = finish_weights([last_terms(sends[0])], dqkv, block_pieces)
            rows2 = sends[2].send((*core2, dqkv))
            arrived = [block_pieces, *rows1, done0]
        if part == 2:
            rows2 = sends[2].send((*rows2, dqkv))
        if part == 3:
            arrived = [arrived0]
            done1, arrived1 = finish_weights(
                [last_terms(sends[1]), last_terms(sends[2])], dqkv, arrived0, *rows2
            )
            arrived = [arrived0, done1]
        dqkv, table_sum, bias_sum = attend_back(
            after(qkv, *arrived),
            info,
            exps,
            inv,
            att,
            att_grad,
            tables,
            shifts,
            onehot,
            base,
            cols // SPLITS,
            held,
            cols,
            per,
        )
        held = (dqkv,)
        table_sums.append(table_sum)
        bias_sums.append(bias_sum)
    table_sum = sum(table_sums[1:], table_sums[0])
    bias_sum = jnp.concatenate(bias_sums, axis=1)
    bias_cols = jnp.sum(bias_sum, axis=0).reshape(cols, 3, width)
    table_h_grad, table_w_grad = split_table(table_sum)
    table_flat = jnp.concatenate([table_h_grad.reshape(-1), table_w_grad.reshape(-1)])
    small = jnp.concatenate(
        [by_col(sums2), bias_cols[:, 0], bias_cols[:, 2]] + hidden_sums, axis=1
    )
    early = sum_cols(small, table_flat, me, cols)
    next(early)
    keep, send = qkv_grad(after(n1, dqkv), dqkv, cols, rows, nr)
    sends.append(reduce_weight(keep, send, -2, cols, nr))
    core3 = next(sends[3])
    block_out = collect(after(block_pieces, keep), sets, info, BF)
    rows3 = sends[3].send((*core3, block_out))
    small, table_flat = early.send((block_out,))
    in_sent, in_sums = input_back(
        qkv_a,
        qkv_b,
        after(dqkv, block_out, arrived1, small, *rows3.sent),
        x_full,
        resid_grad,
        gain1,
        info,
        cols,
        rows,
        nr,
    )
    late = sum_cols(by_col(in_sums), None, me, cols)
    late_arrived = next(late)
    in_pieces = col_exchange(after(in_sent, *late_arrived))
    rows3 = sends[3].send((in_sent,))
    for _ in range(len(outer_bits(nr)) - 2):
        rows3 = sends[3].send(None)
    sizes = [2 * width, small.shape[0], table_flat.shape[0]]
    total = sum_rows(
        jnp.concatenate([late.send(None), small, after(table_flat, *rows3.sent)]), nr
    )
    done3, arrived3 = finish_weights([sends[3].send(None)], in_pieces, total)
    late, small = total[: sizes[0]], total[sizes[0] : sizes[0] + sizes[1]]
    table_flat = total[sizes[0] + sizes[1] :].reshape(2, 27, HD)
    input_grad = collect(after(in_pieces, done3), sets, info, F32)
    (qkv_w_grad,) = last_sum(arrived3, [3 * width])
    fc_grads = last_sum(arrived0, [2 * half], done3)
    fc_grad, proj_w_grad = last_sum(arrived1, [2 * half, width], done3)
    fc_grads.append(fc_grad)

    def part(i):
        return small[i * width : (i + 1) * width]

    return (
        block_out,
        input_grad,
        late[:width],
        late[width:],
        qkv_w_grad.reshape(bw, 3, width),
        jnp.stack([part(4), part(5)]),
        table_flat[0],
        table_flat[1],
        proj_w_grad.T,
        part(0),
        part(1),
        part(2),
        jnp.concatenate([grad[:, :half] for grad in fc_grads], axis=1),
        small[6 * width :],
        jnp.concatenate([grad[:, half:] for grad in fc_grads], axis=1).T,
        part(3),
    )


def solution(mesh):
    placed = (
        P("row", "col"),
        P("row", None),
        P("col"),
        P("col"),
        P("row", None, "col"),
        P(None, "col"),
        P(),
        P(),
        P("col", "row"),
        P("col"),
        P("col"),
        P("col"),
        P("row", "col"),
        P("col"),
        P("col", "row"),
        P("col"),
        P("row", "col"),
    )
    return jax.shard_map(
        partial(body, mesh.shape["col"], mesh.shape["row"]),
        mesh=mesh,
        in_specs=placed,
        out_specs=(
            P("row", "col"),
            P("row", "col"),
            P("col"),
            P("col"),
            P("row", None, "col"),
            P(None, "col"),
            P(),
            P(),
            P("col", "row"),
            P("col"),
            P("col"),
            P("col"),
            P("row", "col"),
            P("col"),
            P("col", "row"),
            P("col"),
        ),
        check_vma=False,
    )
```

```python
from functools import partial

import jax
import jax.numpy as jnp
import numpy as np
from jax import lax
from jax.experimental import pallas as pl
from jax.experimental.pallas import tpu as pltpu
from jax.sharding import PartitionSpec as P

D = 1024
HD = 64
WIN = 14
SIDE = 64
GRID = 5
WINDOWS = 25
REAL = 196
SLOT = 200
KEYS = 256
PIX = 4096
EPSILON = 1e-06
MARGIN = 6
PADROWS = 84
BF = jnp.bfloat16
F32 = jnp.float32
SPLITS = 4
BLOCKS = 4
SLAB = 224
FIELDS = 7
HEAD = 5
TAIL = 16


def iota(shape, dim):
    return lax.broadcasted_iota(jnp.int32, shape, dim)


def params(n=1, mib=60):
    return pltpu.CompilerParams(
        dimension_semantics=("arbitrary",) * n, vmem_limit_bytes=mib * 1024 * 1024
    )


def cost(micros):
    return pl.CostEstimate(
        flops=int(micros * 1.1e9), bytes_accessed=int(micros * 1e6), transcendentals=0
    )


def nt_dot(a, b):
    return lax.dot_general(a, b, (((1,), (1,)), ((), ())), preferred_element_type=F32)


def tn_dot(a, b):
    return lax.dot_general(a, b, (((0,), (0,)), ((), ())), preferred_element_type=F32)


def nn_dot(a, b):
    return lax.dot_general(a, b, (((1,), (0,)), ((), ())), preferred_element_type=F32)


def window_sets(cols, per):
    units = [[0, 4, 20, 24]]
    units += [[j, 20 + j] for j in (1, 2, 3)] + [[5 * i, 5 * i + 4] for i in (1, 2, 3)]
    units += [[5 * i + j] for i in (1, 2, 3) for j in (1, 2, 3)]
    sizes = [484] + [308] * 6 + [196] * 9
    sets = [[] for _ in range(cols)]
    loads = [0] * cols
    for unit, size in zip(units, sizes):
        open_sets = [d for d in range(cols) if len(sets[d]) + len(unit) <= per]
        best = min(open_sets, key=lambda d: loads[d])
        sets[best] += unit
        loads[best] += size
    capacity = -(-(max(loads) + TAIL) // 64) * 64
    return [own + [WINDOWS] * (per - len(own)) for own in sets], capacity


def plan_kernel(cols, per, ids, offsets, info):
    top, left = offsets[0, 0], offsets[0, 1]
    me = lax.axis_index("col").astype(jnp.int32)
    info[0] = me
    info[1] = top
    info[2] = left
    info[3] = lax.axis_index("row").astype(jnp.int32)

    def each_set(d, carry):
        def each_window(i, base):
            at = d * per + i
            win_row, win_col = ids[at] // GRID, ids[at] % GRID
            row_low = jnp.maximum(0, top - WIN * win_row)
            height = jnp.maximum(jnp.minimum(WIN, SIDE + top - WIN * win_row) - row_low, 0)
            col_low = jnp.maximum(0, left - WIN * win_col)
            width = jnp.maximum(jnp.minimum(WIN, SIDE + left - WIN * win_col) - col_low, 0)
            first = HEAD + at * FIELDS
            info[first] = base
            info[first + 1] = row_low
            info[first + 2] = height
            info[first + 3] = col_low
            info[first + 4] = width
            info[first + 5] = jnp.minimum(win_row, GRID - 1)
            info[first + 6] = win_col
            return base + height * width

        count = lax.fori_loop(0, per, each_window, jnp.int32(0))

        @pl.when(d == me)
        def _():
            info[4] = count

        return carry

    lax.fori_loop(0, cols, each_set, jnp.int32(0))


def plan(sets, offsets):
    cols, per = len(sets), len(sets[0])
    smem = pl.BlockSpec(memory_space=pltpu.SMEM)
    return pl.pallas_call(
        partial(plan_kernel, cols, per),
        out_shape=jax.ShapeDtypeStruct((HEAD + cols * per * FIELDS,), jnp.int32),
        in_specs=[smem, smem],
        out_specs=smem,
        cost_estimate=cost(2),
        name="plan",
    )(jnp.asarray(np.array(sets, np.int32).reshape(-1)), offsets)


def window_at(info, index):
    at = HEAD + index * FIELDS
    return [info[at + f] for f in range(FIELDS)]


def target_of(field, left, row, token_col):
    base, row_low, height, col_low, width, _, win_col = field
    col = token_col + (left - WIN * win_col)
    inside = (row >= row_low) & (row < row_low + height) & (col >= col_low) & (col < col_low + width)
    return jnp.where(inside, base + (row - row_low) * width + (col - col_low), -(1 << 20))


def as_pick(mask):
    return mask.astype(F32).astype(BF)


def spread_kernel(per, info, x_ref, out, padded, total):
    top, left = info[1], info[2]
    cols, rows, width = out.shape
    padded[: MARGIN * SIDE, :] = jnp.zeros((MARGIN * SIDE, width), BF)
    padded[(MARGIN + SIDE) * SIDE :, :] = jnp.zeros(((PADROWS - MARGIN - SIDE) * SIDE, width), BF)
    padded[MARGIN * SIDE : (MARGIN + SIDE) * SIDE, :] = x_ref[...]
    token = iota((1, 256), 1)
    row, col = token // SIDE, token % SIDE
    line = iota((64, 256), 0)
    for d in range(cols):
        total[...] = jnp.zeros_like(total)

        def step(i, carry):
            field = window_at(info, d * per + i)
            base, row_low, height, _, across, win_row, _ = field
            for g in range(4):
                start = base + jnp.clip(4 * g - row_low, 0, height) * across
                start = pl.multiple_of(start // 8 * 8, 8)
                pick = as_pick(line == target_of(field, left, row + 4 * g, col) - start)
                first = pl.multiple_of((WIN * win_row + 4 * g - top + MARGIN) * SIDE, SIDE)
                found = nn_dot(pick, padded[pl.ds(first, 256), :])
                total[pl.ds(start, 8), :] += found[:8]
                total[pl.ds(pl.multiple_of(start + 8, 8), 56), :] = found[8:]
            return carry

        lax.fori_loop(0, per, step, 0)
        out[d] = total[:rows].astype(BF)


def spread(x, info, cols, per, rows):
    width = x.shape[1]
    return pl.pallas_call(
        partial(spread_kernel, per),
        out_shape=jax.ShapeDtypeStruct((cols, rows, width), BF),
        grid_spec=pltpu.PrefetchScalarGridSpec(
            num_scalar_prefetch=1,
            grid=(1,),
            in_specs=[pl.BlockSpec((PIX, width), lambda i, s: (0, 0))],
            out_specs=pl.BlockSpec((cols, rows, width), lambda i, s: (0, 0, 0)),
            scratch_shapes=[
                pltpu.VMEM((PADROWS * SIDE, width), BF),
                pltpu.VMEM((rows + 64, width), F32),
            ],
        ),
        compiler_params=params(),
        cost_estimate=cost(7),
        name="spread",
    )(info, x)


def collect_kernel(places, per, info, pieces, out, padded):
    top, left = info[1], info[2]
    _, rows, _ = pieces.shape
    token = iota((1, 256), 1)
    row, col = token // SIDE, token % SIDE
    line = iota((80, 256), 0)
    for win_row in range(GRID):

        def step(g, carry):
            picks, slabs = [], []
            for win_col in range(GRID):
                d, i = places[win_row * GRID + win_col]
                field = window_at(info, d * per + i)
                base, row_low, height, _, across, _, _ = field
                start = base + jnp.clip(4 * g - row_low, 0, height) * across
                start = pl.multiple_of(jnp.minimum(start // 16 * 16, rows - 80), 16)
                picks.append(as_pick(line == target_of(field, left, row + 4 * g, col) - start))
                slabs.append(pieces[d, pl.ds(start, 80), :])
            found = tn_dot(jnp.concatenate(picks, axis=0), jnp.concatenate(slabs, axis=0))
            first = pl.multiple_of((WIN * win_row + 4 * g - top + MARGIN) * SIDE, SIDE)
            padded[pl.ds(first, 256), :] = found.astype(BF)
            return carry

        lax.fori_loop(0, 4, step, 0)
    out[...] = padded[MARGIN * SIDE : (MARGIN + SIDE) * SIDE, :].astype(out.dtype)


def collect(pieces, sets, info, dtype):
    cols, rows, width = pieces.shape
    per = len(sets[0])
    places = {w: (d, i) for d, own in enumerate(sets) for i, w in enumerate(own)}
    return pl.pallas_call(
        partial(collect_kernel, places, per),
        out_shape=jax.ShapeDtypeStruct((PIX, width), dtype),
        grid_spec=pltpu.PrefetchScalarGridSpec(
            num_scalar_prefetch=1,
            grid=(1,),
            in_specs=[pl.BlockSpec((cols, rows, width), lambda i, s: (0, 0, 0))],
            out_specs=pl.BlockSpec((PIX, width), lambda i, s: (0, 0)),
            scratch_shapes=[pltpu.VMEM((PADROWS * SIDE, width), BF)],
        ),
        compiler_params=params(),
        cost_estimate=cost(8),
        name="collect",
    )(info, pieces)


def chunk_place(col, part, width, info, parts):
    return (col * (width // 128) + part) ^ (info[3] // parts)


def swap_halves(values, info, parts):
    if parts == 1:
        return values
    return jnp.where(info[3] % 2 == 1, pltpu.roll(values.astype(F32), 64, 1), values.astype(F32))


def place_features(pieces, info, parts, whole):
    cols, _, width = pieces.shape
    for d in range(cols):
        for c in range(width // 128):
            at = pl.multiple_of(chunk_place(d, c, width, info, parts) * 128, 128)
            values = swap_halves(pieces[d, :, c * 128 : (c + 1) * 128], info, parts)
            whole[:, pl.ds(at, 128)] = values.astype(whole.dtype)


def take_features(whole, pieces, info, parts):
    cols, _, width = pieces.shape
    for d in range(cols):
        for c in range(width // 128):
            at = pl.multiple_of(chunk_place(d, c, width, info, parts) * 128, 128)
            values = swap_halves(whole[:, pl.ds(at, 128)], info, parts)
            pieces[d, :, c * 128 : (c + 1) * 128] = values.astype(BF)


def eight(values):
    total = values[:8]
    for r in range(8, values.shape[0], 8):
        total = total + values[r : r + 8]
    return total


def row_places(nr, flip):
    order = outer_bits(nr)
    order = order[::-1] if flip else order
    held = [0]
    for bit in order[:-1]:
        held = held + [place | bit for place in held]
    groups = [held, [place | order[-1] for place in held]]
    groups = groups + [[place | 1 for place in group] for group in groups]
    where = {place: (g, i) for g, group in enumerate(groups) for i, place in enumerate(group)}
    return [where[place] for place in range(nr)]


def outer_bits(nr):
    return [1 << b for b in range(1, nr.bit_length() - 1)]


def load_rows(bufs, flip, scratch, nr, first=0):
    stride = D // nr
    for p, (g, i) in enumerate(row_places(nr, flip)):
        cols, size, n = bufs[g].shape[1], bufs[g].shape[-2], bufs[g].shape[-1]
        at = p * stride + first
        for k in range(cols):
            if len(bufs[g].shape) == 4:
                scratch[at : at + size, k * n : (k + 1) * n] = bufs[g][i, k]
                continue
            for part in range(3):
                lane = (3 * k + part) * n
                scratch[at : at + size, lane : lane + n] = bufs[g][i, k, part]


def const_spec(shape):
    zeros = (0,) * len(shape)
    return pl.BlockSpec(shape, lambda *a: zeros, pipeline_mode=pl.Buffered(1))


def norm_qkv_kernel(cols, nr, info, *refs):
    pieces = refs[0]
    bufs_a, bufs_b = refs[1:5], refs[5:9]
    gain, bias, bias_qkv, x_out, n_out, qkv_out, whole, weight = refs[9:]
    parts = max(1, 128 * nr // D)
    bw = D // nr

    @pl.when(pl.program_id(0) == 0)
    def _():
        load_rows(bufs_a, False, weight, nr)
        load_rows(bufs_b, True, weight, nr, bw // 2)

    place_features(pieces, info, parts, whole)
    values = whole[...]
    x_out[...] = values.astype(BF)
    mean = jnp.mean(values, axis=1, keepdims=True)
    centred = values - mean
    spread_sq = jnp.mean(centred * centred, axis=1, keepdims=True)
    normed = centred * lax.rsqrt(spread_sq + EPSILON) * gain[...] + bias[...]
    size = values.shape[0]
    real = iota((size, 1), 0) < info[4] - pl.program_id(0) * size
    normed = jnp.where(real, normed, 0.0).astype(BF)
    n_out[...] = normed
    qkv_out[...] = (nn_dot(normed, weight[...]) + bias_qkv[...]).astype(BF)


def norm_qkv(pieces, bufs_a, bufs_b, info, gain, bias, bias_qkv, cols, rows, nr):
    width = D // cols
    return pl.pallas_call(
        partial(norm_qkv_kernel, cols, nr),
        out_shape=[
            jax.ShapeDtypeStruct((rows, D), BF),
            jax.ShapeDtypeStruct((rows, D), BF),
            jax.ShapeDtypeStruct((rows, 3 * D), BF),
        ],
        grid_spec=pltpu.PrefetchScalarGridSpec(
            num_scalar_prefetch=1,
            grid=(BLOCKS,),
            in_specs=[pl.BlockSpec((cols, rows // BLOCKS, width), lambda i, s: (0, i, 0))]
            + [const_spec(bufs_a[0].shape)] * 8
            + [const_spec((1, D)), const_spec((1, D)), const_spec((1, 3 * D))],
            out_specs=[
                pl.BlockSpec((rows // BLOCKS, D), lambda i, s: (i, 0)),
                pl.BlockSpec((rows // BLOCKS, D), lambda i, s: (i, 0)),
                pl.BlockSpec((rows // BLOCKS, 3 * D), lambda i, s: (i, 0)),
            ],
            scratch_shapes=[pltpu.VMEM((rows // BLOCKS, D), F32), pltpu.VMEM((D, 3 * D), BF)],
        ),
        compiler_params=params(),
        cost_estimate=cost(19),
        name="norm_qkv",
    )(info, pieces, *bufs_a, *bufs_b, gain, bias, bias_qkv)


def join_kernel(cols, nr, info, *refs):
    place_features(refs[0], info, max(1, 128 * nr // D), refs[1])


def join(pieces, info, cols, rows, nr):
    width = pieces.shape[-1]
    return pl.pallas_call(
        partial(join_kernel, cols, nr),
        out_shape=jax.ShapeDtypeStruct((rows, D), BF),
        grid_spec=pltpu.PrefetchScalarGridSpec(
            num_scalar_prefetch=1,
            grid=(BLOCKS,),
            in_specs=[pl.BlockSpec((cols, rows // BLOCKS, width), lambda i, s: (0, i, 0))],
            out_specs=pl.BlockSpec((rows // BLOCKS, D), lambda i, s: (i, 0)),
        ),
        compiler_params=params(),
        cost_estimate=cost(7),
        name="join",
    )(info, pieces)


def proj_norm_kernel(nr, *refs):
    att, x, bias_p, gain, bias, resid_out, n_out, weight = refs[4:]

    @pl.when(pl.program_id(0) == 0)
    def _():
        load_rows(refs[:4], False, weight, nr)

    values = x[...].astype(F32) + nt_dot(att[...], weight[...]) + bias_p[...]
    resid_out[...] = values
    mean = jnp.mean(values, axis=1, keepdims=True)
    centred = values - mean
    spread_sq = jnp.mean(centred * centred, axis=1, keepdims=True)
    n_out[...] = (centred * lax.rsqrt(spread_sq + EPSILON) * gain[...] + bias[...]).astype(BF)


def proj_spec(buf, cols, whole):
    n = D // cols
    shape = (buf.shape[0], cols if whole else 1, buf.shape[2], n)
    last = buf.shape[3] // n - 1
    if whole:
        return pl.BlockSpec(shape, lambda *a: (0, 0, 0, last), pipeline_mode=pl.Buffered(1))
    return pl.BlockSpec(shape, lambda k: (0, k, 0, last))


def proj_norm(bufs, att, x, bias_p, gain, bias, cols, rows, nr):
    row_spec = pl.BlockSpec((rows // BLOCKS, D), lambda i: (i, 0))
    return pl.pallas_call(
        partial(proj_norm_kernel, nr),
        out_shape=[jax.ShapeDtypeStruct((rows, D), F32), jax.ShapeDtypeStruct((rows, D), BF)],
        grid=(BLOCKS,),
        in_specs=[proj_spec(bufs[0], cols, True)] * 4
        + [row_spec, row_spec, const_spec((1, D)), const_spec((1, D)), const_spec((1, D))],
        out_specs=[row_spec, row_spec],
        scratch_shapes=[pltpu.VMEM((D, D), BF)],
        compiler_params=params(),
        cost_estimate=cost(11),
        name="proj_norm",
    )(*bufs, att, x, bias_p, gain, bias)


def gelu_and_slope(v):
    below = 0.5 + 0.5 * lax.erf(v * 0.7071067811865476)
    bell = jnp.exp(v * v * -0.5)
    return v * below, below + v * bell * 0.3989422804014327


def store_halves(grad, keep, send, nr, lanes=slice(None)):
    bw = D // nr
    for q in range(nr // 2):
        at = 2 * q * bw
        keep[q, 0, :, lanes] = grad[at : at + bw].astype(BF)
        send[q, 0, :, lanes] = grad[at + bw : at + 2 * bw].astype(BF)


def mlp_grads_kernel(nr, *refs):
    n2, g, bias, act, pre_grad, keep, send, bias_sum, w1, w2 = refs[8:]
    n = w1.shape[1]
    load_rows(refs[:4], False, w1, nr)
    load_rows(refs[4:8], True, w2, nr)
    total = None
    size = n2.shape[0] // BLOCKS
    for r in range(0, n2.shape[0], size):
        pre = nn_dot(n2[r : r + size], w1[...]) + bias[0]
        act_grad = nn_dot(g[r : r + size], w2[...])
        value, slope = gelu_and_slope(pre)
        act[r : r + size] = value.astype(BF)
        grad = act_grad * slope
        pre_grad[r : r + size] = grad.astype(BF)
        part = eight(grad)
        total = part if total is None else total + part
    bias_sum[0] = total
    store_halves(tn_dot(n2[...], pre_grad[...]), keep, send, nr, slice(0, n))
    store_halves(tn_dot(g[...], act[...]), keep, send, nr, slice(n, 2 * n))


def mlp_grads(bufs1, bufs2, n2, g, bias, cols, rows, nr):
    bw = D // nr
    n = bufs2[0].shape[-1]
    w_spec = pl.BlockSpec((nr // 4, 1, bw, n), lambda k: (0, k, 0, 0))
    row_spec = pl.BlockSpec((rows, n), lambda k: (0, k))
    half_spec = pl.BlockSpec((nr // 2, 1, bw, 2 * n), lambda k: (0, k, 0, 0))
    half = jax.ShapeDtypeStruct((nr // 2, cols, bw, 2 * n), BF)
    act = jax.ShapeDtypeStruct((rows, cols * n), BF)
    return pl.pallas_call(
        partial(mlp_grads_kernel, nr),
        out_shape=[act, act, half, half, jax.ShapeDtypeStruct((cols, 8, n), F32)],
        grid=(cols,),
        in_specs=[w_spec] * 8
        + [const_spec((rows, D)), const_spec((rows, D)), pl.BlockSpec((1, 1, n), lambda k: (k, 0, 0))],
        out_specs=[row_spec, row_spec, half_spec, half_spec]
        + [pl.BlockSpec((1, 8, n), lambda k: (k, 0, 0))],
        scratch_shapes=[pltpu.VMEM((D, n), BF)] * 2,
        compiler_params=params(),
        cost_estimate=cost(38),
        name="mlp_grads",
    )(*bufs1, *bufs2, n2, g, bias)


def norm_back(grad, values, gain):
    mean = jnp.mean(values, axis=1, keepdims=True)
    centred = values - mean
    spread_sq = jnp.mean(centred * centred, axis=1, keepdims=True)
    inv = lax.rsqrt(spread_sq + EPSILON)
    hat = centred * inv
    scaled = grad * gain
    first = jnp.mean(scaled, axis=1, keepdims=True)
    second = jnp.mean(scaled * hat, axis=1, keepdims=True)
    return (scaled - first - hat * second) * inv, hat


def block_out_kernel(cols, nr, info, *refs):
    act0, act1, resid, bias_2 = refs[8:12]
    pieces, weight, whole = refs[12:]

    @pl.when(pl.program_id(0) == 0)
    def _():
        load_rows(refs[:4], True, weight.at[0], nr)
        load_rows(refs[4:8], True, weight.at[1], nr)

    out = nt_dot(act0[...], weight[0]) + nt_dot(act1[...], weight[1])
    whole[...] = resid[...] + out + bias_2[...]
    take_features(whole, pieces, info, max(1, 128 * nr // D))


def block_rows(groups, acts, resid, bias_2, info, cols, rows, nr):
    width = D // cols
    wide = acts[0].shape[1]
    row_spec = pl.BlockSpec((rows // BLOCKS, D), lambda i, s: (i, 0))
    wide_spec = pl.BlockSpec((rows // BLOCKS, wide), lambda i, s: (i, 0))
    flat = [b for group in groups for b in group]
    return pl.pallas_call(
        partial(block_out_kernel, cols, nr),
        out_shape=[jax.ShapeDtypeStruct((cols, rows, width), BF)],
        grid_spec=pltpu.PrefetchScalarGridSpec(
            num_scalar_prefetch=1,
            grid=(BLOCKS,),
            in_specs=[const_spec(flat[-1].shape)] * 8
            + [wide_spec] * 2
            + [row_spec, const_spec((1, D))],
            out_specs=[pl.BlockSpec((cols, rows // BLOCKS, width), lambda i, s: (0, i, 0))],
            scratch_shapes=[pltpu.VMEM((2, D, wide), BF), pltpu.VMEM((rows // BLOCKS, D), F32)],
        ),
        compiler_params=params(),
        cost_estimate=cost(26),
        name="block_rows",
    )(info, *flat, *acts, resid, bias_2)[0]


def mlp_back_kernel(nr, *refs):
    grad0, grad1, resid, g, gain, resid_grad, proj_grad, sums, weight = refs[8:]

    @pl.when(pl.program_id(0) == 0)
    def _():
        load_rows(refs[:4], False, weight.at[0], nr)
        load_rows(refs[4:8], False, weight.at[1], nr)
        sums[...] = jnp.zeros_like(sums)

    grad = nt_dot(grad0[...], weight[0]) + nt_dot(grad1[...], weight[1])
    g_f = g[...].astype(F32)
    back, hat = norm_back(grad, resid[...], gain[...])
    total = g_f + back
    resid_grad[...] = total
    low = total.astype(BF)
    proj_grad[...] = low
    sums[0] += eight(low.astype(F32))
    sums[1] += eight(grad * hat)
    sums[2] += eight(grad)
    sums[3] += eight(g_f)


def mlp_back(groups, grads, resid, g, gain, cols, rows, nr):
    wide = grads[0].shape[1]
    row_spec = pl.BlockSpec((rows // BLOCKS, D), lambda i: (i, 0))
    wide_spec = pl.BlockSpec((rows // BLOCKS, wide), lambda i: (i, 0))
    flat = [b for group in groups for b in group]
    shape = flat[-1].shape
    return pl.pallas_call(
        partial(mlp_back_kernel, nr),
        out_shape=[
            jax.ShapeDtypeStruct((rows, D), F32),
            jax.ShapeDtypeStruct((rows, D), BF),
            jax.ShapeDtypeStruct((4, 8, D), F32),
        ],
        grid=(BLOCKS,),
        in_specs=[const_spec(shape)] * 8
        + [wide_spec] * 2
        + [row_spec, row_spec, const_spec((1, D))],
        out_specs=[row_spec, row_spec, pl.BlockSpec((4, 8, D), lambda i: (0, 0, 0))],
        scratch_shapes=[pltpu.VMEM((2, D, wide), BF)],
        compiler_params=params(),
        cost_estimate=cost(28),
        name="mlp_back",
    )(*flat, *grads, resid, g, gain)


def proj_back_kernel(nr, *refs):
    proj_grad, att, att_grad, keep, send, weight = refs[4:]
    load_rows(refs[:4], False, weight, nr)
    store_halves(tn_dot(proj_grad[...], att[...]), keep, send, nr)
    att_grad[...] = nn_dot(proj_grad[...], weight[...]).astype(BF)


def proj_back(bufs, proj_grad, att, cols, rows, nr):
    bw = D // nr
    n = D // cols
    half = jax.ShapeDtypeStruct((nr // 2, cols, bw, n), BF)
    half_spec = pl.BlockSpec((nr // 2, 1, bw, n), lambda k: (0, k, 0, 0))
    col_spec = pl.BlockSpec((rows, n), lambda k: (0, k))
    return pl.pallas_call(
        partial(proj_back_kernel, nr),
        out_shape=[jax.ShapeDtypeStruct((rows, D), BF), half, half],
        grid=(cols,),
        in_specs=[proj_spec(bufs[0], cols, False)] * 4 + [const_spec((rows, D)), col_spec],
        out_specs=[col_spec, half_spec, half_spec],
        scratch_shapes=[pltpu.VMEM((D, n), BF)],
        compiler_params=params(),
        cost_estimate=cost(11),
        name="proj_back",
    )(*bufs, proj_grad, att)


def qkv_grad_kernel(nr, n1, dqkv, keep, send):
    store_halves(tn_dot(n1[...], dqkv[...]), keep, send, nr)


def qkv_grad(n1, dqkv, cols, rows, nr):
    n = 3 * D // cols
    bw = D // nr
    half = jax.ShapeDtypeStruct((nr // 2, cols, bw, n), BF)
    return pl.pallas_call(
        partial(qkv_grad_kernel, nr),
        out_shape=[half] * 2,
        grid=(cols,),
        in_specs=[const_spec((rows, D)), pl.BlockSpec((rows, n), lambda k: (0, k))],
        out_specs=[pl.BlockSpec((nr // 2, 1, bw, n), lambda k: (0, k, 0, 0))] * 2,
        compiler_params=params(),
        cost_estimate=cost(14),
        name="qkv_grad",
    )(n1, dqkv)


def input_back_kernel(cols, nr, info, *refs):
    bufs_a, bufs_b = refs[:4], refs[4:8]
    rest = refs[8:]
    dqkv, x, resid_grad, gain = rest[:4]
    pieces, sums, whole, weight = rest[4:]
    bw = D // nr

    @pl.when(pl.program_id(0) == 0)
    def _():
        load_rows(bufs_a, False, weight, nr)
        load_rows(bufs_b, True, weight, nr, bw // 2)
        sums[...] = jnp.zeros_like(sums)

    grad = nt_dot(dqkv[...], weight[...])
    back, hat = norm_back(grad, x[...].astype(F32), gain[...])
    whole[...] = resid_grad[...] + back
    sums[0] += eight(grad * hat)
    sums[1] += eight(grad)

    @pl.when(pl.program_id(0) == BLOCKS - 1)
    def _():
        lines = []
        for v in range(2):
            left = jnp.sum(sums[v], axis=0, keepdims=True)
            for _ in range(3):
                lines.append(left.astype(BF).astype(F32))
                left = left - lines[-1]
        lines.append(jnp.zeros((2, D), F32))
        whole[whole.shape[0] - TAIL : whole.shape[0] - TAIL + 8, :] = jnp.concatenate(lines, axis=0)

    take_features(whole, pieces, info, max(1, 128 * nr // D))


def input_back(bufs_a, bufs_b, dqkv, x, resid_grad, gain, info, cols, rows, nr):
    width = D // cols
    row_spec = pl.BlockSpec((rows // BLOCKS, D), lambda i, s: (i, 0))
    piece = jax.ShapeDtypeStruct((cols, rows, width), BF)
    return pl.pallas_call(
        partial(input_back_kernel, cols, nr),
        out_shape=[piece],
        grid_spec=pltpu.PrefetchScalarGridSpec(
            num_scalar_prefetch=1,
            grid=(BLOCKS,),
            in_specs=[const_spec(bufs_a[0].shape)] * 8
            + [pl.BlockSpec((rows // BLOCKS, 3 * D), lambda i, s: (i, 0)), row_spec, row_spec]
            + [const_spec((1, D))],
            out_specs=[pl.BlockSpec((cols, rows // BLOCKS, width), lambda i, s: (0, i, 0))]
,
            scratch_shapes=[
                pltpu.VMEM((2, 8, D), F32),
                pltpu.VMEM((rows // BLOCKS, D), F32),
                pltpu.VMEM((D, 3 * D), BF),
            ],
        ),
        compiler_params=params(),
        cost_estimate=cost(25),
        name="input_back",
    )(info, *bufs_a, *bufs_b, dqkv, x, resid_grad, gain)[0]


def rel_constants():
    place = np.arange(SLOT)
    lanes = np.arange(128)
    group = lanes // 32
    row_shift = np.clip(WIN - 1 - place // WIN, 0, WIN - 1)
    col_shift = WIN - 1 - place % WIN
    shifts = np.where(group[None, :] % 2 == 0, row_shift[:, None], col_shift[:, None])
    onehot = np.zeros((2, KEYS, 128), np.float32)
    for head in range(2):
        for key in range(KEYS):
            if key >= REAL:
                onehot[head, key, 64 * head + 28] = -1e9
                continue
            for extra in (0, WIN):
                onehot[head, key, 64 * head + key // WIN + extra] = 1.0
                onehot[head, key, 64 * head + 32 + key % WIN + extra] = 1.0
    return shifts.astype(np.int32), onehot


def table_matrix(table_h, table_w):
    flipped = jnp.stack([table_h, table_w])[:, ::-1, :].astype(BF)
    block = jnp.pad(jnp.transpose(flipped, (2, 0, 1)), ((0, 0), (0, 0), (0, 5)))
    block = block.reshape(HD, HD)
    zero = jnp.zeros_like(block)
    return jnp.concatenate(
        [jnp.concatenate([block, zero], axis=1), jnp.concatenate([zero, block], axis=1)], axis=0
    )


def shift_left(values, shifts):
    for bit in (1, 2, 4, 8):
        values = jnp.where((shifts & bit) != 0, pltpu.roll(values, 128 - bit, 1), values)
    return values


def shift_right(values, shifts):
    for bit in (1, 2, 4, 8):
        values = jnp.where((shifts & bit) != 0, pltpu.roll(values, bit, 1), values)
    return values


def slot_target(field, start, rows, shape):
    base, row_low, height, col_low, width, _, _ = field
    slot = iota(shape, 0 if shape[0] > 1 else 1)
    row, col = slot // WIN, slot % WIN
    inside = (row >= row_low) & (row < row_low + height) & (col >= col_low) & (col < col_low + width)
    return jnp.where(inside, base - start + (row - row_low) * width + (col - col_low), rows)


def slots_from(field, start, source):
    rows = source.shape[0]
    line = iota((SLOT, SLAB + TAIL), 1)
    pick = as_pick(line == slot_target(field, start, SLAB + TAIL - 1, (SLOT, 1)))
    slab = jnp.concatenate([source[pl.ds(start, SLAB), :], source[rows - TAIL :, :]], axis=0)
    return pick, nn_dot(pick, slab)


def pack_of(field, start):
    line = iota((SLAB, SLOT), 0)
    return as_pick(line == slot_target(field, start, -1, (1, SLOT)))


def slab_start(field, rows):
    return pl.multiple_of(jnp.minimum(field[0] // 16 * 16, rows - SLAB), 16)


def attend_kernel(width, held, info, qkv, tables, shifts, onehot, *refs):
    att, exps, inv, keys, vals, slots, total = refs[held:]
    window = pl.program_id(1)
    first = (pl.program_id(0) == 0) & (window == 0)

    @pl.when(first)
    def _():
        for head in range(2 * (width // 128)):
            keys[head, :, :128] = jnp.zeros((KEYS, 128), BF)
            keys[head, :, 128:] = onehot[head % 2]
        for pair in range(width // 128):
            vals[pair, :, :128] = jnp.zeros((KEYS, 128), BF)
            vals[pair, :, 128:] = jnp.ones((KEYS, 128), BF)

    @pl.when(window == 0)
    def _():
        total[...] = jnp.zeros_like(total)

    field = window_at(info, info[0] * pl.num_programs(1) + window)
    start = slab_start(field, qkv.shape[0])
    slots[...] = slots_from(field, start, qkv)[1].astype(BF)

    lane = iota((SLOT, 128), 1)
    low = lane < HD
    inner = lane % 32
    pairs = width // 128
    queries = []
    for pair in range(pairs):
        at = pair * 128
        q2 = slots[:, at : at + 128]
        k2 = slots[:, width + at : width + at + 128]
        vals[pair, :SLOT, :128] = slots[:, 2 * width + at : 2 * width + at + 128]
        zero = jnp.zeros_like(k2)
        keys[2 * pair, :SLOT, :128] = jnp.where(low, k2, zero)
        keys[2 * pair + 1, :SLOT, :128] = jnp.where(low, zero, k2)
        rel = shift_left(nn_dot(q2, tables[...]), shifts[...])
        rel_hi = rel.astype(BF).astype(F32)
        rel_lo = pltpu.roll(rel - rel_hi, WIN, 1)
        rel = jnp.where(inner < WIN, rel_hi, jnp.where(inner < 2 * WIN, rel_lo, 1.0))
        queries.append(jnp.concatenate([q2 * BF(0.125), rel.astype(BF)], axis=1))
    scores = [nt_dot(queries[head // 2], keys[head]) for head in range(2 * pairs)]
    weights = []
    for head in range(2 * pairs):
        peak = jnp.max(scores[head], axis=1, keepdims=True)
        weights.append(jnp.exp(scores[head] - peak).astype(BF))
        exps[head] = weights[head]
    outs = [nn_dot(weights[head], vals[head // 2]) for head in range(2 * pairs)]
    parts = []
    for pair in range(pairs):
        at = pair * 128
        first, second = outs[2 * pair], outs[2 * pair + 1]
        scale = 1.0 / jnp.where(low, first[:, 128:], second[:, 128:])
        inv[:, at : at + 128] = scale
        parts.append((jnp.where(low, first[:, :128], second[:, :128]) * scale).astype(BF))
    pack = pack_of(field, start)
    total[pl.ds(start, SLAB), :] += nn_dot(pack, jnp.concatenate(parts, axis=1))

    @pl.when(window == pl.num_programs(1) - 1)
    def _():
        att[...] = total[...].astype(BF)


def attend(qkv, info, tables, shifts, onehot, base, count, held, cols, per):
    rows = qkv.shape[0]
    width = D // cols
    pairs = width // 128
    held = list(held)
    return pl.pallas_call(
        partial(attend_kernel, width, len(held)),
        out_shape=[
            jax.ShapeDtypeStruct((rows, D), BF),
            jax.ShapeDtypeStruct((D // HD, per * SLOT, KEYS), BF),
            jax.ShapeDtypeStruct((per * SLOT, D), F32),
        ],
        grid_spec=pltpu.PrefetchScalarGridSpec(
            num_scalar_prefetch=1,
            grid=(count, per),
            in_specs=[
                pl.BlockSpec((rows, 3 * width), lambda c, w, s: (0, c + base)),
                pl.BlockSpec((128, 128), lambda c, w, s: (0, 0)),
                pl.BlockSpec((SLOT, 128), lambda c, w, s: (0, 0)),
                pl.BlockSpec((2, KEYS, 128), lambda c, w, s: (0, 0, 0)),
            ]
            + [pl.BlockSpec(memory_space=pl.ANY)] * len(held),
            out_specs=[
                pl.BlockSpec((rows, width), lambda c, w, s: (0, c + base)),
                pl.BlockSpec((2 * pairs, SLOT, KEYS), lambda c, w, s: (c + base, w, 0)),
                pl.BlockSpec((SLOT, width), lambda c, w, s: (w, c + base)),
            ],
            scratch_shapes=[
                pltpu.VMEM((2 * pairs, KEYS, 256), BF),
                pltpu.VMEM((pairs, KEYS, 256), BF),
                pltpu.VMEM((SLOT, 3 * width), BF),
                pltpu.VMEM((rows, width), F32),
            ],
        ),
        input_output_aliases={5 + i: i for i in range(len(held))},
        compiler_params=params(2),
        cost_estimate=cost(58 * count // cols),
        name="attend",
    )(info, qkv, tables, shifts, onehot, *held)


def attend_back_kernel(
    width, held, info, qkv, exps, inv, att, att_grad, tables2, shifts, onehot, *refs
):
    out, table_sum, bias_sum, keys, vals, slots, att_slots, grad_slots, fresh, total = refs[held:]
    window = pl.program_id(1)
    first = (pl.program_id(0) == 0) & (window == 0)

    @pl.when(first)
    def _():
        for head in range(2 * (width // 128)):
            keys[head, :, :128] = jnp.zeros((KEYS, 128), BF)
            keys[head, :, 128:] = onehot[head % 2]
        vals[...] = jnp.zeros_like(vals)
        table_sum[...] = jnp.zeros_like(table_sum)

    @pl.when(window == 0)
    def _():
        bias_sum[...] = jnp.zeros_like(bias_sum)
        total[...] = jnp.zeros_like(total)

    field = window_at(info, info[0] * pl.num_programs(1) + window)
    start = slab_start(field, qkv.shape[0])
    pick, pulled = slots_from(field, start, qkv)
    slots[...] = pulled.astype(BF)
    att_slots[...] = nn_dot(pick[:, :SLAB], att[pl.ds(start, SLAB), :])
    grad_slots[...] = nn_dot(pick[:, :SLAB], att_grad[pl.ds(start, SLAB), :])

    lane = iota((SLOT, 128), 1)
    low = lane < HD
    inner = lane % 32
    pairs = width // 128
    q_all, grads, dots = [], [], []
    for pair in range(pairs):
        at = pair * 128
        q2 = slots[:, at : at + 128]
        k2 = slots[:, width + at : width + at + 128]
        v2 = slots[:, 2 * width + at : 2 * width + at + 128]
        zero = jnp.zeros_like(k2)
        keys[2 * pair, :SLOT, :128] = jnp.where(low, k2, zero)
        keys[2 * pair + 1, :SLOT, :128] = jnp.where(low, zero, k2)
        vals[2 * pair, :SLOT, :] = jnp.where(low, v2, zero)
        vals[2 * pair + 1, :SLOT, :] = jnp.where(low, zero, v2)
        grad = (grad_slots[:, at : at + 128] * inv[:, at : at + 128]).astype(BF)
        cross = grad.astype(F32) * att_slots[:, at : at + 128]
        dots.append(jnp.sum(jnp.where(low, cross, 0.0), axis=1, keepdims=True))
        dots.append(jnp.sum(jnp.where(low, 0.0, cross), axis=1, keepdims=True))
        q_all.append(q2)
        grads.append(grad)
    probs_grads = [nt_dot(grads[head // 2], vals[head]) for head in range(2 * pairs)]
    scores_grads = []
    for head in range(2 * pairs):
        weights = exps[head].astype(F32)
        scores_grads.append((weights * (probs_grads[head] - dots[head])).astype(BF))
    for pair in range(pairs):
        at = pair * 128
        q2, grad = q_all[pair], grads[pair]
        zero = jnp.zeros_like(grad)
        q_scaled = q2 * BF(0.125)
        grad_heads = (jnp.where(low, grad, zero), jnp.where(low, zero, grad))
        q_heads = (jnp.where(low, q_scaled, zero), jnp.where(low, zero, q_scaled))
        q_sum, k_sum, v_sum = None, None, None
        for head in range(2):
            which = 2 * pair + head
            q_part = nn_dot(scores_grads[which], keys[which])
            k_part = tn_dot(scores_grads[which], q_heads[head])
            v_part = tn_dot(exps[which], grad_heads[head])
            q_sum = q_part if q_sum is None else q_sum + q_part
            k_sum = k_part if k_sum is None else k_sum + k_part
            v_sum = v_part if v_sum is None else v_sum + v_part
        rel = shift_right(jnp.where(inner < WIN, q_sum[:, 128:], 0.0), shifts[...])
        rel_hi = rel.astype(BF)
        rel_lo = (rel - rel_hi.astype(F32)).astype(BF)
        rel2 = jnp.concatenate([rel_hi, rel_lo], axis=1)
        q_grad = q_sum[:, :128] * 0.125 + nt_dot(rel2, tables2[...])
        table_sum[...] += tn_dot(q2, rel2)
        v_grad = v_sum[:SLOT]
        fresh[:, at : at + 128] = q_grad.astype(BF)
        fresh[:, width + at : width + at + 128] = k_sum[:SLOT].astype(BF)
        fresh[:, 2 * width + at : 2 * width + at + 128] = v_grad.astype(BF)
        bias_sum[:, at : at + 128] += eight(q_grad)
        bias_sum[:, 2 * width + at : 2 * width + at + 128] += eight(v_grad)
    pack = pack_of(field, start)
    total[pl.ds(start, SLAB), :] += nn_dot(pack, fresh[...])

    @pl.when(window == pl.num_programs(1) - 1)
    def _():
        out[...] = total[...].astype(BF)


def attend_back(
    qkv, info, exps, inv, att, att_grad, tables, shifts, onehot, base, count, held, cols, per
):
    rows = qkv.shape[0]
    width = D // cols
    pairs = width // 128
    tables2 = jnp.concatenate([tables, tables], axis=1)
    row_spec = pl.BlockSpec((rows, width), lambda c, w, s: (0, c + base))
    qkv_spec = pl.BlockSpec((rows, 3 * width), lambda c, w, s: (0, c + base))
    held = list(held)
    return pl.pallas_call(
        partial(attend_back_kernel, width, len(held)),
        out_shape=[
            jax.ShapeDtypeStruct((rows, 3 * D), BF),
            jax.ShapeDtypeStruct((128, 256), F32),
            jax.ShapeDtypeStruct((8, count * 3 * width), F32),
        ],
        grid_spec=pltpu.PrefetchScalarGridSpec(
            num_scalar_prefetch=1,
            grid=(count, per),
            in_specs=[
                qkv_spec,
                pl.BlockSpec((2 * pairs, SLOT, KEYS), lambda c, w, s: (c + base, w, 0)),
                pl.BlockSpec((SLOT, width), lambda c, w, s: (w, c + base)),
                row_spec,
                row_spec,
                pl.BlockSpec((128, 256), lambda c, w, s: (0, 0)),
                pl.BlockSpec((SLOT, 128), lambda c, w, s: (0, 0)),
                pl.BlockSpec((2, KEYS, 128), lambda c, w, s: (0, 0, 0)),
            ]
            + [pl.BlockSpec(memory_space=pl.ANY)] * len(held),
            out_specs=[
                qkv_spec,
                pl.BlockSpec((128, 256), lambda c, w, s: (0, 0)),
                pl.BlockSpec((8, 3 * width), lambda c, w, s: (0, c)),
            ],
            scratch_shapes=[
                pltpu.VMEM((2 * pairs, KEYS, 256), BF),
                pltpu.VMEM((2 * pairs, KEYS, 128), BF),
                pltpu.VMEM((SLOT, 3 * width), BF),
                pltpu.VMEM((SLOT, width), F32),
                pltpu.VMEM((SLOT, width), F32),
                pltpu.VMEM((SLOT, 3 * width), BF),
                pltpu.VMEM((rows, 3 * width), F32),
            ],
        ),
        input_output_aliases={9 + i: i for i in range(len(held))},
        compiler_params=params(2),
        cost_estimate=cost(54 * count // cols),
        name="attend_back",
    )(info, qkv, exps, inv, att, att_grad, tables2, shifts, onehot, *held)


def split_table(total):
    total = (total[:, :128] + total[:, 128:]).reshape(2, HD, 2, 2, 32)
    both = total[0, :, 0] + total[1, :, 1]
    both = jnp.transpose(both, (1, 2, 0))[:, :27][:, ::-1]
    return both[0], both[1]


def col_exchange(values):
    return lax.all_to_all(values, "col", 0, 0, tiled=True)


def row_swap(values, bit, nr):
    return lax.ppermute(values, "row", [(i, i ^ bit) for i in range(nr)])


def after(values, *others):
    return lax.optimization_barrier((values, *others))[0]


def gather_cols(shard, cols):
    return col_exchange(jnp.broadcast_to(shard[None], (cols,) + shard.shape))


def gather_rows(stack, nr, flip):
    order = outer_bits(nr)
    order = order[::-1] if flip else order
    held = stack[None]
    for bit in order[:-1]:
        fresh = row_swap(held, bit, nr)
        gate = yield [fresh]
        held = jnp.concatenate([held, after(fresh, *(gate or ()))], axis=0)
    fresh = row_swap(held, order[-1], nr)
    gate = yield [held, fresh]
    bufs = [held, after(fresh, *(gate or ()))]
    bufs = bufs + [row_swap(buf, 1, nr) for buf in bufs]
    yield bufs


class Hops(list):
    def __init__(self, arrived, sent):
        super().__init__(arrived)
        self.sent = sent


def last_terms(stages):
    found = stages.send(None)
    while isinstance(found, Hops):
        found = stages.send(None)
    return found


def place_of(step, free, fixed, weights):
    total = sum(weights[b] for b in fixed)
    for i, bit in enumerate(free):
        total = total + ((step >> i) & 1) * weights[bit]
    return total


def add_kernel(counts, *refs):
    at = 0
    outs = refs[sum(counts) :]
    for count, out in zip(counts, outs):
        total = refs[at][...].astype(F32)
        for ref in refs[at + 1 : at + count]:
            total = total + ref[...].astype(F32)
        out[...] = total.astype(BF)
        at += count


def split_kernel(counts, axis, lane, *refs):
    out = refs[sum(counts)]
    for k in range(out.shape[0]):
        at = 0
        for h, count in enumerate(counts):
            total = refs[at][0, k].astype(F32)
            for ref in refs[at + 1 : at + count]:
                total = total + ref[0, k].astype(F32)
            at += count
            high, wide = total.shape
            row = h * high if axis == -2 else 0
            col = lane + (h * wide if axis == -1 else 0)
            out[k, row : row + high, col : col + wide] = total.astype(out.dtype)


def reduce_weight(keep, send, axis, cols, nr):
    arrived = row_swap(send, 1, nr)
    gate = yield [arrived]
    bits = outer_bits(nr)
    _, _, bw, n = keep.shape
    shape = [bw, n]
    halves = 1
    if axis is not None:
        halves = 2
        shape[axis] //= 2
    block = (1, cols, shape[0], shape[1])
    terms = [[(keep, bits, True), (arrived, bits, True)] for _ in range(halves)]
    left = [list(bits) for _ in range(halves)]

    def spec(term, h, free, fixed):
        _, own, whole = term
        weights = {b: 1 << i for i, b in enumerate(own)}

        def place(step):
            spot = [place_of(step, free, fixed, weights), 0, 0, 0]
            if whole and axis is not None:
                spot[axis] = h
            return tuple(spot)

        return pl.BlockSpec(block, place)

    for step in range(len(bits)):
        sizes, specs, arrays, taken = [], [], [], []
        for h in range(halves):
            bit = bits[step] if h else bits[-1 - step]
            left[h].remove(bit)
            taken.append(bit)
            sizes.append(len(terms[h]))
            for term in terms[h]:
                specs.append(spec(term, h, left[h], [bit]))
                arrays.append(term[0])
        count = 1 << len(left[0])
        arrays[0] = after(arrays[0], *(gate or ()))
        out_spec = pl.BlockSpec(block, lambda i: (i, 0, 0, 0))
        outs = pl.pallas_call(
            partial(add_kernel, sizes),
            out_shape=[jax.ShapeDtypeStruct((count,) + block[1:], BF)] * halves,
            grid=(count,),
            in_specs=specs,
            out_specs=[out_spec] * halves,
            compiler_params=params(),
            cost_estimate=cost(3),
            name="add_rows",
        )(*arrays)
        fresh = [row_swap(out, bit, nr) for out, bit in zip(outs, taken)]
        for h in range(halves):
            terms[h].append((fresh[h], list(left[h]), False))
        gate = yield Hops(fresh, outs)

    sizes = [len(t) for t in terms]
    specs = [spec(term, h, [], []) for h in range(halves) for term in terms[h]]
    arrays = [term[0] for h in range(halves) for term in terms[h]]
    yield sizes, axis, specs, arrays, (cols, bw, n)


def add_cols_kernel(groups, *refs):
    outs = refs[-1]
    at, lane = 0, 0
    for sizes, axis, n in groups:
        count = sum(sizes)
        split_kernel(sizes, axis, lane, *refs[at : at + count], outs)
        at += count
        lane += n


def finish_weights(parts, *gate):
    cols, bw, _ = parts[0][4]
    groups = [(sizes, axis, shape[2]) for sizes, axis, _, _, shape in parts]
    wide = sum(n for _, _, n in groups)
    arrays = [array for part in parts for array in part[3]]
    arrays[0] = after(arrays[0], *gate)
    outs = pl.pallas_call(
        partial(add_cols_kernel, groups),
        out_shape=jax.ShapeDtypeStruct((cols, bw, wide), BF),
        grid=(1,),
        in_specs=[sp for part in parts for sp in part[2]],
        out_specs=pl.BlockSpec((cols, bw, wide), lambda i: (0, 0, 0)),
        compiler_params=params(),
        cost_estimate=cost(3),
        name="add_cols",
    )(*arrays)
    return outs, col_exchange(outs)


def last_sum(arrived, sizes, *gate):
    total = jnp.sum(after(arrived, *gate).astype(F32), axis=0)
    found, lane = [], 0
    for n in sizes:
        found.append(total[:, lane : lane + n])
        lane += n
    return found


def sum_cols(by_place, whole, me, cols):
    size = by_place.shape[1]
    if whole is not None:
        whole = jnp.broadcast_to(whole, (cols,) + whole.shape)
        by_place = jnp.concatenate([by_place, whole], axis=1)
    arrived = [lax.dynamic_index_in_dim(by_place, me, 0, keepdims=False)]
    for k in range(1, cols):
        sent = lax.dynamic_index_in_dim(by_place, me ^ k, 0, keepdims=False)
        arrived.append(lax.ppermute(sent, "col", [(i, i ^ k) for i in range(cols)]))
    gate = yield arrived[1:]
    arrived = list(lax.optimization_barrier((*arrived, *(gate or ())))[:cols])
    order = me ^ jnp.arange(cols, dtype=jnp.int32)
    total = jnp.sum(pick_rows(jnp.stack(arrived), order), axis=0)
    yield total[:size], total[size:]


def sum_rows(total, nr):
    bit = 1
    while bit < nr:
        total = total + row_swap(total, bit, nr)
        yield total
        bit *= 2


def pick_rows(values, order):
    rows = jnp.arange(values.shape[0], dtype=jnp.int32)
    chosen = (order[:, None] == rows[None, :]).reshape(order.shape + rows.shape + (1,) * (values.ndim - 1))
    return jnp.sum(jnp.where(chosen, values[None], 0.0), axis=1)


def body(
    cols,
    nr,
    tokens_in,
    pad_offsets,
    norm1_gain,
    norm1_bias,
    qkv_weight,
    qv_bias,
    table_height,
    table_width,
    proj_weight,
    proj_bias,
    norm2_gain,
    norm2_bias,
    fc1_weight,
    fc1_bias,
    fc2_weight,
    fc2_bias,
    out_grad,
):
    width = D // cols
    bw = D // nr
    per = -(-WINDOWS // cols)
    me = lax.axis_index("col").astype(jnp.int32)
    my_row = lax.axis_index("row").astype(jnp.int32)
    sets, rows = window_sets(cols, per)
    info = plan(sets, pad_offsets)
    row_order = my_row ^ jnp.arange(nr, dtype=jnp.int32)

    hidden = fc1_weight.shape[1]
    half = hidden // 2
    fc2_t = fc2_weight.T
    qkv_stack = gather_cols(jnp.transpose(qkv_weight, (1, 0, 2)), cols)
    x_sent = spread(tokens_in, info, cols, per, rows)
    x_pieces = col_exchange(x_sent)
    qkv_stack = after(qkv_stack, x_sent)
    hop_a = gather_rows(qkv_stack[:, :, : bw // 2], nr, False)
    hop_b = gather_rows(qkv_stack[:, :, bw // 2 :], nr, True)
    first_a, first_b = next(hop_a), next(hop_b)
    g_sent = spread(after(out_grad, *first_a, *first_b), info, cols, per, rows)
    for _ in outer_bits(nr)[1:]:
        first_a, first_b = hop_a.send(None), hop_b.send(None)
    qkv_a, qkv_b = hop_a.send((g_sent,)), hop_b.send((g_sent,))
    small_args = (norm1_gain, proj_bias, fc2_bias, qv_bias, fc1_bias)
    norm1_gain, proj_bias, fc2_bias, qv_bias, fc1_bias = lax.optimization_barrier(
        (*small_args, *qkv_a, *qkv_b)
    )[:5]
    vec = jnp.concatenate(
        [
            norm1_gain,
            norm1_bias,
            norm2_gain,
            norm2_bias,
            proj_bias.astype(F32),
            fc2_bias.astype(F32),
            qv_bias[0].astype(F32),
            qv_bias[1].astype(F32),
            fc1_bias.astype(F32),
        ]
    )
    vecs = [vec] + [lax.ppermute(vec, "col", [(i, i ^ k) for i in range(cols)]) for k in range(1, cols)]
    vecs = pick_rows(jnp.stack(vecs), me ^ jnp.arange(cols, dtype=jnp.int32))
    wide0 = jnp.concatenate([fc1_weight[:, :half], proj_weight.T, fc2_t[:, :half]], axis=1)
    wide1 = jnp.concatenate([fc1_weight[:, half:], fc2_t[:, half:]], axis=1)
    stack0 = gather_cols(after(wide0, x_pieces, *qkv_a, *qkv_b), cols)
    first = half + width
    features = vecs[:, : 6 * width].reshape(cols, 6, width // bw, bw)
    features = features.transpose(0, 2, 1, 3).reshape(nr, 6, bw)
    features = pick_rows(features, row_order).transpose(1, 0, 2).reshape(6, 1, D)
    gain1, bias1, gain2, bias2, bias_p, bias_2 = [features[i] for i in range(6)]
    q_bias = vecs[:, 6 * width : 7 * width]
    v_bias = vecs[:, 7 * width : 8 * width]
    bias_qkv = jnp.stack([q_bias, jnp.zeros_like(q_bias), v_bias], axis=1).reshape(1, 3 * D)
    bias_h = vecs[:, 8 * width :]

    x_full, n1, qkv = norm_qkv(
        after(x_pieces, g_sent), qkv_a, qkv_b, info, gain1, bias1, bias_qkv, cols, rows, nr
    )
    shifts_np, onehot_np = rel_constants()
    shifts = jnp.asarray(shifts_np)
    onehot = jnp.asarray(onehot_np, BF)
    tables = table_matrix(table_height, table_width)
    stack1 = gather_cols(after(wide1, stack0), cols)
    held = ()
    arrived = []
    bits = outer_bits(nr)
    for part, base in enumerate(range(0, cols, cols // SPLITS)):
        held = attend(
            after(qkv, *arrived),
            info,
            tables,
            shifts,
            onehot,
            base,
            cols // SPLITS,
            held,
            cols,
            per,
        )
        att = held[0]
        arrived = []
        if part == 0:
            stack0 = after(stack0, att)
            hops0 = [
                gather_rows(stack0[:, :, :first], nr, False),
                gather_rows(stack0[:, :, first:], nr, True),
            ]
            bufs0 = [next(hop) for hop in hops0]
        if part == 1:
            stack1 = after(stack1, att)
            g_pieces = col_exchange(after(g_sent, stack1))
            bufs0 = [hop.send((att, *bufs0[0], *bufs0[1])) for hop in hops0]
            arrived = [stack1]
        if part == 3:
            for _ in range(len(bits) - 2):
                bufs0 = [hop.send(None) for hop in hops0]
            bufs0 = [hop.send((att, *bufs0[0], *bufs0[1])) for hop in hops0]
            stack1 = after(stack1, att)
            hops1 = [
                gather_rows(stack1[:, :, :half], nr, False),
                gather_rows(stack1[:, :, half:], nr, True),
            ]
            bufs1 = [next(hop) for hop in hops1]
    att, exps, inv = held
    resid, n2 = proj_norm(bufs0[0], att, x_full, bias_p, gain2, bias2, cols, rows, nr)
    bufs1 = [hop.send((n2, *bufs1[0], *bufs1[1])) for hop in hops1]
    g_full = join(g_pieces, info, cols, rows, nr)
    fc1_bufs, fc2_bufs = [bufs0[0]], [bufs0[1]]

    acts, grads, sends, hidden_sums = [], [], [], []
    for c in range(2):
        if c == 1:
            for _ in range(len(bits) - 2):
                bufs1 = [hop.send(None) for hop in hops1]
            bufs1 = [hop.send((acts[0], *bufs1[0], *bufs1[1])) for hop in hops1]
            fc1_bufs.append(bufs1[0])
            fc2_bufs.append(bufs1[1])
        act, grad, keep, send, bias_sum = mlp_grads(
            fc1_bufs[c],
            fc2_bufs[c],
            n2,
            g_full,
            bias_h[:, None, c * half : (c + 1) * half],
            cols,
            rows,
            nr,
        )
        acts.append(act)
        grads.append(grad)
        hidden_sums.append(jnp.sum(bias_sum, axis=1))
        sends.append(reduce_weight(keep, send, -1, cols, nr))
    core0, core1 = [next(send) for send in sends]
    rows0 = sends[0].send((*core0, acts[1]))
    block_sent = block_rows(
        fc2_bufs, acts, after(resid, *core1), bias_2, info, cols, rows, nr
    )
    block_pieces = col_exchange(block_sent)
    rows0 = sends[0].send((*rows0, block_sent))
    rows1 = sends[1].send((block_sent,))
    resid_grad, proj_grad, sums2 = mlp_back(
        fc1_bufs,
        grads,
        after(resid, block_sent),
        g_full,
        gain2,
        cols,
        rows,
        nr,
    )
    rows1 = sends[1].send((*rows1, proj_grad))
    att_grad, keep, send = proj_back(
        fc1_bufs[0], after(proj_grad, *rows0), att, cols, rows, nr
    )
    sends.append(reduce_weight(keep, send, None, cols, nr))
    core2 = next(sends[2])
    ratio = width // bw
    places = jnp.arange(cols * ratio, dtype=jnp.int32) ^ my_row

    def by_col(sums):
        count = sums.shape[0]
        blocks = jnp.sum(sums, axis=1).reshape(count, nr, bw).transpose(1, 0, 2)
        picked = pick_rows(blocks, places).reshape(cols, ratio, count, bw)
        return picked.transpose(0, 2, 1, 3).reshape(cols, count * width)

    held, table_sums, bias_sums = (), [], []
    for part, base in enumerate(range(0, cols, cols // SPLITS)):
        arrived = []
        if part == 1:
            done0, arrived0 = finish_weights([last_terms(sends[0])], dqkv, block_pieces)
            rows2 = sends[2].send((*core2, dqkv))
            arrived = [block_pieces, *rows1, done0]
        if part == 2:
            rows2 = sends[2].send((*rows2, dqkv))
        if part == 3:
            arrived = [arrived0]
            done1, arrived1 = finish_weights(
                [last_terms(sends[1]), last_terms(sends[2])], dqkv, arrived0, *rows2
            )
            arrived = [arrived0, done1]
        dqkv, table_sum, bias_sum = attend_back(
            after(qkv, *arrived),
            info,
            exps,
            inv,
            att,
            att_grad,
            tables,
            shifts,
            onehot,
            base,
            cols // SPLITS,
            held,
            cols,
            per,
        )
        held = (dqkv,)
        table_sums.append(table_sum)
        bias_sums.append(bias_sum)
    table_sum = sum(table_sums[1:], table_sums[0])
    bias_sum = jnp.concatenate(bias_sums, axis=1)
    bias_cols = jnp.sum(bias_sum, axis=0).reshape(cols, 3, width)
    table_h_grad, table_w_grad = split_table(table_sum)
    table_flat = jnp.concatenate([table_h_grad.reshape(-1), table_w_grad.reshape(-1)])
    small = jnp.concatenate(
        [by_col(sums2), bias_cols[:, 0], bias_cols[:, 2]] + hidden_sums, axis=1
    )
    early = sum_cols(small, table_flat, me, cols)
    early_arrived = next(early)
    keep, send = qkv_grad(after(n1, dqkv), dqkv, cols, rows, nr)
    sends.append(reduce_weight(keep, send, -2, cols, nr))
    core3 = next(sends[3])
    block_out = collect(after(block_pieces, keep), sets, info, BF)
    rows3 = sends[3].send((*core3, block_out))
    small, table_flat = early.send((block_out,))
    in_sent = input_back(
        qkv_a,
        qkv_b,
        after(dqkv, block_out, arrived1, *early_arrived, *rows3.sent),
        x_full,
        resid_grad,
        gain1,
        info,
        cols,
        rows,
        nr,
    )
    in_pieces = col_exchange(in_sent)
    rows3 = sends[3].send((in_sent,))
    for _ in range(len(outer_bits(nr)) - 2):
        rows3 = sends[3].send(None)
    sizes = [2 * width, small.shape[0], table_flat.shape[0]]
    late = in_pieces[:, rows - TAIL : rows - TAIL + 6].astype(F32).reshape(cols, 2, 3, width)
    done3, arrived3 = finish_weights([sends[3].send(None)], in_pieces)
    late = jnp.sum(after(late, done3), axis=(0, 2)).reshape(-1)
    totals = list(sum_rows(jnp.concatenate([late, small, table_flat]), nr))
    total = totals[-1]
    late, small = total[: sizes[0]], total[sizes[0] : sizes[0] + sizes[1]]
    table_flat = total[sizes[0] + sizes[1] :].reshape(2, 27, HD)
    input_grad = collect(after(in_pieces, totals[-2]), sets, info, F32)
    (qkv_w_grad,) = last_sum(arrived3, [3 * width])
    fc_grads = last_sum(arrived0, [2 * half], done3)
    fc_grad, proj_w_grad = last_sum(arrived1, [2 * half, width], done3)
    fc_grads.append(fc_grad)

    def part(i):
        return small[i * width : (i + 1) * width]

    return (
        block_out,
        input_grad,
        late[:width],
        late[width:],
        qkv_w_grad.reshape(bw, 3, width),
        jnp.stack([part(4), part(5)]),
        table_flat[0],
        table_flat[1],
        proj_w_grad.T,
        part(0),
        part(1),
        part(2),
        jnp.concatenate([grad[:, :half] for grad in fc_grads], axis=1),
        small[6 * width :],
        jnp.concatenate([grad[:, half:] for grad in fc_grads], axis=1).T,
        part(3),
    )


def solution(mesh):
    placed = (
        P("row", "col"),
        P("row", None),
        P("col"),
        P("col"),
        P("row", None, "col"),
        P(None, "col"),
        P(),
        P(),
        P("col", "row"),
        P("col"),
        P("col"),
        P("col"),
        P("row", "col"),
        P("col"),
        P("col", "row"),
        P("col"),
        P("row", "col"),
    )
    return jax.shard_map(
        partial(body, mesh.shape["col"], mesh.shape["row"]),
        mesh=mesh,
        in_specs=placed,
        out_specs=(
            P("row", "col"),
            P("row", "col"),
            P("col"),
            P("col"),
            P("row", None, "col"),
            P(None, "col"),
            P(),
            P(),
            P("col", "row"),
            P("col"),
            P("col"),
            P("col"),
            P("row", "col"),
            P("col"),
            P("col", "row"),
            P("col"),
        ),
        check_vma=False,
    )
```

```python
from functools import partial

import jax
import jax.numpy as jnp
import numpy as np
from jax import lax
from jax.experimental import pallas as pl
from jax.experimental.pallas import tpu as pltpu
from jax.sharding import PartitionSpec as P

D = 1024
HD = 64
WIN = 14
SIDE = 64
GRID = 5
WINDOWS = 25
REAL = 196
SLOT = 200
KEYS = 256
PIX = 4096
EPSILON = 1e-06
MARGIN = 6
PADROWS = 84
BF = jnp.bfloat16
F32 = jnp.float32
SPLITS = 4
BLOCKS = 4
SLAB = 224
FIELDS = 7
HEAD = 5
TAIL = 16


def iota(shape, dim):
    return lax.broadcasted_iota(jnp.int32, shape, dim)


def params(n=1, mib=60):
    return pltpu.CompilerParams(
        dimension_semantics=("arbitrary",) * n, vmem_limit_bytes=mib * 1024 * 1024
    )


def cost(micros):
    return pl.CostEstimate(
        flops=int(micros * 1.1e9), bytes_accessed=int(micros * 1e6), transcendentals=0
    )


def nt_dot(a, b):
    return lax.dot_general(a, b, (((1,), (1,)), ((), ())), preferred_element_type=F32)


def tn_dot(a, b):
    return lax.dot_general(a, b, (((0,), (0,)), ((), ())), preferred_element_type=F32)


def nn_dot(a, b):
    return lax.dot_general(a, b, (((1,), (0,)), ((), ())), preferred_element_type=F32)


def window_sets(cols, per):
    units = [[0, 4, 20, 24]]
    units += [[j, 20 + j] for j in (1, 2, 3)] + [[5 * i, 5 * i + 4] for i in (1, 2, 3)]
    units += [[5 * i + j] for i in (1, 2, 3) for j in (1, 2, 3)]
    sizes = [484] + [308] * 6 + [196] * 9
    sets = [[] for _ in range(cols)]
    loads = [0] * cols
    for unit, size in zip(units, sizes):
        open_sets = [d for d in range(cols) if len(sets[d]) + len(unit) <= per]
        best = min(open_sets, key=lambda d: loads[d])
        sets[best] += unit
        loads[best] += size
    capacity = -(-(max(loads) + TAIL) // 64) * 64
    return [own + [WINDOWS] * (per - len(own)) for own in sets], capacity


def plan_kernel(cols, per, ids, offsets, info):
    top, left = offsets[0, 0], offsets[0, 1]
    me = lax.axis_index("col").astype(jnp.int32)
    info[0] = me
    info[1] = top
    info[2] = left
    info[3] = lax.axis_index("row").astype(jnp.int32)

    def each_set(d, carry):
        def each_window(i, base):
            at = d * per + i
            win_row, win_col = ids[at] // GRID, ids[at] % GRID
            row_low = jnp.maximum(0, top - WIN * win_row)
            height = jnp.maximum(jnp.minimum(WIN, SIDE + top - WIN * win_row) - row_low, 0)
            col_low = jnp.maximum(0, left - WIN * win_col)
            width = jnp.maximum(jnp.minimum(WIN, SIDE + left - WIN * win_col) - col_low, 0)
            first = HEAD + at * FIELDS
            info[first] = base
            info[first + 1] = row_low
            info[first + 2] = height
            info[first + 3] = col_low
            info[first + 4] = width
            info[first + 5] = jnp.minimum(win_row, GRID - 1)
            info[first + 6] = win_col
            return base + height * width

        count = lax.fori_loop(0, per, each_window, jnp.int32(0))

        @pl.when(d == me)
        def _():
            info[4] = count

        return carry

    lax.fori_loop(0, cols, each_set, jnp.int32(0))


def plan(sets, offsets):
    cols, per = len(sets), len(sets[0])
    smem = pl.BlockSpec(memory_space=pltpu.SMEM)
    return pl.pallas_call(
        partial(plan_kernel, cols, per),
        out_shape=jax.ShapeDtypeStruct((HEAD + cols * per * FIELDS,), jnp.int32),
        in_specs=[smem, smem],
        out_specs=smem,
        cost_estimate=cost(2),
        name="plan",
    )(jnp.asarray(np.array(sets, np.int32).reshape(-1)), offsets)


def window_at(info, index):
    at = HEAD + index * FIELDS
    return [info[at + f] for f in range(FIELDS)]


def target_of(field, left, row, token_col):
    base, row_low, height, col_low, width, _, win_col = field
    col = token_col + (left - WIN * win_col)
    inside = (row >= row_low) & (row < row_low + height) & (col >= col_low) & (col < col_low + width)
    return jnp.where(inside, base + (row - row_low) * width + (col - col_low), -(1 << 20))


def as_pick(mask):
    return mask.astype(F32).astype(BF)


def spread_kernel(per, info, x_ref, out, padded, total):
    top, left = info[1], info[2]
    cols, rows, width = out.shape
    padded[: MARGIN * SIDE, :] = jnp.zeros((MARGIN * SIDE, width), BF)
    padded[(MARGIN + SIDE) * SIDE :, :] = jnp.zeros(((PADROWS - MARGIN - SIDE) * SIDE, width), BF)
    padded[MARGIN * SIDE : (MARGIN + SIDE) * SIDE, :] = x_ref[...]
    token = iota((1, 256), 1)
    row, col = token // SIDE, token % SIDE
    line = iota((64, 256), 0)
    for d in range(cols):
        total[...] = jnp.zeros_like(total)

        def step(i, carry):
            field = window_at(info, d * per + i)
            base, row_low, height, _, across, win_row, _ = field
            for g in range(4):
                start = base + jnp.clip(4 * g - row_low, 0, height) * across
                start = pl.multiple_of(start // 8 * 8, 8)
                pick = as_pick(line == target_of(field, left, row + 4 * g, col) - start)
                first = pl.multiple_of((WIN * win_row + 4 * g - top + MARGIN) * SIDE, SIDE)
                found = nn_dot(pick, padded[pl.ds(first, 256), :])
                total[pl.ds(start, 8), :] += found[:8]
                total[pl.ds(pl.multiple_of(start + 8, 8), 56), :] = found[8:]
            return carry

        lax.fori_loop(0, per, step, 0)
        out[d] = total[:rows].astype(BF)


def spread(x, info, cols, per, rows):
    width = x.shape[1]
    return pl.pallas_call(
        partial(spread_kernel, per),
        out_shape=jax.ShapeDtypeStruct((cols, rows, width), BF),
        grid_spec=pltpu.PrefetchScalarGridSpec(
            num_scalar_prefetch=1,
            grid=(1,),
            in_specs=[pl.BlockSpec((PIX, width), lambda i, s: (0, 0))],
            out_specs=pl.BlockSpec((cols, rows, width), lambda i, s: (0, 0, 0)),
            scratch_shapes=[
                pltpu.VMEM((PADROWS * SIDE, width), BF),
                pltpu.VMEM((rows + 64, width), F32),
            ],
        ),
        compiler_params=params(),
        cost_estimate=cost(7),
        name="spread",
    )(info, x)


def collect_kernel(places, per, info, pieces, out, padded):
    top, left = info[1], info[2]
    _, rows, _ = pieces.shape
    token = iota((1, 256), 1)
    row, col = token // SIDE, token % SIDE
    line = iota((80, 256), 0)
    for win_row in range(GRID):

        def step(g, carry):
            picks, slabs = [], []
            for win_col in range(GRID):
                d, i = places[win_row * GRID + win_col]
                field = window_at(info, d * per + i)
                base, row_low, height, _, across, _, _ = field
                start = base + jnp.clip(4 * g - row_low, 0, height) * across
                start = pl.multiple_of(jnp.minimum(start // 16 * 16, rows - 80), 16)
                picks.append(as_pick(line == target_of(field, left, row + 4 * g, col) - start))
                slabs.append(pieces[d, pl.ds(start, 80), :])
            found = tn_dot(jnp.concatenate(picks, axis=0), jnp.concatenate(slabs, axis=0))
            first = pl.multiple_of((WIN * win_row + 4 * g - top + MARGIN) * SIDE, SIDE)
            padded[pl.ds(first, 256), :] = found.astype(BF)
            return carry

        lax.fori_loop(0, 4, step, 0)
    out[...] = padded[MARGIN * SIDE : (MARGIN + SIDE) * SIDE, :].astype(out.dtype)


def collect(pieces, sets, info, dtype):
    cols, rows, width = pieces.shape
    per = len(sets[0])
    places = {w: (d, i) for d, own in enumerate(sets) for i, w in enumerate(own)}
    return pl.pallas_call(
        partial(collect_kernel, places, per),
        out_shape=jax.ShapeDtypeStruct((PIX, width), dtype),
        grid_spec=pltpu.PrefetchScalarGridSpec(
            num_scalar_prefetch=1,
            grid=(1,),
            in_specs=[pl.BlockSpec((cols, rows, width), lambda i, s: (0, 0, 0))],
            out_specs=pl.BlockSpec((PIX, width), lambda i, s: (0, 0)),
            scratch_shapes=[pltpu.VMEM((PADROWS * SIDE, width), BF)],
        ),
        compiler_params=params(),
        cost_estimate=cost(8),
        name="collect",
    )(info, pieces)


def chunk_place(col, part, width, info, parts):
    return (col * (width // 128) + part) ^ (info[3] // parts)


def swap_halves(values, info, parts):
    if parts == 1:
        return values
    return jnp.where(info[3] % 2 == 1, pltpu.roll(values.astype(F32), 64, 1), values.astype(F32))


def place_features(pieces, info, parts, whole):
    cols, _, width = pieces.shape
    for d in range(cols):
        for c in range(width // 128):
            at = pl.multiple_of(chunk_place(d, c, width, info, parts) * 128, 128)
            values = swap_halves(pieces[d, :, c * 128 : (c + 1) * 128], info, parts)
            whole[:, pl.ds(at, 128)] = values.astype(whole.dtype)


def take_features(whole, pieces, info, parts):
    cols, _, width = pieces.shape
    for d in range(cols):
        for c in range(width // 128):
            at = pl.multiple_of(chunk_place(d, c, width, info, parts) * 128, 128)
            values = swap_halves(whole[:, pl.ds(at, 128)], info, parts)
            pieces[d, :, c * 128 : (c + 1) * 128] = values.astype(BF)


def eight(values):
    total = values[:8]
    for r in range(8, values.shape[0], 8):
        total = total + values[r : r + 8]
    return total


def row_places(nr, flip):
    order = outer_bits(nr)
    order = order[::-1] if flip else order
    held = [0]
    for bit in order[:-1]:
        held = held + [place | bit for place in held]
    groups = [held, [place | order[-1] for place in held]]
    groups = groups + [[place | 1 for place in group] for group in groups]
    where = {place: (g, i) for g, group in enumerate(groups) for i, place in enumerate(group)}
    return [where[place] for place in range(nr)]


def outer_bits(nr):
    return [1 << b for b in range(1, nr.bit_length() - 1)]


def load_rows(bufs, flip, scratch, nr, first=0, me=0):
    stride = D // nr
    for p, (g, i) in enumerate(row_places(nr, flip)):
        cols, size, n = bufs[g].shape[1], bufs[g].shape[-2], bufs[g].shape[-1]
        at = p * stride + first
        for k in range(cols):
            if len(bufs[g].shape) == 4:
                scratch[at : at + size, k * n : (k + 1) * n] = bufs[g][i, k]
                continue
            for part in range(3):
                lane = (3 * k + part) * n
                scratch[at : at + size, lane : lane + n] = bufs[g][i, me ^ k, part]


def const_spec(shape):
    zeros = (0,) * len(shape)
    return pl.BlockSpec(shape, lambda *a: zeros, pipeline_mode=pl.Buffered(1))


def norm_qkv_kernel(cols, nr, info, *refs):
    pieces = refs[0]
    bufs_a, bufs_b = refs[1:5], refs[5:9]
    gain, bias, bias_qkv, x_out, n_out, qkv_out, whole, weight = refs[9:]
    parts = max(1, 128 * nr // D)
    bw = D // nr

    @pl.when(pl.program_id(0) == 0)
    def _():
        load_rows(bufs_a, False, weight, nr, 0, info[0])
        load_rows(bufs_b, True, weight, nr, bw // 2, info[0])

    place_features(pieces, info, parts, whole)
    values = whole[...]
    x_out[...] = values.astype(BF)
    mean = jnp.mean(values, axis=1, keepdims=True)
    centred = values - mean
    spread_sq = jnp.mean(centred * centred, axis=1, keepdims=True)
    normed = centred * lax.rsqrt(spread_sq + EPSILON) * gain[...] + bias[...]
    size = values.shape[0]
    real = iota((size, 1), 0) < info[4] - pl.program_id(0) * size
    normed = jnp.where(real, normed, 0.0).astype(BF)
    n_out[...] = normed
    qkv_out[...] = (nn_dot(normed, weight[...]) + bias_qkv[...]).astype(BF)


def norm_qkv(pieces, bufs_a, bufs_b, info, gain, bias, bias_qkv, cols, rows, nr):
    width = D // cols
    return pl.pallas_call(
        partial(norm_qkv_kernel, cols, nr),
        out_shape=[
            jax.ShapeDtypeStruct((rows, D), BF),
            jax.ShapeDtypeStruct((rows, D), BF),
            jax.ShapeDtypeStruct((rows, 3 * D), BF),
        ],
        grid_spec=pltpu.PrefetchScalarGridSpec(
            num_scalar_prefetch=1,
            grid=(BLOCKS,),
            in_specs=[pl.BlockSpec((cols, rows // BLOCKS, width), lambda i, s: (0, i, 0))]
            + [const_spec(bufs_a[0].shape)] * 8
            + [const_spec((1, D)), const_spec((1, D)), const_spec((1, 3 * D))],
            out_specs=[
                pl.BlockSpec((rows // BLOCKS, D), lambda i, s: (i, 0)),
                pl.BlockSpec((rows // BLOCKS, D), lambda i, s: (i, 0)),
                pl.BlockSpec((rows // BLOCKS, 3 * D), lambda i, s: (i, 0)),
            ],
            scratch_shapes=[pltpu.VMEM((rows // BLOCKS, D), F32), pltpu.VMEM((D, 3 * D), BF)],
        ),
        compiler_params=params(),
        cost_estimate=cost(19),
        name="norm_qkv",
    )(info, pieces, *bufs_a, *bufs_b, gain, bias, bias_qkv)


def join_kernel(cols, nr, info, *refs):
    place_features(refs[0], info, max(1, 128 * nr // D), refs[1])


def join(pieces, info, cols, rows, nr):
    width = pieces.shape[-1]
    return pl.pallas_call(
        partial(join_kernel, cols, nr),
        out_shape=jax.ShapeDtypeStruct((rows, D), BF),
        grid_spec=pltpu.PrefetchScalarGridSpec(
            num_scalar_prefetch=1,
            grid=(BLOCKS,),
            in_specs=[pl.BlockSpec((cols, rows // BLOCKS, width), lambda i, s: (0, i, 0))],
            out_specs=pl.BlockSpec((rows // BLOCKS, D), lambda i, s: (i, 0)),
        ),
        compiler_params=params(),
        cost_estimate=cost(7),
        name="join",
    )(info, pieces)


def proj_norm_kernel(nr, *refs):
    att, x, bias_p, gain, bias, resid_out, n_out, weight = refs[4:]

    @pl.when(pl.program_id(0) == 0)
    def _():
        load_rows(refs[:4], False, weight, nr)

    values = x[...].astype(F32) + nt_dot(att[...], weight[...]) + bias_p[...]
    resid_out[...] = values
    mean = jnp.mean(values, axis=1, keepdims=True)
    centred = values - mean
    spread_sq = jnp.mean(centred * centred, axis=1, keepdims=True)
    n_out[...] = (centred * lax.rsqrt(spread_sq + EPSILON) * gain[...] + bias[...]).astype(BF)


def proj_spec(buf, cols, whole):
    n = D // cols
    shape = (buf.shape[0], cols if whole else 1, buf.shape[2], n)
    last = buf.shape[3] // n - 1
    if whole:
        return pl.BlockSpec(shape, lambda *a: (0, 0, 0, last), pipeline_mode=pl.Buffered(1))
    return pl.BlockSpec(shape, lambda k: (0, k, 0, last))


def proj_norm(bufs, att, x, bias_p, gain, bias, cols, rows, nr):
    row_spec = pl.BlockSpec((rows // BLOCKS, D), lambda i: (i, 0))
    return pl.pallas_call(
        partial(proj_norm_kernel, nr),
        out_shape=[jax.ShapeDtypeStruct((rows, D), F32), jax.ShapeDtypeStruct((rows, D), BF)],
        grid=(BLOCKS,),
        in_specs=[proj_spec(bufs[0], cols, True)] * 4
        + [row_spec, row_spec, const_spec((1, D)), const_spec((1, D)), const_spec((1, D))],
        out_specs=[row_spec, row_spec],
        scratch_shapes=[pltpu.VMEM((D, D), BF)],
        compiler_params=params(),
        cost_estimate=cost(11),
        name="proj_norm",
    )(*bufs, att, x, bias_p, gain, bias)


def gelu_and_slope(v):
    below = 0.5 + 0.5 * lax.erf(v * 0.7071067811865476)
    bell = jnp.exp(v * v * -0.5)
    return v * below, below + v * bell * 0.3989422804014327


def store_halves(grad, keep, send, nr, lanes=slice(None)):
    bw = D // nr
    for q in range(nr // 2):
        at = 2 * q * bw
        keep[q, 0, :, lanes] = grad[at : at + bw].astype(BF)
        send[q, 0, :, lanes] = grad[at + bw : at + 2 * bw].astype(BF)


def mlp_grads_kernel(nr, *refs):
    n2, g, bias, act, pre_grad, keep, send, bias_sum, w1, w2 = refs[8:]
    n = w1.shape[1]
    load_rows(refs[:4], False, w1, nr)
    load_rows(refs[4:8], True, w2, nr)
    total = None
    size = n2.shape[0] // BLOCKS
    for r in range(0, n2.shape[0], size):
        pre = nn_dot(n2[r : r + size], w1[...]) + bias[0]
        act_grad = nn_dot(g[r : r + size], w2[...])
        value, slope = gelu_and_slope(pre)
        act[r : r + size] = value.astype(BF)
        grad = act_grad * slope
        pre_grad[r : r + size] = grad.astype(BF)
        part = eight(grad)
        total = part if total is None else total + part
    bias_sum[0] = total
    store_halves(tn_dot(n2[...], pre_grad[...]), keep, send, nr, slice(0, n))
    store_halves(tn_dot(g[...], act[...]), keep, send, nr, slice(n, 2 * n))


def mlp_grads(bufs1, bufs2, n2, g, bias, cols, rows, nr):
    bw = D // nr
    n = bufs2[0].shape[-1]
    w_spec = pl.BlockSpec((nr // 4, 1, bw, n), lambda k: (0, k, 0, 0))
    row_spec = pl.BlockSpec((rows, n), lambda k: (0, k))
    half_spec = pl.BlockSpec((nr // 2, 1, bw, 2 * n), lambda k: (0, k, 0, 0))
    half = jax.ShapeDtypeStruct((nr // 2, cols, bw, 2 * n), BF)
    act = jax.ShapeDtypeStruct((rows, cols * n), BF)
    return pl.pallas_call(
        partial(mlp_grads_kernel, nr),
        out_shape=[act, act, half, half, jax.ShapeDtypeStruct((cols, 8, n), F32)],
        grid=(cols,),
        in_specs=[w_spec] * 8
        + [const_spec((rows, D)), const_spec((rows, D)), pl.BlockSpec((1, 1, n), lambda k: (k, 0, 0))],
        out_specs=[row_spec, row_spec, half_spec, half_spec]
        + [pl.BlockSpec((1, 8, n), lambda k: (k, 0, 0))],
        scratch_shapes=[pltpu.VMEM((D, n), BF)] * 2,
        compiler_params=params(),
        cost_estimate=cost(38),
        name="mlp_grads",
    )(*bufs1, *bufs2, n2, g, bias)


def norm_back(grad, values, gain):
    mean = jnp.mean(values, axis=1, keepdims=True)
    centred = values - mean
    spread_sq = jnp.mean(centred * centred, axis=1, keepdims=True)
    inv = lax.rsqrt(spread_sq + EPSILON)
    hat = centred * inv
    scaled = grad * gain
    first = jnp.mean(scaled, axis=1, keepdims=True)
    second = jnp.mean(scaled * hat, axis=1, keepdims=True)
    return (scaled - first - hat * second) * inv, hat


def block_out_kernel(cols, nr, info, *refs):
    act0, act1, resid, bias_2 = refs[8:12]
    pieces, weight, whole = refs[12:]

    @pl.when(pl.program_id(0) == 0)
    def _():
        load_rows(refs[:4], True, weight.at[0], nr)
        load_rows(refs[4:8], True, weight.at[1], nr)

    out = nt_dot(act0[...], weight[0]) + nt_dot(act1[...], weight[1])
    whole[...] = resid[...] + out + bias_2[...]
    take_features(whole, pieces, info, max(1, 128 * nr // D))


def block_rows(groups, acts, resid, bias_2, info, cols, rows, nr):
    width = D // cols
    wide = acts[0].shape[1]
    row_spec = pl.BlockSpec((rows // BLOCKS, D), lambda i, s: (i, 0))
    wide_spec = pl.BlockSpec((rows // BLOCKS, wide), lambda i, s: (i, 0))
    flat = [b for group in groups for b in group]
    return pl.pallas_call(
        partial(block_out_kernel, cols, nr),
        out_shape=[jax.ShapeDtypeStruct((cols, rows, width), BF)],
        grid_spec=pltpu.PrefetchScalarGridSpec(
            num_scalar_prefetch=1,
            grid=(BLOCKS,),
            in_specs=[const_spec(flat[-1].shape)] * 8
            + [wide_spec] * 2
            + [row_spec, const_spec((1, D))],
            out_specs=[pl.BlockSpec((cols, rows // BLOCKS, width), lambda i, s: (0, i, 0))],
            scratch_shapes=[pltpu.VMEM((2, D, wide), BF), pltpu.VMEM((rows // BLOCKS, D), F32)],
        ),
        compiler_params=params(),
        cost_estimate=cost(26),
        name="block_rows",
    )(info, *flat, *acts, resid, bias_2)[0]


def mlp_back_kernel(nr, *refs):
    grad0, grad1, resid, g, gain, resid_grad, proj_grad, sums, weight = refs[8:]

    @pl.when(pl.program_id(0) == 0)
    def _():
        load_rows(refs[:4], False, weight.at[0], nr)
        load_rows(refs[4:8], False, weight.at[1], nr)
        sums[...] = jnp.zeros_like(sums)

    grad = nt_dot(grad0[...], weight[0]) + nt_dot(grad1[...], weight[1])
    g_f = g[...].astype(F32)
    back, hat = norm_back(grad, resid[...], gain[...])
    total = g_f + back
    resid_grad[...] = total
    low = total.astype(BF)
    proj_grad[...] = low
    sums[0] += eight(low.astype(F32))
    sums[1] += eight(grad * hat)
    sums[2] += eight(grad)
    sums[3] += eight(g_f)


def mlp_back(groups, grads, resid, g, gain, cols, rows, nr):
    wide = grads[0].shape[1]
    row_spec = pl.BlockSpec((rows // BLOCKS, D), lambda i: (i, 0))
    wide_spec = pl.BlockSpec((rows // BLOCKS, wide), lambda i: (i, 0))
    flat = [b for group in groups for b in group]
    shape = flat[-1].shape
    return pl.pallas_call(
        partial(mlp_back_kernel, nr),
        out_shape=[
            jax.ShapeDtypeStruct((rows, D), F32),
            jax.ShapeDtypeStruct((rows, D), BF),
            jax.ShapeDtypeStruct((4, 8, D), F32),
        ],
        grid=(BLOCKS,),
        in_specs=[const_spec(shape)] * 8
        + [wide_spec] * 2
        + [row_spec, row_spec, const_spec((1, D))],
        out_specs=[row_spec, row_spec, pl.BlockSpec((4, 8, D), lambda i: (0, 0, 0))],
        scratch_shapes=[pltpu.VMEM((2, D, wide), BF)],
        compiler_params=params(),
        cost_estimate=cost(28),
        name="mlp_back",
    )(*flat, *grads, resid, g, gain)


def proj_back_kernel(nr, *refs):
    proj_grad, att, att_grad, keep, send, weight = refs[4:]
    load_rows(refs[:4], False, weight, nr)
    store_halves(tn_dot(proj_grad[...], att[...]), keep, send, nr)
    att_grad[...] = nn_dot(proj_grad[...], weight[...]).astype(BF)


def proj_back(bufs, proj_grad, att, cols, rows, nr):
    bw = D // nr
    n = D // cols
    half = jax.ShapeDtypeStruct((nr // 2, cols, bw, n), BF)
    half_spec = pl.BlockSpec((nr // 2, 1, bw, n), lambda k: (0, k, 0, 0))
    col_spec = pl.BlockSpec((rows, n), lambda k: (0, k))
    return pl.pallas_call(
        partial(proj_back_kernel, nr),
        out_shape=[jax.ShapeDtypeStruct((rows, D), BF), half, half],
        grid=(cols,),
        in_specs=[proj_spec(bufs[0], cols, False)] * 4 + [const_spec((rows, D)), col_spec],
        out_specs=[col_spec, half_spec, half_spec],
        scratch_shapes=[pltpu.VMEM((D, n), BF)],
        compiler_params=params(),
        cost_estimate=cost(11),
        name="proj_back",
    )(*bufs, proj_grad, att)


def qkv_grad_kernel(nr, n1, dqkv, keep, send):
    store_halves(tn_dot(n1[...], dqkv[...]), keep, send, nr)


def qkv_grad(n1, dqkv, cols, rows, nr):
    n = 3 * D // cols
    bw = D // nr
    half = jax.ShapeDtypeStruct((nr // 2, cols, bw, n), BF)
    return pl.pallas_call(
        partial(qkv_grad_kernel, nr),
        out_shape=[half] * 2,
        grid=(cols,),
        in_specs=[const_spec((rows, D)), pl.BlockSpec((rows, n), lambda k: (0, k))],
        out_specs=[pl.BlockSpec((nr // 2, 1, bw, n), lambda k: (0, k, 0, 0))] * 2,
        compiler_params=params(),
        cost_estimate=cost(14),
        name="qkv_grad",
    )(n1, dqkv)


def input_back_kernel(cols, nr, info, *refs):
    bufs_a, bufs_b = refs[:4], refs[4:8]
    rest = refs[8:]
    dqkv, x, resid_grad, gain = rest[:4]
    pieces, sums, whole, weight = rest[4:]
    bw = D // nr

    @pl.when(pl.program_id(0) == 0)
    def _():
        load_rows(bufs_a, False, weight, nr, 0, info[0])
        load_rows(bufs_b, True, weight, nr, bw // 2, info[0])
        sums[...] = jnp.zeros_like(sums)

    grad = nt_dot(dqkv[...], weight[...])
    back, hat = norm_back(grad, x[...].astype(F32), gain[...])
    whole[...] = resid_grad[...] + back
    sums[0] += eight(grad * hat)
    sums[1] += eight(grad)

    @pl.when(pl.program_id(0) == BLOCKS - 1)
    def _():
        lines = []
        for v in range(2):
            left = jnp.sum(sums[v], axis=0, keepdims=True)
            for _ in range(3):
                lines.append(left.astype(BF).astype(F32))
                left = left - lines[-1]
        lines.append(jnp.zeros((2, D), F32))
        whole[whole.shape[0] - TAIL : whole.shape[0] - TAIL + 8, :] = jnp.concatenate(lines, axis=0)

    take_features(whole, pieces, info, max(1, 128 * nr // D))


def input_back(bufs_a, bufs_b, dqkv, x, resid_grad, gain, info, cols, rows, nr):
    width = D // cols
    row_spec = pl.BlockSpec((rows // BLOCKS, D), lambda i, s: (i, 0))
    piece = jax.ShapeDtypeStruct((cols, rows, width), BF)
    return pl.pallas_call(
        partial(input_back_kernel, cols, nr),
        out_shape=[piece],
        grid_spec=pltpu.PrefetchScalarGridSpec(
            num_scalar_prefetch=1,
            grid=(BLOCKS,),
            in_specs=[const_spec(bufs_a[0].shape)] * 8
            + [pl.BlockSpec((rows // BLOCKS, 3 * D), lambda i, s: (i, 0)), row_spec, row_spec]
            + [const_spec((1, D))],
            out_specs=[pl.BlockSpec((cols, rows // BLOCKS, width), lambda i, s: (0, i, 0))]
,
            scratch_shapes=[
                pltpu.VMEM((2, 8, D), F32),
                pltpu.VMEM((rows // BLOCKS, D), F32),
                pltpu.VMEM((D, 3 * D), BF),
            ],
        ),
        compiler_params=params(),
        cost_estimate=cost(25),
        name="input_back",
    )(info, *bufs_a, *bufs_b, dqkv, x, resid_grad, gain)[0]


def rel_constants():
    place = np.arange(SLOT)
    lanes = np.arange(128)
    group = lanes // 32
    row_shift = np.clip(WIN - 1 - place // WIN, 0, WIN - 1)
    col_shift = WIN - 1 - place % WIN
    shifts = np.where(group[None, :] % 2 == 0, row_shift[:, None], col_shift[:, None])
    onehot = np.zeros((2, KEYS, 128), np.float32)
    for head in range(2):
        for key in range(KEYS):
            if key >= REAL:
                onehot[head, key, 64 * head + 28] = -1e9
                continue
            for extra in (0, WIN):
                onehot[head, key, 64 * head + key // WIN + extra] = 1.0
                onehot[head, key, 64 * head + 32 + key % WIN + extra] = 1.0
    return shifts.astype(np.int32), onehot


def table_matrix(table_h, table_w):
    flipped = jnp.stack([table_h, table_w])[:, ::-1, :].astype(BF)
    block = jnp.pad(jnp.transpose(flipped, (2, 0, 1)), ((0, 0), (0, 0), (0, 5)))
    block = block.reshape(HD, HD)
    zero = jnp.zeros_like(block)
    return jnp.concatenate(
        [jnp.concatenate([block, zero], axis=1), jnp.concatenate([zero, block], axis=1)], axis=0
    )


def shift_left(values, shifts):
    for bit in (1, 2, 4, 8):
        values = jnp.where((shifts & bit) != 0, pltpu.roll(values, 128 - bit, 1), values)
    return values


def shift_right(values, shifts):
    for bit in (1, 2, 4, 8):
        values = jnp.where((shifts & bit) != 0, pltpu.roll(values, bit, 1), values)
    return values


def slot_target(field, start, rows, shape):
    base, row_low, height, col_low, width, _, _ = field
    slot = iota(shape, 0 if shape[0] > 1 else 1)
    row, col = slot // WIN, slot % WIN
    inside = (row >= row_low) & (row < row_low + height) & (col >= col_low) & (col < col_low + width)
    return jnp.where(inside, base - start + (row - row_low) * width + (col - col_low), rows)


def slots_from(field, start, source):
    rows = source.shape[0]
    line = iota((SLOT, SLAB + TAIL), 1)
    pick = as_pick(line == slot_target(field, start, SLAB + TAIL - 1, (SLOT, 1)))
    slab = jnp.concatenate([source[pl.ds(start, SLAB), :], source[rows - TAIL :, :]], axis=0)
    return pick, nn_dot(pick, slab)


def pack_of(field, start):
    line = iota((SLAB, SLOT), 0)
    return as_pick(line == slot_target(field, start, -1, (1, SLOT)))


def slab_start(field, rows):
    return pl.multiple_of(jnp.minimum(field[0] // 16 * 16, rows - SLAB), 16)


def attend_kernel(width, held, info, qkv, tables, shifts, onehot, *refs):
    att, exps, inv, keys, vals, slots, total = refs[held:]
    window = pl.program_id(1)
    first = (pl.program_id(0) == 0) & (window == 0)

    @pl.when(first)
    def _():
        for head in range(2 * (width // 128)):
            keys[head, :, :128] = jnp.zeros((KEYS, 128), BF)
            keys[head, :, 128:] = onehot[head % 2]
        for pair in range(width // 128):
            vals[pair, :, :128] = jnp.zeros((KEYS, 128), BF)
            vals[pair, :, 128:] = jnp.ones((KEYS, 128), BF)

    @pl.when(window == 0)
    def _():
        total[...] = jnp.zeros_like(total)

    field = window_at(info, info[0] * pl.num_programs(1) + window)
    start = slab_start(field, qkv.shape[0])
    slots[...] = slots_from(field, start, qkv)[1].astype(BF)

    lane = iota((SLOT, 128), 1)
    low = lane < HD
    inner = lane % 32
    pairs = width // 128
    queries = []
    for pair in range(pairs):
        at = pair * 128
        q2 = slots[:, at : at + 128]
        k2 = slots[:, width + at : width + at + 128]
        vals[pair, :SLOT, :128] = slots[:, 2 * width + at : 2 * width + at + 128]
        zero = jnp.zeros_like(k2)
        keys[2 * pair, :SLOT, :128] = jnp.where(low, k2, zero)
        keys[2 * pair + 1, :SLOT, :128] = jnp.where(low, zero, k2)
        rel = shift_left(nn_dot(q2, tables[...]), shifts[...])
        rel_hi = rel.astype(BF).astype(F32)
        rel_lo = pltpu.roll(rel - rel_hi, WIN, 1)
        rel = jnp.where(inner < WIN, rel_hi, jnp.where(inner < 2 * WIN, rel_lo, 1.0))
        queries.append(jnp.concatenate([q2 * BF(0.125), rel.astype(BF)], axis=1))
    scores = [nt_dot(queries[head // 2], keys[head]) for head in range(2 * pairs)]
    weights = []
    for head in range(2 * pairs):
        peak = jnp.max(scores[head], axis=1, keepdims=True)
        weights.append(jnp.exp(scores[head] - peak).astype(BF))
        exps[head] = weights[head]
    outs = [nn_dot(weights[head], vals[head // 2]) for head in range(2 * pairs)]
    parts = []
    for pair in range(pairs):
        at = pair * 128
        first, second = outs[2 * pair], outs[2 * pair + 1]
        scale = 1.0 / jnp.where(low, first[:, 128:], second[:, 128:])
        inv[:, at : at + 128] = scale
        parts.append((jnp.where(low, first[:, :128], second[:, :128]) * scale).astype(BF))
    pack = pack_of(field, start)
    total[pl.ds(start, SLAB), :] += nn_dot(pack, jnp.concatenate(parts, axis=1))

    @pl.when(window == pl.num_programs(1) - 1)
    def _():
        att[...] = total[...].astype(BF)


def attend(qkv, info, tables, shifts, onehot, base, count, held, cols, per):
    rows = qkv.shape[0]
    width = D // cols
    pairs = width // 128
    held = list(held)
    return pl.pallas_call(
        partial(attend_kernel, width, len(held)),
        out_shape=[
            jax.ShapeDtypeStruct((rows, D), BF),
            jax.ShapeDtypeStruct((D // HD, per * SLOT, KEYS), BF),
            jax.ShapeDtypeStruct((per * SLOT, D), F32),
        ],
        grid_spec=pltpu.PrefetchScalarGridSpec(
            num_scalar_prefetch=1,
            grid=(count, per),
            in_specs=[
                pl.BlockSpec((rows, 3 * width), lambda c, w, s: (0, c + base)),
                pl.BlockSpec((128, 128), lambda c, w, s: (0, 0)),
                pl.BlockSpec((SLOT, 128), lambda c, w, s: (0, 0)),
                pl.BlockSpec((2, KEYS, 128), lambda c, w, s: (0, 0, 0)),
            ]
            + [pl.BlockSpec(memory_space=pl.ANY)] * len(held),
            out_specs=[
                pl.BlockSpec((rows, width), lambda c, w, s: (0, c + base)),
                pl.BlockSpec((2 * pairs, SLOT, KEYS), lambda c, w, s: (c + base, w, 0)),
                pl.BlockSpec((SLOT, width), lambda c, w, s: (w, c + base)),
            ],
            scratch_shapes=[
                pltpu.VMEM((2 * pairs, KEYS, 256), BF),
                pltpu.VMEM((pairs, KEYS, 256), BF),
                pltpu.VMEM((SLOT, 3 * width), BF),
                pltpu.VMEM((rows, width), F32),
            ],
        ),
        input_output_aliases={5 + i: i for i in range(len(held))},
        compiler_params=params(2),
        cost_estimate=cost(58 * count // cols),
        name="attend",
    )(info, qkv, tables, shifts, onehot, *held)


def attend_back_kernel(
    width, held, info, qkv, exps, inv, att, att_grad, tables2, shifts, onehot, *refs
):
    out, table_sum, bias_sum, keys, vals, slots, att_slots, grad_slots, fresh, total = refs[held:]
    window = pl.program_id(1)
    first = (pl.program_id(0) == 0) & (window == 0)

    @pl.when(first)
    def _():
        for head in range(2 * (width // 128)):
            keys[head, :, :128] = jnp.zeros((KEYS, 128), BF)
            keys[head, :, 128:] = onehot[head % 2]
        vals[...] = jnp.zeros_like(vals)
        table_sum[...] = jnp.zeros_like(table_sum)

    @pl.when(window == 0)
    def _():
        bias_sum[...] = jnp.zeros_like(bias_sum)
        total[...] = jnp.zeros_like(total)

    field = window_at(info, info[0] * pl.num_programs(1) + window)
    start = slab_start(field, qkv.shape[0])
    pick, pulled = slots_from(field, start, qkv)
    slots[...] = pulled.astype(BF)
    att_slots[...] = nn_dot(pick[:, :SLAB], att[pl.ds(start, SLAB), :])
    grad_slots[...] = nn_dot(pick[:, :SLAB], att_grad[pl.ds(start, SLAB), :])

    lane = iota((SLOT, 128), 1)
    low = lane < HD
    inner = lane % 32
    pairs = width // 128
    q_all, grads, dots = [], [], []
    for pair in range(pairs):
        at = pair * 128
        q2 = slots[:, at : at + 128]
        k2 = slots[:, width + at : width + at + 128]
        v2 = slots[:, 2 * width + at : 2 * width + at + 128]
        zero = jnp.zeros_like(k2)
        keys[2 * pair, :SLOT, :128] = jnp.where(low, k2, zero)
        keys[2 * pair + 1, :SLOT, :128] = jnp.where(low, zero, k2)
        vals[2 * pair, :SLOT, :] = jnp.where(low, v2, zero)
        vals[2 * pair + 1, :SLOT, :] = jnp.where(low, zero, v2)
        grad = (grad_slots[:, at : at + 128] * inv[:, at : at + 128]).astype(BF)
        cross = grad.astype(F32) * att_slots[:, at : at + 128]
        dots.append(jnp.sum(jnp.where(low, cross, 0.0), axis=1, keepdims=True))
        dots.append(jnp.sum(jnp.where(low, 0.0, cross), axis=1, keepdims=True))
        q_all.append(q2)
        grads.append(grad)
    probs_grads = [nt_dot(grads[head // 2], vals[head]) for head in range(2 * pairs)]
    scores_grads = []
    for head in range(2 * pairs):
        weights = exps[head].astype(F32)
        scores_grads.append((weights * (probs_grads[head] - dots[head])).astype(BF))
    for pair in range(pairs):
        at = pair * 128
        q2, grad = q_all[pair], grads[pair]
        zero = jnp.zeros_like(grad)
        q_scaled = q2 * BF(0.125)
        grad_heads = (jnp.where(low, grad, zero), jnp.where(low, zero, grad))
        q_heads = (jnp.where(low, q_scaled, zero), jnp.where(low, zero, q_scaled))
        q_sum, k_sum, v_sum = None, None, None
        for head in range(2):
            which = 2 * pair + head
            q_part = nn_dot(scores_grads[which], keys[which])
            k_part = tn_dot(scores_grads[which], q_heads[head])
            v_part = tn_dot(exps[which], grad_heads[head])
            q_sum = q_part if q_sum is None else q_sum + q_part
            k_sum = k_part if k_sum is None else k_sum + k_part
            v_sum = v_part if v_sum is None else v_sum + v_part
        rel = shift_right(jnp.where(inner < WIN, q_sum[:, 128:], 0.0), shifts[...])
        rel_hi = rel.astype(BF)
        rel_lo = (rel - rel_hi.astype(F32)).astype(BF)
        rel2 = jnp.concatenate([rel_hi, rel_lo], axis=1)
        q_grad = q_sum[:, :128] * 0.125 + nt_dot(rel2, tables2[...])
        table_sum[...] += tn_dot(q2, rel2)
        v_grad = v_sum[:SLOT]
        fresh[:, at : at + 128] = q_grad.astype(BF)
        fresh[:, width + at : width + at + 128] = k_sum[:SLOT].astype(BF)
        fresh[:, 2 * width + at : 2 * width + at + 128] = v_grad.astype(BF)
        bias_sum[:, at : at + 128] += eight(q_grad)
        bias_sum[:, 2 * width + at : 2 * width + at + 128] += eight(v_grad)
    pack = pack_of(field, start)
    total[pl.ds(start, SLAB), :] += nn_dot(pack, fresh[...])

    @pl.when(window == pl.num_programs(1) - 1)
    def _():
        out[...] = total[...].astype(BF)


def attend_back(
    qkv, info, exps, inv, att, att_grad, tables, shifts, onehot, base, count, held, cols, per
):
    rows = qkv.shape[0]
    width = D // cols
    pairs = width // 128
    tables2 = jnp.concatenate([tables, tables], axis=1)
    row_spec = pl.BlockSpec((rows, width), lambda c, w, s: (0, c + base))
    qkv_spec = pl.BlockSpec((rows, 3 * width), lambda c, w, s: (0, c + base))
    held = list(held)
    return pl.pallas_call(
        partial(attend_back_kernel, width, len(held)),
        out_shape=[
            jax.ShapeDtypeStruct((rows, 3 * D), BF),
            jax.ShapeDtypeStruct((128, 256), F32),
            jax.ShapeDtypeStruct((8, count * 3 * width), F32),
        ],
        grid_spec=pltpu.PrefetchScalarGridSpec(
            num_scalar_prefetch=1,
            grid=(count, per),
            in_specs=[
                qkv_spec,
                pl.BlockSpec((2 * pairs, SLOT, KEYS), lambda c, w, s: (c + base, w, 0)),
                pl.BlockSpec((SLOT, width), lambda c, w, s: (w, c + base)),
                row_spec,
                row_spec,
                pl.BlockSpec((128, 256), lambda c, w, s: (0, 0)),
                pl.BlockSpec((SLOT, 128), lambda c, w, s: (0, 0)),
                pl.BlockSpec((2, KEYS, 128), lambda c, w, s: (0, 0, 0)),
            ]
            + [pl.BlockSpec(memory_space=pl.ANY)] * len(held),
            out_specs=[
                qkv_spec,
                pl.BlockSpec((128, 256), lambda c, w, s: (0, 0)),
                pl.BlockSpec((8, 3 * width), lambda c, w, s: (0, c)),
            ],
            scratch_shapes=[
                pltpu.VMEM((2 * pairs, KEYS, 256), BF),
                pltpu.VMEM((2 * pairs, KEYS, 128), BF),
                pltpu.VMEM((SLOT, 3 * width), BF),
                pltpu.VMEM((SLOT, width), F32),
                pltpu.VMEM((SLOT, width), F32),
                pltpu.VMEM((SLOT, 3 * width), BF),
                pltpu.VMEM((rows, 3 * width), F32),
            ],
        ),
        input_output_aliases={9 + i: i for i in range(len(held))},
        compiler_params=params(2),
        cost_estimate=cost(54 * count // cols),
        name="attend_back",
    )(info, qkv, exps, inv, att, att_grad, tables2, shifts, onehot, *held)


def split_table(total):
    total = (total[:, :128] + total[:, 128:]).reshape(2, HD, 2, 2, 32)
    both = total[0, :, 0] + total[1, :, 1]
    both = jnp.transpose(both, (1, 2, 0))[:, :27][:, ::-1]
    return both[0], both[1]


def col_exchange(values):
    return lax.all_to_all(values, "col", 0, 0, tiled=True)


def row_swap(values, bit, nr):
    return lax.ppermute(values, "row", [(i, i ^ bit) for i in range(nr)])


def after(values, *others):
    return lax.optimization_barrier((values, *others))[0]


def gather_cols(shard, cols):
    return col_exchange(jnp.broadcast_to(shard[None], (cols,) + shard.shape))


def gather_rows(stack, nr, flip):
    order = outer_bits(nr)
    order = order[::-1] if flip else order
    held = stack[None]
    for bit in order[:-1]:
        fresh = row_swap(held, bit, nr)
        gate = yield [fresh]
        held = jnp.concatenate([held, after(fresh, *(gate or ()))], axis=0)
    fresh = row_swap(held, order[-1], nr)
    gate = yield [held, fresh]
    bufs = [held, after(fresh, *(gate or ()))]
    bufs = bufs + [row_swap(buf, 1, nr) for buf in bufs]
    yield bufs


class Hops(list):
    def __init__(self, arrived, sent):
        super().__init__(arrived)
        self.sent = sent


def last_terms(stages):
    found = stages.send(None)
    while isinstance(found, Hops):
        found = stages.send(None)
    return found


def place_of(step, free, fixed, weights):
    total = sum(weights[b] for b in fixed)
    for i, bit in enumerate(free):
        total = total + ((step >> i) & 1) * weights[bit]
    return total


def add_kernel(counts, *refs):
    at = 0
    outs = refs[sum(counts) :]
    for count, out in zip(counts, outs):
        total = refs[at][...].astype(F32)
        for ref in refs[at + 1 : at + count]:
            total = total + ref[...].astype(F32)
        out[...] = total.astype(BF)
        at += count


def split_kernel(counts, axis, lane, *refs):
    out = refs[sum(counts)]
    for k in range(out.shape[0]):
        at = 0
        for h, count in enumerate(counts):
            total = refs[at][0, k].astype(F32)
            for ref in refs[at + 1 : at + count]:
                total = total + ref[0, k].astype(F32)
            at += count
            high, wide = total.shape
            row = h * high if axis == -2 else 0
            col = lane + (h * wide if axis == -1 else 0)
            out[k, row : row + high, col : col + wide] = total.astype(out.dtype)


def reduce_weight(keep, send, axis, cols, nr):
    arrived = row_swap(send, 1, nr)
    gate = yield [arrived]
    bits = outer_bits(nr)
    _, _, bw, n = keep.shape
    shape = [bw, n]
    halves = 1
    if axis is not None:
        halves = 2
        shape[axis] //= 2
    block = (1, cols, shape[0], shape[1])
    terms = [[(keep, bits, True), (arrived, bits, True)] for _ in range(halves)]
    left = [list(bits) for _ in range(halves)]

    def spec(term, h, free, fixed):
        _, own, whole = term
        weights = {b: 1 << i for i, b in enumerate(own)}

        def place(step):
            spot = [place_of(step, free, fixed, weights), 0, 0, 0]
            if whole and axis is not None:
                spot[axis] = h
            return tuple(spot)

        return pl.BlockSpec(block, place)

    for step in range(len(bits)):
        sizes, specs, arrays, taken = [], [], [], []
        for h in range(halves):
            bit = bits[step] if h else bits[-1 - step]
            left[h].remove(bit)
            taken.append(bit)
            sizes.append(len(terms[h]))
            for term in terms[h]:
                specs.append(spec(term, h, left[h], [bit]))
                arrays.append(term[0])
        count = 1 << len(left[0])
        arrays[0] = after(arrays[0], *(gate or ()))
        out_spec = pl.BlockSpec(block, lambda i: (i, 0, 0, 0))
        outs = pl.pallas_call(
            partial(add_kernel, sizes),
            out_shape=[jax.ShapeDtypeStruct((count,) + block[1:], BF)] * halves,
            grid=(count,),
            in_specs=specs,
            out_specs=[out_spec] * halves,
            compiler_params=params(),
            cost_estimate=cost(3),
            name="add_rows",
        )(*arrays)
        fresh = [row_swap(out, bit, nr) for out, bit in zip(outs, taken)]
        for h in range(halves):
            terms[h].append((fresh[h], list(left[h]), False))
        gate = yield Hops(fresh, outs)

    sizes = [len(t) for t in terms]
    specs = [spec(term, h, [], []) for h in range(halves) for term in terms[h]]
    arrays = [term[0] for h in range(halves) for term in terms[h]]
    yield sizes, axis, specs, arrays, (cols, bw, n)


def add_cols_kernel(groups, *refs):
    outs = refs[-1]
    at, lane = 0, 0
    for sizes, axis, n in groups:
        count = sum(sizes)
        split_kernel(sizes, axis, lane, *refs[at : at + count], outs)
        at += count
        lane += n


def finish_weights(parts, *gate):
    cols, bw, _ = parts[0][4]
    groups = [(sizes, axis, shape[2]) for sizes, axis, _, _, shape in parts]
    wide = sum(n for _, _, n in groups)
    arrays = [array for part in parts for array in part[3]]
    arrays[0] = after(arrays[0], *gate)
    outs = pl.pallas_call(
        partial(add_cols_kernel, groups),
        out_shape=jax.ShapeDtypeStruct((cols, bw, wide), BF),
        grid=(1,),
        in_specs=[sp for part in parts for sp in part[2]],
        out_specs=pl.BlockSpec((cols, bw, wide), lambda i: (0, 0, 0)),
        compiler_params=params(),
        cost_estimate=cost(3),
        name="add_cols",
    )(*arrays)
    return outs, col_exchange(outs)


def last_sum(arrived, sizes, *gate):
    total = jnp.sum(after(arrived, *gate).astype(F32), axis=0)
    found, lane = [], 0
    for n in sizes:
        found.append(total[:, lane : lane + n])
        lane += n
    return found


def sum_cols(by_place, whole, me, cols):
    size = by_place.shape[1]
    if whole is not None:
        whole = jnp.broadcast_to(whole, (cols,) + whole.shape)
        by_place = jnp.concatenate([by_place, whole], axis=1)
    arrived = [lax.dynamic_index_in_dim(by_place, me, 0, keepdims=False)]
    for k in range(1, cols):
        sent = lax.dynamic_index_in_dim(by_place, me ^ k, 0, keepdims=False)
        arrived.append(lax.ppermute(sent, "col", [(i, i ^ k) for i in range(cols)]))
    gate = yield arrived[1:]
    arrived = list(lax.optimization_barrier((*arrived, *(gate or ())))[:cols])
    order = me ^ jnp.arange(cols, dtype=jnp.int32)
    total = jnp.sum(pick_rows(jnp.stack(arrived), order), axis=0)
    yield total[:size], total[size:]


def sum_rows(total, nr):
    bit = 1
    while bit < nr:
        total = total + row_swap(total, bit, nr)
        yield total
        bit *= 2


def pick_rows(values, order):
    rows = jnp.arange(values.shape[0], dtype=jnp.int32)
    chosen = (order[:, None] == rows[None, :]).reshape(order.shape + rows.shape + (1,) * (values.ndim - 1))
    return jnp.sum(jnp.where(chosen, values[None], 0.0), axis=1)


def body(
    cols,
    nr,
    tokens_in,
    pad_offsets,
    norm1_gain,
    norm1_bias,
    qkv_weight,
    qv_bias,
    table_height,
    table_width,
    proj_weight,
    proj_bias,
    norm2_gain,
    norm2_bias,
    fc1_weight,
    fc1_bias,
    fc2_weight,
    fc2_bias,
    out_grad,
):
    width = D // cols
    bw = D // nr
    per = -(-WINDOWS // cols)
    me = lax.axis_index("col").astype(jnp.int32)
    my_row = lax.axis_index("row").astype(jnp.int32)
    sets, rows = window_sets(cols, per)
    info = plan(sets, pad_offsets)
    row_order = my_row ^ jnp.arange(nr, dtype=jnp.int32)

    hidden = fc1_weight.shape[1]
    half = hidden // 2
    fc2_t = fc2_weight.T
    qkv_own = jnp.transpose(qkv_weight, (1, 0, 2))
    qkv_stack = jnp.stack(
        [qkv_own]
        + [lax.ppermute(qkv_own, "col", [(i, i ^ k) for i in range(cols)]) for k in range(1, cols)]
    )
    x_sent = spread(tokens_in, info, cols, per, rows)
    x_pieces = col_exchange(x_sent)
    qkv_stack = after(qkv_stack, x_sent)
    hop_a = gather_rows(qkv_stack[:, :, : bw // 2], nr, False)
    hop_b = gather_rows(qkv_stack[:, :, bw // 2 :], nr, True)
    first_a, first_b = next(hop_a), next(hop_b)
    g_sent = spread(after(out_grad, *first_a, *first_b), info, cols, per, rows)
    for _ in outer_bits(nr)[1:]:
        first_a, first_b = hop_a.send(None), hop_b.send(None)
    qkv_a, qkv_b = hop_a.send((g_sent,)), hop_b.send((g_sent,))
    small_args = (norm1_gain, proj_bias, fc2_bias, qv_bias, fc1_bias)
    norm1_gain, proj_bias, fc2_bias, qv_bias, fc1_bias = lax.optimization_barrier(
        (*small_args, *qkv_a, *qkv_b)
    )[:5]
    vec = jnp.concatenate(
        [
            norm1_gain,
            norm1_bias,
            norm2_gain,
            norm2_bias,
            proj_bias.astype(F32),
            fc2_bias.astype(F32),
            qv_bias[0].astype(F32),
            qv_bias[1].astype(F32),
            fc1_bias.astype(F32),
        ]
    )
    vecs = [vec] + [lax.ppermute(vec, "col", [(i, i ^ k) for i in range(cols)]) for k in range(1, cols)]
    vecs = pick_rows(jnp.stack(vecs), me ^ jnp.arange(cols, dtype=jnp.int32))
    wide0 = jnp.concatenate([fc1_weight[:, :half], proj_weight.T, fc2_t[:, :half]], axis=1)
    wide1 = jnp.concatenate([fc1_weight[:, half:], fc2_t[:, half:]], axis=1)
    stack0 = gather_cols(after(wide0, x_pieces, *qkv_a, *qkv_b), cols)
    first = half + width
    features = vecs[:, : 6 * width].reshape(cols, 6, width // bw, bw)
    features = features.transpose(0, 2, 1, 3).reshape(nr, 6, bw)
    features = pick_rows(features, row_order).transpose(1, 0, 2).reshape(6, 1, D)
    gain1, bias1, gain2, bias2, bias_p, bias_2 = [features[i] for i in range(6)]
    q_bias = vecs[:, 6 * width : 7 * width]
    v_bias = vecs[:, 7 * width : 8 * width]
    bias_qkv = jnp.stack([q_bias, jnp.zeros_like(q_bias), v_bias], axis=1).reshape(1, 3 * D)
    bias_h = vecs[:, 8 * width :]

    x_full, n1, qkv = norm_qkv(
        after(x_pieces, g_sent), qkv_a, qkv_b, info, gain1, bias1, bias_qkv, cols, rows, nr
    )
    shifts_np, onehot_np = rel_constants()
    shifts = jnp.asarray(shifts_np)
    onehot = jnp.asarray(onehot_np, BF)
    tables = table_matrix(table_height, table_width)
    stack1 = gather_cols(after(wide1, stack0), cols)
    held = ()
    arrived = []
    bits = outer_bits(nr)
    for part, base in enumerate(range(0, cols, cols // SPLITS)):
        held = attend(
            after(qkv, *arrived),
            info,
            tables,
            shifts,
            onehot,
            base,
            cols // SPLITS,
            held,
            cols,
            per,
        )
        att = held[0]
        arrived = []
        if part == 0:
            stack0 = after(stack0, att)
            hops0 = [
                gather_rows(stack0[:, :, :first], nr, False),
                gather_rows(stack0[:, :, first:], nr, True),
            ]
            bufs0 = [next(hop) for hop in hops0]
        if part == 1:
            stack1 = after(stack1, att)
            g_pieces = col_exchange(after(g_sent, stack1))
            bufs0 = [hop.send((att, *bufs0[0], *bufs0[1])) for hop in hops0]
            arrived = [stack1]
        if part == 3:
            for _ in range(len(bits) - 2):
                bufs0 = [hop.send(None) for hop in hops0]
            bufs0 = [hop.send((att, *bufs0[0], *bufs0[1])) for hop in hops0]
            stack1 = after(stack1, att)
            hops1 = [
                gather_rows(stack1[:, :, :half], nr, False),
                gather_rows(stack1[:, :, half:], nr, True),
            ]
            bufs1 = [next(hop) for hop in hops1]
    att, exps, inv = held
    resid, n2 = proj_norm(bufs0[0], att, x_full, bias_p, gain2, bias2, cols, rows, nr)
    bufs1 = [hop.send((n2, *bufs1[0], *bufs1[1])) for hop in hops1]
    g_full = join(g_pieces, info, cols, rows, nr)
    fc1_bufs, fc2_bufs = [bufs0[0]], [bufs0[1]]

    acts, grads, sends, hidden_sums = [], [], [], []
    for c in range(2):
        if c == 1:
            for _ in range(len(bits) - 2):
                bufs1 = [hop.send(None) for hop in hops1]
            bufs1 = [hop.send((acts[0], *bufs1[0], *bufs1[1])) for hop in hops1]
            fc1_bufs.append(bufs1[0])
            fc2_bufs.append(bufs1[1])
        act, grad, keep, send, bias_sum = mlp_grads(
            fc1_bufs[c],
            fc2_bufs[c],
            n2,
            g_full,
            bias_h[:, None, c * half : (c + 1) * half],
            cols,
            rows,
            nr,
        )
        acts.append(act)
        grads.append(grad)
        hidden_sums.append(jnp.sum(bias_sum, axis=1))
        sends.append(reduce_weight(keep, send, -1, cols, nr))
    core0, core1 = [next(send) for send in sends]
    rows0 = sends[0].send((*core0, acts[1]))
    block_sent = block_rows(
        fc2_bufs, acts, after(resid, *core1), bias_2, info, cols, rows, nr
    )
    block_pieces = col_exchange(block_sent)
    rows0 = sends[0].send((*rows0, block_sent))
    rows1 = sends[1].send((block_sent,))
    resid_grad, proj_grad, sums2 = mlp_back(
        fc1_bufs,
        grads,
        after(resid, block_sent),
        g_full,
        gain2,
        cols,
        rows,
        nr,
    )
    rows1 = sends[1].send((*rows1, proj_grad))
    att_grad, keep, send = proj_back(
        fc1_bufs[0], after(proj_grad, *rows0), att, cols, rows, nr
    )
    sends.append(reduce_weight(keep, send, None, cols, nr))
    core2 = next(sends[2])
    ratio = width // bw
    places = jnp.arange(cols * ratio, dtype=jnp.int32) ^ my_row

    def by_col(sums):
        count = sums.shape[0]
        blocks = jnp.sum(sums, axis=1).reshape(count, nr, bw).transpose(1, 0, 2)
        picked = pick_rows(blocks, places).reshape(cols, ratio, count, bw)
        return picked.transpose(0, 2, 1, 3).reshape(cols, count * width)

    held, table_sums, bias_sums = (), [], []
    for part, base in enumerate(range(0, cols, cols // SPLITS)):
        arrived = []
        if part == 1:
            done0, arrived0 = finish_weights([last_terms(sends[0])], dqkv, block_pieces)
            rows2 = sends[2].send((*core2, dqkv))
            arrived = [block_pieces, *rows1, done0]
        if part == 2:
            rows2 = sends[2].send((*rows2, dqkv))
        if part == 3:
            arrived = [arrived0]
            done1, arrived1 = finish_weights(
                [last_terms(sends[1]), last_terms(sends[2])], dqkv, arrived0, *rows2
            )
            arrived = [arrived0, done1]
        dqkv, table_sum, bias_sum = attend_back(
            after(qkv, *arrived),
            info,
            exps,
            inv,
            att,
            att_grad,
            tables,
            shifts,
            onehot,
            base,
            cols // SPLITS,
            held,
            cols,
            per,
        )
        held = (dqkv,)
        table_sums.append(table_sum)
        bias_sums.append(bias_sum)
    table_sum = sum(table_sums[1:], table_sums[0])
    bias_sum = jnp.concatenate(bias_sums, axis=1)
    bias_cols = jnp.sum(bias_sum, axis=0).reshape(cols, 3, width)
    table_h_grad, table_w_grad = split_table(table_sum)
    table_flat = jnp.concatenate([table_h_grad.reshape(-1), table_w_grad.reshape(-1)])
    small = jnp.concatenate(
        [by_col(sums2), bias_cols[:, 0], bias_cols[:, 2]] + hidden_sums, axis=1
    )
    early = sum_cols(small, table_flat, me, cols)
    early_arrived = next(early)
    keep, send = qkv_grad(after(n1, dqkv), dqkv, cols, rows, nr)
    sends.append(reduce_weight(keep, send, -2, cols, nr))
    core3 = next(sends[3])
    block_out = collect(after(block_pieces, keep), sets, info, BF)
    rows3 = sends[3].send((*core3, block_out))
    small, table_flat = early.send((block_out,))
    in_sent = input_back(
        qkv_a,
        qkv_b,
        after(dqkv, block_out, arrived1, *early_arrived, *rows3.sent),
        x_full,
        resid_grad,
        gain1,
        info,
        cols,
        rows,
        nr,
    )
    in_pieces = col_exchange(in_sent)
    rows3 = sends[3].send((in_sent,))
    for _ in range(len(outer_bits(nr)) - 2):
        rows3 = sends[3].send(None)
    sizes = [2 * width, small.shape[0], table_flat.shape[0]]
    late = in_pieces[:, rows - TAIL : rows - TAIL + 6].astype(F32).reshape(cols, 2, 3, width)
    done3, arrived3 = finish_weights([sends[3].send(None)], in_pieces)
    late = jnp.sum(after(late, done3), axis=(0, 2)).reshape(-1)
    totals = list(sum_rows(jnp.concatenate([late, small, table_flat]), nr))
    total = totals[-1]
    late, small = total[: sizes[0]], total[sizes[0] : sizes[0] + sizes[1]]
    table_flat = total[sizes[0] + sizes[1] :].reshape(2, 27, HD)
    input_grad = collect(after(in_pieces, totals[-2]), sets, info, F32)
    (qkv_w_grad,) = last_sum(arrived3, [3 * width])
    fc_grads = last_sum(arrived0, [2 * half], done3)
    fc_grad, proj_w_grad = last_sum(arrived1, [2 * half, width], done3)
    fc_grads.append(fc_grad)

    def part(i):
        return small[i * width : (i + 1) * width]

    return (
        block_out,
        input_grad,
        late[:width],
        late[width:],
        qkv_w_grad.reshape(bw, 3, width),
        jnp.stack([part(4), part(5)]),
        table_flat[0],
        table_flat[1],
        proj_w_grad.T,
        part(0),
        part(1),
        part(2),
        jnp.concatenate([grad[:, :half] for grad in fc_grads], axis=1),
        small[6 * width :],
        jnp.concatenate([grad[:, half:] for grad in fc_grads], axis=1).T,
        part(3),
    )


def solution(mesh):
    placed = (
        P("row", "col"),
        P("row", None),
        P("col"),
        P("col"),
        P("row", None, "col"),
        P(None, "col"),
        P(),
        P(),
        P("col", "row"),
        P("col"),
        P("col"),
        P("col"),
        P("row", "col"),
        P("col"),
        P("col", "row"),
        P("col"),
        P("row", "col"),
    )
    return jax.shard_map(
        partial(body, mesh.shape["col"], mesh.shape["row"]),
        mesh=mesh,
        in_specs=placed,
        out_specs=(
            P("row", "col"),
            P("row", "col"),
            P("col"),
            P("col"),
            P("row", None, "col"),
            P(None, "col"),
            P(),
            P(),
            P("col", "row"),
            P("col"),
            P("col"),
            P("col"),
            P("row", "col"),
            P("col"),
            P("col", "row"),
            P("col"),
        ),
        check_vma=False,
    )
```

```python
from functools import partial

import jax
import jax.numpy as jnp
import numpy as np
from jax import lax
from jax.experimental import pallas as pl
from jax.experimental.pallas import tpu as pltpu
from jax.sharding import PartitionSpec as P

D = 1024
HD = 64
WIN = 14
SIDE = 64
GRID = 5
WINDOWS = 25
REAL = 196
SLOT = 200
KEYS = 256
PIX = 4096
EPSILON = 1e-06
MARGIN = 6
PADROWS = 84
BF = jnp.bfloat16
F32 = jnp.float32
SPLITS = 4
BLOCKS = 4
SLAB = 224
FIELDS = 7
HEAD = 5
TAIL = 16


def iota(shape, dim):
    return lax.broadcasted_iota(jnp.int32, shape, dim)


def params(n=1, mib=60):
    return pltpu.CompilerParams(
        dimension_semantics=("arbitrary",) * n, vmem_limit_bytes=mib * 1024 * 1024
    )


def cost(micros):
    return pl.CostEstimate(
        flops=int(micros * 1.1e9), bytes_accessed=int(micros * 1e6), transcendentals=0
    )


def nt_dot(a, b):
    return lax.dot_general(a, b, (((1,), (1,)), ((), ())), preferred_element_type=F32)


def tn_dot(a, b):
    return lax.dot_general(a, b, (((0,), (0,)), ((), ())), preferred_element_type=F32)


def nn_dot(a, b):
    return lax.dot_general(a, b, (((1,), (0,)), ((), ())), preferred_element_type=F32)


def window_sets(cols, per):
    units = [[0, 4, 20, 24]]
    units += [[j, 20 + j] for j in (1, 2, 3)] + [[5 * i, 5 * i + 4] for i in (1, 2, 3)]
    units += [[5 * i + j] for i in (1, 2, 3) for j in (1, 2, 3)]
    sizes = [484] + [308] * 6 + [196] * 9
    sets = [[] for _ in range(cols)]
    loads = [0] * cols
    for unit, size in zip(units, sizes):
        open_sets = [d for d in range(cols) if len(sets[d]) + len(unit) <= per]
        best = min(open_sets, key=lambda d: loads[d])
        sets[best] += unit
        loads[best] += size
    capacity = -(-(max(loads) + TAIL) // 64) * 64
    return [own + [WINDOWS] * (per - len(own)) for own in sets], capacity


def plan_kernel(cols, per, ids, offsets, info):
    top, left = offsets[0, 0], offsets[0, 1]
    me = lax.axis_index("col").astype(jnp.int32)
    info[0] = me
    info[1] = top
    info[2] = left
    info[3] = lax.axis_index("row").astype(jnp.int32)

    def each_set(d, carry):
        def each_window(i, base):
            at = d * per + i
            win_row, win_col = ids[at] // GRID, ids[at] % GRID
            row_low = jnp.maximum(0, top - WIN * win_row)
            height = jnp.maximum(jnp.minimum(WIN, SIDE + top - WIN * win_row) - row_low, 0)
            col_low = jnp.maximum(0, left - WIN * win_col)
            width = jnp.maximum(jnp.minimum(WIN, SIDE + left - WIN * win_col) - col_low, 0)
            first = HEAD + at * FIELDS
            info[first] = base
            info[first + 1] = row_low
            info[first + 2] = height
            info[first + 3] = col_low
            info[first + 4] = width
            info[first + 5] = jnp.minimum(win_row, GRID - 1)
            info[first + 6] = win_col
            return base + height * width

        count = lax.fori_loop(0, per, each_window, jnp.int32(0))

        @pl.when(d == me)
        def _():
            info[4] = count

        return carry

    lax.fori_loop(0, cols, each_set, jnp.int32(0))


def plan(sets, offsets):
    cols, per = len(sets), len(sets[0])
    smem = pl.BlockSpec(memory_space=pltpu.SMEM)
    return pl.pallas_call(
        partial(plan_kernel, cols, per),
        out_shape=jax.ShapeDtypeStruct((HEAD + cols * per * FIELDS,), jnp.int32),
        in_specs=[smem, smem],
        out_specs=smem,
        cost_estimate=cost(2),
        name="plan",
    )(jnp.asarray(np.array(sets, np.int32).reshape(-1)), offsets)


def window_at(info, index):
    at = HEAD + index * FIELDS
    return [info[at + f] for f in range(FIELDS)]


def target_of(field, left, row, token_col):
    base, row_low, height, col_low, width, _, win_col = field
    col = token_col + (left - WIN * win_col)
    inside = (row >= row_low) & (row < row_low + height) & (col >= col_low) & (col < col_low + width)
    return jnp.where(inside, base + (row - row_low) * width + (col - col_low), -(1 << 20))


def as_pick(mask):
    return mask.astype(F32).astype(BF)


def spread_kernel(per, info, x_ref, out, padded, total):
    top, left = info[1], info[2]
    cols, rows, width = out.shape
    padded[: MARGIN * SIDE, :] = jnp.zeros((MARGIN * SIDE, width), BF)
    padded[(MARGIN + SIDE) * SIDE :, :] = jnp.zeros(((PADROWS - MARGIN - SIDE) * SIDE, width), BF)
    padded[MARGIN * SIDE : (MARGIN + SIDE) * SIDE, :] = x_ref[...]
    token = iota((1, 256), 1)
    row, col = token // SIDE, token % SIDE
    line = iota((64, 256), 0)
    for d in range(cols):
        total[...] = jnp.zeros_like(total)

        def step(i, carry):
            field = window_at(info, d * per + i)
            base, row_low, height, _, across, win_row, _ = field
            for g in range(4):
                start = base + jnp.clip(4 * g - row_low, 0, height) * across
                start = pl.multiple_of(start // 8 * 8, 8)
                pick = as_pick(line == target_of(field, left, row + 4 * g, col) - start)
                first = pl.multiple_of((WIN * win_row + 4 * g - top + MARGIN) * SIDE, SIDE)
                found = nn_dot(pick, padded[pl.ds(first, 256), :])
                total[pl.ds(start, 8), :] += found[:8]
                total[pl.ds(pl.multiple_of(start + 8, 8), 56), :] = found[8:]
            return carry

        lax.fori_loop(0, per, step, 0)
        out[d] = total[:rows].astype(BF)


def spread(x, info, cols, per, rows):
    width = x.shape[1]
    return pl.pallas_call(
        partial(spread_kernel, per),
        out_shape=jax.ShapeDtypeStruct((cols, rows, width), BF),
        grid_spec=pltpu.PrefetchScalarGridSpec(
            num_scalar_prefetch=1,
            grid=(1,),
            in_specs=[pl.BlockSpec((PIX, width), lambda i, s: (0, 0))],
            out_specs=pl.BlockSpec((cols, rows, width), lambda i, s: (0, 0, 0)),
            scratch_shapes=[
                pltpu.VMEM((PADROWS * SIDE, width), BF),
                pltpu.VMEM((rows + 64, width), F32),
            ],
        ),
        compiler_params=params(),
        cost_estimate=cost(7),
        name="spread",
    )(info, x)


def collect_kernel(places, per, info, pieces, out, padded):
    top, left = info[1], info[2]
    _, rows, _ = pieces.shape
    token = iota((1, 256), 1)
    row, col = token // SIDE, token % SIDE
    line = iota((80, 256), 0)
    for win_row in range(GRID):

        def step(g, carry):
            picks, slabs = [], []
            for win_col in range(GRID):
                d, i = places[win_row * GRID + win_col]
                field = window_at(info, d * per + i)
                base, row_low, height, _, across, _, _ = field
                start = base + jnp.clip(4 * g - row_low, 0, height) * across
                start = pl.multiple_of(jnp.minimum(start // 16 * 16, rows - 80), 16)
                picks.append(as_pick(line == target_of(field, left, row + 4 * g, col) - start))
                slabs.append(pieces[d, pl.ds(start, 80), :])
            found = tn_dot(jnp.concatenate(picks, axis=0), jnp.concatenate(slabs, axis=0))
            first = pl.multiple_of((WIN * win_row + 4 * g - top + MARGIN) * SIDE, SIDE)
            padded[pl.ds(first, 256), :] = found.astype(BF)
            return carry

        lax.fori_loop(0, 4, step, 0)
    out[...] = padded[MARGIN * SIDE : (MARGIN + SIDE) * SIDE, :].astype(out.dtype)


def collect(pieces, sets, info, dtype):
    cols, rows, width = pieces.shape
    per = len(sets[0])
    places = {w: (d, i) for d, own in enumerate(sets) for i, w in enumerate(own)}
    return pl.pallas_call(
        partial(collect_kernel, places, per),
        out_shape=jax.ShapeDtypeStruct((PIX, width), dtype),
        grid_spec=pltpu.PrefetchScalarGridSpec(
            num_scalar_prefetch=1,
            grid=(1,),
            in_specs=[pl.BlockSpec((cols, rows, width), lambda i, s: (0, 0, 0))],
            out_specs=pl.BlockSpec((PIX, width), lambda i, s: (0, 0)),
            scratch_shapes=[pltpu.VMEM((PADROWS * SIDE, width), BF)],
        ),
        compiler_params=params(),
        cost_estimate=cost(8),
        name="collect",
    )(info, pieces)


def chunk_place(col, part, width, info, parts):
    return (col * (width // 128) + part) ^ (info[3] // parts)


def swap_halves(values, info, parts):
    if parts == 1:
        return values
    return jnp.where(info[3] % 2 == 1, pltpu.roll(values.astype(F32), 64, 1), values.astype(F32))


def place_features(pieces, info, parts, whole):
    cols, _, width = pieces.shape
    for d in range(cols):
        for c in range(width // 128):
            at = pl.multiple_of(chunk_place(d, c, width, info, parts) * 128, 128)
            values = swap_halves(pieces[d, :, c * 128 : (c + 1) * 128], info, parts)
            whole[:, pl.ds(at, 128)] = values.astype(whole.dtype)


def take_features(whole, pieces, info, parts):
    cols, _, width = pieces.shape
    for d in range(cols):
        for c in range(width // 128):
            at = pl.multiple_of(chunk_place(d, c, width, info, parts) * 128, 128)
            values = swap_halves(whole[:, pl.ds(at, 128)], info, parts)
            pieces[d, :, c * 128 : (c + 1) * 128] = values.astype(BF)


def eight(values):
    total = values[:8]
    for r in range(8, values.shape[0], 8):
        total = total + values[r : r + 8]
    return total


def row_places(nr, flip):
    order = outer_bits(nr)
    order = order[::-1] if flip else order
    held = [0]
    for bit in order[:-1]:
        held = held + [place | bit for place in held]
    groups = [held, [place | order[-1] for place in held]]
    groups = groups + [[place | 1 for place in group] for group in groups]
    where = {place: (g, i) for g, group in enumerate(groups) for i, place in enumerate(group)}
    return [where[place] for place in range(nr)]


def outer_bits(nr):
    return [1 << b for b in range(1, nr.bit_length() - 1)]


def load_rows(bufs, flip, scratch, nr, first=0, me=0):
    stride = D // nr
    for p, (g, i) in enumerate(row_places(nr, flip)):
        cols, size, n = bufs[g].shape[1], bufs[g].shape[-2], bufs[g].shape[-1]
        at = p * stride + first
        for k in range(cols):
            if len(bufs[g].shape) == 4:
                scratch[at : at + size, k * n : (k + 1) * n] = bufs[g][i, k]
                continue
            for part in range(3):
                lane = (3 * k + part) * n
                scratch[at : at + size, lane : lane + n] = bufs[g][i, me ^ k, part]


def const_spec(shape):
    zeros = (0,) * len(shape)
    return pl.BlockSpec(shape, lambda *a: zeros, pipeline_mode=pl.Buffered(1))


def norm_qkv_kernel(cols, nr, info, *refs):
    pieces = refs[0]
    bufs_a, bufs_b = refs[1:5], refs[5:9]
    gain, bias, bias_qkv, x_out, n_out, qkv_out, whole, weight = refs[9:]
    parts = max(1, 128 * nr // D)
    bw = D // nr

    @pl.when(pl.program_id(0) == 0)
    def _():
        load_rows(bufs_a, False, weight, nr, 0, info[0])
        load_rows(bufs_b, True, weight, nr, bw // 2, info[0])

    place_features(pieces, info, parts, whole)
    values = whole[...]
    x_out[...] = values.astype(BF)
    mean = jnp.mean(values, axis=1, keepdims=True)
    centred = values - mean
    spread_sq = jnp.mean(centred * centred, axis=1, keepdims=True)
    normed = centred * lax.rsqrt(spread_sq + EPSILON) * gain[...] + bias[...]
    size = values.shape[0]
    real = iota((size, 1), 0) < info[4] - pl.program_id(0) * size
    normed = jnp.where(real, normed, 0.0).astype(BF)
    n_out[...] = normed
    qkv_out[...] = (nn_dot(normed, weight[...]) + bias_qkv[...]).astype(BF)


def norm_qkv(pieces, bufs_a, bufs_b, info, gain, bias, bias_qkv, cols, rows, nr):
    width = D // cols
    return pl.pallas_call(
        partial(norm_qkv_kernel, cols, nr),
        out_shape=[
            jax.ShapeDtypeStruct((rows, D), BF),
            jax.ShapeDtypeStruct((rows, D), BF),
            jax.ShapeDtypeStruct((rows, 3 * D), BF),
        ],
        grid_spec=pltpu.PrefetchScalarGridSpec(
            num_scalar_prefetch=1,
            grid=(BLOCKS,),
            in_specs=[pl.BlockSpec((cols, rows // BLOCKS, width), lambda i, s: (0, i, 0))]
            + [const_spec(bufs_a[0].shape)] * 8
            + [const_spec((1, D)), const_spec((1, D)), const_spec((1, 3 * D))],
            out_specs=[
                pl.BlockSpec((rows // BLOCKS, D), lambda i, s: (i, 0)),
                pl.BlockSpec((rows // BLOCKS, D), lambda i, s: (i, 0)),
                pl.BlockSpec((rows // BLOCKS, 3 * D), lambda i, s: (i, 0)),
            ],
            scratch_shapes=[pltpu.VMEM((rows // BLOCKS, D), F32), pltpu.VMEM((D, 3 * D), BF)],
        ),
        compiler_params=params(),
        cost_estimate=cost(19),
        name="norm_qkv",
    )(info, pieces, *bufs_a, *bufs_b, gain, bias, bias_qkv)


def join_kernel(cols, nr, info, *refs):
    place_features(refs[0], info, max(1, 128 * nr // D), refs[1])


def join(pieces, info, cols, rows, nr):
    width = pieces.shape[-1]
    return pl.pallas_call(
        partial(join_kernel, cols, nr),
        out_shape=jax.ShapeDtypeStruct((rows, D), BF),
        grid_spec=pltpu.PrefetchScalarGridSpec(
            num_scalar_prefetch=1,
            grid=(BLOCKS,),
            in_specs=[pl.BlockSpec((cols, rows // BLOCKS, width), lambda i, s: (0, i, 0))],
            out_specs=pl.BlockSpec((rows // BLOCKS, D), lambda i, s: (i, 0)),
        ),
        compiler_params=params(),
        cost_estimate=cost(7),
        name="join",
    )(info, pieces)


def proj_norm_kernel(nr, *refs):
    att, x, bias_p, gain, bias, resid_out, n_out, weight = refs[4:]

    @pl.when(pl.program_id(0) == 0)
    def _():
        load_rows(refs[:4], False, weight, nr)

    values = x[...].astype(F32) + nt_dot(att[...], weight[...]) + bias_p[...]
    resid_out[...] = values
    mean = jnp.mean(values, axis=1, keepdims=True)
    centred = values - mean
    spread_sq = jnp.mean(centred * centred, axis=1, keepdims=True)
    n_out[...] = (centred * lax.rsqrt(spread_sq + EPSILON) * gain[...] + bias[...]).astype(BF)


def proj_spec(buf, cols, whole):
    n = D // cols
    shape = (buf.shape[0], cols if whole else 1, buf.shape[2], n)
    last = buf.shape[3] // n - 1
    if whole:
        return pl.BlockSpec(shape, lambda *a: (0, 0, 0, last), pipeline_mode=pl.Buffered(1))
    return pl.BlockSpec(shape, lambda k: (0, k, 0, last))


def proj_norm(bufs, att, x, bias_p, gain, bias, cols, rows, nr):
    row_spec = pl.BlockSpec((rows // BLOCKS, D), lambda i: (i, 0))
    return pl.pallas_call(
        partial(proj_norm_kernel, nr),
        out_shape=[jax.ShapeDtypeStruct((rows, D), F32), jax.ShapeDtypeStruct((rows, D), BF)],
        grid=(BLOCKS,),
        in_specs=[proj_spec(bufs[0], cols, True)] * 4
        + [row_spec, row_spec, const_spec((1, D)), const_spec((1, D)), const_spec((1, D))],
        out_specs=[row_spec, row_spec],
        scratch_shapes=[pltpu.VMEM((D, D), BF)],
        compiler_params=params(),
        cost_estimate=cost(11),
        name="proj_norm",
    )(*bufs, att, x, bias_p, gain, bias)


def gelu_and_slope(v):
    below = 0.5 + 0.5 * lax.erf(v * 0.7071067811865476)
    bell = jnp.exp(v * v * -0.5)
    return v * below, below + v * bell * 0.3989422804014327


def store_halves(grad, keep, send, nr, lanes=slice(None)):
    bw = D // nr
    for q in range(nr // 2):
        at = 2 * q * bw
        keep[q, 0, :, lanes] = grad[at : at + bw].astype(BF)
        send[q, 0, :, lanes] = grad[at + bw : at + 2 * bw].astype(BF)


def mlp_grads_kernel(nr, *refs):
    n2, g, bias, act, pre_grad, keep, send, bias_sum, w1, w2 = refs[8:]
    n = w1.shape[1]
    load_rows(refs[:4], False, w1, nr)
    load_rows(refs[4:8], True, w2, nr)
    total = None
    size = n2.shape[0] // BLOCKS
    for r in range(0, n2.shape[0], size):
        pre = nn_dot(n2[r : r + size], w1[...]) + bias[0]
        act_grad = nn_dot(g[r : r + size], w2[...])
        value, slope = gelu_and_slope(pre)
        act[r : r + size] = value.astype(BF)
        grad = act_grad * slope
        pre_grad[r : r + size] = grad.astype(BF)
        part = eight(grad)
        total = part if total is None else total + part
    bias_sum[0] = total
    store_halves(tn_dot(n2[...], pre_grad[...]), keep, send, nr, slice(0, n))
    store_halves(tn_dot(g[...], act[...]), keep, send, nr, slice(n, 2 * n))


def mlp_grads(bufs1, bufs2, n2, g, bias, cols, rows, nr):
    bw = D // nr
    n = bufs2[0].shape[-1]
    w_spec = pl.BlockSpec((nr // 4, 1, bw, n), lambda k: (0, k, 0, 0))
    row_spec = pl.BlockSpec((rows, n), lambda k: (0, k))
    half_spec = pl.BlockSpec((nr // 2, 1, bw, 2 * n), lambda k: (0, k, 0, 0))
    half = jax.ShapeDtypeStruct((nr // 2, cols, bw, 2 * n), BF)
    act = jax.ShapeDtypeStruct((rows, cols * n), BF)
    return pl.pallas_call(
        partial(mlp_grads_kernel, nr),
        out_shape=[act, act, half, half, jax.ShapeDtypeStruct((cols, 8, n), F32)],
        grid=(cols,),
        in_specs=[w_spec] * 8
        + [const_spec((rows, D)), const_spec((rows, D)), pl.BlockSpec((1, 1, n), lambda k: (k, 0, 0))],
        out_specs=[row_spec, row_spec, half_spec, half_spec]
        + [pl.BlockSpec((1, 8, n), lambda k: (k, 0, 0))],
        scratch_shapes=[pltpu.VMEM((D, n), BF)] * 2,
        compiler_params=params(),
        cost_estimate=cost(38),
        name="mlp_grads",
    )(*bufs1, *bufs2, n2, g, bias)


def norm_back(grad, values, gain):
    mean = jnp.mean(values, axis=1, keepdims=True)
    centred = values - mean
    spread_sq = jnp.mean(centred * centred, axis=1, keepdims=True)
    inv = lax.rsqrt(spread_sq + EPSILON)
    hat = centred * inv
    scaled = grad * gain
    first = jnp.mean(scaled, axis=1, keepdims=True)
    second = jnp.mean(scaled * hat, axis=1, keepdims=True)
    return (scaled - first - hat * second) * inv, hat


def block_out_kernel(cols, nr, info, *refs):
    act0, act1, resid, bias_2 = refs[8:12]
    pieces, weight, whole = refs[12:]

    @pl.when(pl.program_id(0) == 0)
    def _():
        load_rows(refs[:4], True, weight.at[0], nr)
        load_rows(refs[4:8], True, weight.at[1], nr)

    out = nt_dot(act0[...], weight[0]) + nt_dot(act1[...], weight[1])
    whole[...] = resid[...] + out + bias_2[...]
    take_features(whole, pieces, info, max(1, 128 * nr // D))


def block_rows(groups, acts, resid, bias_2, info, cols, rows, nr):
    width = D // cols
    wide = acts[0].shape[1]
    row_spec = pl.BlockSpec((rows // BLOCKS, D), lambda i, s: (i, 0))
    wide_spec = pl.BlockSpec((rows // BLOCKS, wide), lambda i, s: (i, 0))
    flat = [b for group in groups for b in group]
    return pl.pallas_call(
        partial(block_out_kernel, cols, nr),
        out_shape=[jax.ShapeDtypeStruct((cols, rows, width), BF)],
        grid_spec=pltpu.PrefetchScalarGridSpec(
            num_scalar_prefetch=1,
            grid=(BLOCKS,),
            in_specs=[const_spec(flat[-1].shape)] * 8
            + [wide_spec] * 2
            + [row_spec, const_spec((1, D))],
            out_specs=[pl.BlockSpec((cols, rows // BLOCKS, width), lambda i, s: (0, i, 0))],
            scratch_shapes=[pltpu.VMEM((2, D, wide), BF), pltpu.VMEM((rows // BLOCKS, D), F32)],
        ),
        compiler_params=params(),
        cost_estimate=cost(26),
        name="block_rows",
    )(info, *flat, *acts, resid, bias_2)[0]


def mlp_back_kernel(nr, *refs):
    grad0, grad1, resid, g, gain, resid_grad, proj_grad, sums, weight = refs[8:]

    @pl.when(pl.program_id(0) == 0)
    def _():
        load_rows(refs[:4], False, weight.at[0], nr)
        load_rows(refs[4:8], False, weight.at[1], nr)
        sums[...] = jnp.zeros_like(sums)

    grad = nt_dot(grad0[...], weight[0]) + nt_dot(grad1[...], weight[1])
    g_f = g[...].astype(F32)
    back, hat = norm_back(grad, resid[...], gain[...])
    total = g_f + back
    resid_grad[...] = total
    low = total.astype(BF)
    proj_grad[...] = low
    sums[0] += eight(low.astype(F32))
    sums[1] += eight(grad * hat)
    sums[2] += eight(grad)
    sums[3] += eight(g_f)


def mlp_back(groups, grads, resid, g, gain, cols, rows, nr):
    wide = grads[0].shape[1]
    row_spec = pl.BlockSpec((rows // BLOCKS, D), lambda i: (i, 0))
    wide_spec = pl.BlockSpec((rows // BLOCKS, wide), lambda i: (i, 0))
    flat = [b for group in groups for b in group]
    shape = flat[-1].shape
    return pl.pallas_call(
        partial(mlp_back_kernel, nr),
        out_shape=[
            jax.ShapeDtypeStruct((rows, D), F32),
            jax.ShapeDtypeStruct((rows, D), BF),
            jax.ShapeDtypeStruct((4, 8, D), F32),
        ],
        grid=(BLOCKS,),
        in_specs=[const_spec(shape)] * 8
        + [wide_spec] * 2
        + [row_spec, row_spec, const_spec((1, D))],
        out_specs=[row_spec, row_spec, pl.BlockSpec((4, 8, D), lambda i: (0, 0, 0))],
        scratch_shapes=[pltpu.VMEM((2, D, wide), BF)],
        compiler_params=params(),
        cost_estimate=cost(28),
        name="mlp_back",
    )(*flat, *grads, resid, g, gain)


def proj_back_kernel(nr, *refs):
    proj_grad, att, att_grad, keep, send, weight = refs[4:]
    load_rows(refs[:4], False, weight, nr)
    store_halves(tn_dot(proj_grad[...], att[...]), keep, send, nr)
    att_grad[...] = nn_dot(proj_grad[...], weight[...]).astype(BF)


def proj_back(bufs, proj_grad, att, cols, rows, nr):
    bw = D // nr
    n = D // cols
    half = jax.ShapeDtypeStruct((nr // 2, cols, bw, n), BF)
    half_spec = pl.BlockSpec((nr // 2, 1, bw, n), lambda k: (0, k, 0, 0))
    col_spec = pl.BlockSpec((rows, n), lambda k: (0, k))
    return pl.pallas_call(
        partial(proj_back_kernel, nr),
        out_shape=[jax.ShapeDtypeStruct((rows, D), BF), half, half],
        grid=(cols,),
        in_specs=[proj_spec(bufs[0], cols, False)] * 4 + [const_spec((rows, D)), col_spec],
        out_specs=[col_spec, half_spec, half_spec],
        scratch_shapes=[pltpu.VMEM((D, n), BF)],
        compiler_params=params(),
        cost_estimate=cost(11),
        name="proj_back",
    )(*bufs, proj_grad, att)


def qkv_grad_kernel(nr, n1, dqkv, keep, send):
    store_halves(tn_dot(n1[...], dqkv[...]), keep, send, nr)


def qkv_grad(n1, dqkv, cols, rows, nr):
    n = 3 * D // cols
    bw = D // nr
    half = jax.ShapeDtypeStruct((nr // 2, cols, bw, n), BF)
    return pl.pallas_call(
        partial(qkv_grad_kernel, nr),
        out_shape=[half] * 2,
        grid=(cols,),
        in_specs=[const_spec((rows, D)), pl.BlockSpec((rows, n), lambda k: (0, k))],
        out_specs=[pl.BlockSpec((nr // 2, 1, bw, n), lambda k: (0, k, 0, 0))] * 2,
        compiler_params=params(),
        cost_estimate=cost(14),
        name="qkv_grad",
    )(n1, dqkv)


def input_back_kernel(cols, nr, info, *refs):
    bufs_a, bufs_b = refs[:4], refs[4:8]
    rest = refs[8:]
    dqkv, x, resid_grad, gain = rest[:4]
    pieces, sums, whole, weight = rest[4:]
    bw = D // nr

    @pl.when(pl.program_id(0) == 0)
    def _():
        load_rows(bufs_a, False, weight, nr, 0, info[0])
        load_rows(bufs_b, True, weight, nr, bw // 2, info[0])
        sums[...] = jnp.zeros_like(sums)

    grad = nt_dot(dqkv[...], weight[...])
    back, hat = norm_back(grad, x[...].astype(F32), gain[...])
    whole[...] = resid_grad[...] + back
    sums[0] += eight(grad * hat)
    sums[1] += eight(grad)

    @pl.when(pl.program_id(0) == BLOCKS - 1)
    def _():
        lines = []
        for v in range(2):
            left = jnp.sum(sums[v], axis=0, keepdims=True)
            for _ in range(3):
                lines.append(left.astype(BF).astype(F32))
                left = left - lines[-1]
        lines.append(jnp.zeros((2, D), F32))
        whole[whole.shape[0] - TAIL : whole.shape[0] - TAIL + 8, :] = jnp.concatenate(lines, axis=0)

    take_features(whole, pieces, info, max(1, 128 * nr // D))


def input_back(bufs_a, bufs_b, dqkv, x, resid_grad, gain, info, cols, rows, nr):
    width = D // cols
    row_spec = pl.BlockSpec((rows // BLOCKS, D), lambda i, s: (i, 0))
    piece = jax.ShapeDtypeStruct((cols, rows, width), BF)
    return pl.pallas_call(
        partial(input_back_kernel, cols, nr),
        out_shape=[piece],
        grid_spec=pltpu.PrefetchScalarGridSpec(
            num_scalar_prefetch=1,
            grid=(BLOCKS,),
            in_specs=[const_spec(bufs_a[0].shape)] * 8
            + [pl.BlockSpec((rows // BLOCKS, 3 * D), lambda i, s: (i, 0)), row_spec, row_spec]
            + [const_spec((1, D))],
            out_specs=[pl.BlockSpec((cols, rows // BLOCKS, width), lambda i, s: (0, i, 0))]
,
            scratch_shapes=[
                pltpu.VMEM((2, 8, D), F32),
                pltpu.VMEM((rows // BLOCKS, D), F32),
                pltpu.VMEM((D, 3 * D), BF),
            ],
        ),
        compiler_params=params(),
        cost_estimate=cost(25),
        name="input_back",
    )(info, *bufs_a, *bufs_b, dqkv, x, resid_grad, gain)[0]


def rel_constants():
    place = np.arange(SLOT)
    lanes = np.arange(128)
    group = lanes // 32
    row_shift = np.clip(WIN - 1 - place // WIN, 0, WIN - 1)
    col_shift = WIN - 1 - place % WIN
    shifts = np.where(group[None, :] % 2 == 0, row_shift[:, None], col_shift[:, None])
    onehot = np.zeros((2, KEYS, 128), np.float32)
    for head in range(2):
        for key in range(KEYS):
            if key >= REAL:
                onehot[head, key, 64 * head + 28] = -1e9
                continue
            for extra in (0, WIN):
                onehot[head, key, 64 * head + key // WIN + extra] = 1.0
                onehot[head, key, 64 * head + 32 + key % WIN + extra] = 1.0
    return shifts.astype(np.int32), onehot


def table_matrix(table_h, table_w):
    flipped = jnp.stack([table_h, table_w])[:, ::-1, :].astype(BF)
    block = jnp.pad(jnp.transpose(flipped, (2, 0, 1)), ((0, 0), (0, 0), (0, 5)))
    block = block.reshape(HD, HD)
    zero = jnp.zeros_like(block)
    return jnp.concatenate(
        [jnp.concatenate([block, zero], axis=1), jnp.concatenate([zero, block], axis=1)], axis=0
    )


def shift_left(values, shifts):
    for bit in (1, 2, 4, 8):
        values = jnp.where((shifts & bit) != 0, pltpu.roll(values, 128 - bit, 1), values)
    return values


def shift_right(values, shifts):
    for bit in (1, 2, 4, 8):
        values = jnp.where((shifts & bit) != 0, pltpu.roll(values, bit, 1), values)
    return values


def slot_target(field, start, rows, shape):
    base, row_low, height, col_low, width, _, _ = field
    slot = iota(shape, 0 if shape[0] > 1 else 1)
    row, col = slot // WIN, slot % WIN
    inside = (row >= row_low) & (row < row_low + height) & (col >= col_low) & (col < col_low + width)
    return jnp.where(inside, base - start + (row - row_low) * width + (col - col_low), rows)


def slots_from(field, start, source):
    rows = source.shape[0]
    line = iota((SLOT, SLAB + TAIL), 1)
    pick = as_pick(line == slot_target(field, start, SLAB + TAIL - 1, (SLOT, 1)))
    slab = jnp.concatenate([source[pl.ds(start, SLAB), :], source[rows - TAIL :, :]], axis=0)
    return pick, nn_dot(pick, slab)


def pack_of(field, start):
    line = iota((SLAB, SLOT), 0)
    return as_pick(line == slot_target(field, start, -1, (1, SLOT)))


def slab_start(field, rows):
    return pl.multiple_of(jnp.minimum(field[0] // 16 * 16, rows - SLAB), 16)


def attend_kernel(width, held, info, qkv, tables, shifts, onehot, *refs):
    att, exps, inv, keys, vals, slots, total = refs[held:]
    window = pl.program_id(1)
    first = (pl.program_id(0) == 0) & (window == 0)

    @pl.when(first)
    def _():
        for head in range(2 * (width // 128)):
            keys[head, :, :128] = jnp.zeros((KEYS, 128), BF)
            keys[head, :, 128:] = onehot[head % 2]
        for pair in range(width // 128):
            vals[pair, :, :128] = jnp.zeros((KEYS, 128), BF)
            vals[pair, :, 128:] = jnp.ones((KEYS, 128), BF)

    @pl.when(window == 0)
    def _():
        total[...] = jnp.zeros_like(total)

    field = window_at(info, info[0] * pl.num_programs(1) + window)
    start = slab_start(field, qkv.shape[0])
    slots[...] = slots_from(field, start, qkv)[1].astype(BF)

    lane = iota((SLOT, 128), 1)
    low = lane < HD
    inner = lane % 32
    pairs = width // 128
    queries = []
    for pair in range(pairs):
        at = pair * 128
        q2 = slots[:, at : at + 128]
        k2 = slots[:, width + at : width + at + 128]
        vals[pair, :SLOT, :128] = slots[:, 2 * width + at : 2 * width + at + 128]
        zero = jnp.zeros_like(k2)
        keys[2 * pair, :SLOT, :128] = jnp.where(low, k2, zero)
        keys[2 * pair + 1, :SLOT, :128] = jnp.where(low, zero, k2)
        rel = shift_left(nn_dot(q2, tables[...]), shifts[...])
        rel_hi = rel.astype(BF).astype(F32)
        rel_lo = pltpu.roll(rel - rel_hi, WIN, 1)
        rel = jnp.where(inner < WIN, rel_hi, jnp.where(inner < 2 * WIN, rel_lo, 1.0))
        queries.append(jnp.concatenate([q2 * BF(0.125), rel.astype(BF)], axis=1))
    scores = [nt_dot(queries[head // 2], keys[head]) for head in range(2 * pairs)]
    weights = []
    for head in range(2 * pairs):
        peak = jnp.max(scores[head], axis=1, keepdims=True)
        weights.append(jnp.exp(scores[head] - peak).astype(BF))
        exps[head] = weights[head]
    outs = [nn_dot(weights[head], vals[head // 2]) for head in range(2 * pairs)]
    parts = []
    for pair in range(pairs):
        at = pair * 128
        first, second = outs[2 * pair], outs[2 * pair + 1]
        scale = 1.0 / jnp.where(low, first[:, 128:], second[:, 128:])
        inv[:, at : at + 128] = scale
        parts.append((jnp.where(low, first[:, :128], second[:, :128]) * scale).astype(BF))
    pack = pack_of(field, start)
    total[pl.ds(start, SLAB), :] += nn_dot(pack, jnp.concatenate(parts, axis=1))

    @pl.when(window == pl.num_programs(1) - 1)
    def _():
        att[...] = total[...].astype(BF)


def attend(qkv, info, tables, shifts, onehot, base, count, held, cols, per):
    rows = qkv.shape[0]
    width = D // cols
    pairs = width // 128
    held = list(held)
    return pl.pallas_call(
        partial(attend_kernel, width, len(held)),
        out_shape=[
            jax.ShapeDtypeStruct((rows, D), BF),
            jax.ShapeDtypeStruct((D // HD, per * SLOT, KEYS), BF),
            jax.ShapeDtypeStruct((per * SLOT, D), F32),
        ],
        grid_spec=pltpu.PrefetchScalarGridSpec(
            num_scalar_prefetch=1,
            grid=(count, per),
            in_specs=[
                pl.BlockSpec((rows, 3 * width), lambda c, w, s: (0, c + base)),
                pl.BlockSpec((128, 128), lambda c, w, s: (0, 0)),
                pl.BlockSpec((SLOT, 128), lambda c, w, s: (0, 0)),
                pl.BlockSpec((2, KEYS, 128), lambda c, w, s: (0, 0, 0)),
            ]
            + [pl.BlockSpec(memory_space=pl.ANY)] * len(held),
            out_specs=[
                pl.BlockSpec((rows, width), lambda c, w, s: (0, c + base)),
                pl.BlockSpec((2 * pairs, SLOT, KEYS), lambda c, w, s: (c + base, w, 0)),
                pl.BlockSpec((SLOT, width), lambda c, w, s: (w, c + base)),
            ],
            scratch_shapes=[
                pltpu.VMEM((2 * pairs, KEYS, 256), BF),
                pltpu.VMEM((pairs, KEYS, 256), BF),
                pltpu.VMEM((SLOT, 3 * width), BF),
                pltpu.VMEM((rows, width), F32),
            ],
        ),
        input_output_aliases={5 + i: i for i in range(len(held))},
        compiler_params=params(2),
        cost_estimate=cost(58 * count // cols),
        name="attend",
    )(info, qkv, tables, shifts, onehot, *held)


def attend_back_kernel(
    width, held, info, qkv, exps, inv, att, att_grad, tables2, shifts, onehot, *refs
):
    out, table_sum, bias_sum, keys, vals, slots, att_slots, grad_slots, fresh, total = refs[held:]
    window = pl.program_id(1)
    first = (pl.program_id(0) == 0) & (window == 0)

    @pl.when(first)
    def _():
        for head in range(2 * (width // 128)):
            keys[head, :, :128] = jnp.zeros((KEYS, 128), BF)
            keys[head, :, 128:] = onehot[head % 2]
        vals[...] = jnp.zeros_like(vals)
        table_sum[...] = jnp.zeros_like(table_sum)

    @pl.when(window == 0)
    def _():
        bias_sum[...] = jnp.zeros_like(bias_sum)
        total[...] = jnp.zeros_like(total)

    field = window_at(info, info[0] * pl.num_programs(1) + window)
    start = slab_start(field, qkv.shape[0])
    pick, pulled = slots_from(field, start, qkv)
    slots[...] = pulled.astype(BF)
    att_slots[...] = nn_dot(pick[:, :SLAB], att[pl.ds(start, SLAB), :])
    grad_slots[...] = nn_dot(pick[:, :SLAB], att_grad[pl.ds(start, SLAB), :])

    lane = iota((SLOT, 128), 1)
    low = lane < HD
    inner = lane % 32
    pairs = width // 128
    q_all, grads, dots = [], [], []
    for pair in range(pairs):
        at = pair * 128
        q2 = slots[:, at : at + 128]
        k2 = slots[:, width + at : width + at + 128]
        v2 = slots[:, 2 * width + at : 2 * width + at + 128]
        zero = jnp.zeros_like(k2)
        keys[2 * pair, :SLOT, :128] = jnp.where(low, k2, zero)
        keys[2 * pair + 1, :SLOT, :128] = jnp.where(low, zero, k2)
        vals[2 * pair, :SLOT, :] = jnp.where(low, v2, zero)
        vals[2 * pair + 1, :SLOT, :] = jnp.where(low, zero, v2)
        grad = (grad_slots[:, at : at + 128] * inv[:, at : at + 128]).astype(BF)
        cross = grad.astype(F32) * att_slots[:, at : at + 128]
        dots.append(jnp.sum(jnp.where(low, cross, 0.0), axis=1, keepdims=True))
        dots.append(jnp.sum(jnp.where(low, 0.0, cross), axis=1, keepdims=True))
        q_all.append(q2)
        grads.append(grad)
    probs_grads = [nt_dot(grads[head // 2], vals[head]) for head in range(2 * pairs)]
    scores_grads = []
    for head in range(2 * pairs):
        weights = exps[head].astype(F32)
        scores_grads.append((weights * (probs_grads[head] - dots[head])).astype(BF))
    for pair in range(pairs):
        at = pair * 128
        q2, grad = q_all[pair], grads[pair]
        zero = jnp.zeros_like(grad)
        q_scaled = q2 * BF(0.125)
        grad_heads = (jnp.where(low, grad, zero), jnp.where(low, zero, grad))
        q_heads = (jnp.where(low, q_scaled, zero), jnp.where(low, zero, q_scaled))
        q_sum, k_sum, v_sum = None, None, None
        for head in range(2):
            which = 2 * pair + head
            q_part = nn_dot(scores_grads[which], keys[which])
            k_part = tn_dot(scores_grads[which], q_heads[head])
            v_part = tn_dot(exps[which], grad_heads[head])
            q_sum = q_part if q_sum is None else q_sum + q_part
            k_sum = k_part if k_sum is None else k_sum + k_part
            v_sum = v_part if v_sum is None else v_sum + v_part
        rel = shift_right(jnp.where(inner < WIN, q_sum[:, 128:], 0.0), shifts[...])
        rel_hi = rel.astype(BF)
        rel_lo = (rel - rel_hi.astype(F32)).astype(BF)
        rel2 = jnp.concatenate([rel_hi, rel_lo], axis=1)
        q_grad = q_sum[:, :128] * 0.125 + nt_dot(rel2, tables2[...])
        table_sum[...] += tn_dot(q2, rel2)
        v_grad = v_sum[:SLOT]
        fresh[:, at : at + 128] = q_grad.astype(BF)
        fresh[:, width + at : width + at + 128] = k_sum[:SLOT].astype(BF)
        fresh[:, 2 * width + at : 2 * width + at + 128] = v_grad.astype(BF)
        bias_sum[:, at : at + 128] += eight(q_grad)
        bias_sum[:, 2 * width + at : 2 * width + at + 128] += eight(v_grad)
    pack = pack_of(field, start)
    total[pl.ds(start, SLAB), :] += nn_dot(pack, fresh[...])

    @pl.when(window == pl.num_programs(1) - 1)
    def _():
        out[...] = total[...].astype(BF)


def attend_back(
    qkv, info, exps, inv, att, att_grad, tables, shifts, onehot, base, count, held, cols, per
):
    rows = qkv.shape[0]
    width = D // cols
    pairs = width // 128
    tables2 = jnp.concatenate([tables, tables], axis=1)
    row_spec = pl.BlockSpec((rows, width), lambda c, w, s: (0, c + base))
    qkv_spec = pl.BlockSpec((rows, 3 * width), lambda c, w, s: (0, c + base))
    held = list(held)
    return pl.pallas_call(
        partial(attend_back_kernel, width, len(held)),
        out_shape=[
            jax.ShapeDtypeStruct((rows, 3 * D), BF),
            jax.ShapeDtypeStruct((128, 256), F32),
            jax.ShapeDtypeStruct((8, count * 3 * width), F32),
        ],
        grid_spec=pltpu.PrefetchScalarGridSpec(
            num_scalar_prefetch=1,
            grid=(count, per),
            in_specs=[
                qkv_spec,
                pl.BlockSpec((2 * pairs, SLOT, KEYS), lambda c, w, s: (c + base, w, 0)),
                pl.BlockSpec((SLOT, width), lambda c, w, s: (w, c + base)),
                row_spec,
                row_spec,
                pl.BlockSpec((128, 256), lambda c, w, s: (0, 0)),
                pl.BlockSpec((SLOT, 128), lambda c, w, s: (0, 0)),
                pl.BlockSpec((2, KEYS, 128), lambda c, w, s: (0, 0, 0)),
            ]
            + [pl.BlockSpec(memory_space=pl.ANY)] * len(held),
            out_specs=[
                qkv_spec,
                pl.BlockSpec((128, 256), lambda c, w, s: (0, 0)),
                pl.BlockSpec((8, 3 * width), lambda c, w, s: (0, c)),
            ],
            scratch_shapes=[
                pltpu.VMEM((2 * pairs, KEYS, 256), BF),
                pltpu.VMEM((2 * pairs, KEYS, 128), BF),
                pltpu.VMEM((SLOT, 3 * width), BF),
                pltpu.VMEM((SLOT, width), F32),
                pltpu.VMEM((SLOT, width), F32),
                pltpu.VMEM((SLOT, 3 * width), BF),
                pltpu.VMEM((rows, 3 * width), F32),
            ],
        ),
        input_output_aliases={9 + i: i for i in range(len(held))},
        compiler_params=params(2),
        cost_estimate=cost(54 * count // cols),
        name="attend_back",
    )(info, qkv, exps, inv, att, att_grad, tables2, shifts, onehot, *held)


def split_table(total):
    total = (total[:, :128] + total[:, 128:]).reshape(2, HD, 2, 2, 32)
    both = total[0, :, 0] + total[1, :, 1]
    both = jnp.transpose(both, (1, 2, 0))[:, :27][:, ::-1]
    return both[0], both[1]


def col_exchange(values):
    return lax.all_to_all(values, "col", 0, 0, tiled=True)


def row_swap(values, bit, nr):
    return lax.ppermute(values, "row", [(i, i ^ bit) for i in range(nr)])


def after(values, *others):
    return lax.optimization_barrier((values, *others))[0]


def gather_cols(shard, cols):
    return col_exchange(jnp.broadcast_to(shard[None], (cols,) + shard.shape))


def gather_rows(stack, nr, flip):
    order = outer_bits(nr)
    order = order[::-1] if flip else order
    held = stack[None]
    for bit in order[:-1]:
        fresh = row_swap(held, bit, nr)
        gate = yield [fresh]
        held = jnp.concatenate([held, after(fresh, *(gate or ()))], axis=0)
    fresh = row_swap(held, order[-1], nr)
    gate = yield [held, fresh]
    bufs = [held, after(fresh, *(gate or ()))]
    bufs = bufs + [row_swap(buf, 1, nr) for buf in bufs]
    yield bufs


class Hops(list):
    def __init__(self, arrived, sent):
        super().__init__(arrived)
        self.sent = sent


def last_terms(stages):
    found = stages.send(None)
    while isinstance(found, Hops):
        found = stages.send(None)
    return found


def place_of(step, free, fixed, weights):
    total = sum(weights[b] for b in fixed)
    for i, bit in enumerate(free):
        total = total + ((step >> i) & 1) * weights[bit]
    return total


def add_kernel(counts, *refs):
    at = 0
    outs = refs[sum(counts) :]
    for count, out in zip(counts, outs):
        total = refs[at][...].astype(F32)
        for ref in refs[at + 1 : at + count]:
            total = total + ref[...].astype(F32)
        out[...] = total.astype(BF)
        at += count


def split_kernel(counts, axis, lane, *refs):
    out = refs[sum(counts)]
    for k in range(out.shape[0]):
        at = 0
        for h, count in enumerate(counts):
            total = refs[at][0, k].astype(F32)
            for ref in refs[at + 1 : at + count]:
                total = total + ref[0, k].astype(F32)
            at += count
            high, wide = total.shape
            row = h * high if axis == -2 else 0
            col = lane + (h * wide if axis == -1 else 0)
            out[k, row : row + high, col : col + wide] = total.astype(out.dtype)


def reduce_weight(keep, send, axis, cols, nr):
    arrived = row_swap(send, 1, nr)
    gate = yield [arrived]
    bits = outer_bits(nr)
    _, _, bw, n = keep.shape
    shape = [bw, n]
    halves = 1
    if axis is not None:
        halves = 2
        shape[axis] //= 2
    block = (1, cols, shape[0], shape[1])
    terms = [[(keep, bits, True), (arrived, bits, True)] for _ in range(halves)]
    left = [list(bits) for _ in range(halves)]

    def spec(term, h, free, fixed):
        _, own, whole = term
        weights = {b: 1 << i for i, b in enumerate(own)}

        def place(step):
            spot = [place_of(step, free, fixed, weights), 0, 0, 0]
            if whole and axis is not None:
                spot[axis] = h
            return tuple(spot)

        return pl.BlockSpec(block, place)

    for step in range(len(bits)):
        sizes, specs, arrays, taken = [], [], [], []
        for h in range(halves):
            bit = bits[step] if h else bits[-1 - step]
            left[h].remove(bit)
            taken.append(bit)
            sizes.append(len(terms[h]))
            for term in terms[h]:
                specs.append(spec(term, h, left[h], [bit]))
                arrays.append(term[0])
        count = 1 << len(left[0])
        arrays[0] = after(arrays[0], *(gate or ()))
        out_spec = pl.BlockSpec(block, lambda i: (i, 0, 0, 0))
        outs = pl.pallas_call(
            partial(add_kernel, sizes),
            out_shape=[jax.ShapeDtypeStruct((count,) + block[1:], BF)] * halves,
            grid=(count,),
            in_specs=specs,
            out_specs=[out_spec] * halves,
            compiler_params=params(),
            cost_estimate=cost(3),
            name="add_rows",
        )(*arrays)
        fresh = [row_swap(out, bit, nr) for out, bit in zip(outs, taken)]
        for h in range(halves):
            terms[h].append((fresh[h], list(left[h]), False))
        gate = yield Hops(fresh, outs)

    sizes = [len(t) for t in terms]
    specs = [spec(term, h, [], []) for h in range(halves) for term in terms[h]]
    arrays = [term[0] for h in range(halves) for term in terms[h]]
    yield sizes, axis, specs, arrays, (cols, bw, n)


def add_cols_kernel(groups, *refs):
    outs = refs[-1]
    at, lane = 0, 0
    for sizes, axis, n in groups:
        count = sum(sizes)
        split_kernel(sizes, axis, lane, *refs[at : at + count], outs)
        at += count
        lane += n


def finish_weights(parts, *gate, last=()):
    cols, bw, _ = parts[0][4]
    groups = [(sizes, axis, shape[2]) for sizes, axis, _, _, shape in parts]
    wide = sum(n for _, _, n in groups)
    arrays = [array for part in parts for array in part[3]]
    arrays[0] = after(arrays[0], *gate)
    outs = pl.pallas_call(
        partial(add_cols_kernel, groups),
        out_shape=jax.ShapeDtypeStruct((cols, bw, wide), BF),
        grid=(1,),
        in_specs=[sp for part in parts for sp in part[2]],
        out_specs=pl.BlockSpec((cols, bw, wide), lambda i: (0, 0, 0)),
        compiler_params=params(),
        cost_estimate=cost(3),
        name="add_cols",
    )(*arrays)
    outs = after(outs, *last)
    return outs, col_exchange(outs)


def last_sum(arrived, sizes, *gate):
    total = jnp.sum(after(arrived, *gate).astype(F32), axis=0)
    found, lane = [], 0
    for n in sizes:
        found.append(total[:, lane : lane + n])
        lane += n
    return found


def sum_cols(by_place, whole, me, cols):
    size = by_place.shape[1]
    if whole is not None:
        whole = jnp.broadcast_to(whole, (cols,) + whole.shape)
        by_place = jnp.concatenate([by_place, whole], axis=1)
    arrived = [lax.dynamic_index_in_dim(by_place, me, 0, keepdims=False)]
    for k in range(1, cols):
        sent = lax.dynamic_index_in_dim(by_place, me ^ k, 0, keepdims=False)
        arrived.append(lax.ppermute(sent, "col", [(i, i ^ k) for i in range(cols)]))
    gate = yield arrived[1:]
    arrived = list(lax.optimization_barrier((*arrived, *(gate or ())))[:cols])
    order = me ^ jnp.arange(cols, dtype=jnp.int32)
    total = jnp.sum(pick_rows(jnp.stack(arrived), order), axis=0)
    yield total[:size], total[size:]


def sum_rows(total, nr):
    bit = 1
    while bit < nr:
        total = total + row_swap(total, bit, nr)
        yield total
        bit *= 2


def pick_rows(values, order):
    rows = jnp.arange(values.shape[0], dtype=jnp.int32)
    chosen = (order[:, None] == rows[None, :]).reshape(order.shape + rows.shape + (1,) * (values.ndim - 1))
    return jnp.sum(jnp.where(chosen, values[None], 0.0), axis=1)


def body(
    cols,
    nr,
    tokens_in,
    pad_offsets,
    norm1_gain,
    norm1_bias,
    qkv_weight,
    qv_bias,
    table_height,
    table_width,
    proj_weight,
    proj_bias,
    norm2_gain,
    norm2_bias,
    fc1_weight,
    fc1_bias,
    fc2_weight,
    fc2_bias,
    out_grad,
):
    width = D // cols
    bw = D // nr
    per = -(-WINDOWS // cols)
    me = lax.axis_index("col").astype(jnp.int32)
    my_row = lax.axis_index("row").astype(jnp.int32)
    sets, rows = window_sets(cols, per)
    info = plan(sets, pad_offsets)
    row_order = my_row ^ jnp.arange(nr, dtype=jnp.int32)

    hidden = fc1_weight.shape[1]
    half = hidden // 2
    fc2_t = fc2_weight.T
    qkv_own = jnp.transpose(qkv_weight, (1, 0, 2))
    qkv_stack = jnp.stack(
        [qkv_own]
        + [lax.ppermute(qkv_own, "col", [(i, i ^ k) for i in range(cols)]) for k in range(1, cols)]
    )
    x_sent = spread(tokens_in, info, cols, per, rows)
    x_pieces = col_exchange(x_sent)
    qkv_stack = after(qkv_stack, x_sent)
    hop_a = gather_rows(qkv_stack[:, :, : bw // 2], nr, False)
    hop_b = gather_rows(qkv_stack[:, :, bw // 2 :], nr, True)
    first_a, first_b = next(hop_a), next(hop_b)
    g_sent = spread(after(out_grad, *first_a, *first_b), info, cols, per, rows)
    for _ in outer_bits(nr)[1:]:
        first_a, first_b = hop_a.send(None), hop_b.send(None)
    qkv_a, qkv_b = hop_a.send((g_sent,)), hop_b.send((g_sent,))
    small_args = (norm1_gain, proj_bias, fc2_bias, qv_bias, fc1_bias)
    norm1_gain, proj_bias, fc2_bias, qv_bias, fc1_bias = lax.optimization_barrier(
        (*small_args, *qkv_a, *qkv_b)
    )[:5]
    vec = jnp.concatenate(
        [
            norm1_gain,
            norm1_bias,
            norm2_gain,
            norm2_bias,
            proj_bias.astype(F32),
            fc2_bias.astype(F32),
            qv_bias[0].astype(F32),
            qv_bias[1].astype(F32),
            fc1_bias.astype(F32),
        ]
    )
    vecs = [vec] + [lax.ppermute(vec, "col", [(i, i ^ k) for i in range(cols)]) for k in range(1, cols)]
    vecs = pick_rows(jnp.stack(vecs), me ^ jnp.arange(cols, dtype=jnp.int32))
    wide0 = jnp.concatenate([fc1_weight[:, :half], proj_weight.T, fc2_t[:, :half]], axis=1)
    wide1 = jnp.concatenate([fc1_weight[:, half:], fc2_t[:, half:]], axis=1)
    stack0 = gather_cols(after(wide0, x_pieces, *qkv_a, *qkv_b), cols)
    first = half + width
    features = vecs[:, : 6 * width].reshape(cols, 6, width // bw, bw)
    features = features.transpose(0, 2, 1, 3).reshape(nr, 6, bw)
    features = pick_rows(features, row_order).transpose(1, 0, 2).reshape(6, 1, D)
    gain1, bias1, gain2, bias2, bias_p, bias_2 = [features[i] for i in range(6)]
    q_bias = vecs[:, 6 * width : 7 * width]
    v_bias = vecs[:, 7 * width : 8 * width]
    bias_qkv = jnp.stack([q_bias, jnp.zeros_like(q_bias), v_bias], axis=1).reshape(1, 3 * D)
    bias_h = vecs[:, 8 * width :]

    x_full, n1, qkv = norm_qkv(
        after(x_pieces, g_sent), qkv_a, qkv_b, info, gain1, bias1, bias_qkv, cols, rows, nr
    )
    shifts_np, onehot_np = rel_constants()
    shifts = jnp.asarray(shifts_np)
    onehot = jnp.asarray(onehot_np, BF)
    tables = table_matrix(table_height, table_width)
    stack1 = gather_cols(after(wide1, stack0), cols)
    held = ()
    arrived = []
    bits = outer_bits(nr)
    for part, base in enumerate(range(0, cols, cols // SPLITS)):
        held = attend(
            after(qkv, *arrived),
            info,
            tables,
            shifts,
            onehot,
            base,
            cols // SPLITS,
            held,
            cols,
            per,
        )
        att = held[0]
        arrived = []
        if part == 0:
            stack0 = after(stack0, att)
            hops0 = [
                gather_rows(stack0[:, :, :first], nr, False),
                gather_rows(stack0[:, :, first:], nr, True),
            ]
            bufs0 = [next(hop) for hop in hops0]
        if part == 1:
            stack1 = after(stack1, att)
            g_pieces = col_exchange(after(g_sent, stack1))
            bufs0 = [hop.send((att, *bufs0[0], *bufs0[1])) for hop in hops0]
            arrived = [stack1]
        if part == 3:
            for _ in range(len(bits) - 2):
                bufs0 = [hop.send(None) for hop in hops0]
            bufs0 = [hop.send((att, *bufs0[0], *bufs0[1])) for hop in hops0]
            stack1 = after(stack1, att)
            hops1 = [
                gather_rows(stack1[:, :, :half], nr, False),
                gather_rows(stack1[:, :, half:], nr, True),
            ]
            bufs1 = [next(hop) for hop in hops1]
    att, exps, inv = held
    resid, n2 = proj_norm(bufs0[0], att, x_full, bias_p, gain2, bias2, cols, rows, nr)
    bufs1 = [hop.send((n2, *bufs1[0], *bufs1[1])) for hop in hops1]
    g_full = join(g_pieces, info, cols, rows, nr)
    fc1_bufs, fc2_bufs = [bufs0[0]], [bufs0[1]]

    acts, grads, sends, hidden_sums = [], [], [], []
    for c in range(2):
        if c == 1:
            for _ in range(len(bits) - 2):
                bufs1 = [hop.send(None) for hop in hops1]
            bufs1 = [hop.send((acts[0], *bufs1[0], *bufs1[1])) for hop in hops1]
            fc1_bufs.append(bufs1[0])
            fc2_bufs.append(bufs1[1])
        act, grad, keep, send, bias_sum = mlp_grads(
            fc1_bufs[c],
            fc2_bufs[c],
            n2,
            g_full,
            bias_h[:, None, c * half : (c + 1) * half],
            cols,
            rows,
            nr,
        )
        acts.append(act)
        grads.append(grad)
        hidden_sums.append(jnp.sum(bias_sum, axis=1))
        sends.append(reduce_weight(keep, send, -1, cols, nr))
    core0, core1 = [next(send) for send in sends]
    rows0 = sends[0].send((*core0, acts[1]))
    block_sent = block_rows(
        fc2_bufs, acts, after(resid, *core1), bias_2, info, cols, rows, nr
    )
    block_pieces = col_exchange(block_sent)
    rows0 = sends[0].send((*rows0, block_sent))
    rows1 = sends[1].send((block_sent,))
    resid_grad, proj_grad, sums2 = mlp_back(
        fc1_bufs,
        grads,
        after(resid, block_sent),
        g_full,
        gain2,
        cols,
        rows,
        nr,
    )
    rows1 = sends[1].send((*rows1, proj_grad))
    att_grad, keep, send = proj_back(
        fc1_bufs[0], after(proj_grad, *rows0), att, cols, rows, nr
    )
    sends.append(reduce_weight(keep, send, None, cols, nr))
    core2 = next(sends[2])
    ratio = width // bw
    places = jnp.arange(cols * ratio, dtype=jnp.int32) ^ my_row

    def by_col(sums):
        count = sums.shape[0]
        blocks = jnp.sum(sums, axis=1).reshape(count, nr, bw).transpose(1, 0, 2)
        picked = pick_rows(blocks, places).reshape(cols, ratio, count, bw)
        return picked.transpose(0, 2, 1, 3).reshape(cols, count * width)

    held, table_sums, bias_sums = (), [], []
    for part, base in enumerate(range(0, cols, cols // SPLITS)):
        arrived = []
        if part == 1:
            done0, arrived0 = finish_weights([last_terms(sends[0])], dqkv, block_pieces)
            rows2 = sends[2].send((*core2, dqkv))
            arrived = [block_pieces, *rows1, done0]
        if part == 2:
            rows2 = sends[2].send((*rows2, dqkv))
        if part == 3:
            arrived = [arrived0]
            done1, arrived1 = finish_weights(
                [last_terms(sends[1]), last_terms(sends[2])], dqkv, arrived0, *rows2
            )
            arrived = [arrived0, done1]
        dqkv, table_sum, bias_sum = attend_back(
            after(qkv, *arrived),
            info,
            exps,
            inv,
            att,
            att_grad,
            tables,
            shifts,
            onehot,
            base,
            cols // SPLITS,
            held,
            cols,
            per,
        )
        held = (dqkv,)
        table_sums.append(table_sum)
        bias_sums.append(bias_sum)
    table_sum = sum(table_sums[1:], table_sums[0])
    bias_sum = jnp.concatenate(bias_sums, axis=1)
    bias_cols = jnp.sum(bias_sum, axis=0).reshape(cols, 3, width)
    table_h_grad, table_w_grad = split_table(table_sum)
    table_flat = jnp.concatenate([table_h_grad.reshape(-1), table_w_grad.reshape(-1)])
    small = jnp.concatenate(
        [by_col(sums2), bias_cols[:, 0], bias_cols[:, 2]] + hidden_sums, axis=1
    )
    early = sum_cols(small, table_flat, me, cols)
    early_arrived = next(early)
    keep, send = qkv_grad(after(n1, dqkv), dqkv, cols, rows, nr)
    sends.append(reduce_weight(keep, send, -2, cols, nr))
    core3 = next(sends[3])
    block_out = collect(after(block_pieces, keep), sets, info, BF)
    rows3 = sends[3].send((*core3, block_out))
    small, table_flat = early.send((block_out,))
    in_sent = input_back(
        qkv_a,
        qkv_b,
        after(dqkv, block_out, arrived1, *early_arrived, *rows3.sent),
        x_full,
        resid_grad,
        gain1,
        info,
        cols,
        rows,
        nr,
    )
    in_pieces = col_exchange(in_sent)
    rows3 = sends[3].send((in_sent,))
    for _ in range(len(outer_bits(nr)) - 2):
        rows3 = sends[3].send(None)
    sizes = [2 * width, small.shape[0], table_flat.shape[0]]
    late = in_pieces[:, rows - TAIL : rows - TAIL + 6].astype(F32).reshape(cols, 2, 3, width)
    done3, arrived3 = finish_weights([sends[3].send(None)], in_sent, last=(in_pieces,))
    late = jnp.sum(after(late, done3), axis=(0, 2)).reshape(-1)
    totals = list(sum_rows(jnp.concatenate([late, small, table_flat]), nr))
    total = totals[-1]
    late, small = total[: sizes[0]], total[sizes[0] : sizes[0] + sizes[1]]
    table_flat = total[sizes[0] + sizes[1] :].reshape(2, 27, HD)
    input_grad = collect(after(in_pieces, totals[0]), sets, info, F32)
    (qkv_w_grad,) = last_sum(arrived3, [3 * width])
    fc_grads = last_sum(arrived0, [2 * half], done3)
    fc_grad, proj_w_grad = last_sum(arrived1, [2 * half, width], done3)
    fc_grads.append(fc_grad)

    def part(i):
        return small[i * width : (i + 1) * width]

    return (
        block_out,
        input_grad,
        late[:width],
        late[width:],
        qkv_w_grad.reshape(bw, 3, width),
        jnp.stack([part(4), part(5)]),
        table_flat[0],
        table_flat[1],
        proj_w_grad.T,
        part(0),
        part(1),
        part(2),
        jnp.concatenate([grad[:, :half] for grad in fc_grads], axis=1),
        small[6 * width :],
        jnp.concatenate([grad[:, half:] for grad in fc_grads], axis=1).T,
        part(3),
    )


def solution(mesh):
    placed = (
        P("row", "col"),
        P("row", None),
        P("col"),
        P("col"),
        P("row", None, "col"),
        P(None, "col"),
        P(),
        P(),
        P("col", "row"),
        P("col"),
        P("col"),
        P("col"),
        P("row", "col"),
        P("col"),
        P("col", "row"),
        P("col"),
        P("row", "col"),
    )
    return jax.shard_map(
        partial(body, mesh.shape["col"], mesh.shape["row"]),
        mesh=mesh,
        in_specs=placed,
        out_specs=(
            P("row", "col"),
            P("row", "col"),
            P("col"),
            P("col"),
            P("row", None, "col"),
            P(None, "col"),
            P(),
            P(),
            P("col", "row"),
            P("col"),
            P("col"),
            P("col"),
            P("row", "col"),
            P("col"),
            P("col", "row"),
            P("col"),
        ),
        check_vma=False,
    )
```
